128 devices in a mesh: dp: 16 (over z_lo, y, core), tensor: 8 (over z_hi, x).
Axes of the slice: x: 4, y: 4, z: 4 (z_hi: 2, z_lo: 2; z = z_hi * 2 + z_lo), core: 2. Of those that a mesh axis runs over, the one named last changes fastest.
Arguments:
- hidden: bfloat16 [16384, 2048], P(('dp', 'tensor')), may hold values from -6 to 6
- routes: int32 [16384, 2], P('dp'), may hold values from 0 to 63, all different within a row; in each aligned block of 1024 rows (0 to 1023, 1024 to 2047, ...) at most 40 rows name the same one
- prefix: int32 [16], P('dp'), may hold values from 1 to 512
- attn_gain: bfloat16 [2048], P('dp'), may hold values from 0.5 to 1.5
- query_proj: bfloat16 [2048, 3072], P('dp', 'tensor'), may hold values from -0.125 to 0.125
- latent_proj: bfloat16 [2048, 576], P('dp'), may hold values from -0.125 to 0.125
- latent_gain: bfloat16 [512], P('dp'), may hold values from 0.5 to 1.5
- expand_proj: bfloat16 [512, 4096], P('dp', 'tensor'), may hold values from -0.25 to 0.25
- output_proj: bfloat16 [2048, 2048], P('tensor', 'dp'), may hold values from -1 to 1
- second_gain: bfloat16 [2048], P('dp'), may hold values from 0.5 to 1.5
- router_proj: bfloat16 [2048, 64], P('dp'), may hold values from -0.09375 to 0.09375
- expert_gate: bfloat16 [64, 1408, 2048], P('dp', 'tensor'), may hold values from -0.125 to 0.125
- expert_up: bfloat16 [64, 1408, 2048], P('dp', 'tensor'), may hold values from -0.125 to 0.125
- expert_down: bfloat16 [64, 1408, 2048], P('dp', 'tensor'), may hold values from -0.15625 to 0.15625
- shared_gate: bfloat16 [2048, 2816], P('dp', 'tensor'), may hold values from -0.125 to 0.125
- shared_up: bfloat16 [2048, 2816], P('dp', 'tensor'), may hold values from -0.125 to 0.125
- shared_down: bfloat16 [2816, 2048], P('tensor', 'dp'), may hold values from -0.109375 to 0.109375
- out_grad: bfloat16 [16384, 2048], P(('dp', 'tensor')), may hold values from -6 to 6
Outputs:
- output: bfloat16 [16384, 2048], P(('dp', 'tensor'))
- hidden_grad: float32 [16384, 2048], P(('dp', 'tensor'))
- attn_gain_grad: float32 [2048], P(('dp', 'tensor'))
- query_proj_grad: float32 [2048, 3072], P('dp', 'tensor')
- latent_proj_grad: float32 [2048, 576], P(('dp', 'tensor'))
- latent_gain_grad: float32 [512], P(('dp', 'tensor'))
- expand_proj_grad: float32 [512, 4096], P('dp', 'tensor')
- output_proj_grad: float32 [2048, 2048], P('tensor', 'dp')
- second_gain_grad: float32 [2048], P(('dp', 'tensor'))
- router_proj_grad: float32 [2048, 64], P(('dp', 'tensor'))
- expert_gate_grad: float32 [64, 1408, 2048], P('dp', 'tensor')
- expert_up_grad: float32 [64, 1408, 2048], P('dp', 'tensor')
- expert_down_grad: float32 [64, 1408, 2048], P('dp', 'tensor')
- shared_gate_grad: float32 [2048, 2816], P('dp', 'tensor')
- shared_up_grad: float32 [2048, 2816], P('dp', 'tensor')
- shared_down_grad: float32 [2816, 2048], P('tensor', 'dp')
The draws below stay inside these ranges and needn't reach their ends.
Inputs may be any that keep to these rules, and one draw needn't show every extreme that they name: `routes`: each row names 2 different experts. Within the rows of one sequence no expert is named more than 40 times, a bound that some block reaches.
All inputs are finite; a program needn't handle non-finite values.
Results may differ from the reference program's by a relative error of at most 0.029.
Values may be sent and summed in bfloat16 or wider, within the bound.
No kernel may reach another device: no remote copies, remote signals or barrier semaphores. Data moves between devices by JAX's collectives and lax.ppermute only.
A program may use at most 320 MiB of HBM per device.

```python
import math
import jax
import jax.numpy as jnp
import numpy as np
from jax import lax

D = 2048
H = 16
DN = 128
DR = 64
DV = 128
KVR = 512
FFE = 1408
SEQ_LEN = 1024
TOP = 2
FFS = 2816
EXPERTS = 64
SEQS = 16
TOKENS = 16384
CAP = 40


def set_ends(array, rng, smallest, high):
    extent = array.shape
    spot = [jax.random.randint(jax.random.fold_in(rng, axis), (), 0, extent[axis]) for axis in range(len(extent))]
    array = array.at[tuple(spot)].set(smallest)
    longest = extent.index(max(extent))
    spot[longest] = (spot[longest] + 1) % extent[longest]
    return array.at[tuple(spot)].set(high)


def level_of(key, extent, split, low, largest):
    factor_of, own = 1.0, jax.random.fold_in(key, 6)
    for dim, parts in split:
        draws = jnp.exp(jax.random.uniform(jax.random.fold_in(own, dim), (parts,), jnp.float32, low / len(split), largest / len(split)))
        factor_of = factor_of * jnp.repeat(draws, extent[dim] // parts).reshape([-1 if axis == dim else 1 for axis in range(len(extent))])
    return factor_of


def routed_block(rng, own, number, rows, number_of, top, limit, slope):
    order = jax.random.permutation(rng, number_of)
    crowded, usual = load_shares(number_of, rows * top, limit, slope, True), load_shares(number_of, rows * top, limit, slope, False)
    places = jnp.arange(number_of)

    def named(tallies, turn):
        used = int((tallies > 0).sum())
        fixed = max(1, used // 4)
        moved = fixed + (places - fixed + turn * (used - fixed)) % max(1, number_of - fixed)
        return jnp.zeros((number_of,), jnp.int32).at[order[jnp.where(places < fixed, places, moved)]].set(jnp.asarray(tallies, jnp.int32))

    tallies = jnp.where(number % 4 == 0, named(crowded, number // 4), named(usual, number - number // 4 - 1))
    mixed = jax.random.permutation(jax.random.fold_in(own, 3), number_of)
    source_of, sink = mixed[0:number_of // 2 * 2:2], mixed[1:number_of // 2 * 2:2]
    room = jnp.minimum(tallies[source_of] - 1, limit - tallies[sink]) // 2
    room = jnp.where((source_of == order[0]) | (sink == order[0]) | (tallies[sink] == 0), 0, jnp.maximum(room, 0))
    moved = jax.random.randint(jax.random.fold_in(own, 4), (number_of // 2,), 0, 1 << 20) % (room + 1)
    tallies = tallies.at[source_of].add(-moved).at[sink].add(moved)
    members = jnp.searchsorted(jnp.cumsum(tallies), jnp.arange(rows * top), side="right").astype(jnp.int32)
    table = members.reshape(top, rows).T
    table = table[jax.random.permutation(jax.random.fold_in(own, 1), rows)]
    turn = jax.random.randint(jax.random.fold_in(own, 2), (rows, 1), 0, top)
    return jnp.take_along_axis(table, (jnp.arange(top)[None, :] + turn) % top, axis=1)


def load_shares(number_of, total, reach, lean, full):
    loads = [(1 << 20) // math.isqrt(standing ** lean) + 1 for standing in range(1, number_of + 1)]
    largest = reach if full else min(reach, max(-(-total // number_of), total * loads[0] // sum(loads)))
    least = 1 if total - largest >= number_of - 1 else 0
    counts, rest = [largest] + [least] * (number_of - 1), total - largest - least * (number_of - 1)
    while rest > 0:
        free = [i for i in range(1, number_of) if counts[i] < largest] or [i for i in range(1, number_of) if counts[i] < reach]
        pool, budget = sum([loads[i] for i in free]), rest
        for i in free:
            extra = min(reach - counts[i], max(1, budget * loads[i] // pool), rest)
            counts[i] = counts[i] + extra
            rest = rest - extra
    return np.array(counts)


def centred(own_key, dims, scale, bound, cuts=(), held_as=jnp.bfloat16):
    values = scale * jax.random.normal(own_key, dims, jnp.float32)
    if cuts:
        values = values * level_of(own_key, dims, cuts, -0.22, 0.18)
    return jnp.clip(values, -bound, bound).astype(held_as)


def setup_inputs(seed: int = 0) -> dict:
    key_of = jax.random.split(jax.random.key(seed), 19)
    hidden = centred(key_of[0], (TOKENS, D), 1.0, 6.0, ((0, 128),))
    routes_keys = jax.random.split(jax.random.fold_in(key_of[1], 1), TOKENS // SEQ_LEN)
    routes_turns = jax.random.permutation(jax.random.fold_in(key_of[1], 3), TOKENS // SEQ_LEN)
    routes = jax.vmap(lambda own, number: routed_block(jax.random.fold_in(key_of[1], 2), own, number, SEQ_LEN, EXPERTS, TOP, CAP, 1))(routes_keys, routes_turns).reshape((TOKENS, TOP))
    prefix = set_ends(jax.random.randint(key_of[2], (SEQS,), 1, SEQ_LEN // 2 + 1), jax.random.fold_in(key_of[2], 1), 1, (SEQ_LEN // 2 + 1) - 1).astype(jnp.int32)
    attn_gain = jnp.clip(1.0 + 0.1 * jax.random.normal(key_of[3], (D,), jnp.float32), 0.5, 1.5).astype(jnp.bfloat16)
    query_proj = centred(key_of[4], (D, H * (DN + DR)), D ** -0.5, 0.125, ((0, 16), (1, 8)))
    latent_proj = centred(key_of[5], (D, KVR + DR), D ** -0.5, 0.125, ((0, 16),))
    latent_gain = jnp.clip(1.0 + 0.1 * jax.random.normal(key_of[6], (KVR,), jnp.float32), 0.5, 1.5).astype(jnp.bfloat16)
    expand_proj = centred(key_of[7], (KVR, H * (DN + DV)), KVR ** -0.5, 0.25, ((0, 16), (1, 8)))
    output_proj = centred(key_of[8], (H * DV, D), (H * DV // 64) ** -0.5, 1.0, ((0, 8), (1, 16)))
    second_gain = jnp.clip(1.0 + 0.1 * jax.random.normal(key_of[9], (D,), jnp.float32), 0.5, 1.5).astype(jnp.bfloat16)
    router_proj = centred(key_of[10], (D, EXPERTS), (2 * D) ** -0.5, 0.09375, ((0, 16),))
    expert_gate = centred(key_of[11], (EXPERTS, FFE, D), D ** -0.5, 0.125, ((0, 16), (1, 8)))
    expert_up = centred(key_of[12], (EXPERTS, FFE, D), D ** -0.5, 0.125, ((0, 16), (1, 8)))
    expert_down = centred(key_of[13], (EXPERTS, FFE, D), FFE ** -0.5, 0.15625, ((0, 16), (1, 8)))
    shared_gate = centred(key_of[14], (D, FFS), D ** -0.5, 0.125, ((0, 16), (1, 8)))
    shared_up = centred(key_of[15], (D, FFS), D ** -0.5, 0.125, ((0, 16), (1, 8)))
    shared_down = centred(key_of[16], (FFS, D), FFS ** -0.5, 0.109375, ((0, 8), (1, 16)))
    out_grad = centred(key_of[17], (TOKENS, D), 1.0, 6.0, ((0, 128),))
    return dict(hidden=hidden, routes=routes, prefix=prefix, attn_gain=attn_gain, query_proj=query_proj, latent_proj=latent_proj, latent_gain=latent_gain, expand_proj=expand_proj, output_proj=output_proj, second_gain=second_gain, router_proj=router_proj, expert_gate=expert_gate, expert_up=expert_up, expert_down=expert_down, shared_gate=shared_gate, shared_up=shared_up, shared_down=shared_down, out_grad=out_grad)


@jax.custom_vjp
def low(v):
    return lax.optimization_barrier(v.astype(jnp.bfloat16)).astype(jnp.float32)

@jax.custom_vjp
def low_back(v):
    return v

def low_keep(v):
    return (low(v), None)

def low_pass(kept, grad):
    return (grad,)

def back_keep(v):
    return (v, None)

def back_low(kept, grad):
    return (low(grad),)
low.defvjp(low_keep, low_pass)
low_back.defvjp(back_keep, back_low)
EPS = 1e-06
HIGH = lax.Precision.HIGHEST
MASKED = -1e+30

def matmul(operand, weights):
    return jnp.dot(operand, weights, precision=HIGH)

def norm_scale(values):
    return lax.rsqrt(lax.optimization_barrier(jnp.mean(values * values, -1, keepdims=True)) + EPS)

def rope_tables(positions, rope_width):
    half_width = rope_width // 2
    frequency = 10000.0 ** (-2.0 * jnp.arange(half_width).astype(jnp.float32) / rope_width)
    angles = positions.astype(jnp.float32)[:, None] * frequency[None, :]
    return (jnp.cos(angles), jnp.sin(angles))

def rotate(vectors, cosines, sine_values):
    half_width = vectors.shape[-1] // 2
    front_half = vectors[..., :half_width]
    back_half = vectors[..., half_width:]
    return jnp.concatenate([front_half * cosines - back_half * sine_values, back_half * cosines + front_half * sine_values], -1)

def attend(packed):
    queries, keys_nope, key_rope, values, prefix_len = packed
    score_scale = 1.0 / math.sqrt(DN + DR)
    raw_scores = jnp.einsum('qhd,khd->hqk', queries[..., :DN], keys_nope, precision=HIGH)
    raw_scores = raw_scores + jnp.einsum('qhr,kr->hqk', queries[..., DN:], key_rope, precision=HIGH)
    scores = low_back(raw_scores * score_scale)
    places = jnp.arange(SEQ_LEN)
    visible = (places[None, :] <= places[:, None]) | (places[None, :] < prefix_len)
    masked = jnp.where(visible[None], scores, MASKED)
    soft_weights = jax.nn.softmax(masked, axis=-1)
    mixed_heads = jnp.einsum('hqk,khv->qhv', low(soft_weights), values, precision=HIGH)
    return low(low_back(mixed_heads)).reshape(SEQ_LEN, H * DV)

def reference(hidden, routes, prefix, attn_gain, query_proj, latent_proj, latent_gain, expand_proj, output_proj, second_gain, router_proj, expert_gate, expert_up, expert_down, shared_gate, shared_up, shared_down, out_grad):
    flat_routes = routes.reshape(SEQS, SEQ_LEN * TOP).astype(jnp.int32)
    flat_hot = (flat_routes[:, :, None] == jnp.arange(EXPERTS).astype(jnp.int32)[None, None, :]).astype(jnp.int32)
    earlier = jnp.cumsum(flat_hot, 1) - flat_hot
    slot_pos = lax.optimization_barrier(jnp.sum(earlier * flat_hot, -1)).astype(jnp.int32)
    seq_ids = jnp.arange(SEQS).astype(jnp.int32)[:, None]
    global_slot = (flat_routes * (SEQS * CAP) + seq_ids * CAP + slot_pos).astype(jnp.int32)
    token_ids = (seq_ids * SEQ_LEN + jnp.arange(SEQ_LEN * TOP).astype(jnp.int32)[None, :] // TOP).astype(jnp.int32)
    slot_token = jnp.full((EXPERTS * SEQS * CAP,), TOKENS, jnp.int32).at[global_slot.reshape(-1)].set(token_ids.reshape(-1))
    assign_slot = global_slot.reshape(TOKENS * TOP)
    positions = jnp.arange(TOKENS).astype(jnp.int32) % SEQ_LEN
    cosines, sine_values = rope_tables(positions, DR)

    def forward(hidden_f, attn_gains, query_weights, latent_weights, kv_gains, expand_weights, output_weights, second_gains, router_weights, gate_experts, up_experts, down_experts, gate_shared, up_shared, down_shared):
        normed = low(hidden_f * norm_scale(hidden_f) * attn_gains)
        latent = low_back(matmul(normed, latent_weights))
        compressed = latent[:, :KVR]
        kv_latent = low(jnp.concatenate([compressed * norm_scale(compressed) * kv_gains, rotate(latent[:, KVR:], cosines, sine_values)], -1))
        query_raw = low_back(matmul(normed, query_weights)).reshape(TOKENS, H, DN + DR)
        queries = low(low_back(jnp.concatenate([query_raw[..., :DN], rotate(query_raw[..., DN:], cosines[:, None, :], sine_values[:, None, :])], -1)))
        expanded = matmul(kv_latent[:, :KVR], expand_weights).reshape(TOKENS, H, DN + DV)
        keys_nope = low(low_back(expanded[..., :DN]))
        values = low(low_back(expanded[..., DN:]))
        mixed_heads = lax.map(jax.checkpoint(attend), (queries.reshape(SEQS, SEQ_LEN, H, DN + DR), keys_nope.reshape(SEQS, SEQ_LEN, H, DN), kv_latent[:, KVR:].reshape(SEQS, SEQ_LEN, DR), values.reshape(SEQS, SEQ_LEN, H, DV), prefix))
        branch = low_back(matmul(mixed_heads.reshape(TOKENS, H * DV), output_weights))
        residual = hidden_f + branch
        normed_two = low(residual * norm_scale(residual) * second_gains)
        logits = matmul(normed_two, router_weights)
        gate_values = jax.nn.softmax(jnp.take_along_axis(logits, routes, axis=1), axis=-1)
        padded = jnp.concatenate([normed_two, jnp.zeros((1, D), normed_two.dtype)], 0)

        def expert_rows(packed):
            gate_matrix, up_matrix, down_matrix, row_index = packed
            expert_in = jnp.take(padded, row_index, axis=0)
            gate_pre = low_back(matmul(expert_in, gate_matrix.T))
            up_pre = low_back(matmul(expert_in, up_matrix.T))
            return low_back(matmul(low(jax.nn.silu(gate_pre) * up_pre), down_matrix))
        expert_out = lax.map(jax.checkpoint(expert_rows), (gate_experts, up_experts, down_experts, slot_token.reshape(EXPERTS, SEQS * CAP)))
        picked = jnp.take(expert_out.reshape(EXPERTS * SEQS * CAP, D), assign_slot, axis=0).reshape(TOKENS, TOP, D)
        shared_pre_gate = low_back(matmul(normed_two, gate_shared))
        shared_pre_up = low_back(matmul(normed_two, up_shared))
        shared_out = matmul(low(jax.nn.silu(shared_pre_gate) * shared_pre_up), down_shared)
        return residual + shared_out + lax.optimization_barrier(jnp.sum(gate_values[:, :, None] * picked, 1))
    arguments = (hidden.astype(jnp.float32), attn_gain.astype(jnp.float32), query_proj.astype(jnp.float32), latent_proj.astype(jnp.float32), latent_gain.astype(jnp.float32), expand_proj.astype(jnp.float32), output_proj.astype(jnp.float32), second_gain.astype(jnp.float32), router_proj.astype(jnp.float32), expert_gate.astype(jnp.float32), expert_up.astype(jnp.float32), expert_down.astype(jnp.float32), shared_gate.astype(jnp.float32), shared_up.astype(jnp.float32), shared_down.astype(jnp.float32))
    result, pullback = jax.vjp(forward, *arguments)
    gradients = pullback(out_grad.astype(jnp.float32))
    return (result.astype(jnp.bfloat16), gradients[0], gradients[1], gradients[2], gradients[3], gradients[4], gradients[5], gradients[6], gradients[7], gradients[8], gradients[9], gradients[10], gradients[11], gradients[12], gradients[13], gradients[14])
```

```python
import math

import jax
import jax.numpy as jnp
from jax import lax
from jax.experimental import pallas as pl
from jax.experimental.pallas import tpu as pltpu
from jax.sharding import PartitionSpec as P

D = 2048
DN = 128
DR = 64
DV = 128
KVR = 512


EPS = 1e-06
HIGH = lax.Precision.HIGHEST
MASKED = -1e30


def norm_scale(values):
    return lax.rsqrt(jnp.mean(values * values, -1, keepdims=True) + EPS)


def norm_back(values, scales, gains, upstream):
    weighted = gains * upstream
    return scales * weighted - values * scales**3 * jnp.mean(values * weighted, -1, keepdims=True)


def rope_tables(positions, rope_width):
    half_width = rope_width // 2
    frequency = 10000.0 ** (-2.0 * jnp.arange(half_width).astype(jnp.float32) / rope_width)
    angles = positions.astype(jnp.float32)[:, None] * frequency[None, :]
    return (jnp.cos(angles), jnp.sin(angles))


def rotate(vectors, cosines, sine_values):
    half_width = vectors.shape[-1] // 2
    front_half = vectors[..., :half_width]
    back_half = vectors[..., half_width:]
    return jnp.concatenate(
        [
            front_half * cosines - back_half * sine_values,
            back_half * cosines + front_half * sine_values,
        ],
        -1,
    )


def rotate_back(gradients, cosines, sine_values):
    half_width = gradients.shape[-1] // 2
    front_half = gradients[..., :half_width]
    back_half = gradients[..., half_width:]
    return jnp.concatenate(
        [
            front_half * cosines + back_half * sine_values,
            back_half * cosines - front_half * sine_values,
        ],
        -1,
    )


def round_trip(values):
    return lax.optimization_barrier(values.astype(jnp.bfloat16)).astype(jnp.float32)


def block_scores(query_block, keys_nope, key_rope, rows_start, prefix_len, score_scale):
    raw_scores = jnp.einsum(
        "qhd,khd->hqk", query_block[..., :DN], keys_nope, preferred_element_type=jnp.float32
    )
    raw_scores = raw_scores + jnp.einsum(
        "qhr,kr->hqk", query_block[..., DN:], key_rope, preferred_element_type=jnp.float32
    )
    query_places = rows_start + jnp.arange(query_block.shape[0])
    key_places = jnp.arange(keys_nope.shape[0])
    visible = (key_places[None, :] <= query_places[:, None]) | (key_places[None, :] < prefix_len)
    return jnp.where(visible[None], raw_scores * score_scale, MASKED)


def silu_back(act_grad, gate_pre, up_pre, sigmoid_gate):
    up_grad = (act_grad * gate_pre * sigmoid_gate).astype(jnp.bfloat16)
    gate_grad = (act_grad * up_pre * sigmoid_gate * (1.0 + gate_pre * (1.0 - sigmoid_gate))).astype(
        jnp.bfloat16
    )
    return (gate_grad, up_grad)


def dispatch_kernel(tok_ref, rows_hbm, grads_hbm, col_ref, out_ref, rows_buf, grads_buf, sems):
    block = rows_buf.shape[0]
    tile_rows = rows_buf.shape[1]
    last = rows_hbm.shape[0] - 1
    base = pl.program_id(0) * block

    def start(r, carry):
        tok = jnp.minimum(tok_ref[base + r], last)
        pltpu.make_async_copy(rows_hbm.at[tok], rows_buf.at[r], sems.at[0, r]).start()
        pltpu.make_async_copy(grads_hbm.at[tok], grads_buf.at[r], sems.at[1, r]).start()
        return carry

    lax.fori_loop(0, block, start, 0)

    def finish(r, carry):
        pltpu.make_async_copy(rows_hbm.at[0], rows_buf.at[r], sems.at[0, r]).wait()
        pltpu.make_async_copy(grads_hbm.at[0], grads_buf.at[r], sems.at[1, r]).wait()
        return carry

    lax.fori_loop(0, block, finish, 0)
    rows = rows_buf[...]
    out_ref[:, :tile_rows, :] = jnp.where(col_ref[0] > 0, rows, jnp.zeros_like(rows))
    out_ref[:, tile_rows:, :] = (grads_buf[...].astype(jnp.float32) * col_ref[1]).astype(
        out_ref.dtype
    )


def dispatch_rows(slot_token, rows, grads, valid, gate, block=128):
    slots = slot_token.shape[0]
    count, width = rows.shape
    tile_rows = width // 128
    cols = jnp.broadcast_to(jnp.stack([valid, gate])[:, :, None, None], (2, slots, 1, 128))
    out = pl.pallas_call(
        dispatch_kernel,
        out_shape=jax.ShapeDtypeStruct((slots, 2 * tile_rows, 128), rows.dtype),
        grid_spec=pltpu.PrefetchScalarGridSpec(
            num_scalar_prefetch=1,
            grid=(slots // block,),
            in_specs=[
                pl.BlockSpec(memory_space=pl.ANY),
                pl.BlockSpec(memory_space=pl.ANY),
                pl.BlockSpec((2, block, 1, 128), lambda i, tok: (0, i, 0, 0)),
            ],
            out_specs=pl.BlockSpec((block, 2 * tile_rows, 128), lambda i, tok: (i, 0, 0)),
            scratch_shapes=[
                pltpu.VMEM((block, tile_rows, 128), rows.dtype),
                pltpu.VMEM((block, tile_rows, 128), grads.dtype),
                pltpu.SemaphoreType.DMA((2, block)),
            ],
        ),
        cost_estimate=pl.CostEstimate(
            flops=slots * width, transcendentals=0, bytes_accessed=4 * slots * 2 * width
        ),
    )(slot_token, rows.reshape(count, tile_rows, 128), grads.reshape(count, tile_rows, 128), cols)
    return out


def combine_kernel(
    slot_ref, table_hbm, gate_ref, grad_ref, shared_out_ref, shared_back_ref,
    feed_ref, back_ref, part_ref, picked, sems,
):
    top = picked.shape[0]
    block = picked.shape[1]
    tile_rows = grad_ref.shape[1]
    last = table_hbm.shape[0] - 1
    base = pl.program_id(0) * block

    def start(r, carry):
        for k in range(top):
            slot = jnp.clip(slot_ref[(base + r) * top + k], 0, last)
            pltpu.make_async_copy(table_hbm.at[slot], picked.at[k, r], sems.at[k, r]).start()
        return carry

    lax.fori_loop(0, block, start, 0)

    def finish(r, carry):
        for k in range(top):
            pltpu.make_async_copy(table_hbm.at[0], picked.at[k, r], sems.at[k, r]).wait()
        return carry

    lax.fori_loop(0, block, finish, 0)
    grad = grad_ref[...].astype(jnp.float32)
    weighted = None
    backs = None
    lanes = lax.broadcasted_iota(jnp.int32, part_ref.shape, 2)
    parts = jnp.zeros(part_ref.shape, jnp.float32)
    for k in range(top):
        out_k = picked[k, :, :tile_rows, :].astype(jnp.float32)
        term = gate_ref[k] * out_k
        weighted = term if weighted is None else weighted + term
        back_k = picked[k, :, tile_rows:, :].astype(jnp.float32)
        backs = back_k if backs is None else backs + back_k
        dot_k = jnp.sum(jnp.sum(grad * out_k, 2, keepdims=True), 1, keepdims=True)
        parts = jnp.where(lanes == k, dot_k, parts)
    feed_ref[...] = (shared_out_ref[...] + weighted).astype(feed_ref.dtype)
    back_ref[...] = (backs + shared_back_ref[...]).astype(back_ref.dtype)
    part_ref[...] = parts


def combine_rows(slot_index, table, gate_values, grad, shared_out, shared_back, block=128):
    tokens, top = gate_values.shape
    width = grad.shape[1]
    tile_rows = width // 128
    gates = jnp.broadcast_to(gate_values.T[:, :, None, None], (top, tokens, 1, 128))
    row_spec = pl.BlockSpec((block, tile_rows, 128), lambda i, s: (i, 0, 0))
    feed, back, parts = pl.pallas_call(
        combine_kernel,
        out_shape=(
            jax.ShapeDtypeStruct((tokens, tile_rows, 128), jnp.bfloat16),
            jax.ShapeDtypeStruct((tokens, tile_rows, 128), jnp.bfloat16),
            jax.ShapeDtypeStruct((tokens, 1, 128), jnp.float32),
        ),
        grid_spec=pltpu.PrefetchScalarGridSpec(
            num_scalar_prefetch=1,
            grid=(tokens // block,),
            in_specs=[
                pl.BlockSpec(memory_space=pl.ANY),
                pl.BlockSpec((top, block, 1, 128), lambda i, s: (0, i, 0, 0)),
                row_spec,
                row_spec,
                row_spec,
            ],
            out_specs=[row_spec, row_spec, pl.BlockSpec((block, 1, 128), lambda i, s: (i, 0, 0))],
            scratch_shapes=[
                pltpu.VMEM((top, block, 2 * tile_rows, 128), table.dtype),
                pltpu.SemaphoreType.DMA((top, block)),
            ],
        ),
        cost_estimate=pl.CostEstimate(
            flops=8 * tokens * top * width,
            transcendentals=0,
            bytes_accessed=tokens * (top * 4 * width + 2 * width + 8 * width + 4 * width),
        ),
    )(
        slot_index.reshape(-1),
        table.reshape(table.shape[0], 2 * tile_rows, 128),
        gates,
        grad.reshape(tokens, tile_rows, 128),
        shared_out.reshape(tokens, tile_rows, 128),
        shared_back.reshape(tokens, tile_rows, 128),
    )
    return feed.reshape(tokens, width), back.reshape(tokens, width), parts[:, 0, :top]


def shards(
    hidden,
    routes,
    prefix,
    attn_gain,
    query_proj,
    latent_proj,
    latent_gain,
    expand_proj,
    output_proj,
    second_gain,
    router_proj,
    expert_gate,
    expert_up,
    expert_down,
    shared_gate,
    shared_up,
    shared_down,
    out_grad,
):
    tok_dev = hidden.shape[0]
    tensor_size = lax.axis_size("tensor")
    tensor_rank = lax.axis_index("tensor")
    dp_size = lax.axis_size("dp")
    seq_len = tok_dev * tensor_size
    start_row = tensor_rank * tok_dev
    rows_dp = attn_gain.shape[0]
    kv_rows = latent_gain.shape[0]
    head_cols = query_proj.shape[1]
    latent_cols = latent_proj.shape[1]
    expand_cols = expand_proj.shape[1]
    expand_flat_cols = kv_rows * expand_cols // rows_dp
    first_pack = jnp.concatenate(
        [
            query_proj,
            latent_proj,
            expand_proj.reshape(rows_dp, expand_flat_cols),
            attn_gain[:, None],
            jnp.pad(latent_gain, (0, rows_dp - kv_rows))[:, None],
        ],
        1,
    )
    first_all = lax.all_gather(first_pack, "dp", axis=0, tiled=True)
    cut = [0]
    for width in (head_cols, latent_cols, expand_flat_cols, 1, 1):
        cut.append(cut[-1] + width)
    query_weights = first_all[:, cut[0] : cut[1]]
    latent_weights = first_all[:, cut[1] : cut[2]]
    expand_weights = first_all[:, cut[2] : cut[3]].reshape(dp_size * kv_rows, expand_cols)
    attn_gains = first_all[:, cut[3]]
    kv_gains = first_all[:, cut[4]].reshape(dp_size, rows_dp)[:, :kv_rows].reshape(-1)
    out_cols = output_proj.shape[0]
    experts = router_proj.shape[1]
    shared_cols = shared_gate.shape[1]
    second_pack = jnp.concatenate([output_proj.T, second_gain[:, None], router_proj], 1)
    second_all = lax.all_gather(second_pack, "dp", axis=0, tiled=True)
    output_weights_t = second_all[:, :out_cols]
    second_gains = second_all[:, out_cols]
    router_weights = second_all[:, out_cols + 1 :]
    shared_local = jnp.concatenate([shared_gate, shared_up, shared_down.T], 1)

    hidden_all = lax.all_gather(hidden, "tensor", axis=0, tiled=True)
    grad_seq = lax.all_gather(out_grad, "tensor", axis=0, tiled=True)
    hidden_all_f = hidden_all.astype(jnp.float32)
    scale_one_all = norm_scale(hidden_all_f)
    gain_one = attn_gains.astype(jnp.float32)
    normed_all = (hidden_all_f * scale_one_all * gain_one).astype(jnp.bfloat16)
    hidden_f = lax.dynamic_slice_in_dim(hidden_all_f, start_row, tok_dev, 0)
    scale_one = lax.dynamic_slice_in_dim(scale_one_all, start_row, tok_dev, 0)
    normed_own = lax.dynamic_slice_in_dim(normed_all, start_row, tok_dev, 0)
    latent_raw_all = jnp.dot(normed_all, latent_weights, preferred_element_type=jnp.float32)
    compressed_all = latent_raw_all[:, :KVR]
    scale_kv_all = norm_scale(compressed_all)
    gain_kv = kv_gains.astype(jnp.float32)
    all_cosines, all_sines = rope_tables(jnp.arange(seq_len), DR)
    latent_seq = jnp.concatenate(
        [
            compressed_all * scale_kv_all * gain_kv,
            rotate(latent_raw_all[:, KVR:], all_cosines, all_sines),
        ],
        -1,
    ).astype(jnp.bfloat16)
    compressed = lax.dynamic_slice_in_dim(compressed_all, start_row, tok_dev, 0)
    scale_kv = lax.dynamic_slice_in_dim(scale_kv_all, start_row, tok_dev, 0)
    own_cosines = lax.dynamic_slice_in_dim(all_cosines, start_row, tok_dev, 0)
    own_sines = lax.dynamic_slice_in_dim(all_sines, start_row, tok_dev, 0)
    head_count = query_weights.shape[1] // (DN + DR)
    query_raw = jnp.dot(normed_all, query_weights, preferred_element_type=jnp.float32).reshape(
        seq_len, head_count, DN + DR
    )
    query_low = jnp.concatenate(
        [
            query_raw[..., :DN],
            rotate(query_raw[..., DN:], all_cosines[:, None, :], all_sines[:, None, :]),
        ],
        -1,
    ).astype(jnp.bfloat16)
    compressed_seq = latent_seq[:, :KVR]
    key_rope = latent_seq[:, KVR:]
    expanded = jnp.dot(compressed_seq, expand_weights, preferred_element_type=jnp.float32).reshape(
        seq_len, head_count, DN + DV
    )
    keys_nope = expanded[..., :DN].astype(jnp.bfloat16)
    values_low = expanded[..., DN:].astype(jnp.bfloat16)
    score_scale = 1.0 / math.sqrt(DN + DR)
    block_rows = min(512, seq_len)
    prefix_len = prefix[0]
    lse_list = []
    mixed_list = []
    for rows_start in range(0, seq_len, block_rows):
        query_block = query_low[rows_start : rows_start + block_rows]
        masked = block_scores(query_block, keys_nope, key_rope, rows_start, prefix_len, score_scale)
        top_score = jnp.max(masked, -1, keepdims=True)
        exp_scores = jnp.exp(masked - top_score)
        totals = jnp.sum(exp_scores, -1, keepdims=True)
        prob_low = (exp_scores / totals).astype(jnp.bfloat16)
        lse_list.append(top_score + jnp.log(totals))
        mixed_list.append(
            jnp.einsum(
                "hqk,khv->qhv", prob_low, values_low, preferred_element_type=jnp.float32
            ).astype(jnp.bfloat16)
        )
    mixed_all = jnp.concatenate(mixed_list, 0).reshape(seq_len, head_count * DV)
    attn_part = jnp.einsum(
        "tk,dk->td", mixed_all, output_weights_t, preferred_element_type=jnp.float32
    )
    branch_all = lax.psum(attn_part.astype(jnp.bfloat16), "tensor").astype(jnp.float32)
    residual_all = hidden_all_f + branch_all
    residual_own = lax.dynamic_slice_in_dim(residual_all, start_row, tok_dev, 0)
    scale_two = norm_scale(residual_all)
    gain_two = second_gains.astype(jnp.float32)
    normed_two = (residual_all * scale_two * gain_two).astype(jnp.bfloat16)
    logits = jnp.dot(normed_two, router_weights, preferred_element_type=jnp.float32)
    top_count = routes.shape[1]
    chosen_hot = routes[:, :, None] == jnp.arange(experts)[None, None, :]
    chosen_logits = jnp.sum(jnp.where(chosen_hot, logits[:, None, :], 0.0), -1)
    gate_values = jax.nn.softmax(chosen_logits, axis=-1)
    assignments = seq_len * top_count
    flat_hot = chosen_hot.reshape(assignments, experts).astype(jnp.bfloat16)
    lower = (jnp.arange(assignments)[:, None] > jnp.arange(assignments)[None, :]).astype(jnp.bfloat16)
    earlier = jnp.dot(lower, flat_hot, preferred_element_type=jnp.float32)
    slot_pos = jnp.sum(earlier * flat_hot.astype(jnp.float32), -1).astype(jnp.int32)
    expert_ids = routes.reshape(-1)
    exp_dev = expert_gate.shape[0]
    capacity = tensor_size * (5 * seq_len * top_count // (4 * experts * tensor_size))
    slot_index = expert_ids * capacity + slot_pos
    token_ids = jnp.arange(seq_len * top_count) // top_count
    slot_token = jnp.full((experts * capacity,), seq_len, jnp.int32).at[slot_index].set(token_ids)
    slot_gate = (
        jnp.zeros((experts * capacity,), jnp.float32).at[slot_index].set(gate_values.reshape(-1))
    )
    slot_valid = (slot_token < seq_len).astype(jnp.float32)
    tile_rows = D // 128
    send_both = dispatch_rows(slot_token, normed_two, grad_seq, slot_valid, slot_gate).reshape(
        dp_size, exp_dev, capacity, 2 * tile_rows, 128
    )
    shared_local, send_both = lax.optimization_barrier((shared_local, send_both))
    shared_all = lax.all_gather(shared_local, "dp", axis=0, tiled=True)
    gate_shared = shared_all[:, :shared_cols]
    up_shared = shared_all[:, shared_cols : 2 * shared_cols]
    down_shared_t = shared_all[:, 2 * shared_cols :]
    recv_both = lax.all_to_all(send_both, "dp", split_axis=0, concat_axis=0, tiled=True)
    recv_both = recv_both.reshape(dp_size, exp_dev, capacity, 2 * D)
    recv_rows = recv_both[..., :D]
    recv_grads = recv_both[..., D:]
    gate_pre = jnp.einsum(
        "sjcd,jfd->sjcf", recv_rows, expert_gate, preferred_element_type=jnp.float32
    )
    up_pre = jnp.einsum("sjcd,jfd->sjcf", recv_rows, expert_up, preferred_element_type=jnp.float32)
    sigmoid_gate = jax.nn.sigmoid(gate_pre)
    expert_act = (gate_pre * sigmoid_gate * up_pre).astype(jnp.bfloat16)
    expert_out = jnp.einsum(
        "sjcf,jfd->sjcd", expert_act, expert_down, preferred_element_type=jnp.float32
    )
    act_grad = jnp.einsum(
        "sjcd,jfd->sjcf", recv_grads, expert_down, preferred_element_type=jnp.float32
    )
    gate_low_grad, up_low_grad = silu_back(act_grad, gate_pre, up_pre, sigmoid_gate)
    expert_down_grad = jnp.einsum(
        "sjcf,sjcd->jfd", expert_act, recv_grads, preferred_element_type=jnp.float32
    )
    expert_gate_grad = jnp.einsum(
        "sjcf,sjcd->jfd", gate_low_grad, recv_rows, preferred_element_type=jnp.float32
    )
    expert_up_grad = jnp.einsum(
        "sjcf,sjcd->jfd", up_low_grad, recv_rows, preferred_element_type=jnp.float32
    )
    row_grads = jnp.einsum(
        "sjcf,jfd->sjcd", gate_low_grad, expert_gate, preferred_element_type=jnp.float32
    )
    row_grads = row_grads + jnp.einsum(
        "sjcf,jfd->sjcd", up_low_grad, expert_up, preferred_element_type=jnp.float32
    )
    back_both = lax.all_to_all(
        jnp.concatenate(
            [expert_out.astype(jnp.bfloat16), row_grads.astype(jnp.bfloat16)], -1
        ).reshape(dp_size, exp_dev, capacity, 2 * tile_rows, 128),
        "dp",
        split_axis=0,
        concat_axis=0,
        tiled=True,
    )
    shared_pre_gate = jnp.dot(normed_two, gate_shared, preferred_element_type=jnp.float32)
    shared_pre_up = jnp.dot(normed_two, up_shared, preferred_element_type=jnp.float32)
    shared_sigmoid = jax.nn.sigmoid(shared_pre_gate)
    shared_act = (shared_pre_gate * shared_sigmoid * shared_pre_up).astype(jnp.bfloat16)
    shared_out = jnp.einsum(
        "tf,df->td", shared_act, down_shared_t, preferred_element_type=jnp.float32
    )
    shared_act_grad = jnp.dot(grad_seq, down_shared_t, preferred_element_type=jnp.float32)
    shared_gate_low, shared_up_low = silu_back(
        shared_act_grad, shared_pre_gate, shared_pre_up, shared_sigmoid
    )
    shared_down_grad_t = jnp.dot(grad_seq.T, shared_act, preferred_element_type=jnp.float32)
    shared_gate_grad = jnp.dot(normed_two.T, shared_gate_low, preferred_element_type=jnp.float32)
    shared_up_grad = jnp.dot(normed_two.T, shared_up_low, preferred_element_type=jnp.float32)
    shared_back = jnp.einsum(
        "tf,df->td", shared_gate_low, gate_shared, preferred_element_type=jnp.float32
    )
    shared_back = shared_back + jnp.einsum(
        "tf,df->td", shared_up_low, up_shared, preferred_element_type=jnp.float32
    )
    shared_grads_in = jnp.concatenate(
        [shared_gate_grad, shared_up_grad, shared_down_grad_t], 1
    ).astype(jnp.bfloat16)
    grad_seq_f = grad_seq.astype(jnp.float32)
    table_rows = experts * capacity
    feed_part, back_part, gate_cols = combine_rows(
        slot_index.reshape(seq_len, top_count),
        back_both.reshape(table_rows, 2 * tile_rows, 128),
        gate_values,
        grad_seq,
        shared_out,
        shared_back,
    )
    gate_part = gate_cols[:, :top_count]
    feed_own = lax.psum_scatter(feed_part, "tensor", scatter_dimension=0, tiled=True).astype(
        jnp.float32
    )
    output = (residual_own + feed_own).astype(jnp.bfloat16)
    normed_two_grad, gate_grads = lax.psum(
        (back_part, gate_part.astype(jnp.bfloat16)),
        "tensor",
    )
    normed_two_grad = normed_two_grad.astype(jnp.float32)
    gate_grads = gate_grads.astype(jnp.float32)
    weighted_total = jnp.sum(gate_values * gate_grads, -1, keepdims=True)
    chosen_grads = gate_values * (gate_grads - weighted_total)
    logit_grads = jnp.sum(jnp.where(chosen_hot, chosen_grads[:, :, None], 0.0), 1)
    normed_two_grad = normed_two_grad + jnp.dot(
        logit_grads, router_weights.astype(jnp.float32).T, precision=HIGH
    )
    residual_grad = grad_seq_f + norm_back(residual_all, scale_two, gain_two, normed_two_grad)
    branch_grad = residual_grad.astype(jnp.bfloat16)
    shared_grads_in, branch_grad = lax.optimization_barrier((shared_grads_in, branch_grad))
    shared_pack = lax.psum_scatter(
        shared_grads_in, "dp", scatter_dimension=0, tiled=True
    ).astype(jnp.float32)
    output_grad_w_t = jnp.dot(branch_grad.T, mixed_all, preferred_element_type=jnp.float32)
    mixed_grad = (
        jnp.dot(branch_grad, output_weights_t, preferred_element_type=jnp.float32)
        .astype(jnp.bfloat16)
        .reshape(seq_len, head_count, DV)
    )
    keys_nope_grad = jnp.zeros((seq_len, head_count, DN), jnp.float32)
    key_rope_grad = jnp.zeros((seq_len, DR), jnp.float32)
    values_grad = jnp.zeros((seq_len, head_count, DV), jnp.float32)
    query_grad_list = []
    for block_index, rows_start in enumerate(range(0, seq_len, block_rows)):
        query_block = query_low[rows_start : rows_start + block_rows]
        masked = block_scores(query_block, keys_nope, key_rope, rows_start, prefix_len, score_scale)
        prob_full = jnp.exp(masked - lse_list[block_index])
        prob_low = prob_full.astype(jnp.bfloat16)
        mixed_block = mixed_grad[rows_start : rows_start + block_rows]
        prob_grads = jnp.einsum(
            "qhv,khv->hqk", mixed_block, values_low, preferred_element_type=jnp.float32
        )
        row_delta = jnp.sum(prob_full * prob_grads, -1, keepdims=True)
        score_grads = (prob_full * (prob_grads - row_delta)).astype(jnp.bfloat16)
        query_nope_grad = (
            jnp.einsum("hqk,khd->qhd", score_grads, keys_nope, preferred_element_type=jnp.float32)
            * score_scale
        )
        query_rope_grad = (
            jnp.einsum("hqk,kr->qhr", score_grads, key_rope, preferred_element_type=jnp.float32)
            * score_scale
        )
        keys_nope_grad = (
            keys_nope_grad
            + jnp.einsum(
                "hqk,qhd->khd",
                score_grads,
                query_block[..., :DN],
                preferred_element_type=jnp.float32,
            )
            * score_scale
        )
        key_rope_grad = (
            key_rope_grad
            + jnp.einsum(
                "hqk,qhr->kr",
                score_grads,
                query_block[..., DN:],
                preferred_element_type=jnp.float32,
            )
            * score_scale
        )
        values_grad = values_grad + jnp.einsum(
            "hqk,qhv->khv", prob_low, mixed_block, preferred_element_type=jnp.float32
        )
        block_cosines = all_cosines[rows_start : rows_start + block_rows, None, :]
        block_sines = all_sines[rows_start : rows_start + block_rows, None, :]
        query_grad_list.append(
            jnp.concatenate(
                [
                    query_nope_grad,
                    rotate_back(round_trip(query_rope_grad), block_cosines, block_sines),
                ],
                -1,
            ).astype(jnp.bfloat16)
        )
    query_grads = jnp.concatenate(query_grad_list, 0).reshape(seq_len, head_count * (DN + DR))
    query_grad_w = jnp.dot(normed_all.T, query_grads, preferred_element_type=jnp.float32)
    normed_grad_part = jnp.dot(query_grads, query_weights.T, preferred_element_type=jnp.float32)
    expand_grads = jnp.concatenate(
        [keys_nope_grad.astype(jnp.bfloat16), values_grad.astype(jnp.bfloat16)], -1
    ).reshape(seq_len, head_count * (DN + DV))
    expand_grad_w = jnp.dot(compressed_seq.T, expand_grads, preferred_element_type=jnp.float32)
    compressed_grad_part = jnp.dot(
        expand_grads, expand_weights.T, preferred_element_type=jnp.float32
    )
    latent_grad_part = jnp.concatenate([compressed_grad_part, key_rope_grad], -1)
    attn_pack = lax.psum_scatter(
        jnp.concatenate(
            [
                query_grad_w,
                output_grad_w_t,
                expand_grad_w.reshape(dp_size * rows_dp, expand_flat_cols),
            ],
            1,
        ).astype(jnp.bfloat16),
        "dp",
        scatter_dimension=0,
        tiled=True,
    ).astype(jnp.float32)
    token_all = lax.psum(
        jnp.concatenate([normed_grad_part, latent_grad_part], 1).astype(jnp.bfloat16), "tensor"
    ).astype(jnp.float32)
    compressed_grad_all = token_all[:, D : D + KVR]
    kv_gain_full = jnp.sum(compressed_grad_all * compressed_all * scale_kv_all, 0)
    raw_grad_all = jnp.concatenate(
        [
            norm_back(compressed_all, scale_kv_all, gain_kv, compressed_grad_all),
            rotate_back(token_all[:, D + KVR :], all_cosines, all_sines),
        ],
        -1,
    ).astype(jnp.bfloat16)
    normed_grad_all = token_all[:, :D] + jnp.dot(
        raw_grad_all, latent_weights.T, preferred_element_type=jnp.float32
    )
    normed_grad = lax.dynamic_slice_in_dim(normed_grad_all, start_row, tok_dev, 0)
    hidden_grad = lax.dynamic_slice_in_dim(residual_grad, start_row, tok_dev, 0) + norm_back(
        hidden_f, scale_one, gain_one, normed_grad
    )
    row_per = D // (dp_size * tensor_size)

    def own_rows(values):
        split = values.reshape(values.shape[0], dp_size, tensor_size, row_per)
        return lax.dynamic_slice_in_dim(split, tensor_rank, 1, 2).reshape(values.shape[0], -1)

    latent_rows = jnp.dot(own_rows(normed_all).T, raw_grad_all, preferred_element_type=jnp.float32)
    attn_gain_rows = jnp.sum(
        own_rows(normed_grad_all) * own_rows(hidden_all_f) * scale_one_all, 0
    )
    second_gain_rows = jnp.sum(
        own_rows(normed_two_grad) * own_rows(residual_all) * scale_two, 0
    )
    router_rows = jnp.dot(
        own_rows(normed_two).astype(jnp.float32).T, logit_grads, precision=HIGH
    )
    kv_per = kv_gain_full.shape[0] // (dp_size * tensor_size)
    kv_rows_own = lax.dynamic_slice_in_dim(
        kv_gain_full.reshape(dp_size, tensor_size, kv_per), tensor_rank, 1, 1
    ).reshape(dp_size, kv_per)
    kv_column = jnp.pad(kv_rows_own, ((0, 0), (0, row_per - kv_per))).reshape(-1)
    small_pack = jnp.concatenate(
        [
            latent_rows,
            router_rows,
            attn_gain_rows[:, None],
            second_gain_rows[:, None],
            kv_column[:, None],
        ],
        1,
    )
    small_own = lax.psum_scatter(small_pack, "dp", scatter_dimension=0, tiled=True)
    cut = [0]
    for width in (latent_cols, experts, 1, 1, 1):
        cut.append(cut[-1] + width)
    latent_proj_grad = small_own[:, cut[0] : cut[1]]
    router_out = small_own[:, cut[1] : cut[2]]
    attn_gain_out = small_own[:, cut[2]]
    second_gain_out = small_own[:, cut[3]]
    latent_gain_out = small_own[:kv_per, cut[4]]
    cut = [0]
    for width in (head_cols, out_cols, expand_flat_cols):
        cut.append(cut[-1] + width)
    query_proj_grad = attn_pack[:, cut[0] : cut[1]]
    output_proj_grad = attn_pack[:, cut[1] : cut[2]].T
    expand_proj_grad = attn_pack[:, cut[2] : cut[3]].reshape(kv_rows, expand_cols)
    shared_gate_out = shared_pack[:, :shared_cols]
    shared_up_out = shared_pack[:, shared_cols : 2 * shared_cols]
    shared_down_out = shared_pack[:, 2 * shared_cols :].T
    return (
        output,
        hidden_grad,
        attn_gain_out,
        query_proj_grad,
        latent_proj_grad,
        latent_gain_out,
        expand_proj_grad,
        output_proj_grad,
        second_gain_out,
        router_out,
        expert_gate_grad,
        expert_up_grad,
        expert_down_grad,
        shared_gate_out,
        shared_up_out,
        shared_down_out,
    )


def solution(mesh):
    return jax.shard_map(
        shards,
        mesh=mesh,
        in_specs=(
            P(("dp", "tensor"), None),
            P("dp", None),
            P("dp"),
            P("dp"),
            P("dp", "tensor"),
            P("dp", None),
            P("dp"),
            P("dp", "tensor"),
            P("tensor", "dp"),
            P("dp"),
            P("dp", None),
            P("dp", "tensor", None),
            P("dp", "tensor", None),
            P("dp", "tensor", None),
            P("dp", "tensor"),
            P("dp", "tensor"),
            P("tensor", "dp"),
            P(("dp", "tensor"), None),
        ),
        out_specs=(
            P(("dp", "tensor"), None),
            P(("dp", "tensor"), None),
            P(("dp", "tensor")),
            P("dp", "tensor"),
            P(("dp", "tensor"), None),
            P(("dp", "tensor")),
            P("dp", "tensor"),
            P("tensor", "dp"),
            P(("dp", "tensor")),
            P(("dp", "tensor"), None),
            P("dp", "tensor", None),
            P("dp", "tensor", None),
            P("dp", "tensor", None),
            P("dp", "tensor"),
            P("dp", "tensor"),
            P("tensor", "dp"),
        ),
        check_vma=False,
    )
```

```python
import math

import jax
import jax.numpy as jnp
from jax import lax
from jax.experimental import pallas as pl
from jax.experimental.pallas import tpu as pltpu
from jax.sharding import PartitionSpec as P

D = 2048
DN = 128
DR = 64
DV = 128
KVR = 512


EPS = 1e-06
HIGH = lax.Precision.HIGHEST
MASKED = -1e30


def norm_scale(values):
    return lax.rsqrt(jnp.mean(values * values, -1, keepdims=True) + EPS)


def norm_back(values, scales, gains, upstream):
    weighted = gains * upstream
    return scales * weighted - values * scales**3 * jnp.mean(values * weighted, -1, keepdims=True)


def rope_tables(positions, rope_width):
    half_width = rope_width // 2
    frequency = 10000.0 ** (-2.0 * jnp.arange(half_width).astype(jnp.float32) / rope_width)
    angles = positions.astype(jnp.float32)[:, None] * frequency[None, :]
    return (jnp.cos(angles), jnp.sin(angles))


def rotate(vectors, cosines, sine_values):
    half_width = vectors.shape[-1] // 2
    front_half = vectors[..., :half_width]
    back_half = vectors[..., half_width:]
    return jnp.concatenate(
        [
            front_half * cosines - back_half * sine_values,
            back_half * cosines + front_half * sine_values,
        ],
        -1,
    )


def rotate_back(gradients, cosines, sine_values):
    half_width = gradients.shape[-1] // 2
    front_half = gradients[..., :half_width]
    back_half = gradients[..., half_width:]
    return jnp.concatenate(
        [
            front_half * cosines + back_half * sine_values,
            back_half * cosines - front_half * sine_values,
        ],
        -1,
    )


def round_trip(values):
    return lax.optimization_barrier(values.astype(jnp.bfloat16)).astype(jnp.float32)


def block_scores(query_block, keys_nope, key_rope, rows_start, prefix_len, score_scale):
    raw_scores = jnp.einsum(
        "qhd,khd->hqk", query_block[..., :DN], keys_nope, preferred_element_type=jnp.float32
    )
    raw_scores = raw_scores + jnp.einsum(
        "qhr,kr->hqk", query_block[..., DN:], key_rope, preferred_element_type=jnp.float32
    )
    query_places = rows_start + jnp.arange(query_block.shape[0])
    key_places = jnp.arange(keys_nope.shape[0])
    visible = (key_places[None, :] <= query_places[:, None]) | (key_places[None, :] < prefix_len)
    return jnp.where(visible[None], raw_scores * score_scale, MASKED)


def silu_back(act_grad, gate_pre, up_pre, sigmoid_gate):
    up_grad = (act_grad * gate_pre * sigmoid_gate).astype(jnp.bfloat16)
    gate_grad = (act_grad * up_pre * sigmoid_gate * (1.0 + gate_pre * (1.0 - sigmoid_gate))).astype(
        jnp.bfloat16
    )
    return (gate_grad, up_grad)


def dispatch_kernel(tok_ref, rows_hbm, grads_hbm, col_ref, out_ref, rows_buf, grads_buf, sems):
    block = rows_buf.shape[0]
    tile_rows = rows_buf.shape[1]
    last = rows_hbm.shape[0] - 1
    base = pl.program_id(0) * block

    def start(r, carry):
        tok = jnp.minimum(tok_ref[base + r], last)
        pltpu.make_async_copy(rows_hbm.at[tok], rows_buf.at[r], sems.at[0, r]).start()
        pltpu.make_async_copy(grads_hbm.at[tok], grads_buf.at[r], sems.at[1, r]).start()
        return carry

    lax.fori_loop(0, block, start, 0)

    def finish(r, carry):
        pltpu.make_async_copy(rows_hbm.at[0], rows_buf.at[r], sems.at[0, r]).wait()
        pltpu.make_async_copy(grads_hbm.at[0], grads_buf.at[r], sems.at[1, r]).wait()
        return carry

    lax.fori_loop(0, block, finish, 0)
    rows = rows_buf[...]
    out_ref[:, :tile_rows, :] = jnp.where(col_ref[0] > 0, rows, jnp.zeros_like(rows))
    out_ref[:, tile_rows:, :] = (grads_buf[...].astype(jnp.float32) * col_ref[1]).astype(
        out_ref.dtype
    )


def dispatch_rows(slot_token, rows, grads, valid, gate, block=128):
    slots = slot_token.shape[0]
    count, width = rows.shape
    tile_rows = width // 128
    cols = jnp.broadcast_to(jnp.stack([valid, gate])[:, :, None, None], (2, slots, 1, 128))
    out = pl.pallas_call(
        dispatch_kernel,
        out_shape=jax.ShapeDtypeStruct((slots, 2 * tile_rows, 128), rows.dtype),
        grid_spec=pltpu.PrefetchScalarGridSpec(
            num_scalar_prefetch=1,
            grid=(slots // block,),
            in_specs=[
                pl.BlockSpec(memory_space=pl.ANY),
                pl.BlockSpec(memory_space=pl.ANY),
                pl.BlockSpec((2, block, 1, 128), lambda i, tok: (0, i, 0, 0)),
            ],
            out_specs=pl.BlockSpec((block, 2 * tile_rows, 128), lambda i, tok: (i, 0, 0)),
            scratch_shapes=[
                pltpu.VMEM((block, tile_rows, 128), rows.dtype),
                pltpu.VMEM((block, tile_rows, 128), grads.dtype),
                pltpu.SemaphoreType.DMA((2, block)),
            ],
        ),
        cost_estimate=pl.CostEstimate(
            flops=slots * width, transcendentals=0, bytes_accessed=4 * slots * 2 * width
        ),
    )(slot_token, rows.reshape(count, tile_rows, 128), grads.reshape(count, tile_rows, 128), cols)
    return out


def combine_kernel(
    slot_ref, table_hbm, gate_ref, grad_ref, shared_out_ref, shared_back_ref,
    feed_ref, back_ref, part_ref, picked, sems,
):
    top = picked.shape[0]
    block = picked.shape[1]
    tile_rows = grad_ref.shape[1]
    last = table_hbm.shape[0] - 1
    base = pl.program_id(0) * block

    def start(r, carry):
        for k in range(top):
            slot = jnp.clip(slot_ref[(base + r) * top + k], 0, last)
            pltpu.make_async_copy(table_hbm.at[slot], picked.at[k, r], sems.at[k, r]).start()
        return carry

    lax.fori_loop(0, block, start, 0)

    def finish(r, carry):
        for k in range(top):
            pltpu.make_async_copy(table_hbm.at[0], picked.at[k, r], sems.at[k, r]).wait()
        return carry

    lax.fori_loop(0, block, finish, 0)
    grad = grad_ref[...].astype(jnp.float32)
    weighted = None
    backs = None
    lanes = lax.broadcasted_iota(jnp.int32, part_ref.shape, 2)
    parts = jnp.zeros(part_ref.shape, jnp.float32)
    for k in range(top):
        out_k = picked[k, :, :tile_rows, :].astype(jnp.float32)
        term = gate_ref[k] * out_k
        weighted = term if weighted is None else weighted + term
        back_k = picked[k, :, tile_rows:, :].astype(jnp.float32)
        backs = back_k if backs is None else backs + back_k
        dot_k = jnp.sum(jnp.sum(grad * out_k, 2, keepdims=True), 1, keepdims=True)
        parts = jnp.where(lanes == k, dot_k, parts)
    feed_ref[...] = (shared_out_ref[...] + weighted).astype(feed_ref.dtype)
    back_ref[...] = (backs + shared_back_ref[...]).astype(back_ref.dtype)
    part_ref[...] = parts


def combine_rows(slot_index, table, gate_values, grad, shared_out, shared_back, block=128):
    tokens, top = gate_values.shape
    width = grad.shape[1]
    tile_rows = width // 128
    gates = jnp.broadcast_to(gate_values.T[:, :, None, None], (top, tokens, 1, 128))
    row_spec = pl.BlockSpec((block, tile_rows, 128), lambda i, s: (i, 0, 0))
    feed, back, parts = pl.pallas_call(
        combine_kernel,
        out_shape=(
            jax.ShapeDtypeStruct((tokens, tile_rows, 128), jnp.bfloat16),
            jax.ShapeDtypeStruct((tokens, tile_rows, 128), jnp.bfloat16),
            jax.ShapeDtypeStruct((tokens, 1, 128), jnp.float32),
        ),
        grid_spec=pltpu.PrefetchScalarGridSpec(
            num_scalar_prefetch=1,
            grid=(tokens // block,),
            in_specs=[
                pl.BlockSpec(memory_space=pl.ANY),
                pl.BlockSpec((top, block, 1, 128), lambda i, s: (0, i, 0, 0)),
                row_spec,
                row_spec,
                row_spec,
            ],
            out_specs=[row_spec, row_spec, pl.BlockSpec((block, 1, 128), lambda i, s: (i, 0, 0))],
            scratch_shapes=[
                pltpu.VMEM((top, block, 2 * tile_rows, 128), table.dtype),
                pltpu.SemaphoreType.DMA((top, block)),
            ],
        ),
        cost_estimate=pl.CostEstimate(
            flops=8 * tokens * top * width,
            transcendentals=0,
            bytes_accessed=tokens * (top * 4 * width + 2 * width + 8 * width + 4 * width),
        ),
    )(
        slot_index.reshape(-1),
        table.reshape(table.shape[0], 2 * tile_rows, 128),
        gates,
        grad.reshape(tokens, tile_rows, 128),
        shared_out.reshape(tokens, tile_rows, 128),
        shared_back.reshape(tokens, tile_rows, 128),
    )
    return feed.reshape(tokens, width), back.reshape(tokens, width), parts[:, 0, :top]


def shards(
    hidden,
    routes,
    prefix,
    attn_gain,
    query_proj,
    latent_proj,
    latent_gain,
    expand_proj,
    output_proj,
    second_gain,
    router_proj,
    expert_gate,
    expert_up,
    expert_down,
    shared_gate,
    shared_up,
    shared_down,
    out_grad,
):
    tok_dev = hidden.shape[0]
    tensor_size = lax.axis_size("tensor")
    tensor_rank = lax.axis_index("tensor")
    dp_size = lax.axis_size("dp")
    seq_len = tok_dev * tensor_size
    start_row = tensor_rank * tok_dev
    rows_dp = attn_gain.shape[0]
    kv_rows = latent_gain.shape[0]
    head_cols = query_proj.shape[1]
    latent_cols = latent_proj.shape[1]
    expand_cols = expand_proj.shape[1]
    expand_flat_cols = kv_rows * expand_cols // rows_dp
    first_pack = jnp.concatenate(
        [
            query_proj,
            latent_proj,
            expand_proj.reshape(rows_dp, expand_flat_cols),
            attn_gain[:, None],
            jnp.pad(latent_gain, (0, rows_dp - kv_rows))[:, None],
        ],
        1,
    )
    first_all = lax.all_gather(first_pack, "dp", axis=0, tiled=True)
    cut = [0]
    for width in (head_cols, latent_cols, expand_flat_cols, 1, 1):
        cut.append(cut[-1] + width)
    query_weights = first_all[:, cut[0] : cut[1]]
    latent_weights = first_all[:, cut[1] : cut[2]]
    expand_weights = first_all[:, cut[2] : cut[3]].reshape(dp_size * kv_rows, expand_cols)
    attn_gains = first_all[:, cut[3]]
    kv_gains = first_all[:, cut[4]].reshape(dp_size, rows_dp)[:, :kv_rows].reshape(-1)
    out_cols = output_proj.shape[0]
    experts = router_proj.shape[1]
    shared_cols = shared_gate.shape[1]
    second_pack = jnp.concatenate([output_proj.T, second_gain[:, None], router_proj], 1)
    second_all = lax.all_gather(second_pack, "dp", axis=0, tiled=True)
    output_weights_t = second_all[:, :out_cols]
    second_gains = second_all[:, out_cols]
    router_weights = second_all[:, out_cols + 1 :]
    shared_local = jnp.concatenate([shared_gate, shared_up, shared_down.T], 1)

    hidden_all = lax.all_gather(hidden, "tensor", axis=0, tiled=True)
    grad_seq = lax.all_gather(out_grad, "tensor", axis=0, tiled=True)
    hidden_all_f = hidden_all.astype(jnp.float32)
    scale_one_all = norm_scale(hidden_all_f)
    gain_one = attn_gains.astype(jnp.float32)
    normed_all = (hidden_all_f * scale_one_all * gain_one).astype(jnp.bfloat16)
    hidden_f = lax.dynamic_slice_in_dim(hidden_all_f, start_row, tok_dev, 0)
    scale_one = lax.dynamic_slice_in_dim(scale_one_all, start_row, tok_dev, 0)
    normed_own = lax.dynamic_slice_in_dim(normed_all, start_row, tok_dev, 0)
    latent_raw_all = jnp.dot(normed_all, latent_weights, preferred_element_type=jnp.float32)
    compressed_all = latent_raw_all[:, :KVR]
    scale_kv_all = norm_scale(compressed_all)
    gain_kv = kv_gains.astype(jnp.float32)
    all_cosines, all_sines = rope_tables(jnp.arange(seq_len), DR)
    latent_seq = jnp.concatenate(
        [
            compressed_all * scale_kv_all * gain_kv,
            rotate(latent_raw_all[:, KVR:], all_cosines, all_sines),
        ],
        -1,
    ).astype(jnp.bfloat16)
    compressed = lax.dynamic_slice_in_dim(compressed_all, start_row, tok_dev, 0)
    scale_kv = lax.dynamic_slice_in_dim(scale_kv_all, start_row, tok_dev, 0)
    own_cosines = lax.dynamic_slice_in_dim(all_cosines, start_row, tok_dev, 0)
    own_sines = lax.dynamic_slice_in_dim(all_sines, start_row, tok_dev, 0)
    head_count = query_weights.shape[1] // (DN + DR)
    query_raw = jnp.dot(normed_all, query_weights, preferred_element_type=jnp.float32).reshape(
        seq_len, head_count, DN + DR
    )
    query_low = jnp.concatenate(
        [
            query_raw[..., :DN],
            rotate(query_raw[..., DN:], all_cosines[:, None, :], all_sines[:, None, :]),
        ],
        -1,
    ).astype(jnp.bfloat16)
    compressed_seq = latent_seq[:, :KVR]
    key_rope = latent_seq[:, KVR:]
    expanded = jnp.dot(compressed_seq, expand_weights, preferred_element_type=jnp.float32).reshape(
        seq_len, head_count, DN + DV
    )
    keys_nope = expanded[..., :DN].astype(jnp.bfloat16)
    values_low = expanded[..., DN:].astype(jnp.bfloat16)
    score_scale = 1.0 / math.sqrt(DN + DR)
    block_rows = min(512, seq_len)
    prefix_len = prefix[0]
    lse_list = []
    mixed_list = []
    for rows_start in range(0, seq_len, block_rows):
        query_block = query_low[rows_start : rows_start + block_rows]
        masked = block_scores(query_block, keys_nope, key_rope, rows_start, prefix_len, score_scale)
        top_score = jnp.max(masked, -1, keepdims=True)
        exp_scores = jnp.exp(masked - top_score)
        totals = jnp.sum(exp_scores, -1, keepdims=True)
        prob_low = (exp_scores / totals).astype(jnp.bfloat16)
        lse_list.append(top_score + jnp.log(totals))
        mixed_list.append(
            jnp.einsum(
                "hqk,khv->qhv", prob_low, values_low, preferred_element_type=jnp.float32
            ).astype(jnp.bfloat16)
        )
    mixed_all = jnp.concatenate(mixed_list, 0).reshape(seq_len, head_count * DV)
    attn_part = jnp.einsum(
        "tk,dk->td", mixed_all, output_weights_t, preferred_element_type=jnp.float32
    )
    branch_all = lax.psum(attn_part.astype(jnp.bfloat16), "tensor").astype(jnp.float32)
    residual_all = hidden_all_f + branch_all
    residual_own = lax.dynamic_slice_in_dim(residual_all, start_row, tok_dev, 0)
    scale_two = norm_scale(residual_all)
    gain_two = second_gains.astype(jnp.float32)
    normed_two = (residual_all * scale_two * gain_two).astype(jnp.bfloat16)
    logits = jnp.dot(normed_two, router_weights, preferred_element_type=jnp.float32)
    top_count = routes.shape[1]
    chosen_hot = routes[:, :, None] == jnp.arange(experts)[None, None, :]
    chosen_logits = jnp.sum(jnp.where(chosen_hot, logits[:, None, :], 0.0), -1)
    gate_values = jax.nn.softmax(chosen_logits, axis=-1)
    assignments = seq_len * top_count
    flat_hot = chosen_hot.reshape(assignments, experts).astype(jnp.bfloat16)
    lower = (jnp.arange(assignments)[:, None] > jnp.arange(assignments)[None, :]).astype(jnp.bfloat16)
    earlier = jnp.dot(lower, flat_hot, preferred_element_type=jnp.float32)
    slot_pos = jnp.sum(earlier * flat_hot.astype(jnp.float32), -1).astype(jnp.int32)
    expert_ids = routes.reshape(-1)
    exp_dev = expert_gate.shape[0]
    capacity = tensor_size * (5 * seq_len * top_count // (4 * experts * tensor_size))
    slot_index = expert_ids * capacity + slot_pos
    token_ids = jnp.arange(seq_len * top_count) // top_count
    slot_token = jnp.full((experts * capacity,), seq_len, jnp.int32).at[slot_index].set(token_ids)
    slot_gate = (
        jnp.zeros((experts * capacity,), jnp.float32).at[slot_index].set(gate_values.reshape(-1))
    )
    slot_valid = (slot_token < seq_len).astype(jnp.float32)
    tile_rows = D // 128
    send_both = dispatch_rows(slot_token, normed_two, grad_seq, slot_valid, slot_gate).reshape(
        dp_size, exp_dev, capacity, 2 * tile_rows, 128
    )
    shared_local, send_both = lax.optimization_barrier((shared_local, send_both))
    shared_all = lax.all_gather(shared_local, "dp", axis=0, tiled=True)
    gate_shared = shared_all[:, :shared_cols]
    up_shared = shared_all[:, shared_cols : 2 * shared_cols]
    down_shared_t = shared_all[:, 2 * shared_cols :]
    recv_both = lax.all_to_all(send_both, "dp", split_axis=0, concat_axis=0, tiled=True)
    recv_both = recv_both.reshape(dp_size, exp_dev, capacity, 2 * D)
    recv_rows = recv_both[..., :D]
    recv_grads = recv_both[..., D:]
    gate_pre = jnp.einsum(
        "sjcd,jfd->sjcf", recv_rows, expert_gate, preferred_element_type=jnp.float32
    )
    up_pre = jnp.einsum("sjcd,jfd->sjcf", recv_rows, expert_up, preferred_element_type=jnp.float32)
    sigmoid_gate = jax.nn.sigmoid(gate_pre)
    expert_act = (gate_pre * sigmoid_gate * up_pre).astype(jnp.bfloat16)
    expert_out = jnp.einsum(
        "sjcf,jfd->sjcd", expert_act, expert_down, preferred_element_type=jnp.float32
    )
    act_grad = jnp.einsum(
        "sjcd,jfd->sjcf", recv_grads, expert_down, preferred_element_type=jnp.float32
    )
    gate_low_grad, up_low_grad = silu_back(act_grad, gate_pre, up_pre, sigmoid_gate)
    expert_down_grad = jnp.einsum(
        "sjcf,sjcd->jfd", expert_act, recv_grads, preferred_element_type=jnp.float32
    )
    expert_gate_grad = jnp.einsum(
        "sjcf,sjcd->jfd", gate_low_grad, recv_rows, preferred_element_type=jnp.float32
    )
    expert_up_grad = jnp.einsum(
        "sjcf,sjcd->jfd", up_low_grad, recv_rows, preferred_element_type=jnp.float32
    )
    row_grads = jnp.einsum(
        "sjcf,jfd->sjcd", gate_low_grad, expert_gate, preferred_element_type=jnp.float32
    )
    row_grads = row_grads + jnp.einsum(
        "sjcf,jfd->sjcd", up_low_grad, expert_up, preferred_element_type=jnp.float32
    )
    back_both = lax.all_to_all(
        jnp.concatenate(
            [expert_out.astype(jnp.bfloat16), row_grads.astype(jnp.bfloat16)], -1
        ).reshape(dp_size, exp_dev, capacity, 2 * tile_rows, 128),
        "dp",
        split_axis=0,
        concat_axis=0,
        tiled=True,
    )
    shared_pre_gate = jnp.dot(normed_two, gate_shared, preferred_element_type=jnp.float32)
    shared_pre_up = jnp.dot(normed_two, up_shared, preferred_element_type=jnp.float32)
    shared_sigmoid = jax.nn.sigmoid(shared_pre_gate)
    shared_act = (shared_pre_gate * shared_sigmoid * shared_pre_up).astype(jnp.bfloat16)
    shared_out = jnp.einsum(
        "tf,df->td", shared_act, down_shared_t, preferred_element_type=jnp.float32
    )
    shared_act_grad = jnp.dot(grad_seq, down_shared_t, preferred_element_type=jnp.float32)
    shared_gate_low, shared_up_low = silu_back(
        shared_act_grad, shared_pre_gate, shared_pre_up, shared_sigmoid
    )
    shared_down_grad_t = jnp.dot(grad_seq.T, shared_act, preferred_element_type=jnp.float32)
    shared_gate_grad = jnp.dot(normed_two.T, shared_gate_low, preferred_element_type=jnp.float32)
    shared_up_grad = jnp.dot(normed_two.T, shared_up_low, preferred_element_type=jnp.float32)
    shared_back = jnp.einsum(
        "tf,df->td", shared_gate_low, gate_shared, preferred_element_type=jnp.float32
    )
    shared_back = shared_back + jnp.einsum(
        "tf,df->td", shared_up_low, up_shared, preferred_element_type=jnp.float32
    )
    shared_grads_in = jnp.concatenate(
        [shared_gate_grad, shared_up_grad, shared_down_grad_t], 1
    ).astype(jnp.bfloat16)
    grad_seq_f = grad_seq.astype(jnp.float32)
    table_rows = experts * capacity
    feed_part, back_part, gate_cols = combine_rows(
        slot_index.reshape(seq_len, top_count),
        back_both.reshape(table_rows, 2 * tile_rows, 128),
        gate_values,
        grad_seq,
        shared_out,
        shared_back,
    )
    gate_part = gate_cols[:, :top_count]
    feed_own = lax.psum_scatter(feed_part, "tensor", scatter_dimension=0, tiled=True).astype(
        jnp.float32
    )
    output = (residual_own + feed_own).astype(jnp.bfloat16)
    normed_two_grad, gate_grads = lax.psum(
        (back_part, gate_part.astype(jnp.bfloat16)),
        "tensor",
    )
    normed_two_grad = normed_two_grad.astype(jnp.float32)
    gate_grads = gate_grads.astype(jnp.float32)
    weighted_total = jnp.sum(gate_values * gate_grads, -1, keepdims=True)
    chosen_grads = gate_values * (gate_grads - weighted_total)
    logit_grads = jnp.sum(jnp.where(chosen_hot, chosen_grads[:, :, None], 0.0), 1)
    normed_two_grad = normed_two_grad + jnp.dot(
        logit_grads, router_weights.astype(jnp.float32).T, precision=HIGH
    )
    residual_grad = grad_seq_f + norm_back(residual_all, scale_two, gain_two, normed_two_grad)
    branch_grad = residual_grad.astype(jnp.bfloat16)
    shared_grads_in, branch_grad = lax.optimization_barrier((shared_grads_in, branch_grad))
    shared_pack = lax.psum_scatter(
        shared_grads_in, "dp", scatter_dimension=0, tiled=True
    ).astype(jnp.float32)
    output_grad_w_t = jnp.dot(branch_grad.T, mixed_all, preferred_element_type=jnp.float32)
    mixed_grad = (
        jnp.dot(branch_grad, output_weights_t, preferred_element_type=jnp.float32)
        .astype(jnp.bfloat16)
        .reshape(seq_len, head_count, DV)
    )
    keys_nope_grad = jnp.zeros((seq_len, head_count, DN), jnp.float32)
    key_rope_grad = jnp.zeros((seq_len, DR), jnp.float32)
    values_grad = jnp.zeros((seq_len, head_count, DV), jnp.float32)
    query_grad_list = []
    for block_index, rows_start in enumerate(range(0, seq_len, block_rows)):
        query_block = query_low[rows_start : rows_start + block_rows]
        masked = block_scores(query_block, keys_nope, key_rope, rows_start, prefix_len, score_scale)
        prob_full = jnp.exp(masked - lse_list[block_index])
        prob_low = prob_full.astype(jnp.bfloat16)
        mixed_block = mixed_grad[rows_start : rows_start + block_rows]
        prob_grads = jnp.einsum(
            "qhv,khv->hqk", mixed_block, values_low, preferred_element_type=jnp.float32
        )
        row_delta = jnp.sum(prob_full * prob_grads, -1, keepdims=True)
        score_grads = (prob_full * (prob_grads - row_delta)).astype(jnp.bfloat16)
        query_nope_grad = (
            jnp.einsum("hqk,khd->qhd", score_grads, keys_nope, preferred_element_type=jnp.float32)
            * score_scale
        )
        query_rope_grad = (
            jnp.einsum("hqk,kr->qhr", score_grads, key_rope, preferred_element_type=jnp.float32)
            * score_scale
        )
        keys_nope_grad = (
            keys_nope_grad
            + jnp.einsum(
                "hqk,qhd->khd",
                score_grads,
                query_block[..., :DN],
                preferred_element_type=jnp.float32,
            )
            * score_scale
        )
        key_rope_grad = (
            key_rope_grad
            + jnp.einsum(
                "hqk,qhr->kr",
                score_grads,
                query_block[..., DN:],
                preferred_element_type=jnp.float32,
            )
            * score_scale
        )
        values_grad = values_grad + jnp.einsum(
            "hqk,qhv->khv", prob_low, mixed_block, preferred_element_type=jnp.float32
        )
        block_cosines = all_cosines[rows_start : rows_start + block_rows, None, :]
        block_sines = all_sines[rows_start : rows_start + block_rows, None, :]
        query_grad_list.append(
            jnp.concatenate(
                [
                    query_nope_grad,
                    rotate_back(round_trip(query_rope_grad), block_cosines, block_sines),
                ],
                -1,
            ).astype(jnp.bfloat16)
        )
    query_grads = jnp.concatenate(query_grad_list, 0).reshape(seq_len, head_count * (DN + DR))
    feed_own, shared_pack, query_grads = lax.optimization_barrier((feed_own, shared_pack, query_grads))
    query_grad_w = jnp.dot(normed_all.T, query_grads, preferred_element_type=jnp.float32)
    normed_grad_part = jnp.dot(query_grads, query_weights.T, preferred_element_type=jnp.float32)
    expand_grads = jnp.concatenate(
        [keys_nope_grad.astype(jnp.bfloat16), values_grad.astype(jnp.bfloat16)], -1
    ).reshape(seq_len, head_count * (DN + DV))
    expand_grad_w = jnp.dot(compressed_seq.T, expand_grads, preferred_element_type=jnp.float32)
    compressed_grad_part = jnp.dot(
        expand_grads, expand_weights.T, preferred_element_type=jnp.float32
    )
    latent_grad_part = jnp.concatenate([compressed_grad_part, key_rope_grad], -1)
    attn_pack = lax.psum_scatter(
        jnp.concatenate(
            [
                query_grad_w,
                output_grad_w_t,
                expand_grad_w.reshape(dp_size * rows_dp, expand_flat_cols),
            ],
            1,
        ).astype(jnp.bfloat16),
        "dp",
        scatter_dimension=0,
        tiled=True,
    ).astype(jnp.float32)
    token_all = lax.psum(
        jnp.concatenate([normed_grad_part, latent_grad_part], 1).astype(jnp.bfloat16), "tensor"
    ).astype(jnp.float32)
    compressed_grad_all = token_all[:, D : D + KVR]
    kv_gain_full = jnp.sum(compressed_grad_all * compressed_all * scale_kv_all, 0)
    raw_grad_all = jnp.concatenate(
        [
            norm_back(compressed_all, scale_kv_all, gain_kv, compressed_grad_all),
            rotate_back(token_all[:, D + KVR :], all_cosines, all_sines),
        ],
        -1,
    ).astype(jnp.bfloat16)
    normed_grad_all = token_all[:, :D] + jnp.dot(
        raw_grad_all, latent_weights.T, preferred_element_type=jnp.float32
    )
    normed_grad = lax.dynamic_slice_in_dim(normed_grad_all, start_row, tok_dev, 0)
    hidden_grad = lax.dynamic_slice_in_dim(residual_grad, start_row, tok_dev, 0) + norm_back(
        hidden_f, scale_one, gain_one, normed_grad
    )
    row_per = D // (dp_size * tensor_size)

    def own_rows(values):
        split = values.reshape(values.shape[0], dp_size, tensor_size, row_per)
        return lax.dynamic_slice_in_dim(split, tensor_rank, 1, 2).reshape(values.shape[0], -1)

    latent_rows = jnp.dot(own_rows(normed_all).T, raw_grad_all, preferred_element_type=jnp.float32)
    attn_gain_rows = jnp.sum(
        own_rows(normed_grad_all) * own_rows(hidden_all_f) * scale_one_all, 0
    )
    second_gain_rows = jnp.sum(
        own_rows(normed_two_grad) * own_rows(residual_all) * scale_two, 0
    )
    router_rows = jnp.dot(
        own_rows(normed_two).astype(jnp.float32).T, logit_grads, precision=HIGH
    )
    kv_per = kv_gain_full.shape[0] // (dp_size * tensor_size)
    kv_rows_own = lax.dynamic_slice_in_dim(
        kv_gain_full.reshape(dp_size, tensor_size, kv_per), tensor_rank, 1, 1
    ).reshape(dp_size, kv_per)
    kv_column = jnp.pad(kv_rows_own, ((0, 0), (0, row_per - kv_per))).reshape(-1)
    small_pack = jnp.concatenate(
        [
            latent_rows,
            router_rows,
            attn_gain_rows[:, None],
            second_gain_rows[:, None],
            kv_column[:, None],
        ],
        1,
    )
    small_own = lax.psum_scatter(small_pack, "dp", scatter_dimension=0, tiled=True)
    cut = [0]
    for width in (latent_cols, experts, 1, 1, 1):
        cut.append(cut[-1] + width)
    latent_proj_grad = small_own[:, cut[0] : cut[1]]
    router_out = small_own[:, cut[1] : cut[2]]
    attn_gain_out = small_own[:, cut[2]]
    second_gain_out = small_own[:, cut[3]]
    latent_gain_out = small_own[:kv_per, cut[4]]
    cut = [0]
    for width in (head_cols, out_cols, expand_flat_cols):
        cut.append(cut[-1] + width)
    query_proj_grad = attn_pack[:, cut[0] : cut[1]]
    output_proj_grad = attn_pack[:, cut[1] : cut[2]].T
    expand_proj_grad = attn_pack[:, cut[2] : cut[3]].reshape(kv_rows, expand_cols)
    shared_gate_out = shared_pack[:, :shared_cols]
    shared_up_out = shared_pack[:, shared_cols : 2 * shared_cols]
    shared_down_out = shared_pack[:, 2 * shared_cols :].T
    return (
        output,
        hidden_grad,
        attn_gain_out,
        query_proj_grad,
        latent_proj_grad,
        latent_gain_out,
        expand_proj_grad,
        output_proj_grad,
        second_gain_out,
        router_out,
        expert_gate_grad,
        expert_up_grad,
        expert_down_grad,
        shared_gate_out,
        shared_up_out,
        shared_down_out,
    )


def solution(mesh):
    return jax.shard_map(
        shards,
        mesh=mesh,
        in_specs=(
            P(("dp", "tensor"), None),
            P("dp", None),
            P("dp"),
            P("dp"),
            P("dp", "tensor"),
            P("dp", None),
            P("dp"),
            P("dp", "tensor"),
            P("tensor", "dp"),
            P("dp"),
            P("dp", None),
            P("dp", "tensor", None),
            P("dp", "tensor", None),
            P("dp", "tensor", None),
            P("dp", "tensor"),
            P("dp", "tensor"),
            P("tensor", "dp"),
            P(("dp", "tensor"), None),
        ),
        out_specs=(
            P(("dp", "tensor"), None),
            P(("dp", "tensor"), None),
            P(("dp", "tensor")),
            P("dp", "tensor"),
            P(("dp", "tensor"), None),
            P(("dp", "tensor")),
            P("dp", "tensor"),
            P("tensor", "dp"),
            P(("dp", "tensor")),
            P(("dp", "tensor"), None),
            P("dp", "tensor", None),
            P("dp", "tensor", None),
            P("dp", "tensor", None),
            P("dp", "tensor"),
            P("dp", "tensor"),
            P("tensor", "dp"),
        ),
        check_vma=False,
    )
```

```python
import math

import jax
import jax.numpy as jnp
from jax import lax
from jax.experimental import pallas as pl
from jax.experimental.pallas import tpu as pltpu
from jax.sharding import PartitionSpec as P

D = 2048
DN = 128
DR = 64
DV = 128
KVR = 512


EPS = 1e-06
HIGH = lax.Precision.HIGHEST
MASKED = -1e30


def norm_scale(values):
    return lax.rsqrt(jnp.mean(values * values, -1, keepdims=True) + EPS)


def norm_back(values, scales, gains, upstream):
    weighted = gains * upstream
    return scales * weighted - values * scales**3 * jnp.mean(values * weighted, -1, keepdims=True)


def rope_tables(positions, rope_width):
    half_width = rope_width // 2
    frequency = 10000.0 ** (-2.0 * jnp.arange(half_width).astype(jnp.float32) / rope_width)
    angles = positions.astype(jnp.float32)[:, None] * frequency[None, :]
    return (jnp.cos(angles), jnp.sin(angles))


def rotate(vectors, cosines, sine_values):
    half_width = vectors.shape[-1] // 2
    front_half = vectors[..., :half_width]
    back_half = vectors[..., half_width:]
    return jnp.concatenate(
        [
            front_half * cosines - back_half * sine_values,
            back_half * cosines + front_half * sine_values,
        ],
        -1,
    )


def rotate_back(gradients, cosines, sine_values):
    half_width = gradients.shape[-1] // 2
    front_half = gradients[..., :half_width]
    back_half = gradients[..., half_width:]
    return jnp.concatenate(
        [
            front_half * cosines + back_half * sine_values,
            back_half * cosines - front_half * sine_values,
        ],
        -1,
    )


def round_trip(values):
    return lax.optimization_barrier(values.astype(jnp.bfloat16)).astype(jnp.float32)


def block_scores(query_block, keys_nope, key_rope, rows_start, prefix_len, score_scale):
    raw_scores = jnp.einsum(
        "qhd,khd->hqk", query_block[..., :DN], keys_nope, preferred_element_type=jnp.float32
    )
    raw_scores = raw_scores + jnp.einsum(
        "qhr,kr->hqk", query_block[..., DN:], key_rope, preferred_element_type=jnp.float32
    )
    query_places = rows_start + jnp.arange(query_block.shape[0])
    key_places = jnp.arange(keys_nope.shape[0])
    visible = (key_places[None, :] <= query_places[:, None]) | (key_places[None, :] < prefix_len)
    return jnp.where(visible[None], raw_scores * score_scale, MASKED)


def silu_back(act_grad, gate_pre, up_pre, sigmoid_gate):
    up_grad = (act_grad * gate_pre * sigmoid_gate).astype(jnp.bfloat16)
    gate_grad = (act_grad * up_pre * sigmoid_gate * (1.0 + gate_pre * (1.0 - sigmoid_gate))).astype(
        jnp.bfloat16
    )
    return (gate_grad, up_grad)


def dispatch_kernel(tok_ref, both_hbm, col_ref, out_ref, both_buf, sems):
    block = both_buf.shape[0]
    tile_rows = both_buf.shape[1] // 2
    last = both_hbm.shape[0] - 1
    base = pl.program_id(0) * block

    def start(r, carry):
        tok = jnp.minimum(tok_ref[base + r], last)
        pltpu.make_async_copy(both_hbm.at[tok], both_buf.at[r], sems.at[r]).start()
        return carry

    lax.fori_loop(0, block, start, 0, unroll=4)

    def finish(r, carry):
        pltpu.make_async_copy(both_hbm.at[0], both_buf.at[r], sems.at[r]).wait()
        return carry

    lax.fori_loop(0, block, finish, 0, unroll=4)
    rows = both_buf[:, :tile_rows, :]
    out_ref[:, :tile_rows, :] = jnp.where(col_ref[0] > 0, rows, jnp.zeros_like(rows))
    out_ref[:, tile_rows:, :] = (
        both_buf[:, tile_rows:, :].astype(jnp.float32) * col_ref[1]
    ).astype(out_ref.dtype)


def dispatch_rows(slot_token, rows, grads, valid, gate, block=128):
    slots = slot_token.shape[0]
    count, width = rows.shape
    tile_rows = width // 128
    cols = jnp.broadcast_to(jnp.stack([valid, gate])[:, :, None, None], (2, slots, 1, 128))
    both = jnp.concatenate([rows, grads], 1).reshape(count, 2 * tile_rows, 128)
    out = pl.pallas_call(
        dispatch_kernel,
        out_shape=jax.ShapeDtypeStruct((slots, 2 * tile_rows, 128), rows.dtype),
        grid_spec=pltpu.PrefetchScalarGridSpec(
            num_scalar_prefetch=1,
            grid=(slots // block,),
            in_specs=[
                pl.BlockSpec(memory_space=pl.ANY),
                pl.BlockSpec((2, block, 1, 128), lambda i, tok: (0, i, 0, 0)),
            ],
            out_specs=pl.BlockSpec((block, 2 * tile_rows, 128), lambda i, tok: (i, 0, 0)),
            scratch_shapes=[
                pltpu.VMEM((block, 2 * tile_rows, 128), rows.dtype),
                pltpu.SemaphoreType.DMA((block,)),
            ],
        ),
        cost_estimate=pl.CostEstimate(
            flops=slots * width, transcendentals=0, bytes_accessed=4 * slots * 2 * width
        ),
    )(slot_token, both, cols)
    return out


def combine_kernel(
    slot_ref, table_hbm, gate_ref, grad_ref, shared_out_ref, shared_back_ref,
    feed_ref, back_ref, part_ref, picked, sems,
):
    top = picked.shape[0]
    block = picked.shape[1]
    tile_rows = grad_ref.shape[1]
    last = table_hbm.shape[0] - 1
    base = pl.program_id(0) * block

    def start(r, carry):
        for k in range(top):
            slot = jnp.clip(slot_ref[(base + r) * top + k], 0, last)
            pltpu.make_async_copy(table_hbm.at[slot], picked.at[k, r], sems.at[k, r]).start()
        return carry

    lax.fori_loop(0, block, start, 0)

    def finish(r, carry):
        for k in range(top):
            pltpu.make_async_copy(table_hbm.at[0], picked.at[k, r], sems.at[k, r]).wait()
        return carry

    lax.fori_loop(0, block, finish, 0)
    grad = grad_ref[...].astype(jnp.float32)
    weighted = None
    backs = None
    lanes = lax.broadcasted_iota(jnp.int32, part_ref.shape, 2)
    parts = jnp.zeros(part_ref.shape, jnp.float32)
    for k in range(top):
        out_k = picked[k, :, :tile_rows, :].astype(jnp.float32)
        term = gate_ref[k] * out_k
        weighted = term if weighted is None else weighted + term
        back_k = picked[k, :, tile_rows:, :].astype(jnp.float32)
        backs = back_k if backs is None else backs + back_k
        dot_k = jnp.sum(jnp.sum(grad * out_k, 2, keepdims=True), 1, keepdims=True)
        parts = jnp.where(lanes == k, dot_k, parts)
    feed_ref[...] = (shared_out_ref[...] + weighted).astype(feed_ref.dtype)
    back_ref[...] = (backs + shared_back_ref[...]).astype(back_ref.dtype)
    part_ref[...] = parts


def combine_rows(slot_index, table, gate_values, grad, shared_out, shared_back, block=128):
    tokens, top = gate_values.shape
    width = grad.shape[1]
    tile_rows = width // 128
    gates = jnp.broadcast_to(gate_values.T[:, :, None, None], (top, tokens, 1, 128))
    row_spec = pl.BlockSpec((block, tile_rows, 128), lambda i, s: (i, 0, 0))
    feed, back, parts = pl.pallas_call(
        combine_kernel,
        out_shape=(
            jax.ShapeDtypeStruct((tokens, tile_rows, 128), jnp.bfloat16),
            jax.ShapeDtypeStruct((tokens, tile_rows, 128), jnp.bfloat16),
            jax.ShapeDtypeStruct((tokens, 1, 128), jnp.float32),
        ),
        grid_spec=pltpu.PrefetchScalarGridSpec(
            num_scalar_prefetch=1,
            grid=(tokens // block,),
            in_specs=[
                pl.BlockSpec(memory_space=pl.ANY),
                pl.BlockSpec((top, block, 1, 128), lambda i, s: (0, i, 0, 0)),
                row_spec,
                row_spec,
                row_spec,
            ],
            out_specs=[row_spec, row_spec, pl.BlockSpec((block, 1, 128), lambda i, s: (i, 0, 0))],
            scratch_shapes=[
                pltpu.VMEM((top, block, 2 * tile_rows, 128), table.dtype),
                pltpu.SemaphoreType.DMA((top, block)),
            ],
        ),
        cost_estimate=pl.CostEstimate(
            flops=8 * tokens * top * width,
            transcendentals=0,
            bytes_accessed=tokens * (top * 4 * width + 2 * width + 8 * width + 4 * width),
        ),
    )(
        slot_index.reshape(-1),
        table.reshape(table.shape[0], 2 * tile_rows, 128),
        gates,
        grad.reshape(tokens, tile_rows, 128),
        shared_out.reshape(tokens, tile_rows, 128),
        shared_back.reshape(tokens, tile_rows, 128),
    )
    return feed.reshape(tokens, width), back.reshape(tokens, width), parts[:, 0, :top]


def shards(
    hidden,
    routes,
    prefix,
    attn_gain,
    query_proj,
    latent_proj,
    latent_gain,
    expand_proj,
    output_proj,
    second_gain,
    router_proj,
    expert_gate,
    expert_up,
    expert_down,
    shared_gate,
    shared_up,
    shared_down,
    out_grad,
):
    tok_dev = hidden.shape[0]
    tensor_size = lax.axis_size("tensor")
    tensor_rank = lax.axis_index("tensor")
    dp_size = lax.axis_size("dp")
    seq_len = tok_dev * tensor_size
    start_row = tensor_rank * tok_dev
    rows_dp = attn_gain.shape[0]
    kv_rows = latent_gain.shape[0]
    head_cols = query_proj.shape[1]
    latent_cols = latent_proj.shape[1]
    expand_cols = expand_proj.shape[1]
    expand_flat_cols = kv_rows * expand_cols // rows_dp
    first_pack = jnp.concatenate(
        [
            query_proj,
            latent_proj,
            expand_proj.reshape(rows_dp, expand_flat_cols),
            attn_gain[:, None],
            jnp.pad(latent_gain, (0, rows_dp - kv_rows))[:, None],
        ],
        1,
    )
    first_all = lax.all_gather(first_pack, "dp", axis=0, tiled=True)
    cut = [0]
    for width in (head_cols, latent_cols, expand_flat_cols, 1, 1):
        cut.append(cut[-1] + width)
    query_weights = first_all[:, cut[0] : cut[1]]
    latent_weights = first_all[:, cut[1] : cut[2]]
    expand_weights = first_all[:, cut[2] : cut[3]].reshape(dp_size * kv_rows, expand_cols)
    attn_gains = first_all[:, cut[3]]
    kv_gains = first_all[:, cut[4]].reshape(dp_size, rows_dp)[:, :kv_rows].reshape(-1)
    out_cols = output_proj.shape[0]
    experts = router_proj.shape[1]
    shared_cols = shared_gate.shape[1]
    second_pack = jnp.concatenate([output_proj.T, second_gain[:, None], router_proj], 1)
    second_all = lax.all_gather(second_pack, "dp", axis=0, tiled=True)
    output_weights_t = second_all[:, :out_cols]
    second_gains = second_all[:, out_cols]
    router_weights = second_all[:, out_cols + 1 :]
    shared_local = jnp.concatenate([shared_gate, shared_up, shared_down.T], 1)

    hidden_all = lax.all_gather(hidden, "tensor", axis=0, tiled=True)
    grad_seq = lax.all_gather(out_grad, "tensor", axis=0, tiled=True)
    hidden_all_f = hidden_all.astype(jnp.float32)
    scale_one_all = norm_scale(hidden_all_f)
    gain_one = attn_gains.astype(jnp.float32)
    normed_all = (hidden_all_f * scale_one_all * gain_one).astype(jnp.bfloat16)
    hidden_f = lax.dynamic_slice_in_dim(hidden_all_f, start_row, tok_dev, 0)
    scale_one = lax.dynamic_slice_in_dim(scale_one_all, start_row, tok_dev, 0)
    normed_own = lax.dynamic_slice_in_dim(normed_all, start_row, tok_dev, 0)
    latent_raw_all = jnp.dot(normed_all, latent_weights, preferred_element_type=jnp.float32)
    compressed_all = latent_raw_all[:, :KVR]
    scale_kv_all = norm_scale(compressed_all)
    gain_kv = kv_gains.astype(jnp.float32)
    all_cosines, all_sines = rope_tables(jnp.arange(seq_len), DR)
    latent_seq = jnp.concatenate(
        [
            compressed_all * scale_kv_all * gain_kv,
            rotate(latent_raw_all[:, KVR:], all_cosines, all_sines),
        ],
        -1,
    ).astype(jnp.bfloat16)
    compressed = lax.dynamic_slice_in_dim(compressed_all, start_row, tok_dev, 0)
    scale_kv = lax.dynamic_slice_in_dim(scale_kv_all, start_row, tok_dev, 0)
    own_cosines = lax.dynamic_slice_in_dim(all_cosines, start_row, tok_dev, 0)
    own_sines = lax.dynamic_slice_in_dim(all_sines, start_row, tok_dev, 0)
    head_count = query_weights.shape[1] // (DN + DR)
    query_raw = jnp.dot(normed_all, query_weights, preferred_element_type=jnp.float32).reshape(
        seq_len, head_count, DN + DR
    )
    query_low = jnp.concatenate(
        [
            query_raw[..., :DN],
            rotate(query_raw[..., DN:], all_cosines[:, None, :], all_sines[:, None, :]),
        ],
        -1,
    ).astype(jnp.bfloat16)
    compressed_seq = latent_seq[:, :KVR]
    key_rope = latent_seq[:, KVR:]
    expanded = jnp.dot(compressed_seq, expand_weights, preferred_element_type=jnp.float32).reshape(
        seq_len, head_count, DN + DV
    )
    keys_nope = expanded[..., :DN].astype(jnp.bfloat16)
    values_low = expanded[..., DN:].astype(jnp.bfloat16)
    score_scale = 1.0 / math.sqrt(DN + DR)
    block_rows = min(512, seq_len)
    prefix_len = prefix[0]
    lse_list = []
    mixed_list = []
    for rows_start in range(0, seq_len, block_rows):
        query_block = query_low[rows_start : rows_start + block_rows]
        masked = block_scores(query_block, keys_nope, key_rope, rows_start, prefix_len, score_scale)
        top_score = jnp.max(masked, -1, keepdims=True)
        exp_scores = jnp.exp(masked - top_score)
        totals = jnp.sum(exp_scores, -1, keepdims=True)
        prob_low = (exp_scores / totals).astype(jnp.bfloat16)
        lse_list.append(top_score + jnp.log(totals))
        mixed_list.append(
            jnp.einsum(
                "hqk,khv->qhv", prob_low, values_low, preferred_element_type=jnp.float32
            ).astype(jnp.bfloat16)
        )
    mixed_all = jnp.concatenate(mixed_list, 0).reshape(seq_len, head_count * DV)
    attn_part = jnp.einsum(
        "tk,dk->td", mixed_all, output_weights_t, preferred_element_type=jnp.float32
    )
    branch_all = lax.psum(attn_part.astype(jnp.bfloat16), "tensor").astype(jnp.float32)
    residual_all = hidden_all_f + branch_all
    residual_own = lax.dynamic_slice_in_dim(residual_all, start_row, tok_dev, 0)
    scale_two = norm_scale(residual_all)
    gain_two = second_gains.astype(jnp.float32)
    normed_two = (residual_all * scale_two * gain_two).astype(jnp.bfloat16)
    logits = jnp.dot(normed_two, router_weights, preferred_element_type=jnp.float32)
    top_count = routes.shape[1]
    chosen_hot = routes[:, :, None] == jnp.arange(experts)[None, None, :]
    chosen_logits = jnp.sum(jnp.where(chosen_hot, logits[:, None, :], 0.0), -1)
    gate_values = jax.nn.softmax(chosen_logits, axis=-1)
    assignments = seq_len * top_count
    flat_hot = chosen_hot.reshape(assignments, experts).astype(jnp.bfloat16)
    lower = (jnp.arange(assignments)[:, None] > jnp.arange(assignments)[None, :]).astype(jnp.bfloat16)
    earlier = jnp.dot(lower, flat_hot, preferred_element_type=jnp.float32)
    slot_pos = jnp.sum(earlier * flat_hot.astype(jnp.float32), -1).astype(jnp.int32)
    expert_ids = routes.reshape(-1)
    exp_dev = expert_gate.shape[0]
    capacity = tensor_size * (5 * seq_len * top_count // (4 * experts * tensor_size))
    slot_index = expert_ids * capacity + slot_pos
    token_ids = jnp.arange(seq_len * top_count) // top_count
    slot_token = jnp.full((experts * capacity,), seq_len, jnp.int32).at[slot_index].set(token_ids)
    slot_gate = (
        jnp.zeros((experts * capacity,), jnp.float32).at[slot_index].set(gate_values.reshape(-1))
    )
    slot_valid = (slot_token < seq_len).astype(jnp.float32)
    tile_rows = D // 128
    send_both = dispatch_rows(slot_token, normed_two, grad_seq, slot_valid, slot_gate).reshape(
        dp_size, exp_dev, capacity, 2 * tile_rows, 128
    )
    shared_local, send_both = lax.optimization_barrier((shared_local, send_both))
    shared_all = lax.all_gather(shared_local, "dp", axis=0, tiled=True)
    gate_shared = shared_all[:, :shared_cols]
    up_shared = shared_all[:, shared_cols : 2 * shared_cols]
    down_shared_t = shared_all[:, 2 * shared_cols :]
    recv_both = lax.all_to_all(send_both, "dp", split_axis=0, concat_axis=0, tiled=True)
    recv_both = recv_both.reshape(dp_size, exp_dev, capacity, 2 * D)
    recv_rows = recv_both[..., :D]
    recv_grads = recv_both[..., D:]
    gate_pre = jnp.einsum(
        "sjcd,jfd->sjcf", recv_rows, expert_gate, preferred_element_type=jnp.float32
    )
    up_pre = jnp.einsum("sjcd,jfd->sjcf", recv_rows, expert_up, preferred_element_type=jnp.float32)
    sigmoid_gate = jax.nn.sigmoid(gate_pre)
    expert_act = (gate_pre * sigmoid_gate * up_pre).astype(jnp.bfloat16)
    expert_out = jnp.einsum(
        "sjcf,jfd->sjcd", expert_act, expert_down, preferred_element_type=jnp.float32
    )
    act_grad = jnp.einsum(
        "sjcd,jfd->sjcf", recv_grads, expert_down, preferred_element_type=jnp.float32
    )
    gate_low_grad, up_low_grad = silu_back(act_grad, gate_pre, up_pre, sigmoid_gate)
    expert_down_grad = jnp.einsum(
        "sjcf,sjcd->jfd", expert_act, recv_grads, preferred_element_type=jnp.float32
    )
    expert_gate_grad = jnp.einsum(
        "sjcf,sjcd->jfd", gate_low_grad, recv_rows, preferred_element_type=jnp.float32
    )
    expert_up_grad = jnp.einsum(
        "sjcf,sjcd->jfd", up_low_grad, recv_rows, preferred_element_type=jnp.float32
    )
    row_grads = jnp.einsum(
        "sjcf,jfd->sjcd", gate_low_grad, expert_gate, preferred_element_type=jnp.float32
    )
    row_grads = row_grads + jnp.einsum(
        "sjcf,jfd->sjcd", up_low_grad, expert_up, preferred_element_type=jnp.float32
    )
    back_both = lax.all_to_all(
        jnp.concatenate(
            [expert_out.astype(jnp.bfloat16), row_grads.astype(jnp.bfloat16)], -1
        ).reshape(dp_size, exp_dev, capacity, 2 * tile_rows, 128),
        "dp",
        split_axis=0,
        concat_axis=0,
        tiled=True,
    )
    shared_pre_gate = jnp.dot(normed_two, gate_shared, preferred_element_type=jnp.float32)
    shared_pre_up = jnp.dot(normed_two, up_shared, preferred_element_type=jnp.float32)
    shared_sigmoid = jax.nn.sigmoid(shared_pre_gate)
    shared_act = (shared_pre_gate * shared_sigmoid * shared_pre_up).astype(jnp.bfloat16)
    shared_out = jnp.einsum(
        "tf,df->td", shared_act, down_shared_t, preferred_element_type=jnp.float32
    )
    shared_act_grad = jnp.dot(grad_seq, down_shared_t, preferred_element_type=jnp.float32)
    shared_gate_low, shared_up_low = silu_back(
        shared_act_grad, shared_pre_gate, shared_pre_up, shared_sigmoid
    )
    shared_down_grad_t = jnp.dot(grad_seq.T, shared_act, preferred_element_type=jnp.float32)
    shared_gate_grad = jnp.dot(normed_two.T, shared_gate_low, preferred_element_type=jnp.float32)
    shared_up_grad = jnp.dot(normed_two.T, shared_up_low, preferred_element_type=jnp.float32)
    shared_back = jnp.einsum(
        "tf,df->td", shared_gate_low, gate_shared, preferred_element_type=jnp.float32
    )
    shared_back = shared_back + jnp.einsum(
        "tf,df->td", shared_up_low, up_shared, preferred_element_type=jnp.float32
    )
    shared_grads_in = jnp.concatenate(
        [shared_gate_grad, shared_up_grad, shared_down_grad_t], 1
    ).astype(jnp.bfloat16)
    grad_seq_f = grad_seq.astype(jnp.float32)
    table_rows = experts * capacity
    feed_part, back_part, gate_cols = combine_rows(
        slot_index.reshape(seq_len, top_count),
        back_both.reshape(table_rows, 2 * tile_rows, 128),
        gate_values,
        grad_seq,
        shared_out,
        shared_back,
    )
    gate_part = gate_cols[:, :top_count]
    feed_own = lax.psum_scatter(feed_part, "tensor", scatter_dimension=0, tiled=True).astype(
        jnp.float32
    )
    output = (residual_own + feed_own).astype(jnp.bfloat16)
    normed_two_grad, gate_grads = lax.psum(
        (back_part, gate_part.astype(jnp.bfloat16)),
        "tensor",
    )
    normed_two_grad = normed_two_grad.astype(jnp.float32)
    gate_grads = gate_grads.astype(jnp.float32)
    weighted_total = jnp.sum(gate_values * gate_grads, -1, keepdims=True)
    chosen_grads = gate_values * (gate_grads - weighted_total)
    logit_grads = jnp.sum(jnp.where(chosen_hot, chosen_grads[:, :, None], 0.0), 1)
    normed_two_grad = normed_two_grad + jnp.dot(
        logit_grads, router_weights.astype(jnp.float32).T, precision=HIGH
    )
    residual_grad = grad_seq_f + norm_back(residual_all, scale_two, gain_two, normed_two_grad)
    branch_grad = residual_grad.astype(jnp.bfloat16)
    shared_grads_in, branch_grad = lax.optimization_barrier((shared_grads_in, branch_grad))
    shared_pack = lax.psum_scatter(
        shared_grads_in, "dp", scatter_dimension=0, tiled=True
    ).astype(jnp.float32)
    output_grad_w_t = jnp.dot(branch_grad.T, mixed_all, preferred_element_type=jnp.float32)
    mixed_grad = (
        jnp.dot(branch_grad, output_weights_t, preferred_element_type=jnp.float32)
        .astype(jnp.bfloat16)
        .reshape(seq_len, head_count, DV)
    )
    keys_nope_grad = jnp.zeros((seq_len, head_count, DN), jnp.float32)
    key_rope_grad = jnp.zeros((seq_len, DR), jnp.float32)
    values_grad = jnp.zeros((seq_len, head_count, DV), jnp.float32)
    query_grad_list = []
    for block_index, rows_start in enumerate(range(0, seq_len, block_rows)):
        query_block = query_low[rows_start : rows_start + block_rows]
        masked = block_scores(query_block, keys_nope, key_rope, rows_start, prefix_len, score_scale)
        prob_full = jnp.exp(masked - lse_list[block_index])
        prob_low = prob_full.astype(jnp.bfloat16)
        mixed_block = mixed_grad[rows_start : rows_start + block_rows]
        prob_grads = jnp.einsum(
            "qhv,khv->hqk", mixed_block, values_low, preferred_element_type=jnp.float32
        )
        row_delta = jnp.sum(prob_full * prob_grads, -1, keepdims=True)
        score_grads = (prob_full * (prob_grads - row_delta)).astype(jnp.bfloat16)
        query_nope_grad = (
            jnp.einsum("hqk,khd->qhd", score_grads, keys_nope, preferred_element_type=jnp.float32)
            * score_scale
        )
        query_rope_grad = (
            jnp.einsum("hqk,kr->qhr", score_grads, key_rope, preferred_element_type=jnp.float32)
            * score_scale
        )
        keys_nope_grad = (
            keys_nope_grad
            + jnp.einsum(
                "hqk,qhd->khd",
                score_grads,
                query_block[..., :DN],
                preferred_element_type=jnp.float32,
            )
            * score_scale
        )
        key_rope_grad = (
            key_rope_grad
            + jnp.einsum(
                "hqk,qhr->kr",
                score_grads,
                query_block[..., DN:],
                preferred_element_type=jnp.float32,
            )
            * score_scale
        )
        values_grad = values_grad + jnp.einsum(
            "hqk,qhv->khv", prob_low, mixed_block, preferred_element_type=jnp.float32
        )
        block_cosines = all_cosines[rows_start : rows_start + block_rows, None, :]
        block_sines = all_sines[rows_start : rows_start + block_rows, None, :]
        query_grad_list.append(
            jnp.concatenate(
                [
                    query_nope_grad,
                    rotate_back(round_trip(query_rope_grad), block_cosines, block_sines),
                ],
                -1,
            ).astype(jnp.bfloat16)
        )
    query_grads = jnp.concatenate(query_grad_list, 0).reshape(seq_len, head_count * (DN + DR))
    feed_own, shared_pack, query_grads = lax.optimization_barrier((feed_own, shared_pack, query_grads))
    query_grad_w = jnp.dot(normed_all.T, query_grads, preferred_element_type=jnp.float32)
    normed_grad_part = jnp.dot(query_grads, query_weights.T, preferred_element_type=jnp.float32)
    expand_grads = jnp.concatenate(
        [keys_nope_grad.astype(jnp.bfloat16), values_grad.astype(jnp.bfloat16)], -1
    ).reshape(seq_len, head_count * (DN + DV))
    expand_grad_w = jnp.dot(compressed_seq.T, expand_grads, preferred_element_type=jnp.float32)
    compressed_grad_part = jnp.dot(
        expand_grads, expand_weights.T, preferred_element_type=jnp.float32
    )
    latent_grad_part = jnp.concatenate([compressed_grad_part, key_rope_grad], -1)
    attn_grads_in = jnp.concatenate(
        [
            query_grad_w,
            output_grad_w_t,
            expand_grad_w.reshape(dp_size * rows_dp, expand_flat_cols),
        ],
        1,
    )
    token_all = lax.psum(
        jnp.concatenate([normed_grad_part, latent_grad_part], 1).astype(jnp.bfloat16), "tensor"
    ).astype(jnp.float32)
    compressed_grad_all = token_all[:, D : D + KVR]
    kv_gain_full = jnp.sum(compressed_grad_all * compressed_all * scale_kv_all, 0)
    raw_grad_all = jnp.concatenate(
        [
            norm_back(compressed_all, scale_kv_all, gain_kv, compressed_grad_all),
            rotate_back(token_all[:, D + KVR :], all_cosines, all_sines),
        ],
        -1,
    ).astype(jnp.bfloat16)
    normed_grad_all = token_all[:, :D] + jnp.dot(
        raw_grad_all, latent_weights.T, preferred_element_type=jnp.float32
    )
    normed_grad = lax.dynamic_slice_in_dim(normed_grad_all, start_row, tok_dev, 0)
    hidden_grad = lax.dynamic_slice_in_dim(residual_grad, start_row, tok_dev, 0) + norm_back(
        hidden_f, scale_one, gain_one, normed_grad
    )
    row_per = D // (dp_size * tensor_size)

    def own_rows(values):
        split = values.reshape(values.shape[0], dp_size, tensor_size, row_per)
        return lax.dynamic_slice_in_dim(split, tensor_rank, 1, 2).reshape(values.shape[0], -1)

    latent_rows = jnp.dot(own_rows(normed_all).T, raw_grad_all, preferred_element_type=jnp.float32)
    attn_gain_rows = jnp.sum(
        own_rows(normed_grad_all) * own_rows(hidden_all_f) * scale_one_all, 0
    )
    second_gain_rows = jnp.sum(
        own_rows(normed_two_grad) * own_rows(residual_all) * scale_two, 0
    )
    router_rows = jnp.dot(
        own_rows(normed_two).astype(jnp.float32).T, logit_grads, precision=HIGH
    )
    kv_per = kv_gain_full.shape[0] // (dp_size * tensor_size)
    kv_rows_own = lax.dynamic_slice_in_dim(
        kv_gain_full.reshape(dp_size, tensor_size, kv_per), tensor_rank, 1, 1
    ).reshape(dp_size, kv_per)
    kv_column = jnp.pad(kv_rows_own, ((0, 0), (0, row_per - kv_per))).reshape(-1)
    small_pack = jnp.concatenate(
        [
            latent_rows,
            router_rows,
            attn_gain_rows[:, None],
            second_gain_rows[:, None],
            kv_column[:, None],
        ],
        1,
    )
    attn_width = attn_grads_in.shape[1]
    small_width = small_pack.shape[1]
    small_count = row_per * small_width
    small_cols = -(-small_count // rows_dp)
    small_flat = jnp.pad(
        small_pack.reshape(dp_size, small_count), ((0, 0), (0, small_cols * rows_dp - small_count))
    ).reshape(dp_size * rows_dp, small_cols)
    merged_own = lax.psum_scatter(
        jnp.concatenate([attn_grads_in, small_flat], 1), "dp", scatter_dimension=0, tiled=True
    )
    attn_pack = merged_own[:, :attn_width]
    small_own = merged_own[:, attn_width:].reshape(-1)[:small_count].reshape(row_per, small_width)
    cut = [0]
    for width in (latent_cols, experts, 1, 1, 1):
        cut.append(cut[-1] + width)
    latent_proj_grad = small_own[:, cut[0] : cut[1]]
    router_out = small_own[:, cut[1] : cut[2]]
    attn_gain_out = small_own[:, cut[2]]
    second_gain_out = small_own[:, cut[3]]
    latent_gain_out = small_own[:kv_per, cut[4]]
    cut = [0]
    for width in (head_cols, out_cols, expand_flat_cols):
        cut.append(cut[-1] + width)
    query_proj_grad = attn_pack[:, cut[0] : cut[1]]
    output_proj_grad = attn_pack[:, cut[1] : cut[2]].T
    expand_proj_grad = attn_pack[:, cut[2] : cut[3]].reshape(kv_rows, expand_cols)
    shared_gate_out = shared_pack[:, :shared_cols]
    shared_up_out = shared_pack[:, shared_cols : 2 * shared_cols]
    shared_down_out = shared_pack[:, 2 * shared_cols :].T
    return (
        output,
        hidden_grad,
        attn_gain_out,
        query_proj_grad,
        latent_proj_grad,
        latent_gain_out,
        expand_proj_grad,
        output_proj_grad,
        second_gain_out,
        router_out,
        expert_gate_grad,
        expert_up_grad,
        expert_down_grad,
        shared_gate_out,
        shared_up_out,
        shared_down_out,
    )


def solution(mesh):
    return jax.shard_map(
        shards,
        mesh=mesh,
        in_specs=(
            P(("dp", "tensor"), None),
            P("dp", None),
            P("dp"),
            P("dp"),
            P("dp", "tensor"),
            P("dp", None),
            P("dp"),
            P("dp", "tensor"),
            P("tensor", "dp"),
            P("dp"),
            P("dp", None),
            P("dp", "tensor", None),
            P("dp", "tensor", None),
            P("dp", "tensor", None),
            P("dp", "tensor"),
            P("dp", "tensor"),
            P("tensor", "dp"),
            P(("dp", "tensor"), None),
        ),
        out_specs=(
            P(("dp", "tensor"), None),
            P(("dp", "tensor"), None),
            P(("dp", "tensor")),
            P("dp", "tensor"),
            P(("dp", "tensor"), None),
            P(("dp", "tensor")),
            P("dp", "tensor"),
            P("tensor", "dp"),
            P(("dp", "tensor")),
            P(("dp", "tensor"), None),
            P("dp", "tensor", None),
            P("dp", "tensor", None),
            P("dp", "tensor", None),
            P("dp", "tensor"),
            P("dp", "tensor"),
            P("tensor", "dp"),
        ),
        check_vma=False,
    )
```

```python
import math

import jax
import jax.numpy as jnp
from jax import lax
from jax.experimental import pallas as pl
from jax.experimental.pallas import tpu as pltpu
from jax.sharding import PartitionSpec as P

D = 2048
DN = 128
DR = 64
DV = 128
KVR = 512


EPS = 1e-06
HIGH = lax.Precision.HIGHEST
MASKED = -1e30


def norm_scale(values):
    return lax.rsqrt(jnp.mean(values * values, -1, keepdims=True) + EPS)


def norm_back(values, scales, gains, upstream):
    weighted = gains * upstream
    return scales * weighted - values * scales**3 * jnp.mean(values * weighted, -1, keepdims=True)


def rope_tables(positions, rope_width):
    half_width = rope_width // 2
    frequency = 10000.0 ** (-2.0 * jnp.arange(half_width).astype(jnp.float32) / rope_width)
    angles = positions.astype(jnp.float32)[:, None] * frequency[None, :]
    return (jnp.cos(angles), jnp.sin(angles))


def rotate(vectors, cosines, sine_values):
    half_width = vectors.shape[-1] // 2
    front_half = vectors[..., :half_width]
    back_half = vectors[..., half_width:]
    return jnp.concatenate(
        [
            front_half * cosines - back_half * sine_values,
            back_half * cosines + front_half * sine_values,
        ],
        -1,
    )


def rotate_back(gradients, cosines, sine_values):
    half_width = gradients.shape[-1] // 2
    front_half = gradients[..., :half_width]
    back_half = gradients[..., half_width:]
    return jnp.concatenate(
        [
            front_half * cosines + back_half * sine_values,
            back_half * cosines - front_half * sine_values,
        ],
        -1,
    )


def round_trip(values):
    return lax.optimization_barrier(values.astype(jnp.bfloat16)).astype(jnp.float32)


def block_scores(query_block, keys_nope, key_rope, rows_start, prefix_len, score_scale):
    raw_scores = jnp.einsum(
        "qhd,khd->hqk", query_block[..., :DN], keys_nope, preferred_element_type=jnp.float32
    )
    raw_scores = raw_scores + jnp.einsum(
        "qhr,kr->hqk", query_block[..., DN:], key_rope, preferred_element_type=jnp.float32
    )
    query_places = rows_start + jnp.arange(query_block.shape[0])
    key_places = jnp.arange(keys_nope.shape[0])
    visible = (key_places[None, :] <= query_places[:, None]) | (key_places[None, :] < prefix_len)
    return jnp.where(visible[None], raw_scores * score_scale, MASKED)


def silu_back(act_grad, gate_pre, up_pre, sigmoid_gate):
    up_grad = (act_grad * gate_pre * sigmoid_gate).astype(jnp.bfloat16)
    gate_grad = (act_grad * up_pre * sigmoid_gate * (1.0 + gate_pre * (1.0 - sigmoid_gate))).astype(
        jnp.bfloat16
    )
    return (gate_grad, up_grad)


def dispatch_kernel(tok_ref, both_hbm, col_ref, out_ref, both_buf, sems):
    block = both_buf.shape[0]
    tile_rows = both_buf.shape[1] // 2
    last = both_hbm.shape[0] - 1
    base = pl.program_id(0) * block

    def start(r, carry):
        tok = jnp.minimum(tok_ref[base + r], last)
        pltpu.make_async_copy(both_hbm.at[tok], both_buf.at[r], sems.at[r]).start()
        return carry

    lax.fori_loop(0, block, start, 0, unroll=4)

    def finish(r, carry):
        pltpu.make_async_copy(both_hbm.at[0], both_buf.at[r], sems.at[r]).wait()
        return carry

    lax.fori_loop(0, block, finish, 0, unroll=4)
    rows = both_buf[:, :tile_rows, :]
    out_ref[:, :tile_rows, :] = jnp.where(col_ref[0] > 0, rows, jnp.zeros_like(rows))
    out_ref[:, tile_rows:, :] = (
        both_buf[:, tile_rows:, :].astype(jnp.float32) * col_ref[1]
    ).astype(out_ref.dtype)


def dispatch_rows(slot_token, rows, grads, valid, gate, block=128):
    slots = slot_token.shape[0]
    count, width = rows.shape
    tile_rows = width // 128
    cols = jnp.broadcast_to(jnp.stack([valid, gate])[:, :, None, None], (2, slots, 1, 128))
    both = jnp.concatenate([rows, grads], 1).reshape(count, 2 * tile_rows, 128)
    out = pl.pallas_call(
        dispatch_kernel,
        out_shape=jax.ShapeDtypeStruct((slots, 2 * tile_rows, 128), rows.dtype),
        grid_spec=pltpu.PrefetchScalarGridSpec(
            num_scalar_prefetch=1,
            grid=(slots // block,),
            in_specs=[
                pl.BlockSpec(memory_space=pl.ANY),
                pl.BlockSpec((2, block, 1, 128), lambda i, tok: (0, i, 0, 0)),
            ],
            out_specs=pl.BlockSpec((block, 2 * tile_rows, 128), lambda i, tok: (i, 0, 0)),
            scratch_shapes=[
                pltpu.VMEM((block, 2 * tile_rows, 128), rows.dtype),
                pltpu.SemaphoreType.DMA((block,)),
            ],
        ),
        cost_estimate=pl.CostEstimate(
            flops=slots * width, transcendentals=0, bytes_accessed=4 * slots * 2 * width
        ),
    )(slot_token, both, cols)
    return out


def combine_kernel(
    slot_ref, table_hbm, gate_ref, grad_ref, shared_out_ref, shared_back_ref,
    feed_ref, back_ref, part_ref, picked, sems,
):
    top = picked.shape[0]
    block = picked.shape[1]
    tile_rows = grad_ref.shape[1]
    last = table_hbm.shape[0] - 1
    base = pl.program_id(0) * block

    def start(r, carry):
        for k in range(top):
            slot = jnp.clip(slot_ref[(base + r) * top + k], 0, last)
            pltpu.make_async_copy(table_hbm.at[slot], picked.at[k, r], sems.at[k, r]).start()
        return carry

    lax.fori_loop(0, block, start, 0)

    def finish(r, carry):
        for k in range(top):
            pltpu.make_async_copy(table_hbm.at[0], picked.at[k, r], sems.at[k, r]).wait()
        return carry

    lax.fori_loop(0, block, finish, 0)
    grad = grad_ref[...].astype(jnp.float32)
    weighted = None
    backs = None
    lanes = lax.broadcasted_iota(jnp.int32, part_ref.shape, 2)
    parts = jnp.zeros(part_ref.shape, jnp.float32)
    for k in range(top):
        out_k = picked[k, :, :tile_rows, :].astype(jnp.float32)
        term = gate_ref[k] * out_k
        weighted = term if weighted is None else weighted + term
        back_k = picked[k, :, tile_rows:, :].astype(jnp.float32)
        backs = back_k if backs is None else backs + back_k
        dot_k = jnp.sum(jnp.sum(grad * out_k, 2, keepdims=True), 1, keepdims=True)
        parts = jnp.where(lanes == k, dot_k, parts)
    feed_ref[...] = (shared_out_ref[...] + weighted).astype(feed_ref.dtype)
    back_ref[...] = (backs + shared_back_ref[...]).astype(back_ref.dtype)
    part_ref[...] = parts


def combine_rows(slot_index, table, gate_values, grad, shared_out, shared_back, block=128):
    tokens, top = gate_values.shape
    width = grad.shape[1]
    tile_rows = width // 128
    gates = jnp.broadcast_to(gate_values.T[:, :, None, None], (top, tokens, 1, 128))
    row_spec = pl.BlockSpec((block, tile_rows, 128), lambda i, s: (i, 0, 0))
    feed, back, parts = pl.pallas_call(
        combine_kernel,
        out_shape=(
            jax.ShapeDtypeStruct((tokens, tile_rows, 128), jnp.bfloat16),
            jax.ShapeDtypeStruct((tokens, tile_rows, 128), jnp.bfloat16),
            jax.ShapeDtypeStruct((tokens, 1, 128), jnp.float32),
        ),
        grid_spec=pltpu.PrefetchScalarGridSpec(
            num_scalar_prefetch=1,
            grid=(tokens // block,),
            in_specs=[
                pl.BlockSpec(memory_space=pl.ANY),
                pl.BlockSpec((top, block, 1, 128), lambda i, s: (0, i, 0, 0)),
                row_spec,
                row_spec,
                row_spec,
            ],
            out_specs=[row_spec, row_spec, pl.BlockSpec((block, 1, 128), lambda i, s: (i, 0, 0))],
            scratch_shapes=[
                pltpu.VMEM((top, block, 2 * tile_rows, 128), table.dtype),
                pltpu.SemaphoreType.DMA((top, block)),
            ],
        ),
        cost_estimate=pl.CostEstimate(
            flops=8 * tokens * top * width,
            transcendentals=0,
            bytes_accessed=tokens * (top * 4 * width + 2 * width + 8 * width + 4 * width),
        ),
    )(
        slot_index.reshape(-1),
        table.reshape(table.shape[0], 2 * tile_rows, 128),
        gates,
        grad.reshape(tokens, tile_rows, 128),
        shared_out.reshape(tokens, tile_rows, 128),
        shared_back.reshape(tokens, tile_rows, 128),
    )
    return feed.reshape(tokens, width), back.reshape(tokens, width), parts[:, 0, :top]


def shards(
    hidden,
    routes,
    prefix,
    attn_gain,
    query_proj,
    latent_proj,
    latent_gain,
    expand_proj,
    output_proj,
    second_gain,
    router_proj,
    expert_gate,
    expert_up,
    expert_down,
    shared_gate,
    shared_up,
    shared_down,
    out_grad,
):
    tok_dev = hidden.shape[0]
    tensor_size = lax.axis_size("tensor")
    tensor_rank = lax.axis_index("tensor")
    dp_size = lax.axis_size("dp")
    seq_len = tok_dev * tensor_size
    start_row = tensor_rank * tok_dev
    rows_dp = attn_gain.shape[0]
    kv_rows = latent_gain.shape[0]
    head_cols = query_proj.shape[1]
    latent_cols = latent_proj.shape[1]
    expand_cols = expand_proj.shape[1]
    expand_flat_cols = kv_rows * expand_cols // rows_dp
    first_pack = jnp.concatenate(
        [
            query_proj,
            latent_proj,
            expand_proj.reshape(rows_dp, expand_flat_cols),
            attn_gain[:, None],
            jnp.pad(latent_gain, (0, rows_dp - kv_rows))[:, None],
        ],
        1,
    )
    first_all = lax.all_gather(first_pack, "dp", axis=0, tiled=True)
    cut = [0]
    for width in (head_cols, latent_cols, expand_flat_cols, 1, 1):
        cut.append(cut[-1] + width)
    query_weights = first_all[:, cut[0] : cut[1]]
    latent_weights = first_all[:, cut[1] : cut[2]]
    expand_weights = first_all[:, cut[2] : cut[3]].reshape(dp_size * kv_rows, expand_cols)
    attn_gains = first_all[:, cut[3]]
    kv_gains = first_all[:, cut[4]].reshape(dp_size, rows_dp)[:, :kv_rows].reshape(-1)
    out_cols = output_proj.shape[0]
    experts = router_proj.shape[1]
    shared_cols = shared_gate.shape[1]
    second_pack = jnp.concatenate([output_proj.T, second_gain[:, None], router_proj], 1)
    second_all = lax.all_gather(second_pack, "dp", axis=0, tiled=True)
    output_weights_t = second_all[:, :out_cols]
    second_gains = second_all[:, out_cols]
    router_weights = second_all[:, out_cols + 1 :]
    shared_local = jnp.concatenate([shared_gate, shared_up, shared_down.T], 1)

    hidden_all = lax.all_gather(hidden, "tensor", axis=0, tiled=True)
    grad_seq = lax.all_to_all(
        jnp.broadcast_to(out_grad[None], (tensor_size,) + out_grad.shape),
        "tensor",
        split_axis=0,
        concat_axis=0,
        tiled=True,
    ).reshape(tensor_size * tok_dev, D)
    grad_seq, hidden_all = lax.optimization_barrier((grad_seq, hidden_all))
    hidden_all_f = hidden_all.astype(jnp.float32)
    scale_one_all = norm_scale(hidden_all_f)
    gain_one = attn_gains.astype(jnp.float32)
    normed_all = (hidden_all_f * scale_one_all * gain_one).astype(jnp.bfloat16)
    hidden_f = lax.dynamic_slice_in_dim(hidden_all_f, start_row, tok_dev, 0)
    scale_one = lax.dynamic_slice_in_dim(scale_one_all, start_row, tok_dev, 0)
    normed_own = lax.dynamic_slice_in_dim(normed_all, start_row, tok_dev, 0)
    latent_raw_all = jnp.dot(normed_all, latent_weights, preferred_element_type=jnp.float32)
    compressed_all = latent_raw_all[:, :KVR]
    scale_kv_all = norm_scale(compressed_all)
    gain_kv = kv_gains.astype(jnp.float32)
    all_cosines, all_sines = rope_tables(jnp.arange(seq_len), DR)
    latent_seq = jnp.concatenate(
        [
            compressed_all * scale_kv_all * gain_kv,
            rotate(latent_raw_all[:, KVR:], all_cosines, all_sines),
        ],
        -1,
    ).astype(jnp.bfloat16)
    compressed = lax.dynamic_slice_in_dim(compressed_all, start_row, tok_dev, 0)
    scale_kv = lax.dynamic_slice_in_dim(scale_kv_all, start_row, tok_dev, 0)
    own_cosines = lax.dynamic_slice_in_dim(all_cosines, start_row, tok_dev, 0)
    own_sines = lax.dynamic_slice_in_dim(all_sines, start_row, tok_dev, 0)
    head_count = query_weights.shape[1] // (DN + DR)
    query_raw = jnp.dot(normed_all, query_weights, preferred_element_type=jnp.float32).reshape(
        seq_len, head_count, DN + DR
    )
    query_low = jnp.concatenate(
        [
            query_raw[..., :DN],
            rotate(query_raw[..., DN:], all_cosines[:, None, :], all_sines[:, None, :]),
        ],
        -1,
    ).astype(jnp.bfloat16)
    compressed_seq = latent_seq[:, :KVR]
    key_rope = latent_seq[:, KVR:]
    expanded = jnp.dot(compressed_seq, expand_weights, preferred_element_type=jnp.float32).reshape(
        seq_len, head_count, DN + DV
    )
    keys_nope = expanded[..., :DN].astype(jnp.bfloat16)
    values_low = expanded[..., DN:].astype(jnp.bfloat16)
    score_scale = 1.0 / math.sqrt(DN + DR)
    block_rows = min(512, seq_len)
    prefix_len = prefix[0]
    lse_list = []
    mixed_list = []
    for rows_start in range(0, seq_len, block_rows):
        query_block = query_low[rows_start : rows_start + block_rows]
        masked = block_scores(query_block, keys_nope, key_rope, rows_start, prefix_len, score_scale)
        top_score = jnp.max(masked, -1, keepdims=True)
        exp_scores = jnp.exp(masked - top_score)
        totals = jnp.sum(exp_scores, -1, keepdims=True)
        prob_low = (exp_scores / totals).astype(jnp.bfloat16)
        lse_list.append(top_score + jnp.log(totals))
        mixed_list.append(
            jnp.einsum(
                "hqk,khv->qhv", prob_low, values_low, preferred_element_type=jnp.float32
            ).astype(jnp.bfloat16)
        )
    mixed_all = jnp.concatenate(mixed_list, 0).reshape(seq_len, head_count * DV)
    attn_part = jnp.einsum(
        "tk,dk->td", mixed_all, output_weights_t, preferred_element_type=jnp.float32
    )
    branch_all = lax.psum(attn_part.astype(jnp.bfloat16), "tensor").astype(jnp.float32)
    residual_all = hidden_all_f + branch_all
    residual_own = lax.dynamic_slice_in_dim(residual_all, start_row, tok_dev, 0)
    scale_two = norm_scale(residual_all)
    gain_two = second_gains.astype(jnp.float32)
    normed_two = (residual_all * scale_two * gain_two).astype(jnp.bfloat16)
    logits = jnp.dot(normed_two, router_weights, preferred_element_type=jnp.float32)
    top_count = routes.shape[1]
    chosen_hot = routes[:, :, None] == jnp.arange(experts)[None, None, :]
    chosen_logits = jnp.sum(jnp.where(chosen_hot, logits[:, None, :], 0.0), -1)
    gate_values = jax.nn.softmax(chosen_logits, axis=-1)
    assignments = seq_len * top_count
    flat_hot = chosen_hot.reshape(assignments, experts).astype(jnp.bfloat16)
    lower = (jnp.arange(assignments)[:, None] > jnp.arange(assignments)[None, :]).astype(jnp.bfloat16)
    earlier = jnp.dot(lower, flat_hot, preferred_element_type=jnp.float32)
    slot_pos = jnp.sum(earlier * flat_hot.astype(jnp.float32), -1).astype(jnp.int32)
    expert_ids = routes.reshape(-1)
    exp_dev = expert_gate.shape[0]
    capacity = tensor_size * (5 * seq_len * top_count // (4 * experts * tensor_size))
    slot_index = expert_ids * capacity + slot_pos
    token_ids = jnp.arange(seq_len * top_count) // top_count
    slot_token = jnp.full((experts * capacity,), seq_len, jnp.int32).at[slot_index].set(token_ids)
    slot_gate = (
        jnp.zeros((experts * capacity,), jnp.float32).at[slot_index].set(gate_values.reshape(-1))
    )
    slot_valid = (slot_token < seq_len).astype(jnp.float32)
    tile_rows = D // 128
    send_both = dispatch_rows(slot_token, normed_two, grad_seq, slot_valid, slot_gate).reshape(
        dp_size, exp_dev, capacity, 2 * tile_rows, 128
    )
    shared_local, send_both = lax.optimization_barrier((shared_local, send_both))
    shared_all = lax.all_gather(shared_local, "dp", axis=0, tiled=True)
    gate_shared = shared_all[:, :shared_cols]
    up_shared = shared_all[:, shared_cols : 2 * shared_cols]
    down_shared_t = shared_all[:, 2 * shared_cols :]
    recv_both = lax.all_to_all(send_both, "dp", split_axis=0, concat_axis=0, tiled=True)
    recv_both = recv_both.reshape(dp_size, exp_dev, capacity, 2 * D)
    recv_rows = recv_both[..., :D]
    recv_grads = recv_both[..., D:]
    gate_pre = jnp.einsum(
        "sjcd,jfd->sjcf", recv_rows, expert_gate, preferred_element_type=jnp.float32
    )
    up_pre = jnp.einsum("sjcd,jfd->sjcf", recv_rows, expert_up, preferred_element_type=jnp.float32)
    sigmoid_gate = jax.nn.sigmoid(gate_pre)
    expert_act = (gate_pre * sigmoid_gate * up_pre).astype(jnp.bfloat16)
    expert_out = jnp.einsum(
        "sjcf,jfd->sjcd", expert_act, expert_down, preferred_element_type=jnp.float32
    )
    act_grad = jnp.einsum(
        "sjcd,jfd->sjcf", recv_grads, expert_down, preferred_element_type=jnp.float32
    )
    gate_low_grad, up_low_grad = silu_back(act_grad, gate_pre, up_pre, sigmoid_gate)
    expert_down_grad = jnp.einsum(
        "sjcf,sjcd->jfd", expert_act, recv_grads, preferred_element_type=jnp.float32
    )
    expert_gate_grad = jnp.einsum(
        "sjcf,sjcd->jfd", gate_low_grad, recv_rows, preferred_element_type=jnp.float32
    )
    expert_up_grad = jnp.einsum(
        "sjcf,sjcd->jfd", up_low_grad, recv_rows, preferred_element_type=jnp.float32
    )
    row_grads = jnp.einsum(
        "sjcf,jfd->sjcd", gate_low_grad, expert_gate, preferred_element_type=jnp.float32
    )
    row_grads = row_grads + jnp.einsum(
        "sjcf,jfd->sjcd", up_low_grad, expert_up, preferred_element_type=jnp.float32
    )
    back_both = lax.all_to_all(
        jnp.concatenate(
            [expert_out.astype(jnp.bfloat16), row_grads.astype(jnp.bfloat16)], -1
        ).reshape(dp_size, exp_dev, capacity, 2 * tile_rows, 128),
        "dp",
        split_axis=0,
        concat_axis=0,
        tiled=True,
    )
    shared_pre_gate = jnp.dot(normed_two, gate_shared, preferred_element_type=jnp.float32)
    shared_pre_up = jnp.dot(normed_two, up_shared, preferred_element_type=jnp.float32)
    shared_sigmoid = jax.nn.sigmoid(shared_pre_gate)
    shared_act = (shared_pre_gate * shared_sigmoid * shared_pre_up).astype(jnp.bfloat16)
    shared_out = jnp.einsum(
        "tf,df->td", shared_act, down_shared_t, preferred_element_type=jnp.float32
    )
    shared_act_grad = jnp.dot(grad_seq, down_shared_t, preferred_element_type=jnp.float32)
    shared_gate_low, shared_up_low = silu_back(
        shared_act_grad, shared_pre_gate, shared_pre_up, shared_sigmoid
    )
    shared_down_grad_t = jnp.dot(grad_seq.T, shared_act, preferred_element_type=jnp.float32)
    shared_gate_grad = jnp.dot(normed_two.T, shared_gate_low, preferred_element_type=jnp.float32)
    shared_up_grad = jnp.dot(normed_two.T, shared_up_low, preferred_element_type=jnp.float32)
    shared_back = jnp.einsum(
        "tf,df->td", shared_gate_low, gate_shared, preferred_element_type=jnp.float32
    )
    shared_back = shared_back + jnp.einsum(
        "tf,df->td", shared_up_low, up_shared, preferred_element_type=jnp.float32
    )
    shared_grads_in = jnp.concatenate(
        [shared_gate_grad, shared_up_grad, shared_down_grad_t], 1
    ).astype(jnp.bfloat16)
    grad_seq_f = grad_seq.astype(jnp.float32)
    table_rows = experts * capacity
    feed_part, back_part, gate_cols = combine_rows(
        slot_index.reshape(seq_len, top_count),
        back_both.reshape(table_rows, 2 * tile_rows, 128),
        gate_values,
        grad_seq,
        shared_out,
        shared_back,
    )
    gate_part = gate_cols[:, :top_count]
    feed_own = lax.psum_scatter(feed_part, "tensor", scatter_dimension=0, tiled=True).astype(
        jnp.float32
    )
    output = (residual_own + feed_own).astype(jnp.bfloat16)
    reduced_back = lax.psum(
        jnp.concatenate([back_part, gate_cols.astype(jnp.bfloat16)], 1), "tensor"
    ).astype(jnp.float32)
    normed_two_grad = reduced_back[:, :D]
    gate_grads = reduced_back[:, D : D + top_count]
    weighted_total = jnp.sum(gate_values * gate_grads, -1, keepdims=True)
    chosen_grads = gate_values * (gate_grads - weighted_total)
    logit_grads = jnp.sum(jnp.where(chosen_hot, chosen_grads[:, :, None], 0.0), 1)
    normed_two_grad = normed_two_grad + jnp.dot(
        logit_grads, router_weights.astype(jnp.float32).T, precision=HIGH
    )
    residual_grad = grad_seq_f + norm_back(residual_all, scale_two, gain_two, normed_two_grad)
    branch_grad = residual_grad.astype(jnp.bfloat16)
    shared_grads_in, branch_grad = lax.optimization_barrier((shared_grads_in, branch_grad))
    shared_pack = lax.psum_scatter(
        shared_grads_in, "dp", scatter_dimension=0, tiled=True
    ).astype(jnp.float32)
    output_grad_w_t = jnp.dot(branch_grad.T, mixed_all, preferred_element_type=jnp.float32)
    mixed_grad = (
        jnp.dot(branch_grad, output_weights_t, preferred_element_type=jnp.float32)
        .astype(jnp.bfloat16)
        .reshape(seq_len, head_count, DV)
    )
    keys_nope_grad = jnp.zeros((seq_len, head_count, DN), jnp.float32)
    key_rope_grad = jnp.zeros((seq_len, DR), jnp.float32)
    values_grad = jnp.zeros((seq_len, head_count, DV), jnp.float32)
    query_grad_list = []
    for block_index, rows_start in enumerate(range(0, seq_len, block_rows)):
        query_block = query_low[rows_start : rows_start + block_rows]
        masked = block_scores(query_block, keys_nope, key_rope, rows_start, prefix_len, score_scale)
        prob_full = jnp.exp(masked - lse_list[block_index])
        prob_low = prob_full.astype(jnp.bfloat16)
        mixed_block = mixed_grad[rows_start : rows_start + block_rows]
        prob_grads = jnp.einsum(
            "qhv,khv->hqk", mixed_block, values_low, preferred_element_type=jnp.float32
        )
        row_delta = jnp.sum(prob_full * prob_grads, -1, keepdims=True)
        score_grads = (prob_full * (prob_grads - row_delta)).astype(jnp.bfloat16)
        query_nope_grad = (
            jnp.einsum("hqk,khd->qhd", score_grads, keys_nope, preferred_element_type=jnp.float32)
            * score_scale
        )
        query_rope_grad = (
            jnp.einsum("hqk,kr->qhr", score_grads, key_rope, preferred_element_type=jnp.float32)
            * score_scale
        )
        keys_nope_grad = (
            keys_nope_grad
            + jnp.einsum(
                "hqk,qhd->khd",
                score_grads,
                query_block[..., :DN],
                preferred_element_type=jnp.float32,
            )
            * score_scale
        )
        key_rope_grad = (
            key_rope_grad
            + jnp.einsum(
                "hqk,qhr->kr",
                score_grads,
                query_block[..., DN:],
                preferred_element_type=jnp.float32,
            )
            * score_scale
        )
        values_grad = values_grad + jnp.einsum(
            "hqk,qhv->khv", prob_low, mixed_block, preferred_element_type=jnp.float32
        )
        block_cosines = all_cosines[rows_start : rows_start + block_rows, None, :]
        block_sines = all_sines[rows_start : rows_start + block_rows, None, :]
        query_grad_list.append(
            jnp.concatenate(
                [
                    query_nope_grad,
                    rotate_back(round_trip(query_rope_grad), block_cosines, block_sines),
                ],
                -1,
            ).astype(jnp.bfloat16)
        )
    query_grads = jnp.concatenate(query_grad_list, 0).reshape(seq_len, head_count * (DN + DR))
    feed_own, shared_pack, query_grads = lax.optimization_barrier((feed_own, shared_pack, query_grads))
    query_grad_w = jnp.dot(normed_all.T, query_grads, preferred_element_type=jnp.float32)
    normed_grad_part = jnp.dot(query_grads, query_weights.T, preferred_element_type=jnp.float32)
    expand_grads = jnp.concatenate(
        [keys_nope_grad.astype(jnp.bfloat16), values_grad.astype(jnp.bfloat16)], -1
    ).reshape(seq_len, head_count * (DN + DV))
    expand_grad_w = jnp.dot(compressed_seq.T, expand_grads, preferred_element_type=jnp.float32)
    compressed_grad_part = jnp.dot(
        expand_grads, expand_weights.T, preferred_element_type=jnp.float32
    )
    latent_grad_part = jnp.concatenate([compressed_grad_part, key_rope_grad], -1)
    attn_grads_in = jnp.concatenate(
        [
            query_grad_w,
            output_grad_w_t,
            expand_grad_w.reshape(dp_size * rows_dp, expand_flat_cols),
        ],
        1,
    )
    token_all = lax.psum(
        jnp.concatenate([normed_grad_part, latent_grad_part], 1).astype(jnp.bfloat16), "tensor"
    ).astype(jnp.float32)
    compressed_grad_all = token_all[:, D : D + KVR]
    kv_gain_full = jnp.sum(compressed_grad_all * compressed_all * scale_kv_all, 0)
    raw_grad_all = jnp.concatenate(
        [
            norm_back(compressed_all, scale_kv_all, gain_kv, compressed_grad_all),
            rotate_back(token_all[:, D + KVR :], all_cosines, all_sines),
        ],
        -1,
    ).astype(jnp.bfloat16)
    normed_grad_all = token_all[:, :D] + jnp.dot(
        raw_grad_all, latent_weights.T, preferred_element_type=jnp.float32
    )
    normed_grad = lax.dynamic_slice_in_dim(normed_grad_all, start_row, tok_dev, 0)
    hidden_grad = lax.dynamic_slice_in_dim(residual_grad, start_row, tok_dev, 0) + norm_back(
        hidden_f, scale_one, gain_one, normed_grad
    )
    row_per = D // (dp_size * tensor_size)

    def own_rows(values):
        split = values.reshape(values.shape[0], dp_size, tensor_size, row_per)
        return lax.dynamic_slice_in_dim(split, tensor_rank, 1, 2).reshape(values.shape[0], -1)

    latent_rows = jnp.dot(own_rows(normed_all).T, raw_grad_all, preferred_element_type=jnp.float32)
    attn_gain_rows = jnp.sum(
        own_rows(normed_grad_all) * own_rows(hidden_all_f) * scale_one_all, 0
    )
    second_gain_rows = jnp.sum(
        own_rows(normed_two_grad) * own_rows(residual_all) * scale_two, 0
    )
    router_rows = jnp.dot(
        own_rows(normed_two).astype(jnp.float32).T, logit_grads, precision=HIGH
    )
    kv_per = kv_gain_full.shape[0] // (dp_size * tensor_size)
    kv_rows_own = lax.dynamic_slice_in_dim(
        kv_gain_full.reshape(dp_size, tensor_size, kv_per), tensor_rank, 1, 1
    ).reshape(dp_size, kv_per)
    kv_column = jnp.pad(kv_rows_own, ((0, 0), (0, row_per - kv_per))).reshape(-1)
    small_pack = jnp.concatenate(
        [
            latent_rows,
            router_rows,
            attn_gain_rows[:, None],
            second_gain_rows[:, None],
            kv_column[:, None],
        ],
        1,
    )
    attn_width = attn_grads_in.shape[1]
    small_width = small_pack.shape[1]
    small_count = row_per * small_width
    small_cols = -(-small_count // rows_dp)
    small_flat = jnp.pad(
        small_pack.reshape(dp_size, small_count), ((0, 0), (0, small_cols * rows_dp - small_count))
    ).reshape(dp_size * rows_dp, small_cols)
    merged_own = lax.psum_scatter(
        jnp.concatenate([attn_grads_in, small_flat], 1), "dp", scatter_dimension=0, tiled=True
    )
    attn_pack = merged_own[:, :attn_width]
    small_own = merged_own[:, attn_width:].reshape(-1)[:small_count].reshape(row_per, small_width)
    cut = [0]
    for width in (latent_cols, experts, 1, 1, 1):
        cut.append(cut[-1] + width)
    latent_proj_grad = small_own[:, cut[0] : cut[1]]
    router_out = small_own[:, cut[1] : cut[2]]
    attn_gain_out = small_own[:, cut[2]]
    second_gain_out = small_own[:, cut[3]]
    latent_gain_out = small_own[:kv_per, cut[4]]
    cut = [0]
    for width in (head_cols, out_cols, expand_flat_cols):
        cut.append(cut[-1] + width)
    query_proj_grad = attn_pack[:, cut[0] : cut[1]]
    output_proj_grad = attn_pack[:, cut[1] : cut[2]].T
    expand_proj_grad = attn_pack[:, cut[2] : cut[3]].reshape(kv_rows, expand_cols)
    shared_gate_out = shared_pack[:, :shared_cols]
    shared_up_out = shared_pack[:, shared_cols : 2 * shared_cols]
    shared_down_out = shared_pack[:, 2 * shared_cols :].T
    return (
        output,
        hidden_grad,
        attn_gain_out,
        query_proj_grad,
        latent_proj_grad,
        latent_gain_out,
        expand_proj_grad,
        output_proj_grad,
        second_gain_out,
        router_out,
        expert_gate_grad,
        expert_up_grad,
        expert_down_grad,
        shared_gate_out,
        shared_up_out,
        shared_down_out,
    )


def solution(mesh):
    return jax.shard_map(
        shards,
        mesh=mesh,
        in_specs=(
            P(("dp", "tensor"), None),
            P("dp", None),
            P("dp"),
            P("dp"),
            P("dp", "tensor"),
            P("dp", None),
            P("dp"),
            P("dp", "tensor"),
            P("tensor", "dp"),
            P("dp"),
            P("dp", None),
            P("dp", "tensor", None),
            P("dp", "tensor", None),
            P("dp", "tensor", None),
            P("dp", "tensor"),
            P("dp", "tensor"),
            P("tensor", "dp"),
            P(("dp", "tensor"), None),
        ),
        out_specs=(
            P(("dp", "tensor"), None),
            P(("dp", "tensor"), None),
            P(("dp", "tensor")),
            P("dp", "tensor"),
            P(("dp", "tensor"), None),
            P(("dp", "tensor")),
            P("dp", "tensor"),
            P("tensor", "dp"),
            P(("dp", "tensor")),
            P(("dp", "tensor"), None),
            P("dp", "tensor", None),
            P("dp", "tensor", None),
            P("dp", "tensor", None),
            P("dp", "tensor"),
            P("dp", "tensor"),
            P("tensor", "dp"),
        ),
        check_vma=False,
    )
```

```python
import math

import jax
import jax.numpy as jnp
from jax import lax
from jax.experimental import pallas as pl
from jax.experimental.pallas import tpu as pltpu
from jax.sharding import PartitionSpec as P

D = 2048
DN = 128
DR = 64
DV = 128
KVR = 512


EPS = 1e-06
HIGH = lax.Precision.HIGHEST
MASKED = -1e30


def norm_scale(values):
    return lax.rsqrt(jnp.mean(values * values, -1, keepdims=True) + EPS)


def norm_back(values, scales, gains, upstream):
    weighted = gains * upstream
    return scales * weighted - values * scales**3 * jnp.mean(values * weighted, -1, keepdims=True)


def rope_tables(positions, rope_width):
    half_width = rope_width // 2
    frequency = 10000.0 ** (-2.0 * jnp.arange(half_width).astype(jnp.float32) / rope_width)
    angles = positions.astype(jnp.float32)[:, None] * frequency[None, :]
    return (jnp.cos(angles), jnp.sin(angles))


def rotate(vectors, cosines, sine_values):
    half_width = vectors.shape[-1] // 2
    front_half = vectors[..., :half_width]
    back_half = vectors[..., half_width:]
    return jnp.concatenate(
        [
            front_half * cosines - back_half * sine_values,
            back_half * cosines + front_half * sine_values,
        ],
        -1,
    )


def rotate_back(gradients, cosines, sine_values):
    half_width = gradients.shape[-1] // 2
    front_half = gradients[..., :half_width]
    back_half = gradients[..., half_width:]
    return jnp.concatenate(
        [
            front_half * cosines + back_half * sine_values,
            back_half * cosines - front_half * sine_values,
        ],
        -1,
    )


def round_trip(values):
    return lax.optimization_barrier(values.astype(jnp.bfloat16)).astype(jnp.float32)


def block_scores(query_block, keys_nope, key_rope, rows_start, prefix_len, score_scale):
    raw_scores = jnp.einsum(
        "qhd,khd->hqk", query_block[..., :DN], keys_nope, preferred_element_type=jnp.float32
    )
    raw_scores = raw_scores + jnp.einsum(
        "qhr,kr->hqk", query_block[..., DN:], key_rope, preferred_element_type=jnp.float32
    )
    query_places = rows_start + jnp.arange(query_block.shape[0])
    key_places = jnp.arange(keys_nope.shape[0])
    visible = (key_places[None, :] <= query_places[:, None]) | (key_places[None, :] < prefix_len)
    return jnp.where(visible[None], raw_scores * score_scale, MASKED)


def silu_back(act_grad, gate_pre, up_pre, sigmoid_gate):
    up_grad = (act_grad * gate_pre * sigmoid_gate).astype(jnp.bfloat16)
    gate_grad = (act_grad * up_pre * sigmoid_gate * (1.0 + gate_pre * (1.0 - sigmoid_gate))).astype(
        jnp.bfloat16
    )
    return (gate_grad, up_grad)


def dispatch_kernel(tok_ref, both_hbm, col_ref, out_ref, both_buf, sems):
    block = both_buf.shape[0]
    tile_rows = both_buf.shape[1] // 2
    last = both_hbm.shape[0] - 1
    base = pl.program_id(0) * block

    def start(r, carry):
        tok = jnp.minimum(tok_ref[base + r], last)
        pltpu.make_async_copy(both_hbm.at[tok], both_buf.at[r], sems.at[r]).start()
        return carry

    lax.fori_loop(0, block, start, 0, unroll=4)

    def finish(r, carry):
        pltpu.make_async_copy(both_hbm.at[0], both_buf.at[r], sems.at[r]).wait()
        return carry

    lax.fori_loop(0, block, finish, 0, unroll=4)
    rows = both_buf[:, :tile_rows, :]
    out_ref[:, :tile_rows, :] = jnp.where(col_ref[0] > 0, rows, jnp.zeros_like(rows))
    out_ref[:, tile_rows:, :] = (
        both_buf[:, tile_rows:, :].astype(jnp.float32) * col_ref[1]
    ).astype(out_ref.dtype)


def dispatch_rows(slot_token, rows, grads, valid, gate, block=128):
    slots = slot_token.shape[0]
    count, width = rows.shape
    tile_rows = width // 128
    cols = jnp.broadcast_to(jnp.stack([valid, gate])[:, :, None, None], (2, slots, 1, 128))
    both = jnp.concatenate([rows, grads], 1).reshape(count, 2 * tile_rows, 128)
    out = pl.pallas_call(
        dispatch_kernel,
        out_shape=jax.ShapeDtypeStruct((slots, 2 * tile_rows, 128), rows.dtype),
        grid_spec=pltpu.PrefetchScalarGridSpec(
            num_scalar_prefetch=1,
            grid=(slots // block,),
            in_specs=[
                pl.BlockSpec(memory_space=pl.ANY),
                pl.BlockSpec((2, block, 1, 128), lambda i, tok: (0, i, 0, 0)),
            ],
            out_specs=pl.BlockSpec((block, 2 * tile_rows, 128), lambda i, tok: (i, 0, 0)),
            scratch_shapes=[
                pltpu.VMEM((block, 2 * tile_rows, 128), rows.dtype),
                pltpu.SemaphoreType.DMA((block,)),
            ],
        ),
        cost_estimate=pl.CostEstimate(
            flops=slots * width, transcendentals=0, bytes_accessed=4 * slots * 2 * width
        ),
    )(slot_token, both, cols)
    return out


def combine_kernel(
    slot_ref, table_hbm, gate_ref, grad_ref, shared_out_ref, shared_back_ref,
    feed_ref, back_ref, part_ref, picked, sems,
):
    top = picked.shape[0]
    block = picked.shape[1]
    tile_rows = grad_ref.shape[1]
    last = table_hbm.shape[0] - 1
    base = pl.program_id(0) * block

    def start(r, carry):
        for k in range(top):
            slot = jnp.clip(slot_ref[(base + r) * top + k], 0, last)
            pltpu.make_async_copy(table_hbm.at[slot], picked.at[k, r], sems.at[k, r]).start()
        return carry

    lax.fori_loop(0, block, start, 0)

    def finish(r, carry):
        for k in range(top):
            pltpu.make_async_copy(table_hbm.at[0], picked.at[k, r], sems.at[k, r]).wait()
        return carry

    lax.fori_loop(0, block, finish, 0)
    grad = grad_ref[...].astype(jnp.float32)
    weighted = None
    backs = None
    lanes = lax.broadcasted_iota(jnp.int32, part_ref.shape, 2)
    parts = jnp.zeros(part_ref.shape, jnp.float32)
    for k in range(top):
        out_k = picked[k, :, :tile_rows, :].astype(jnp.float32)
        term = gate_ref[k] * out_k
        weighted = term if weighted is None else weighted + term
        back_k = picked[k, :, tile_rows:, :].astype(jnp.float32)
        backs = back_k if backs is None else backs + back_k
        dot_k = jnp.sum(jnp.sum(grad * out_k, 2, keepdims=True), 1, keepdims=True)
        parts = jnp.where(lanes == k, dot_k, parts)
    feed_ref[...] = (shared_out_ref[...] + weighted).astype(feed_ref.dtype)
    back_ref[...] = (backs + shared_back_ref[...]).astype(back_ref.dtype)
    part_ref[...] = parts


def combine_rows(slot_index, table, gate_values, grad, shared_out, shared_back, block=128):
    tokens, top = gate_values.shape
    width = grad.shape[1]
    tile_rows = width // 128
    gates = jnp.broadcast_to(gate_values.T[:, :, None, None], (top, tokens, 1, 128))
    row_spec = pl.BlockSpec((block, tile_rows, 128), lambda i, s: (i, 0, 0))
    feed, back, parts = pl.pallas_call(
        combine_kernel,
        out_shape=(
            jax.ShapeDtypeStruct((tokens, tile_rows, 128), jnp.bfloat16),
            jax.ShapeDtypeStruct((tokens, tile_rows, 128), jnp.bfloat16),
            jax.ShapeDtypeStruct((tokens, 1, 128), jnp.float32),
        ),
        grid_spec=pltpu.PrefetchScalarGridSpec(
            num_scalar_prefetch=1,
            grid=(tokens // block,),
            in_specs=[
                pl.BlockSpec(memory_space=pl.ANY),
                pl.BlockSpec((top, block, 1, 128), lambda i, s: (0, i, 0, 0)),
                row_spec,
                row_spec,
                row_spec,
            ],
            out_specs=[row_spec, row_spec, pl.BlockSpec((block, 1, 128), lambda i, s: (i, 0, 0))],
            scratch_shapes=[
                pltpu.VMEM((top, block, 2 * tile_rows, 128), table.dtype),
                pltpu.SemaphoreType.DMA((top, block)),
            ],
        ),
        cost_estimate=pl.CostEstimate(
            flops=8 * tokens * top * width,
            transcendentals=0,
            bytes_accessed=tokens * (top * 4 * width + 2 * width + 8 * width + 4 * width),
        ),
    )(
        slot_index.reshape(-1),
        table.reshape(table.shape[0], 2 * tile_rows, 128),
        gates,
        grad.reshape(tokens, tile_rows, 128),
        shared_out.reshape(tokens, tile_rows, 128),
        shared_back.reshape(tokens, tile_rows, 128),
    )
    return feed.reshape(tokens, width), back.reshape(tokens, width), parts[:, 0, :top]


def shards(
    hidden,
    routes,
    prefix,
    attn_gain,
    query_proj,
    latent_proj,
    latent_gain,
    expand_proj,
    output_proj,
    second_gain,
    router_proj,
    expert_gate,
    expert_up,
    expert_down,
    shared_gate,
    shared_up,
    shared_down,
    out_grad,
):
    tok_dev = hidden.shape[0]
    tensor_size = lax.axis_size("tensor")
    tensor_rank = lax.axis_index("tensor")
    dp_size = lax.axis_size("dp")
    seq_len = tok_dev * tensor_size
    start_row = tensor_rank * tok_dev
    rows_dp = attn_gain.shape[0]
    kv_rows = latent_gain.shape[0]
    head_cols = query_proj.shape[1]
    latent_cols = latent_proj.shape[1]
    expand_cols = expand_proj.shape[1]
    expand_flat_cols = kv_rows * expand_cols // rows_dp
    first_pack = jnp.concatenate(
        [
            query_proj,
            latent_proj,
            expand_proj.reshape(rows_dp, expand_flat_cols),
            attn_gain[:, None],
            jnp.pad(latent_gain, (0, rows_dp - kv_rows))[:, None],
        ],
        1,
    )
    first_all = lax.all_gather(first_pack, "dp", axis=0, tiled=True)
    cut = [0]
    for width in (head_cols, latent_cols, expand_flat_cols, 1, 1):
        cut.append(cut[-1] + width)
    query_weights = first_all[:, cut[0] : cut[1]]
    latent_weights = first_all[:, cut[1] : cut[2]]
    expand_weights = first_all[:, cut[2] : cut[3]].reshape(dp_size * kv_rows, expand_cols)
    attn_gains = first_all[:, cut[3]]
    kv_gains = first_all[:, cut[4]].reshape(dp_size, rows_dp)[:, :kv_rows].reshape(-1)
    out_cols = output_proj.shape[0]
    experts = router_proj.shape[1]
    shared_cols = shared_gate.shape[1]
    second_pack = jnp.concatenate([output_proj.T, second_gain[:, None], router_proj], 1)
    second_all = lax.all_gather(second_pack, "dp", axis=0, tiled=True)
    output_weights_t = second_all[:, :out_cols]
    second_gains = second_all[:, out_cols]
    router_weights = second_all[:, out_cols + 1 :]
    shared_local = jnp.concatenate([shared_gate, shared_up, shared_down.T], 1)

    hidden_all = lax.all_gather(hidden, "tensor", axis=0, tiled=True)
    grad_seq = lax.all_to_all(
        jnp.broadcast_to(out_grad[None], (tensor_size,) + out_grad.shape),
        "tensor",
        split_axis=0,
        concat_axis=0,
        tiled=True,
    ).reshape(tensor_size * tok_dev, D)
    grad_seq, hidden_all = lax.optimization_barrier((grad_seq, hidden_all))
    hidden_all_f = hidden_all.astype(jnp.float32)
    scale_one_all = norm_scale(hidden_all_f)
    gain_one = attn_gains.astype(jnp.float32)
    normed_all = (hidden_all_f * scale_one_all * gain_one).astype(jnp.bfloat16)
    hidden_f = lax.dynamic_slice_in_dim(hidden_all_f, start_row, tok_dev, 0)
    scale_one = lax.dynamic_slice_in_dim(scale_one_all, start_row, tok_dev, 0)
    normed_own = lax.dynamic_slice_in_dim(normed_all, start_row, tok_dev, 0)
    latent_raw_all = jnp.dot(normed_all, latent_weights, preferred_element_type=jnp.float32)
    compressed_all = latent_raw_all[:, :KVR]
    scale_kv_all = norm_scale(compressed_all)
    gain_kv = kv_gains.astype(jnp.float32)
    all_cosines, all_sines = rope_tables(jnp.arange(seq_len), DR)
    latent_seq = jnp.concatenate(
        [
            compressed_all * scale_kv_all * gain_kv,
            rotate(latent_raw_all[:, KVR:], all_cosines, all_sines),
        ],
        -1,
    ).astype(jnp.bfloat16)
    compressed = lax.dynamic_slice_in_dim(compressed_all, start_row, tok_dev, 0)
    scale_kv = lax.dynamic_slice_in_dim(scale_kv_all, start_row, tok_dev, 0)
    own_cosines = lax.dynamic_slice_in_dim(all_cosines, start_row, tok_dev, 0)
    own_sines = lax.dynamic_slice_in_dim(all_sines, start_row, tok_dev, 0)
    head_count = query_weights.shape[1] // (DN + DR)
    query_raw = jnp.dot(normed_all, query_weights, preferred_element_type=jnp.float32).reshape(
        seq_len, head_count, DN + DR
    )
    query_low = jnp.concatenate(
        [
            query_raw[..., :DN],
            rotate(query_raw[..., DN:], all_cosines[:, None, :], all_sines[:, None, :]),
        ],
        -1,
    ).astype(jnp.bfloat16)
    compressed_seq = latent_seq[:, :KVR]
    key_rope = latent_seq[:, KVR:]
    expanded = jnp.dot(compressed_seq, expand_weights, preferred_element_type=jnp.float32).reshape(
        seq_len, head_count, DN + DV
    )
    keys_nope = expanded[..., :DN].astype(jnp.bfloat16)
    values_low = expanded[..., DN:].astype(jnp.bfloat16)
    score_scale = 1.0 / math.sqrt(DN + DR)
    block_rows = min(512, seq_len)
    prefix_len = prefix[0]
    lse_list = []
    mixed_list = []
    for rows_start in range(0, seq_len, block_rows):
        query_block = query_low[rows_start : rows_start + block_rows]
        masked = block_scores(query_block, keys_nope, key_rope, rows_start, prefix_len, score_scale)
        top_score = jnp.max(masked, -1, keepdims=True)
        exp_scores = jnp.exp(masked - top_score)
        totals = jnp.sum(exp_scores, -1, keepdims=True)
        prob_low = (exp_scores / totals).astype(jnp.bfloat16)
        lse_list.append(top_score + jnp.log(totals))
        mixed_list.append(
            jnp.einsum(
                "hqk,khv->qhv", prob_low, values_low, preferred_element_type=jnp.float32
            ).astype(jnp.bfloat16)
        )
    mixed_all = jnp.concatenate(mixed_list, 0).reshape(seq_len, head_count * DV)
    attn_part = jnp.einsum(
        "tk,dk->td", mixed_all, output_weights_t, preferred_element_type=jnp.float32
    )
    branch_all = lax.psum(attn_part.astype(jnp.bfloat16), "tensor").astype(jnp.float32)
    shared_local, branch_all = lax.optimization_barrier((shared_local, branch_all))
    residual_all = hidden_all_f + branch_all
    residual_own = lax.dynamic_slice_in_dim(residual_all, start_row, tok_dev, 0)
    scale_two = norm_scale(residual_all)
    gain_two = second_gains.astype(jnp.float32)
    normed_two = (residual_all * scale_two * gain_two).astype(jnp.bfloat16)
    logits = jnp.dot(normed_two, router_weights, preferred_element_type=jnp.float32)
    top_count = routes.shape[1]
    chosen_hot = routes[:, :, None] == jnp.arange(experts)[None, None, :]
    chosen_logits = jnp.sum(jnp.where(chosen_hot, logits[:, None, :], 0.0), -1)
    gate_values = jax.nn.softmax(chosen_logits, axis=-1)
    assignments = seq_len * top_count
    flat_hot = chosen_hot.reshape(assignments, experts).astype(jnp.bfloat16)
    lower = (jnp.arange(assignments)[:, None] > jnp.arange(assignments)[None, :]).astype(jnp.bfloat16)
    earlier = jnp.dot(lower, flat_hot, preferred_element_type=jnp.float32)
    slot_pos = jnp.sum(earlier * flat_hot.astype(jnp.float32), -1).astype(jnp.int32)
    expert_ids = routes.reshape(-1)
    exp_dev = expert_gate.shape[0]
    capacity = tensor_size * (5 * seq_len * top_count // (4 * experts * tensor_size))
    slot_index = expert_ids * capacity + slot_pos
    token_ids = jnp.arange(seq_len * top_count) // top_count
    slot_token = jnp.full((experts * capacity,), seq_len, jnp.int32).at[slot_index].set(token_ids)
    slot_gate = (
        jnp.zeros((experts * capacity,), jnp.float32).at[slot_index].set(gate_values.reshape(-1))
    )
    slot_valid = (slot_token < seq_len).astype(jnp.float32)
    tile_rows = D // 128
    send_both = dispatch_rows(slot_token, normed_two, grad_seq, slot_valid, slot_gate).reshape(
        dp_size, exp_dev, capacity, 2 * tile_rows, 128
    )
    shared_all = lax.all_gather(shared_local, "dp", axis=0, tiled=True)
    shared_all, send_both = lax.optimization_barrier((shared_all, send_both))
    gate_shared = shared_all[:, :shared_cols]
    up_shared = shared_all[:, shared_cols : 2 * shared_cols]
    down_shared_t = shared_all[:, 2 * shared_cols :]
    recv_both = lax.all_to_all(send_both, "dp", split_axis=0, concat_axis=0, tiled=True)
    recv_both = recv_both.reshape(dp_size, exp_dev, capacity, 2 * D)
    recv_rows = recv_both[..., :D]
    recv_grads = recv_both[..., D:]
    gate_pre = jnp.einsum(
        "sjcd,jfd->sjcf", recv_rows, expert_gate, preferred_element_type=jnp.float32
    )
    up_pre = jnp.einsum("sjcd,jfd->sjcf", recv_rows, expert_up, preferred_element_type=jnp.float32)
    sigmoid_gate = jax.nn.sigmoid(gate_pre)
    expert_act = (gate_pre * sigmoid_gate * up_pre).astype(jnp.bfloat16)
    expert_out = jnp.einsum(
        "sjcf,jfd->sjcd", expert_act, expert_down, preferred_element_type=jnp.float32
    )
    act_grad = jnp.einsum(
        "sjcd,jfd->sjcf", recv_grads, expert_down, preferred_element_type=jnp.float32
    )
    gate_low_grad, up_low_grad = silu_back(act_grad, gate_pre, up_pre, sigmoid_gate)
    expert_down_grad = jnp.einsum(
        "sjcf,sjcd->jfd", expert_act, recv_grads, preferred_element_type=jnp.float32
    )
    expert_gate_grad = jnp.einsum(
        "sjcf,sjcd->jfd", gate_low_grad, recv_rows, preferred_element_type=jnp.float32
    )
    expert_up_grad = jnp.einsum(
        "sjcf,sjcd->jfd", up_low_grad, recv_rows, preferred_element_type=jnp.float32
    )
    row_grads = jnp.einsum(
        "sjcf,jfd->sjcd", gate_low_grad, expert_gate, preferred_element_type=jnp.float32
    )
    row_grads = row_grads + jnp.einsum(
        "sjcf,jfd->sjcd", up_low_grad, expert_up, preferred_element_type=jnp.float32
    )
    back_both = lax.all_to_all(
        jnp.concatenate(
            [expert_out.astype(jnp.bfloat16), row_grads.astype(jnp.bfloat16)], -1
        ).reshape(dp_size, exp_dev, capacity, 2 * tile_rows, 128),
        "dp",
        split_axis=0,
        concat_axis=0,
        tiled=True,
    )
    shared_pre_gate = jnp.dot(normed_two, gate_shared, preferred_element_type=jnp.float32)
    shared_pre_up = jnp.dot(normed_two, up_shared, preferred_element_type=jnp.float32)
    shared_sigmoid = jax.nn.sigmoid(shared_pre_gate)
    shared_act = (shared_pre_gate * shared_sigmoid * shared_pre_up).astype(jnp.bfloat16)
    shared_out = jnp.einsum(
        "tf,df->td", shared_act, down_shared_t, preferred_element_type=jnp.float32
    )
    shared_act_grad = jnp.dot(grad_seq, down_shared_t, preferred_element_type=jnp.float32)
    shared_gate_low, shared_up_low = silu_back(
        shared_act_grad, shared_pre_gate, shared_pre_up, shared_sigmoid
    )
    shared_down_grad_t = jnp.dot(grad_seq.T, shared_act, preferred_element_type=jnp.float32)
    shared_gate_grad = jnp.dot(normed_two.T, shared_gate_low, preferred_element_type=jnp.float32)
    shared_up_grad = jnp.dot(normed_two.T, shared_up_low, preferred_element_type=jnp.float32)
    shared_back = jnp.einsum(
        "tf,df->td", shared_gate_low, gate_shared, preferred_element_type=jnp.float32
    )
    shared_back = shared_back + jnp.einsum(
        "tf,df->td", shared_up_low, up_shared, preferred_element_type=jnp.float32
    )
    shared_grads_in = jnp.concatenate(
        [shared_gate_grad, shared_up_grad, shared_down_grad_t], 1
    ).astype(jnp.bfloat16)
    grad_seq_f = grad_seq.astype(jnp.float32)
    table_rows = experts * capacity
    feed_part, back_part, gate_cols = combine_rows(
        slot_index.reshape(seq_len, top_count),
        back_both.reshape(table_rows, 2 * tile_rows, 128),
        gate_values,
        grad_seq,
        shared_out,
        shared_back,
    )
    gate_part = gate_cols[:, :top_count]
    feed_own = lax.psum_scatter(feed_part, "tensor", scatter_dimension=0, tiled=True).astype(
        jnp.float32
    )
    reduced_back = lax.psum(
        jnp.concatenate([back_part, gate_cols.astype(jnp.bfloat16)], 1), "tensor"
    ).astype(jnp.float32)
    normed_two_grad = reduced_back[:, :D]
    gate_grads = reduced_back[:, D : D + top_count]
    weighted_total = jnp.sum(gate_values * gate_grads, -1, keepdims=True)
    chosen_grads = gate_values * (gate_grads - weighted_total)
    logit_grads = jnp.sum(jnp.where(chosen_hot, chosen_grads[:, :, None], 0.0), 1)
    normed_two_grad = normed_two_grad + jnp.dot(
        logit_grads, router_weights.astype(jnp.float32).T, precision=HIGH
    )
    residual_grad = grad_seq_f + norm_back(residual_all, scale_two, gain_two, normed_two_grad)
    branch_grad = residual_grad.astype(jnp.bfloat16)
    shared_grads_in, branch_grad = lax.optimization_barrier((shared_grads_in, branch_grad))
    shared_pack = lax.psum_scatter(
        shared_grads_in, "dp", scatter_dimension=0, tiled=True
    ).astype(jnp.float32)
    output_grad_w_t = jnp.dot(branch_grad.T, mixed_all, preferred_element_type=jnp.float32)
    mixed_grad = (
        jnp.dot(branch_grad, output_weights_t, preferred_element_type=jnp.float32)
        .astype(jnp.bfloat16)
        .reshape(seq_len, head_count, DV)
    )
    keys_nope_grad = jnp.zeros((seq_len, head_count, DN), jnp.float32)
    key_rope_grad = jnp.zeros((seq_len, DR), jnp.float32)
    values_grad = jnp.zeros((seq_len, head_count, DV), jnp.float32)
    query_grad_list = []
    for block_index, rows_start in enumerate(range(0, seq_len, block_rows)):
        query_block = query_low[rows_start : rows_start + block_rows]
        masked = block_scores(query_block, keys_nope, key_rope, rows_start, prefix_len, score_scale)
        prob_full = jnp.exp(masked - lse_list[block_index])
        prob_low = prob_full.astype(jnp.bfloat16)
        mixed_block = mixed_grad[rows_start : rows_start + block_rows]
        prob_grads = jnp.einsum(
            "qhv,khv->hqk", mixed_block, values_low, preferred_element_type=jnp.float32
        )
        row_delta = jnp.sum(prob_full * prob_grads, -1, keepdims=True)
        score_grads = (prob_full * (prob_grads - row_delta)).astype(jnp.bfloat16)
        query_nope_grad = (
            jnp.einsum("hqk,khd->qhd", score_grads, keys_nope, preferred_element_type=jnp.float32)
            * score_scale
        )
        query_rope_grad = (
            jnp.einsum("hqk,kr->qhr", score_grads, key_rope, preferred_element_type=jnp.float32)
            * score_scale
        )
        keys_nope_grad = (
            keys_nope_grad
            + jnp.einsum(
                "hqk,qhd->khd",
                score_grads,
                query_block[..., :DN],
                preferred_element_type=jnp.float32,
            )
            * score_scale
        )
        key_rope_grad = (
            key_rope_grad
            + jnp.einsum(
                "hqk,qhr->kr",
                score_grads,
                query_block[..., DN:],
                preferred_element_type=jnp.float32,
            )
            * score_scale
        )
        values_grad = values_grad + jnp.einsum(
            "hqk,qhv->khv", prob_low, mixed_block, preferred_element_type=jnp.float32
        )
        block_cosines = all_cosines[rows_start : rows_start + block_rows, None, :]
        block_sines = all_sines[rows_start : rows_start + block_rows, None, :]
        query_grad_list.append(
            jnp.concatenate(
                [
                    query_nope_grad,
                    rotate_back(round_trip(query_rope_grad), block_cosines, block_sines),
                ],
                -1,
            ).astype(jnp.bfloat16)
        )
    query_grads = jnp.concatenate(query_grad_list, 0).reshape(seq_len, head_count * (DN + DR))
    feed_own, shared_pack, query_grads = lax.optimization_barrier((feed_own, shared_pack, query_grads))
    output = (residual_own + feed_own).astype(jnp.bfloat16)
    query_grad_w = jnp.dot(normed_all.T, query_grads, preferred_element_type=jnp.float32)
    normed_grad_part = jnp.dot(query_grads, query_weights.T, preferred_element_type=jnp.float32)
    expand_grads = jnp.concatenate(
        [keys_nope_grad.astype(jnp.bfloat16), values_grad.astype(jnp.bfloat16)], -1
    ).reshape(seq_len, head_count * (DN + DV))
    expand_grad_w = jnp.dot(compressed_seq.T, expand_grads, preferred_element_type=jnp.float32)
    compressed_grad_part = jnp.dot(
        expand_grads, expand_weights.T, preferred_element_type=jnp.float32
    )
    latent_grad_part = jnp.concatenate([compressed_grad_part, key_rope_grad], -1)
    attn_grads_in = jnp.concatenate(
        [
            query_grad_w,
            output_grad_w_t,
            expand_grad_w.reshape(dp_size * rows_dp, expand_flat_cols),
        ],
        1,
    )
    token_all = lax.psum(
        jnp.concatenate([normed_grad_part, latent_grad_part], 1).astype(jnp.bfloat16), "tensor"
    ).astype(jnp.float32)
    compressed_grad_all = token_all[:, D : D + KVR]
    kv_gain_full = jnp.sum(compressed_grad_all * compressed_all * scale_kv_all, 0)
    raw_grad_all = jnp.concatenate(
        [
            norm_back(compressed_all, scale_kv_all, gain_kv, compressed_grad_all),
            rotate_back(token_all[:, D + KVR :], all_cosines, all_sines),
        ],
        -1,
    ).astype(jnp.bfloat16)
    normed_grad_all = token_all[:, :D] + jnp.dot(
        raw_grad_all, latent_weights.T, preferred_element_type=jnp.float32
    )
    normed_grad = lax.dynamic_slice_in_dim(normed_grad_all, start_row, tok_dev, 0)
    hidden_grad = lax.dynamic_slice_in_dim(residual_grad, start_row, tok_dev, 0) + norm_back(
        hidden_f, scale_one, gain_one, normed_grad
    )
    row_per = D // (dp_size * tensor_size)

    def own_rows(values):
        split = values.reshape(values.shape[0], dp_size, tensor_size, row_per)
        return lax.dynamic_slice_in_dim(split, tensor_rank, 1, 2).reshape(values.shape[0], -1)

    latent_rows = jnp.dot(own_rows(normed_all).T, raw_grad_all, preferred_element_type=jnp.float32)
    attn_gain_rows = jnp.sum(
        own_rows(normed_grad_all) * own_rows(hidden_all_f) * scale_one_all, 0
    )
    second_gain_rows = jnp.sum(
        own_rows(normed_two_grad) * own_rows(residual_all) * scale_two, 0
    )
    router_rows = jnp.dot(
        own_rows(normed_two).astype(jnp.float32).T, logit_grads, precision=HIGH
    )
    kv_per = kv_gain_full.shape[0] // (dp_size * tensor_size)
    kv_rows_own = lax.dynamic_slice_in_dim(
        kv_gain_full.reshape(dp_size, tensor_size, kv_per), tensor_rank, 1, 1
    ).reshape(dp_size, kv_per)
    kv_column = jnp.pad(kv_rows_own, ((0, 0), (0, row_per - kv_per))).reshape(-1)
    small_pack = jnp.concatenate(
        [
            latent_rows,
            router_rows,
            attn_gain_rows[:, None],
            second_gain_rows[:, None],
            kv_column[:, None],
        ],
        1,
    )
    attn_width = attn_grads_in.shape[1]
    small_width = small_pack.shape[1]
    small_count = row_per * small_width
    small_cols = -(-small_count // rows_dp)
    small_flat = jnp.pad(
        small_pack.reshape(dp_size, small_count), ((0, 0), (0, small_cols * rows_dp - small_count))
    ).reshape(dp_size * rows_dp, small_cols)
    merged_own = lax.psum_scatter(
        jnp.concatenate([attn_grads_in, small_flat], 1), "dp", scatter_dimension=0, tiled=True
    )
    attn_pack = merged_own[:, :attn_width]
    small_own = merged_own[:, attn_width:].reshape(-1)[:small_count].reshape(row_per, small_width)
    cut = [0]
    for width in (latent_cols, experts, 1, 1, 1):
        cut.append(cut[-1] + width)
    latent_proj_grad = small_own[:, cut[0] : cut[1]]
    router_out = small_own[:, cut[1] : cut[2]]
    attn_gain_out = small_own[:, cut[2]]
    second_gain_out = small_own[:, cut[3]]
    latent_gain_out = small_own[:kv_per, cut[4]]
    cut = [0]
    for width in (head_cols, out_cols, expand_flat_cols):
        cut.append(cut[-1] + width)
    query_proj_grad = attn_pack[:, cut[0] : cut[1]]
    output_proj_grad = attn_pack[:, cut[1] : cut[2]].T
    expand_proj_grad = attn_pack[:, cut[2] : cut[3]].reshape(kv_rows, expand_cols)
    shared_gate_out = shared_pack[:, :shared_cols]
    shared_up_out = shared_pack[:, shared_cols : 2 * shared_cols]
    shared_down_out = shared_pack[:, 2 * shared_cols :].T
    return (
        output,
        hidden_grad,
        attn_gain_out,
        query_proj_grad,
        latent_proj_grad,
        latent_gain_out,
        expand_proj_grad,
        output_proj_grad,
        second_gain_out,
        router_out,
        expert_gate_grad,
        expert_up_grad,
        expert_down_grad,
        shared_gate_out,
        shared_up_out,
        shared_down_out,
    )


def solution(mesh):
    return jax.shard_map(
        shards,
        mesh=mesh,
        in_specs=(
            P(("dp", "tensor"), None),
            P("dp", None),
            P("dp"),
            P("dp"),
            P("dp", "tensor"),
            P("dp", None),
            P("dp"),
            P("dp", "tensor"),
            P("tensor", "dp"),
            P("dp"),
            P("dp", None),
            P("dp", "tensor", None),
            P("dp", "tensor", None),
            P("dp", "tensor", None),
            P("dp", "tensor"),
            P("dp", "tensor"),
            P("tensor", "dp"),
            P(("dp", "tensor"), None),
        ),
        out_specs=(
            P(("dp", "tensor"), None),
            P(("dp", "tensor"), None),
            P(("dp", "tensor")),
            P("dp", "tensor"),
            P(("dp", "tensor"), None),
            P(("dp", "tensor")),
            P("dp", "tensor"),
            P("tensor", "dp"),
            P(("dp", "tensor")),
            P(("dp", "tensor"), None),
            P("dp", "tensor", None),
            P("dp", "tensor", None),
            P("dp", "tensor", None),
            P("dp", "tensor"),
            P("dp", "tensor"),
            P("tensor", "dp"),
        ),
        check_vma=False,
    )
```

```python
import math

import jax
import jax.numpy as jnp
from jax import lax
from jax.experimental import pallas as pl
from jax.experimental.pallas import tpu as pltpu
from jax.sharding import PartitionSpec as P

D = 2048
DN = 128
DR = 64
DV = 128
KVR = 512


EPS = 1e-06
HIGH = lax.Precision.HIGHEST
MASKED = -1e30


def norm_scale(values):
    return lax.rsqrt(jnp.mean(values * values, -1, keepdims=True) + EPS)


def norm_back(values, scales, gains, upstream):
    weighted = gains * upstream
    return scales * weighted - values * scales**3 * jnp.mean(values * weighted, -1, keepdims=True)


def rope_tables(positions, rope_width):
    half_width = rope_width // 2
    frequency = 10000.0 ** (-2.0 * jnp.arange(half_width).astype(jnp.float32) / rope_width)
    angles = positions.astype(jnp.float32)[:, None] * frequency[None, :]
    return (jnp.cos(angles), jnp.sin(angles))


def rotate(vectors, cosines, sine_values):
    half_width = vectors.shape[-1] // 2
    front_half = vectors[..., :half_width]
    back_half = vectors[..., half_width:]
    return jnp.concatenate(
        [
            front_half * cosines - back_half * sine_values,
            back_half * cosines + front_half * sine_values,
        ],
        -1,
    )


def rotate_back(gradients, cosines, sine_values):
    half_width = gradients.shape[-1] // 2
    front_half = gradients[..., :half_width]
    back_half = gradients[..., half_width:]
    return jnp.concatenate(
        [
            front_half * cosines + back_half * sine_values,
            back_half * cosines - front_half * sine_values,
        ],
        -1,
    )


def round_trip(values):
    return lax.optimization_barrier(values.astype(jnp.bfloat16)).astype(jnp.float32)


def block_scores(query_block, keys_nope, key_rope, rows_start, prefix_len, score_scale):
    raw_scores = jnp.einsum(
        "qhd,khd->hqk", query_block[..., :DN], keys_nope, preferred_element_type=jnp.float32
    )
    raw_scores = raw_scores + jnp.einsum(
        "qhr,kr->hqk", query_block[..., DN:], key_rope, preferred_element_type=jnp.float32
    )
    query_places = rows_start + jnp.arange(query_block.shape[0])
    key_places = jnp.arange(keys_nope.shape[0])
    visible = (key_places[None, :] <= query_places[:, None]) | (key_places[None, :] < prefix_len)
    return jnp.where(visible[None], raw_scores * score_scale, MASKED)


def silu_back(act_grad, gate_pre, up_pre, sigmoid_gate):
    up_grad = (act_grad * gate_pre * sigmoid_gate).astype(jnp.bfloat16)
    gate_grad = (act_grad * up_pre * sigmoid_gate * (1.0 + gate_pre * (1.0 - sigmoid_gate))).astype(
        jnp.bfloat16
    )
    return (gate_grad, up_grad)


def dispatch_kernel(tok_ref, both_hbm, col_ref, out_ref, both_buf, sems):
    block = both_buf.shape[0]
    tile_rows = both_buf.shape[1] // 2
    last = both_hbm.shape[0] - 1
    base = pl.program_id(0) * block

    def start(r, carry):
        tok = jnp.minimum(tok_ref[base + r], last)
        pltpu.make_async_copy(both_hbm.at[tok], both_buf.at[r], sems.at[r]).start()
        return carry

    lax.fori_loop(0, block, start, 0, unroll=4)

    def finish(r, carry):
        pltpu.make_async_copy(both_hbm.at[0], both_buf.at[r], sems.at[r]).wait()
        return carry

    lax.fori_loop(0, block, finish, 0, unroll=4)
    rows = both_buf[:, :tile_rows, :]
    out_ref[:, :tile_rows, :] = jnp.where(col_ref[0] > 0, rows, jnp.zeros_like(rows))
    out_ref[:, tile_rows:, :] = (
        both_buf[:, tile_rows:, :].astype(jnp.float32) * col_ref[1]
    ).astype(out_ref.dtype)


def dispatch_rows(slot_token, rows, grads, valid, gate, block=128):
    slots = slot_token.shape[0]
    count, width = rows.shape
    tile_rows = width // 128
    cols = jnp.broadcast_to(jnp.stack([valid, gate])[:, :, None, None], (2, slots, 1, 128))
    both = jnp.concatenate([rows, grads], 1).reshape(count, 2 * tile_rows, 128)
    out = pl.pallas_call(
        dispatch_kernel,
        out_shape=jax.ShapeDtypeStruct((slots, 2 * tile_rows, 128), rows.dtype),
        grid_spec=pltpu.PrefetchScalarGridSpec(
            num_scalar_prefetch=1,
            grid=(slots // block,),
            in_specs=[
                pl.BlockSpec(memory_space=pl.ANY),
                pl.BlockSpec((2, block, 1, 128), lambda i, tok: (0, i, 0, 0)),
            ],
            out_specs=pl.BlockSpec((block, 2 * tile_rows, 128), lambda i, tok: (i, 0, 0)),
            scratch_shapes=[
                pltpu.VMEM((block, 2 * tile_rows, 128), rows.dtype),
                pltpu.SemaphoreType.DMA((block,)),
            ],
        ),
        cost_estimate=pl.CostEstimate(
            flops=slots * width, transcendentals=0, bytes_accessed=4 * slots * 2 * width
        ),
    )(slot_token, both, cols)
    return out


def combine_kernel(
    slot_ref, table_hbm, gate_ref, grad_ref, shared_out_ref, shared_back_ref,
    feed_ref, back_ref, part_ref, picked, sems,
):
    top = picked.shape[0]
    block = picked.shape[1]
    tile_rows = grad_ref.shape[1]
    last = table_hbm.shape[0] - 1
    base = pl.program_id(0) * block

    def start(r, carry):
        for k in range(top):
            slot = jnp.clip(slot_ref[(base + r) * top + k], 0, last)
            pltpu.make_async_copy(table_hbm.at[slot], picked.at[k, r], sems.at[k, r]).start()
        return carry

    lax.fori_loop(0, block, start, 0)

    def finish(r, carry):
        for k in range(top):
            pltpu.make_async_copy(table_hbm.at[0], picked.at[k, r], sems.at[k, r]).wait()
        return carry

    lax.fori_loop(0, block, finish, 0)
    grad = grad_ref[...].astype(jnp.float32)
    weighted = None
    backs = None
    lanes = lax.broadcasted_iota(jnp.int32, part_ref.shape, 2)
    parts = jnp.zeros(part_ref.shape, jnp.float32)
    for k in range(top):
        out_k = picked[k, :, :tile_rows, :].astype(jnp.float32)
        term = gate_ref[k] * out_k
        weighted = term if weighted is None else weighted + term
        back_k = picked[k, :, tile_rows:, :].astype(jnp.float32)
        backs = back_k if backs is None else backs + back_k
        dot_k = jnp.sum(jnp.sum(grad * out_k, 2, keepdims=True), 1, keepdims=True)
        parts = jnp.where(lanes == k, dot_k, parts)
    feed_ref[...] = (shared_out_ref[...] + weighted).astype(feed_ref.dtype)
    back_ref[...] = (backs + shared_back_ref[...]).astype(back_ref.dtype)
    part_ref[...] = parts


def combine_rows(slot_index, table, gate_values, grad, shared_out, shared_back, block=128):
    tokens, top = gate_values.shape
    width = grad.shape[1]
    tile_rows = width // 128
    gates = jnp.broadcast_to(gate_values.T[:, :, None, None], (top, tokens, 1, 128))
    row_spec = pl.BlockSpec((block, tile_rows, 128), lambda i, s: (i, 0, 0))
    feed, back, parts = pl.pallas_call(
        combine_kernel,
        out_shape=(
            jax.ShapeDtypeStruct((tokens, tile_rows, 128), jnp.bfloat16),
            jax.ShapeDtypeStruct((tokens, tile_rows, 128), jnp.bfloat16),
            jax.ShapeDtypeStruct((tokens, 1, 128), jnp.float32),
        ),
        grid_spec=pltpu.PrefetchScalarGridSpec(
            num_scalar_prefetch=1,
            grid=(tokens // block,),
            in_specs=[
                pl.BlockSpec(memory_space=pl.ANY),
                pl.BlockSpec((top, block, 1, 128), lambda i, s: (0, i, 0, 0)),
                row_spec,
                row_spec,
                row_spec,
            ],
            out_specs=[row_spec, row_spec, pl.BlockSpec((block, 1, 128), lambda i, s: (i, 0, 0))],
            scratch_shapes=[
                pltpu.VMEM((top, block, 2 * tile_rows, 128), table.dtype),
                pltpu.SemaphoreType.DMA((top, block)),
            ],
        ),
        cost_estimate=pl.CostEstimate(
            flops=8 * tokens * top * width,
            transcendentals=0,
            bytes_accessed=tokens * (top * 4 * width + 2 * width + 8 * width + 4 * width),
        ),
    )(
        slot_index.reshape(-1),
        table.reshape(table.shape[0], 2 * tile_rows, 128),
        gates,
        grad.reshape(tokens, tile_rows, 128),
        shared_out.reshape(tokens, tile_rows, 128),
        shared_back.reshape(tokens, tile_rows, 128),
    )
    return feed.reshape(tokens, width), back.reshape(tokens, width), parts[:, 0, :top]


def shards(
    hidden,
    routes,
    prefix,
    attn_gain,
    query_proj,
    latent_proj,
    latent_gain,
    expand_proj,
    output_proj,
    second_gain,
    router_proj,
    expert_gate,
    expert_up,
    expert_down,
    shared_gate,
    shared_up,
    shared_down,
    out_grad,
):
    tok_dev = hidden.shape[0]
    tensor_size = lax.axis_size("tensor")
    tensor_rank = lax.axis_index("tensor")
    dp_size = lax.axis_size("dp")
    seq_len = tok_dev * tensor_size
    start_row = tensor_rank * tok_dev
    rows_dp = attn_gain.shape[0]
    kv_rows = latent_gain.shape[0]
    head_cols = query_proj.shape[1]
    latent_cols = latent_proj.shape[1]
    expand_cols = expand_proj.shape[1]
    expand_flat_cols = kv_rows * expand_cols // rows_dp
    first_pack = jnp.concatenate(
        [
            query_proj,
            latent_proj,
            expand_proj.reshape(rows_dp, expand_flat_cols),
            attn_gain[:, None],
            jnp.pad(latent_gain, (0, rows_dp - kv_rows))[:, None],
        ],
        1,
    )
    first_all = lax.all_gather(first_pack, "dp", axis=0, tiled=True)
    cut = [0]
    for width in (head_cols, latent_cols, expand_flat_cols, 1, 1):
        cut.append(cut[-1] + width)
    query_weights = first_all[:, cut[0] : cut[1]]
    latent_weights = first_all[:, cut[1] : cut[2]]
    expand_weights = first_all[:, cut[2] : cut[3]].reshape(dp_size * kv_rows, expand_cols)
    attn_gains = first_all[:, cut[3]]
    kv_gains = first_all[:, cut[4]].reshape(dp_size, rows_dp)[:, :kv_rows].reshape(-1)
    out_cols = output_proj.shape[0]
    experts = router_proj.shape[1]
    shared_cols = shared_gate.shape[1]
    second_pack = jnp.concatenate([output_proj.T, second_gain[:, None], router_proj], 1)
    second_all = lax.all_gather(second_pack, "dp", axis=0, tiled=True)
    output_weights_t = second_all[:, :out_cols]
    second_gains = second_all[:, out_cols]
    router_weights = second_all[:, out_cols + 1 :]
    shared_local = jnp.concatenate([shared_gate, shared_up, shared_down.T], 1)

    hidden_all = lax.all_gather(hidden, "tensor", axis=0, tiled=True)
    grad_seq = lax.all_to_all(
        jnp.broadcast_to(out_grad[None], (tensor_size,) + out_grad.shape),
        "tensor",
        split_axis=0,
        concat_axis=0,
        tiled=True,
    ).reshape(tensor_size * tok_dev, D)
    grad_seq, hidden_all = lax.optimization_barrier((grad_seq, hidden_all))
    hidden_all_f = hidden_all.astype(jnp.float32)
    scale_one_all = norm_scale(hidden_all_f)
    gain_one = attn_gains.astype(jnp.float32)
    normed_all = (hidden_all_f * scale_one_all * gain_one).astype(jnp.bfloat16)
    hidden_f = lax.dynamic_slice_in_dim(hidden_all_f, start_row, tok_dev, 0)
    scale_one = lax.dynamic_slice_in_dim(scale_one_all, start_row, tok_dev, 0)
    normed_own = lax.dynamic_slice_in_dim(normed_all, start_row, tok_dev, 0)
    latent_raw_all = jnp.dot(normed_all, latent_weights, preferred_element_type=jnp.float32)
    compressed_all = latent_raw_all[:, :KVR]
    scale_kv_all = norm_scale(compressed_all)
    gain_kv = kv_gains.astype(jnp.float32)
    all_cosines, all_sines = rope_tables(jnp.arange(seq_len), DR)
    latent_seq = jnp.concatenate(
        [
            compressed_all * scale_kv_all * gain_kv,
            rotate(latent_raw_all[:, KVR:], all_cosines, all_sines),
        ],
        -1,
    ).astype(jnp.bfloat16)
    compressed = lax.dynamic_slice_in_dim(compressed_all, start_row, tok_dev, 0)
    scale_kv = lax.dynamic_slice_in_dim(scale_kv_all, start_row, tok_dev, 0)
    own_cosines = lax.dynamic_slice_in_dim(all_cosines, start_row, tok_dev, 0)
    own_sines = lax.dynamic_slice_in_dim(all_sines, start_row, tok_dev, 0)
    head_count = query_weights.shape[1] // (DN + DR)
    query_raw = jnp.dot(normed_all, query_weights, preferred_element_type=jnp.float32).reshape(
        seq_len, head_count, DN + DR
    )
    query_low = jnp.concatenate(
        [
            query_raw[..., :DN],
            rotate(query_raw[..., DN:], all_cosines[:, None, :], all_sines[:, None, :]),
        ],
        -1,
    ).astype(jnp.bfloat16)
    compressed_seq = latent_seq[:, :KVR]
    key_rope = latent_seq[:, KVR:]
    expanded = jnp.dot(compressed_seq, expand_weights, preferred_element_type=jnp.float32).reshape(
        seq_len, head_count, DN + DV
    )
    keys_nope = expanded[..., :DN].astype(jnp.bfloat16)
    values_low = expanded[..., DN:].astype(jnp.bfloat16)
    score_scale = 1.0 / math.sqrt(DN + DR)
    block_rows = min(512, seq_len)
    prefix_len = prefix[0]
    lse_list = []
    mixed_list = []
    for rows_start in range(0, seq_len, block_rows):
        query_block = query_low[rows_start : rows_start + block_rows]
        masked = block_scores(query_block, keys_nope, key_rope, rows_start, prefix_len, score_scale)
        top_score = jnp.max(masked, -1, keepdims=True)
        exp_scores = jnp.exp(masked - top_score)
        totals = jnp.sum(exp_scores, -1, keepdims=True)
        prob_low = (exp_scores / totals).astype(jnp.bfloat16)
        lse_list.append(top_score + jnp.log(totals))
        mixed_list.append(
            jnp.einsum(
                "hqk,khv->qhv", prob_low, values_low, preferred_element_type=jnp.float32
            ).astype(jnp.bfloat16)
        )
    mixed_all = jnp.concatenate(mixed_list, 0).reshape(seq_len, head_count * DV)
    attn_part = jnp.einsum(
        "tk,dk->td", mixed_all, output_weights_t, preferred_element_type=jnp.float32
    )
    branch_all = lax.psum(attn_part.astype(jnp.bfloat16), "tensor").astype(jnp.float32)
    shared_local, branch_all = lax.optimization_barrier((shared_local, branch_all))
    residual_all = hidden_all_f + branch_all
    residual_own = lax.dynamic_slice_in_dim(residual_all, start_row, tok_dev, 0)
    scale_two = norm_scale(residual_all)
    gain_two = second_gains.astype(jnp.float32)
    normed_two = (residual_all * scale_two * gain_two).astype(jnp.bfloat16)
    logits = jnp.dot(normed_two, router_weights, preferred_element_type=jnp.float32)
    top_count = routes.shape[1]
    chosen_hot = routes[:, :, None] == jnp.arange(experts)[None, None, :]
    chosen_logits = jnp.sum(jnp.where(chosen_hot, logits[:, None, :], 0.0), -1)
    gate_values = jax.nn.softmax(chosen_logits, axis=-1)
    assignments = seq_len * top_count
    flat_hot = chosen_hot.reshape(assignments, experts).astype(jnp.bfloat16)
    lower = (jnp.arange(assignments)[:, None] > jnp.arange(assignments)[None, :]).astype(jnp.bfloat16)
    earlier = jnp.dot(lower, flat_hot, preferred_element_type=jnp.float32)
    slot_pos = jnp.sum(earlier * flat_hot.astype(jnp.float32), -1).astype(jnp.int32)
    expert_ids = routes.reshape(-1)
    exp_dev = expert_gate.shape[0]
    capacity = tensor_size * (5 * seq_len * top_count // (4 * experts * tensor_size))
    slot_index = expert_ids * capacity + slot_pos
    token_ids = jnp.arange(seq_len * top_count) // top_count
    slot_token = jnp.full((experts * capacity,), seq_len, jnp.int32).at[slot_index].set(token_ids)
    slot_gate = (
        jnp.zeros((experts * capacity,), jnp.float32).at[slot_index].set(gate_values.reshape(-1))
    )
    slot_valid = (slot_token < seq_len).astype(jnp.float32)
    tile_rows = D // 128
    send_both = dispatch_rows(slot_token, normed_two, grad_seq, slot_valid, slot_gate).reshape(
        dp_size, exp_dev, capacity, 2 * tile_rows, 128
    )
    shared_all = lax.all_gather(shared_local, "dp", axis=0, tiled=True)
    shared_all, send_both = lax.optimization_barrier((shared_all, send_both))
    gate_shared = shared_all[:, :shared_cols]
    up_shared = shared_all[:, shared_cols : 2 * shared_cols]
    down_shared_t = shared_all[:, 2 * shared_cols :]
    recv_both = lax.all_to_all(send_both, "dp", split_axis=0, concat_axis=0, tiled=True)
    recv_both = recv_both.reshape(dp_size, exp_dev, capacity, 2 * D)
    recv_rows = recv_both[..., :D]
    recv_grads = recv_both[..., D:]
    gate_pre = jnp.einsum(
        "sjcd,jfd->sjcf", recv_rows, expert_gate, preferred_element_type=jnp.float32
    )
    up_pre = jnp.einsum("sjcd,jfd->sjcf", recv_rows, expert_up, preferred_element_type=jnp.float32)
    sigmoid_gate = jax.nn.sigmoid(gate_pre)
    expert_act = (gate_pre * sigmoid_gate * up_pre).astype(jnp.bfloat16)
    expert_out = jnp.einsum(
        "sjcf,jfd->sjcd", expert_act, expert_down, preferred_element_type=jnp.float32
    )
    act_grad = jnp.einsum(
        "sjcd,jfd->sjcf", recv_grads, expert_down, preferred_element_type=jnp.float32
    )
    gate_low_grad, up_low_grad = silu_back(act_grad, gate_pre, up_pre, sigmoid_gate)
    expert_down_grad = jnp.einsum(
        "sjcf,sjcd->jfd", expert_act, recv_grads, preferred_element_type=jnp.float32
    )
    expert_gate_grad = jnp.einsum(
        "sjcf,sjcd->jfd", gate_low_grad, recv_rows, preferred_element_type=jnp.float32
    )
    expert_up_grad = jnp.einsum(
        "sjcf,sjcd->jfd", up_low_grad, recv_rows, preferred_element_type=jnp.float32
    )
    row_grads = jnp.einsum(
        "sjcf,jfd->sjcd", gate_low_grad, expert_gate, preferred_element_type=jnp.float32
    )
    row_grads = row_grads + jnp.einsum(
        "sjcf,jfd->sjcd", up_low_grad, expert_up, preferred_element_type=jnp.float32
    )
    back_both = lax.all_to_all(
        jnp.concatenate(
            [expert_out.astype(jnp.bfloat16), row_grads.astype(jnp.bfloat16)], -1
        ).reshape(dp_size, exp_dev, capacity, 2 * tile_rows, 128),
        "dp",
        split_axis=0,
        concat_axis=0,
        tiled=True,
    )
    shared_pre_gate = jnp.dot(normed_two, gate_shared, preferred_element_type=jnp.float32)
    shared_pre_up = jnp.dot(normed_two, up_shared, preferred_element_type=jnp.float32)
    shared_sigmoid = jax.nn.sigmoid(shared_pre_gate)
    shared_act = (shared_pre_gate * shared_sigmoid * shared_pre_up).astype(jnp.bfloat16)
    shared_out = jnp.einsum(
        "tf,df->td", shared_act, down_shared_t, preferred_element_type=jnp.float32
    )
    shared_act_grad = jnp.dot(grad_seq, down_shared_t, preferred_element_type=jnp.float32)
    shared_gate_low, shared_up_low = silu_back(
        shared_act_grad, shared_pre_gate, shared_pre_up, shared_sigmoid
    )
    shared_down_grad_t = jnp.dot(grad_seq.T, shared_act, preferred_element_type=jnp.float32)
    shared_gate_grad = jnp.dot(normed_two.T, shared_gate_low, preferred_element_type=jnp.float32)
    shared_up_grad = jnp.dot(normed_two.T, shared_up_low, preferred_element_type=jnp.float32)
    shared_back = jnp.einsum(
        "tf,df->td", shared_gate_low, gate_shared, preferred_element_type=jnp.float32
    )
    shared_back = shared_back + jnp.einsum(
        "tf,df->td", shared_up_low, up_shared, preferred_element_type=jnp.float32
    )
    shared_grads_in = jnp.concatenate(
        [shared_gate_grad, shared_up_grad, shared_down_grad_t], 1
    ).astype(jnp.bfloat16)
    grad_seq_f = grad_seq.astype(jnp.float32)
    table_rows = experts * capacity
    feed_part, back_part, gate_cols = combine_rows(
        slot_index.reshape(seq_len, top_count),
        back_both.reshape(table_rows, 2 * tile_rows, 128),
        gate_values,
        grad_seq,
        shared_out,
        shared_back,
    )
    gate_part = gate_cols[:, :top_count]
    feed_own = jnp.sum(
        lax.all_to_all(
            feed_part.reshape(tensor_size, tok_dev, D), "tensor", split_axis=0, concat_axis=0, tiled=True
        ).astype(jnp.float32),
        0,
    )
    reduced_back = lax.psum(
        jnp.concatenate([back_part, gate_cols.astype(jnp.bfloat16)], 1), "tensor"
    ).astype(jnp.float32)
    normed_two_grad = reduced_back[:, :D]
    gate_grads = reduced_back[:, D : D + top_count]
    weighted_total = jnp.sum(gate_values * gate_grads, -1, keepdims=True)
    chosen_grads = gate_values * (gate_grads - weighted_total)
    logit_grads = jnp.sum(jnp.where(chosen_hot, chosen_grads[:, :, None], 0.0), 1)
    normed_two_grad = normed_two_grad + jnp.dot(
        logit_grads, router_weights.astype(jnp.float32).T, precision=HIGH
    )
    residual_grad = grad_seq_f + norm_back(residual_all, scale_two, gain_two, normed_two_grad)
    branch_grad = residual_grad.astype(jnp.bfloat16)
    shared_grads_in, branch_grad = lax.optimization_barrier((shared_grads_in, branch_grad))
    shared_pack = jnp.sum(
        lax.all_to_all(
            shared_grads_in.reshape(dp_size, rows_dp, shared_grads_in.shape[1]),
            "dp",
            split_axis=0,
            concat_axis=0,
            tiled=True,
        ).astype(jnp.float32),
        0,
    )
    output_grad_w_t = jnp.dot(branch_grad.T, mixed_all, preferred_element_type=jnp.float32)
    mixed_grad = (
        jnp.dot(branch_grad, output_weights_t, preferred_element_type=jnp.float32)
        .astype(jnp.bfloat16)
        .reshape(seq_len, head_count, DV)
    )
    keys_nope_grad = jnp.zeros((seq_len, head_count, DN), jnp.float32)
    key_rope_grad = jnp.zeros((seq_len, DR), jnp.float32)
    values_grad = jnp.zeros((seq_len, head_count, DV), jnp.float32)
    query_grad_list = []
    for block_index, rows_start in enumerate(range(0, seq_len, block_rows)):
        query_block = query_low[rows_start : rows_start + block_rows]
        masked = block_scores(query_block, keys_nope, key_rope, rows_start, prefix_len, score_scale)
        prob_full = jnp.exp(masked - lse_list[block_index])
        prob_low = prob_full.astype(jnp.bfloat16)
        mixed_block = mixed_grad[rows_start : rows_start + block_rows]
        prob_grads = jnp.einsum(
            "qhv,khv->hqk", mixed_block, values_low, preferred_element_type=jnp.float32
        )
        row_delta = jnp.sum(prob_full * prob_grads, -1, keepdims=True)
        score_grads = (prob_full * (prob_grads - row_delta)).astype(jnp.bfloat16)
        query_nope_grad = (
            jnp.einsum("hqk,khd->qhd", score_grads, keys_nope, preferred_element_type=jnp.float32)
            * score_scale
        )
        query_rope_grad = (
            jnp.einsum("hqk,kr->qhr", score_grads, key_rope, preferred_element_type=jnp.float32)
            * score_scale
        )
        keys_nope_grad = (
            keys_nope_grad
            + jnp.einsum(
                "hqk,qhd->khd",
                score_grads,
                query_block[..., :DN],
                preferred_element_type=jnp.float32,
            )
            * score_scale
        )
        key_rope_grad = (
            key_rope_grad
            + jnp.einsum(
                "hqk,qhr->kr",
                score_grads,
                query_block[..., DN:],
                preferred_element_type=jnp.float32,
            )
            * score_scale
        )
        values_grad = values_grad + jnp.einsum(
            "hqk,qhv->khv", prob_low, mixed_block, preferred_element_type=jnp.float32
        )
        block_cosines = all_cosines[rows_start : rows_start + block_rows, None, :]
        block_sines = all_sines[rows_start : rows_start + block_rows, None, :]
        query_grad_list.append(
            jnp.concatenate(
                [
                    query_nope_grad,
                    rotate_back(round_trip(query_rope_grad), block_cosines, block_sines),
                ],
                -1,
            ).astype(jnp.bfloat16)
        )
    query_grads = jnp.concatenate(query_grad_list, 0).reshape(seq_len, head_count * (DN + DR))
    feed_own, shared_pack, query_grads = lax.optimization_barrier((feed_own, shared_pack, query_grads))
    output = (residual_own + feed_own).astype(jnp.bfloat16)
    query_grad_w = jnp.dot(normed_all.T, query_grads, preferred_element_type=jnp.float32)
    normed_grad_part = jnp.dot(query_grads, query_weights.T, preferred_element_type=jnp.float32)
    expand_grads = jnp.concatenate(
        [keys_nope_grad.astype(jnp.bfloat16), values_grad.astype(jnp.bfloat16)], -1
    ).reshape(seq_len, head_count * (DN + DV))
    expand_grad_w = jnp.dot(compressed_seq.T, expand_grads, preferred_element_type=jnp.float32)
    compressed_grad_part = jnp.dot(
        expand_grads, expand_weights.T, preferred_element_type=jnp.float32
    )
    latent_grad_part = jnp.concatenate([compressed_grad_part, key_rope_grad], -1)
    attn_grads_in = jnp.concatenate(
        [
            query_grad_w,
            output_grad_w_t,
            expand_grad_w.reshape(dp_size * rows_dp, expand_flat_cols),
        ],
        1,
    )
    token_all = lax.psum(
        jnp.concatenate([normed_grad_part, latent_grad_part], 1).astype(jnp.bfloat16), "tensor"
    ).astype(jnp.float32)
    compressed_grad_all = token_all[:, D : D + KVR]
    kv_gain_full = jnp.sum(compressed_grad_all * compressed_all * scale_kv_all, 0)
    raw_grad_all = jnp.concatenate(
        [
            norm_back(compressed_all, scale_kv_all, gain_kv, compressed_grad_all),
            rotate_back(token_all[:, D + KVR :], all_cosines, all_sines),
        ],
        -1,
    ).astype(jnp.bfloat16)
    normed_grad_all = token_all[:, :D] + jnp.dot(
        raw_grad_all, latent_weights.T, preferred_element_type=jnp.float32
    )
    normed_grad = lax.dynamic_slice_in_dim(normed_grad_all, start_row, tok_dev, 0)
    hidden_grad = lax.dynamic_slice_in_dim(residual_grad, start_row, tok_dev, 0) + norm_back(
        hidden_f, scale_one, gain_one, normed_grad
    )
    row_per = D // (dp_size * tensor_size)

    def own_rows(values):
        split = values.reshape(values.shape[0], dp_size, tensor_size, row_per)
        return lax.dynamic_slice_in_dim(split, tensor_rank, 1, 2).reshape(values.shape[0], -1)

    latent_rows = jnp.dot(own_rows(normed_all).T, raw_grad_all, preferred_element_type=jnp.float32)
    attn_gain_rows = jnp.sum(
        own_rows(normed_grad_all) * own_rows(hidden_all_f) * scale_one_all, 0
    )
    second_gain_rows = jnp.sum(
        own_rows(normed_two_grad) * own_rows(residual_all) * scale_two, 0
    )
    router_rows = jnp.dot(
        own_rows(normed_two).astype(jnp.float32).T, logit_grads, precision=HIGH
    )
    kv_per = kv_gain_full.shape[0] // (dp_size * tensor_size)
    kv_rows_own = lax.dynamic_slice_in_dim(
        kv_gain_full.reshape(dp_size, tensor_size, kv_per), tensor_rank, 1, 1
    ).reshape(dp_size, kv_per)
    kv_column = jnp.pad(kv_rows_own, ((0, 0), (0, row_per - kv_per))).reshape(-1)
    small_pack = jnp.concatenate(
        [
            latent_rows,
            router_rows,
            attn_gain_rows[:, None],
            second_gain_rows[:, None],
            kv_column[:, None],
        ],
        1,
    )
    attn_width = attn_grads_in.shape[1]
    small_width = small_pack.shape[1]
    small_count = row_per * small_width
    small_cols = -(-small_count // rows_dp)
    small_flat = jnp.pad(
        small_pack.reshape(dp_size, small_count), ((0, 0), (0, small_cols * rows_dp - small_count))
    ).reshape(dp_size * rows_dp, small_cols)
    merged_own = lax.psum_scatter(
        jnp.concatenate([attn_grads_in, small_flat], 1), "dp", scatter_dimension=0, tiled=True
    )
    attn_pack = merged_own[:, :attn_width]
    small_own = merged_own[:, attn_width:].reshape(-1)[:small_count].reshape(row_per, small_width)
    cut = [0]
    for width in (latent_cols, experts, 1, 1, 1):
        cut.append(cut[-1] + width)
    latent_proj_grad = small_own[:, cut[0] : cut[1]]
    router_out = small_own[:, cut[1] : cut[2]]
    attn_gain_out = small_own[:, cut[2]]
    second_gain_out = small_own[:, cut[3]]
    latent_gain_out = small_own[:kv_per, cut[4]]
    cut = [0]
    for width in (head_cols, out_cols, expand_flat_cols):
        cut.append(cut[-1] + width)
    query_proj_grad = attn_pack[:, cut[0] : cut[1]]
    output_proj_grad = attn_pack[:, cut[1] : cut[2]].T
    expand_proj_grad = attn_pack[:, cut[2] : cut[3]].reshape(kv_rows, expand_cols)
    shared_gate_out = shared_pack[:, :shared_cols]
    shared_up_out = shared_pack[:, shared_cols : 2 * shared_cols]
    shared_down_out = shared_pack[:, 2 * shared_cols :].T
    return (
        output,
        hidden_grad,
        attn_gain_out,
        query_proj_grad,
        latent_proj_grad,
        latent_gain_out,
        expand_proj_grad,
        output_proj_grad,
        second_gain_out,
        router_out,
        expert_gate_grad,
        expert_up_grad,
        expert_down_grad,
        shared_gate_out,
        shared_up_out,
        shared_down_out,
    )


def solution(mesh):
    return jax.shard_map(
        shards,
        mesh=mesh,
        in_specs=(
            P(("dp", "tensor"), None),
            P("dp", None),
            P("dp"),
            P("dp"),
            P("dp", "tensor"),
            P("dp", None),
            P("dp"),
            P("dp", "tensor"),
            P("tensor", "dp"),
            P("dp"),
            P("dp", None),
            P("dp", "tensor", None),
            P("dp", "tensor", None),
            P("dp", "tensor", None),
            P("dp", "tensor"),
            P("dp", "tensor"),
            P("tensor", "dp"),
            P(("dp", "tensor"), None),
        ),
        out_specs=(
            P(("dp", "tensor"), None),
            P(("dp", "tensor"), None),
            P(("dp", "tensor")),
            P("dp", "tensor"),
            P(("dp", "tensor"), None),
            P(("dp", "tensor")),
            P("dp", "tensor"),
            P("tensor", "dp"),
            P(("dp", "tensor")),
            P(("dp", "tensor"), None),
            P("dp", "tensor", None),
            P("dp", "tensor", None),
            P("dp", "tensor", None),
            P("dp", "tensor"),
            P("dp", "tensor"),
            P("tensor", "dp"),
        ),
        check_vma=False,
    )
```

```python
import math

import jax
import jax.numpy as jnp
from jax import lax
from jax.experimental import pallas as pl
from jax.experimental.pallas import tpu as pltpu
from jax.sharding import PartitionSpec as P

D = 2048
DN = 128
DR = 64
DV = 128
KVR = 512


EPS = 1e-06
HIGH = lax.Precision.HIGHEST
MASKED = -1e30


def norm_scale(values):
    return lax.rsqrt(jnp.mean(values * values, -1, keepdims=True) + EPS)


def norm_back(values, scales, gains, upstream):
    weighted = gains * upstream
    return scales * weighted - values * scales**3 * jnp.mean(values * weighted, -1, keepdims=True)


def rope_tables(positions, rope_width):
    half_width = rope_width // 2
    frequency = 10000.0 ** (-2.0 * jnp.arange(half_width).astype(jnp.float32) / rope_width)
    angles = positions.astype(jnp.float32)[:, None] * frequency[None, :]
    return (jnp.cos(angles), jnp.sin(angles))


def rotate(vectors, cosines, sine_values):
    half_width = vectors.shape[-1] // 2
    front_half = vectors[..., :half_width]
    back_half = vectors[..., half_width:]
    return jnp.concatenate(
        [
            front_half * cosines - back_half * sine_values,
            back_half * cosines + front_half * sine_values,
        ],
        -1,
    )


def rotate_back(gradients, cosines, sine_values):
    half_width = gradients.shape[-1] // 2
    front_half = gradients[..., :half_width]
    back_half = gradients[..., half_width:]
    return jnp.concatenate(
        [
            front_half * cosines + back_half * sine_values,
            back_half * cosines - front_half * sine_values,
        ],
        -1,
    )


def round_trip(values):
    return lax.optimization_barrier(values.astype(jnp.bfloat16)).astype(jnp.float32)


def block_scores(query_block, keys_nope, key_rope, rows_start, prefix_len, score_scale):
    raw_scores = jnp.einsum(
        "qhd,khd->hqk", query_block[..., :DN], keys_nope, preferred_element_type=jnp.float32
    )
    raw_scores = raw_scores + jnp.einsum(
        "qhr,kr->hqk", query_block[..., DN:], key_rope, preferred_element_type=jnp.float32
    )
    query_places = rows_start + jnp.arange(query_block.shape[0])
    key_places = jnp.arange(keys_nope.shape[0])
    visible = (key_places[None, :] <= query_places[:, None]) | (key_places[None, :] < prefix_len)
    return jnp.where(visible[None], raw_scores * score_scale, MASKED)


def silu_back(act_grad, gate_pre, up_pre, sigmoid_gate):
    up_grad = (act_grad * gate_pre * sigmoid_gate).astype(jnp.bfloat16)
    gate_grad = (act_grad * up_pre * sigmoid_gate * (1.0 + gate_pre * (1.0 - sigmoid_gate))).astype(
        jnp.bfloat16
    )
    return (gate_grad, up_grad)


def dispatch_kernel(tok_ref, both_hbm, col_ref, out_ref, both_buf, sems):
    block = both_buf.shape[0]
    tile_rows = both_buf.shape[1] // 2
    last = both_hbm.shape[0] - 1
    base = pl.program_id(0) * block

    def start(r, carry):
        tok = jnp.minimum(tok_ref[base + r], last)
        pltpu.make_async_copy(both_hbm.at[tok], both_buf.at[r], sems.at[r]).start()
        return carry

    lax.fori_loop(0, block, start, 0, unroll=4)

    def finish(r, carry):
        pltpu.make_async_copy(both_hbm.at[0], both_buf.at[r], sems.at[r]).wait()
        return carry

    lax.fori_loop(0, block, finish, 0, unroll=4)
    rows = both_buf[:, :tile_rows, :]
    out_ref[:, :tile_rows, :] = jnp.where(col_ref[0] > 0, rows, jnp.zeros_like(rows))
    out_ref[:, tile_rows:, :] = (
        both_buf[:, tile_rows:, :].astype(jnp.float32) * col_ref[1]
    ).astype(out_ref.dtype)


def dispatch_rows(slot_token, rows, grads, valid, gate, block=128):
    slots = slot_token.shape[0]
    count, width = rows.shape
    tile_rows = width // 128
    cols = jnp.broadcast_to(jnp.stack([valid, gate])[:, :, None, None], (2, slots, 1, 128))
    both = jnp.concatenate([rows, grads], 1).reshape(count, 2 * tile_rows, 128)
    out = pl.pallas_call(
        dispatch_kernel,
        out_shape=jax.ShapeDtypeStruct((slots, 2 * tile_rows, 128), rows.dtype),
        grid_spec=pltpu.PrefetchScalarGridSpec(
            num_scalar_prefetch=1,
            grid=(slots // block,),
            in_specs=[
                pl.BlockSpec(memory_space=pl.ANY),
                pl.BlockSpec((2, block, 1, 128), lambda i, tok: (0, i, 0, 0)),
            ],
            out_specs=pl.BlockSpec((block, 2 * tile_rows, 128), lambda i, tok: (i, 0, 0)),
            scratch_shapes=[
                pltpu.VMEM((block, 2 * tile_rows, 128), rows.dtype),
                pltpu.SemaphoreType.DMA((block,)),
            ],
        ),
        cost_estimate=pl.CostEstimate(
            flops=slots * width, transcendentals=0, bytes_accessed=4 * slots * 2 * width
        ),
    )(slot_token, both, cols)
    return out


def combine_kernel(
    slot_ref, out_hbm, back_hbm, gate_ref, grad_ref, shared_out_ref, shared_back_ref,
    feed_ref, back_ref, part_ref, picked_out, picked_back, sems,
):
    top = picked_out.shape[0]
    block = picked_out.shape[1]
    last = out_hbm.shape[0] - 1
    base = pl.program_id(0) * block

    def start(r, carry):
        for k in range(top):
            slot = jnp.clip(slot_ref[(base + r) * top + k], 0, last)
            pltpu.make_async_copy(out_hbm.at[slot], picked_out.at[k, r], sems.at[0, k, r]).start()
            pltpu.make_async_copy(back_hbm.at[slot], picked_back.at[k, r], sems.at[1, k, r]).start()
        return carry

    lax.fori_loop(0, block, start, 0, unroll=2)

    def finish(r, carry):
        for k in range(top):
            pltpu.make_async_copy(out_hbm.at[0], picked_out.at[k, r], sems.at[0, k, r]).wait()
            pltpu.make_async_copy(back_hbm.at[0], picked_back.at[k, r], sems.at[1, k, r]).wait()
        return carry

    lax.fori_loop(0, block, finish, 0, unroll=2)
    grad = grad_ref[...].astype(jnp.float32)
    weighted = None
    backs = None
    lanes = lax.broadcasted_iota(jnp.int32, part_ref.shape, 2)
    parts = jnp.zeros(part_ref.shape, jnp.float32)
    for k in range(top):
        out_k = picked_out[k].astype(jnp.float32)
        term = gate_ref[k] * out_k
        weighted = term if weighted is None else weighted + term
        back_k = picked_back[k].astype(jnp.float32)
        backs = back_k if backs is None else backs + back_k
        dot_k = jnp.sum(jnp.sum(grad * out_k, 2, keepdims=True), 1, keepdims=True)
        parts = jnp.where(lanes == k, dot_k, parts)
    feed_ref[...] = (shared_out_ref[...] + weighted).astype(feed_ref.dtype)
    back_ref[...] = (backs + shared_back_ref[...]).astype(back_ref.dtype)
    part_ref[...] = parts


def combine_rows(slot_index, out_table, back_table, gate_values, grad, shared_out, shared_back, block=128):
    tokens, top = gate_values.shape
    width = grad.shape[1]
    tile_rows = width // 128
    gates = jnp.broadcast_to(gate_values.T[:, :, None, None], (top, tokens, 1, 128))
    row_spec = pl.BlockSpec((block, tile_rows, 128), lambda i, s: (i, 0, 0))
    feed, back, parts = pl.pallas_call(
        combine_kernel,
        out_shape=(
            jax.ShapeDtypeStruct((tokens, tile_rows, 128), jnp.bfloat16),
            jax.ShapeDtypeStruct((tokens, tile_rows, 128), jnp.bfloat16),
            jax.ShapeDtypeStruct((tokens, 1, 128), jnp.float32),
        ),
        grid_spec=pltpu.PrefetchScalarGridSpec(
            num_scalar_prefetch=1,
            grid=(tokens // block,),
            in_specs=[
                pl.BlockSpec(memory_space=pl.ANY),
                pl.BlockSpec(memory_space=pl.ANY),
                pl.BlockSpec((top, block, 1, 128), lambda i, s: (0, i, 0, 0)),
                row_spec,
                row_spec,
                row_spec,
            ],
            out_specs=[row_spec, row_spec, pl.BlockSpec((block, 1, 128), lambda i, s: (i, 0, 0))],
            scratch_shapes=[
                pltpu.VMEM((top, block, tile_rows, 128), out_table.dtype),
                pltpu.VMEM((top, block, tile_rows, 128), back_table.dtype),
                pltpu.SemaphoreType.DMA((2, top, block)),
            ],
        ),
        cost_estimate=pl.CostEstimate(
            flops=8 * tokens * top * width,
            transcendentals=0,
            bytes_accessed=tokens * (top * 4 * width + 2 * width + 8 * width + 4 * width),
        ),
    )(
        slot_index.reshape(-1),
        out_table,
        back_table,
        gates,
        grad.reshape(tokens, tile_rows, 128),
        shared_out.reshape(tokens, tile_rows, 128),
        shared_back.reshape(tokens, tile_rows, 128),
    )
    return feed.reshape(tokens, width), back.reshape(tokens, width), parts[:, 0, :top]


def shards(
    hidden,
    routes,
    prefix,
    attn_gain,
    query_proj,
    latent_proj,
    latent_gain,
    expand_proj,
    output_proj,
    second_gain,
    router_proj,
    expert_gate,
    expert_up,
    expert_down,
    shared_gate,
    shared_up,
    shared_down,
    out_grad,
):
    tok_dev = hidden.shape[0]
    tensor_size = lax.axis_size("tensor")
    tensor_rank = lax.axis_index("tensor")
    dp_size = lax.axis_size("dp")
    seq_len = tok_dev * tensor_size
    start_row = tensor_rank * tok_dev
    rows_dp = attn_gain.shape[0]
    kv_rows = latent_gain.shape[0]
    head_cols = query_proj.shape[1]
    latent_cols = latent_proj.shape[1]
    expand_cols = expand_proj.shape[1]
    expand_flat_cols = kv_rows * expand_cols // rows_dp
    first_pack = jnp.concatenate(
        [
            query_proj,
            latent_proj,
            expand_proj.reshape(rows_dp, expand_flat_cols),
            attn_gain[:, None],
            jnp.pad(latent_gain, (0, rows_dp - kv_rows))[:, None],
        ],
        1,
    )
    first_all = lax.all_gather(first_pack, "dp", axis=0, tiled=True)
    cut = [0]
    for width in (head_cols, latent_cols, expand_flat_cols, 1, 1):
        cut.append(cut[-1] + width)
    query_weights = first_all[:, cut[0] : cut[1]]
    latent_weights = first_all[:, cut[1] : cut[2]]
    expand_weights = first_all[:, cut[2] : cut[3]].reshape(dp_size * kv_rows, expand_cols)
    attn_gains = first_all[:, cut[3]]
    kv_gains = first_all[:, cut[4]].reshape(dp_size, rows_dp)[:, :kv_rows].reshape(-1)
    out_cols = output_proj.shape[0]
    experts = router_proj.shape[1]
    shared_cols = shared_gate.shape[1]
    second_pack = jnp.concatenate([output_proj.T, second_gain[:, None], router_proj], 1)
    second_all = lax.all_gather(second_pack, "dp", axis=0, tiled=True)
    output_weights_t = second_all[:, :out_cols]
    second_gains = second_all[:, out_cols]
    router_weights = second_all[:, out_cols + 1 :]
    shared_local = jnp.concatenate([shared_gate, shared_up, shared_down.T], 1)

    hidden_all = lax.all_gather(hidden, "tensor", axis=0, tiled=True)
    grad_seq = lax.all_to_all(
        jnp.broadcast_to(out_grad[None], (tensor_size,) + out_grad.shape),
        "tensor",
        split_axis=0,
        concat_axis=0,
        tiled=True,
    ).reshape(tensor_size * tok_dev, D)
    grad_seq, hidden_all = lax.optimization_barrier((grad_seq, hidden_all))
    hidden_all_f = hidden_all.astype(jnp.float32)
    scale_one_all = norm_scale(hidden_all_f)
    gain_one = attn_gains.astype(jnp.float32)
    normed_all = (hidden_all_f * scale_one_all * gain_one).astype(jnp.bfloat16)
    hidden_f = lax.dynamic_slice_in_dim(hidden_all_f, start_row, tok_dev, 0)
    scale_one = lax.dynamic_slice_in_dim(scale_one_all, start_row, tok_dev, 0)
    normed_own = lax.dynamic_slice_in_dim(normed_all, start_row, tok_dev, 0)
    latent_raw_all = jnp.dot(normed_all, latent_weights, preferred_element_type=jnp.float32)
    compressed_all = latent_raw_all[:, :KVR]
    scale_kv_all = norm_scale(compressed_all)
    gain_kv = kv_gains.astype(jnp.float32)
    all_cosines, all_sines = rope_tables(jnp.arange(seq_len), DR)
    latent_seq = jnp.concatenate(
        [
            compressed_all * scale_kv_all * gain_kv,
            rotate(latent_raw_all[:, KVR:], all_cosines, all_sines),
        ],
        -1,
    ).astype(jnp.bfloat16)
    compressed = lax.dynamic_slice_in_dim(compressed_all, start_row, tok_dev, 0)
    scale_kv = lax.dynamic_slice_in_dim(scale_kv_all, start_row, tok_dev, 0)
    own_cosines = lax.dynamic_slice_in_dim(all_cosines, start_row, tok_dev, 0)
    own_sines = lax.dynamic_slice_in_dim(all_sines, start_row, tok_dev, 0)
    head_count = query_weights.shape[1] // (DN + DR)
    query_raw = jnp.dot(normed_all, query_weights, preferred_element_type=jnp.float32).reshape(
        seq_len, head_count, DN + DR
    )
    query_low = jnp.concatenate(
        [
            query_raw[..., :DN],
            rotate(query_raw[..., DN:], all_cosines[:, None, :], all_sines[:, None, :]),
        ],
        -1,
    ).astype(jnp.bfloat16)
    compressed_seq = latent_seq[:, :KVR]
    key_rope = latent_seq[:, KVR:]
    expanded = jnp.dot(compressed_seq, expand_weights, preferred_element_type=jnp.float32).reshape(
        seq_len, head_count, DN + DV
    )
    keys_nope = expanded[..., :DN].astype(jnp.bfloat16)
    values_low = expanded[..., DN:].astype(jnp.bfloat16)
    score_scale = 1.0 / math.sqrt(DN + DR)
    block_rows = min(512, seq_len)
    prefix_len = prefix[0]
    lse_list = []
    mixed_list = []
    for rows_start in range(0, seq_len, block_rows):
        query_block = query_low[rows_start : rows_start + block_rows]
        masked = block_scores(query_block, keys_nope, key_rope, rows_start, prefix_len, score_scale)
        top_score = jnp.max(masked, -1, keepdims=True)
        exp_scores = jnp.exp(masked - top_score)
        totals = jnp.sum(exp_scores, -1, keepdims=True)
        prob_low = (exp_scores / totals).astype(jnp.bfloat16)
        lse_list.append(top_score + jnp.log(totals))
        mixed_list.append(
            jnp.einsum(
                "hqk,khv->qhv", prob_low, values_low, preferred_element_type=jnp.float32
            ).astype(jnp.bfloat16)
        )
    mixed_all = jnp.concatenate(mixed_list, 0).reshape(seq_len, head_count * DV)
    attn_part = jnp.einsum(
        "tk,dk->td", mixed_all, output_weights_t, preferred_element_type=jnp.float32
    )
    branch_all = lax.psum(attn_part.astype(jnp.bfloat16), "tensor").astype(jnp.float32)
    shared_local, branch_all = lax.optimization_barrier((shared_local, branch_all))
    residual_all = hidden_all_f + branch_all
    residual_own = lax.dynamic_slice_in_dim(residual_all, start_row, tok_dev, 0)
    scale_two = norm_scale(residual_all)
    gain_two = second_gains.astype(jnp.float32)
    normed_two = (residual_all * scale_two * gain_two).astype(jnp.bfloat16)
    logits = jnp.dot(normed_two, router_weights, preferred_element_type=jnp.float32)
    top_count = routes.shape[1]
    chosen_hot = routes[:, :, None] == jnp.arange(experts)[None, None, :]
    chosen_logits = jnp.sum(jnp.where(chosen_hot, logits[:, None, :], 0.0), -1)
    gate_values = jax.nn.softmax(chosen_logits, axis=-1)
    assignments = seq_len * top_count
    flat_hot = chosen_hot.reshape(assignments, experts).astype(jnp.bfloat16)
    lower = (jnp.arange(assignments)[:, None] > jnp.arange(assignments)[None, :]).astype(jnp.bfloat16)
    earlier = jnp.dot(lower, flat_hot, preferred_element_type=jnp.float32)
    slot_pos = jnp.sum(earlier * flat_hot.astype(jnp.float32), -1).astype(jnp.int32)
    expert_ids = routes.reshape(-1)
    exp_dev = expert_gate.shape[0]
    capacity = tensor_size * (5 * seq_len * top_count // (4 * experts * tensor_size))
    slot_index = expert_ids * capacity + slot_pos
    token_ids = jnp.arange(seq_len * top_count) // top_count
    slot_token = jnp.full((experts * capacity,), seq_len, jnp.int32).at[slot_index].set(token_ids)
    slot_gate = (
        jnp.zeros((experts * capacity,), jnp.float32).at[slot_index].set(gate_values.reshape(-1))
    )
    slot_valid = (slot_token < seq_len).astype(jnp.float32)
    tile_rows = D // 128
    send_both = dispatch_rows(slot_token, normed_two, grad_seq, slot_valid, slot_gate).reshape(
        dp_size, exp_dev, capacity, 2 * tile_rows, 128
    )
    shared_all = lax.all_gather(shared_local, "dp", axis=0, tiled=True)
    shared_all, send_both = lax.optimization_barrier((shared_all, send_both))
    gate_shared = shared_all[:, :shared_cols]
    up_shared = shared_all[:, shared_cols : 2 * shared_cols]
    down_shared_t = shared_all[:, 2 * shared_cols :]
    recv_both = lax.all_to_all(send_both, "dp", split_axis=0, concat_axis=0, tiled=True)
    recv_both = recv_both.reshape(dp_size, exp_dev, capacity, 2 * D)
    recv_rows = recv_both[..., :D]
    recv_grads = recv_both[..., D:]
    gate_pre = jnp.einsum(
        "sjcd,jfd->sjcf", recv_rows, expert_gate, preferred_element_type=jnp.float32
    )
    up_pre = jnp.einsum("sjcd,jfd->sjcf", recv_rows, expert_up, preferred_element_type=jnp.float32)
    sigmoid_gate = jax.nn.sigmoid(gate_pre)
    expert_act = (gate_pre * sigmoid_gate * up_pre).astype(jnp.bfloat16)
    expert_out = jnp.einsum(
        "sjcf,jfd->sjcd", expert_act, expert_down, preferred_element_type=jnp.float32
    )
    back_out = lax.all_to_all(
        expert_out.astype(jnp.bfloat16).reshape(dp_size, exp_dev, capacity, tile_rows, 128),
        "dp",
        split_axis=0,
        concat_axis=0,
        tiled=True,
    )
    act_grad = jnp.einsum(
        "sjcd,jfd->sjcf", recv_grads, expert_down, preferred_element_type=jnp.float32
    )
    gate_low_grad, up_low_grad = silu_back(act_grad, gate_pre, up_pre, sigmoid_gate)
    expert_down_grad = jnp.einsum(
        "sjcf,sjcd->jfd", expert_act, recv_grads, preferred_element_type=jnp.float32
    )
    expert_gate_grad = jnp.einsum(
        "sjcf,sjcd->jfd", gate_low_grad, recv_rows, preferred_element_type=jnp.float32
    )
    expert_up_grad = jnp.einsum(
        "sjcf,sjcd->jfd", up_low_grad, recv_rows, preferred_element_type=jnp.float32
    )
    row_grads = jnp.einsum(
        "sjcf,jfd->sjcd", gate_low_grad, expert_gate, preferred_element_type=jnp.float32
    )
    row_grads = row_grads + jnp.einsum(
        "sjcf,jfd->sjcd", up_low_grad, expert_up, preferred_element_type=jnp.float32
    )
    grads_low = row_grads.astype(jnp.bfloat16).reshape(dp_size, exp_dev, capacity, tile_rows, 128)
    back_out, grads_low = lax.optimization_barrier((back_out, grads_low))
    back_grads = lax.all_to_all(
        grads_low,
        "dp",
        split_axis=0,
        concat_axis=0,
        tiled=True,
    )
    shared_pre_gate = jnp.dot(normed_two, gate_shared, preferred_element_type=jnp.float32)
    shared_pre_up = jnp.dot(normed_two, up_shared, preferred_element_type=jnp.float32)
    shared_sigmoid = jax.nn.sigmoid(shared_pre_gate)
    shared_act = (shared_pre_gate * shared_sigmoid * shared_pre_up).astype(jnp.bfloat16)
    shared_out = jnp.einsum(
        "tf,df->td", shared_act, down_shared_t, preferred_element_type=jnp.float32
    )
    shared_act_grad = jnp.dot(grad_seq, down_shared_t, preferred_element_type=jnp.float32)
    shared_gate_low, shared_up_low = silu_back(
        shared_act_grad, shared_pre_gate, shared_pre_up, shared_sigmoid
    )
    shared_down_grad_t = jnp.dot(grad_seq.T, shared_act, preferred_element_type=jnp.float32)
    shared_gate_grad = jnp.dot(normed_two.T, shared_gate_low, preferred_element_type=jnp.float32)
    shared_up_grad = jnp.dot(normed_two.T, shared_up_low, preferred_element_type=jnp.float32)
    shared_back = jnp.einsum(
        "tf,df->td", shared_gate_low, gate_shared, preferred_element_type=jnp.float32
    )
    shared_back = shared_back + jnp.einsum(
        "tf,df->td", shared_up_low, up_shared, preferred_element_type=jnp.float32
    )
    shared_grads_in = jnp.concatenate(
        [shared_gate_grad, shared_up_grad, shared_down_grad_t], 1
    ).astype(jnp.bfloat16)
    grad_seq_f = grad_seq.astype(jnp.float32)
    table_rows = experts * capacity
    feed_part, back_part, gate_cols = combine_rows(
        slot_index.reshape(seq_len, top_count),
        back_out.reshape(table_rows, tile_rows, 128),
        back_grads.reshape(table_rows, tile_rows, 128),
        gate_values,
        grad_seq,
        shared_out,
        shared_back,
    )
    gate_part = gate_cols[:, :top_count]
    feed_own = jnp.sum(
        lax.all_to_all(
            feed_part.reshape(tensor_size, tok_dev, D), "tensor", split_axis=0, concat_axis=0, tiled=True
        ).astype(jnp.float32),
        0,
    )
    reduced_back = lax.psum(
        jnp.concatenate([back_part, gate_cols.astype(jnp.bfloat16)], 1), "tensor"
    ).astype(jnp.float32)
    normed_two_grad = reduced_back[:, :D]
    gate_grads = reduced_back[:, D : D + top_count]
    weighted_total = jnp.sum(gate_values * gate_grads, -1, keepdims=True)
    chosen_grads = gate_values * (gate_grads - weighted_total)
    logit_grads = jnp.sum(jnp.where(chosen_hot, chosen_grads[:, :, None], 0.0), 1)
    normed_two_grad = normed_two_grad + jnp.dot(
        logit_grads, router_weights.astype(jnp.float32).T, precision=HIGH
    )
    residual_grad = grad_seq_f + norm_back(residual_all, scale_two, gain_two, normed_two_grad)
    branch_grad = residual_grad.astype(jnp.bfloat16)
    shared_grads_in, branch_grad = lax.optimization_barrier((shared_grads_in, branch_grad))
    shared_pack = jnp.sum(
        lax.all_to_all(
            shared_grads_in.reshape(dp_size, rows_dp, shared_grads_in.shape[1]),
            "dp",
            split_axis=0,
            concat_axis=0,
            tiled=True,
        ).astype(jnp.float32),
        0,
    )
    output_grad_w_t = jnp.dot(branch_grad.T, mixed_all, preferred_element_type=jnp.float32)
    mixed_grad = (
        jnp.dot(branch_grad, output_weights_t, preferred_element_type=jnp.float32)
        .astype(jnp.bfloat16)
        .reshape(seq_len, head_count, DV)
    )
    keys_nope_grad = jnp.zeros((seq_len, head_count, DN), jnp.float32)
    key_rope_grad = jnp.zeros((seq_len, DR), jnp.float32)
    values_grad = jnp.zeros((seq_len, head_count, DV), jnp.float32)
    query_grad_list = []
    for block_index, rows_start in enumerate(range(0, seq_len, block_rows)):
        query_block = query_low[rows_start : rows_start + block_rows]
        masked = block_scores(query_block, keys_nope, key_rope, rows_start, prefix_len, score_scale)
        prob_full = jnp.exp(masked - lse_list[block_index])
        prob_low = prob_full.astype(jnp.bfloat16)
        mixed_block = mixed_grad[rows_start : rows_start + block_rows]
        prob_grads = jnp.einsum(
            "qhv,khv->hqk", mixed_block, values_low, preferred_element_type=jnp.float32
        )
        row_delta = jnp.sum(prob_full * prob_grads, -1, keepdims=True)
        score_grads = (prob_full * (prob_grads - row_delta)).astype(jnp.bfloat16)
        query_nope_grad = (
            jnp.einsum("hqk,khd->qhd", score_grads, keys_nope, preferred_element_type=jnp.float32)
            * score_scale
        )
        query_rope_grad = (
            jnp.einsum("hqk,kr->qhr", score_grads, key_rope, preferred_element_type=jnp.float32)
            * score_scale
        )
        keys_nope_grad = (
            keys_nope_grad
            + jnp.einsum(
                "hqk,qhd->khd",
                score_grads,
                query_block[..., :DN],
                preferred_element_type=jnp.float32,
            )
            * score_scale
        )
        key_rope_grad = (
            key_rope_grad
            + jnp.einsum(
                "hqk,qhr->kr",
                score_grads,
                query_block[..., DN:],
                preferred_element_type=jnp.float32,
            )
            * score_scale
        )
        values_grad = values_grad + jnp.einsum(
            "hqk,qhv->khv", prob_low, mixed_block, preferred_element_type=jnp.float32
        )
        block_cosines = all_cosines[rows_start : rows_start + block_rows, None, :]
        block_sines = all_sines[rows_start : rows_start + block_rows, None, :]
        query_grad_list.append(
            jnp.concatenate(
                [
                    query_nope_grad,
                    rotate_back(round_trip(query_rope_grad), block_cosines, block_sines),
                ],
                -1,
            ).astype(jnp.bfloat16)
        )
    query_grads = jnp.concatenate(query_grad_list, 0).reshape(seq_len, head_count * (DN + DR))
    feed_own, shared_pack, query_grads = lax.optimization_barrier((feed_own, shared_pack, query_grads))
    output = (residual_own + feed_own).astype(jnp.bfloat16)
    query_grad_w = jnp.dot(normed_all.T, query_grads, preferred_element_type=jnp.float32)
    normed_grad_part = jnp.dot(query_grads, query_weights.T, preferred_element_type=jnp.float32)
    expand_grads = jnp.concatenate(
        [keys_nope_grad.astype(jnp.bfloat16), values_grad.astype(jnp.bfloat16)], -1
    ).reshape(seq_len, head_count * (DN + DV))
    expand_grad_w = jnp.dot(compressed_seq.T, expand_grads, preferred_element_type=jnp.float32)
    compressed_grad_part = jnp.dot(
        expand_grads, expand_weights.T, preferred_element_type=jnp.float32
    )
    latent_grad_part = jnp.concatenate([compressed_grad_part, key_rope_grad], -1)
    attn_grads_in = jnp.concatenate(
        [
            query_grad_w,
            output_grad_w_t,
            expand_grad_w.reshape(dp_size * rows_dp, expand_flat_cols),
        ],
        1,
    )
    token_all = lax.psum(
        jnp.concatenate([normed_grad_part, latent_grad_part], 1).astype(jnp.bfloat16), "tensor"
    ).astype(jnp.float32)
    compressed_grad_all = token_all[:, D : D + KVR]
    kv_gain_full = jnp.sum(compressed_grad_all * compressed_all * scale_kv_all, 0)
    raw_grad_all = jnp.concatenate(
        [
            norm_back(compressed_all, scale_kv_all, gain_kv, compressed_grad_all),
            rotate_back(token_all[:, D + KVR :], all_cosines, all_sines),
        ],
        -1,
    ).astype(jnp.bfloat16)
    normed_grad_all = token_all[:, :D] + jnp.dot(
        raw_grad_all, latent_weights.T, preferred_element_type=jnp.float32
    )
    normed_grad = lax.dynamic_slice_in_dim(normed_grad_all, start_row, tok_dev, 0)
    hidden_grad = lax.dynamic_slice_in_dim(residual_grad, start_row, tok_dev, 0) + norm_back(
        hidden_f, scale_one, gain_one, normed_grad
    )
    row_per = D // (dp_size * tensor_size)

    def own_rows(values):
        split = values.reshape(values.shape[0], dp_size, tensor_size, row_per)
        return lax.dynamic_slice_in_dim(split, tensor_rank, 1, 2).reshape(values.shape[0], -1)

    latent_rows = jnp.dot(own_rows(normed_all).T, raw_grad_all, preferred_element_type=jnp.float32)
    attn_gain_rows = jnp.sum(
        own_rows(normed_grad_all) * own_rows(hidden_all_f) * scale_one_all, 0
    )
    second_gain_rows = jnp.sum(
        own_rows(normed_two_grad) * own_rows(residual_all) * scale_two, 0
    )
    router_rows = jnp.dot(
        own_rows(normed_two).astype(jnp.float32).T, logit_grads, precision=HIGH
    )
    kv_per = kv_gain_full.shape[0] // (dp_size * tensor_size)
    kv_rows_own = lax.dynamic_slice_in_dim(
        kv_gain_full.reshape(dp_size, tensor_size, kv_per), tensor_rank, 1, 1
    ).reshape(dp_size, kv_per)
    kv_column = jnp.pad(kv_rows_own, ((0, 0), (0, row_per - kv_per))).reshape(-1)
    small_pack = jnp.concatenate(
        [
            latent_rows,
            router_rows,
            attn_gain_rows[:, None],
            second_gain_rows[:, None],
            kv_column[:, None],
        ],
        1,
    )
    attn_width = attn_grads_in.shape[1]
    small_width = small_pack.shape[1]
    small_count = row_per * small_width
    small_cols = -(-small_count // rows_dp)
    small_flat = jnp.pad(
        small_pack.reshape(dp_size, small_count), ((0, 0), (0, small_cols * rows_dp - small_count))
    ).reshape(dp_size * rows_dp, small_cols)
    merged_own = lax.psum_scatter(
        jnp.concatenate([attn_grads_in, small_flat], 1), "dp", scatter_dimension=0, tiled=True
    )
    attn_pack = merged_own[:, :attn_width]
    small_own = merged_own[:, attn_width:].reshape(-1)[:small_count].reshape(row_per, small_width)
    cut = [0]
    for width in (latent_cols, experts, 1, 1, 1):
        cut.append(cut[-1] + width)
    latent_proj_grad = small_own[:, cut[0] : cut[1]]
    router_out = small_own[:, cut[1] : cut[2]]
    attn_gain_out = small_own[:, cut[2]]
    second_gain_out = small_own[:, cut[3]]
    latent_gain_out = small_own[:kv_per, cut[4]]
    cut = [0]
    for width in (head_cols, out_cols, expand_flat_cols):
        cut.append(cut[-1] + width)
    query_proj_grad = attn_pack[:, cut[0] : cut[1]]
    output_proj_grad = attn_pack[:, cut[1] : cut[2]].T
    expand_proj_grad = attn_pack[:, cut[2] : cut[3]].reshape(kv_rows, expand_cols)
    shared_gate_out = shared_pack[:, :shared_cols]
    shared_up_out = shared_pack[:, shared_cols : 2 * shared_cols]
    shared_down_out = shared_pack[:, 2 * shared_cols :].T
    return (
        output,
        hidden_grad,
        attn_gain_out,
        query_proj_grad,
        latent_proj_grad,
        latent_gain_out,
        expand_proj_grad,
        output_proj_grad,
        second_gain_out,
        router_out,
        expert_gate_grad,
        expert_up_grad,
        expert_down_grad,
        shared_gate_out,
        shared_up_out,
        shared_down_out,
    )


def solution(mesh):
    return jax.shard_map(
        shards,
        mesh=mesh,
        in_specs=(
            P(("dp", "tensor"), None),
            P("dp", None),
            P("dp"),
            P("dp"),
            P("dp", "tensor"),
            P("dp", None),
            P("dp"),
            P("dp", "tensor"),
            P("tensor", "dp"),
            P("dp"),
            P("dp", None),
            P("dp", "tensor", None),
            P("dp", "tensor", None),
            P("dp", "tensor", None),
            P("dp", "tensor"),
            P("dp", "tensor"),
            P("tensor", "dp"),
            P(("dp", "tensor"), None),
        ),
        out_specs=(
            P(("dp", "tensor"), None),
            P(("dp", "tensor"), None),
            P(("dp", "tensor")),
            P("dp", "tensor"),
            P(("dp", "tensor"), None),
            P(("dp", "tensor")),
            P("dp", "tensor"),
            P("tensor", "dp"),
            P(("dp", "tensor")),
            P(("dp", "tensor"), None),
            P("dp", "tensor", None),
            P("dp", "tensor", None),
            P("dp", "tensor", None),
            P("dp", "tensor"),
            P("dp", "tensor"),
            P("tensor", "dp"),
        ),
        check_vma=False,
    )
```

```python
import math

import jax
import jax.numpy as jnp
from jax import lax
from jax.experimental import pallas as pl
from jax.experimental.pallas import tpu as pltpu
from jax.sharding import PartitionSpec as P

D = 2048
DN = 128
DR = 64
DV = 128
KVR = 512


EPS = 1e-06
HIGH = lax.Precision.HIGHEST
MASKED = -1e30


def norm_scale(values):
    return lax.rsqrt(jnp.mean(values * values, -1, keepdims=True) + EPS)


def norm_back(values, scales, gains, upstream):
    weighted = gains * upstream
    return scales * weighted - values * scales**3 * jnp.mean(values * weighted, -1, keepdims=True)


def rope_tables(positions, rope_width):
    half_width = rope_width // 2
    frequency = 10000.0 ** (-2.0 * jnp.arange(half_width).astype(jnp.float32) / rope_width)
    angles = positions.astype(jnp.float32)[:, None] * frequency[None, :]
    return (jnp.cos(angles), jnp.sin(angles))


def rotate(vectors, cosines, sine_values):
    half_width = vectors.shape[-1] // 2
    front_half = vectors[..., :half_width]
    back_half = vectors[..., half_width:]
    return jnp.concatenate(
        [
            front_half * cosines - back_half * sine_values,
            back_half * cosines + front_half * sine_values,
        ],
        -1,
    )


def rotate_back(gradients, cosines, sine_values):
    half_width = gradients.shape[-1] // 2
    front_half = gradients[..., :half_width]
    back_half = gradients[..., half_width:]
    return jnp.concatenate(
        [
            front_half * cosines + back_half * sine_values,
            back_half * cosines - front_half * sine_values,
        ],
        -1,
    )


def round_trip(values):
    return lax.optimization_barrier(values.astype(jnp.bfloat16)).astype(jnp.float32)


def block_scores(query_block, keys_nope, key_rope, rows_start, prefix_len, score_scale):
    raw_scores = jnp.einsum(
        "qhd,khd->hqk", query_block[..., :DN], keys_nope, preferred_element_type=jnp.float32
    )
    raw_scores = raw_scores + jnp.einsum(
        "qhr,kr->hqk", query_block[..., DN:], key_rope, preferred_element_type=jnp.float32
    )
    query_places = rows_start + jnp.arange(query_block.shape[0])
    key_places = jnp.arange(keys_nope.shape[0])
    visible = (key_places[None, :] <= query_places[:, None]) | (key_places[None, :] < prefix_len)
    return jnp.where(visible[None], raw_scores * score_scale, MASKED)


def silu_back(act_grad, gate_pre, up_pre, sigmoid_gate):
    up_grad = (act_grad * gate_pre * sigmoid_gate).astype(jnp.bfloat16)
    gate_grad = (act_grad * up_pre * sigmoid_gate * (1.0 + gate_pre * (1.0 - sigmoid_gate))).astype(
        jnp.bfloat16
    )
    return (gate_grad, up_grad)


def dispatch_kernel(tok_ref, both_hbm, col_ref, out_ref, both_buf, sems):
    block = both_buf.shape[0]
    tile_rows = both_buf.shape[1] // 2
    last = both_hbm.shape[0] - 1
    base = pl.program_id(0) * block

    def start(r, carry):
        tok = jnp.minimum(tok_ref[base + r], last)
        pltpu.make_async_copy(both_hbm.at[tok], both_buf.at[r], sems.at[r]).start()
        return carry

    lax.fori_loop(0, block, start, 0, unroll=4)

    def finish(r, carry):
        pltpu.make_async_copy(both_hbm.at[0], both_buf.at[r], sems.at[r]).wait()
        return carry

    lax.fori_loop(0, block, finish, 0, unroll=4)
    rows = both_buf[:, :tile_rows, :]
    out_ref[:, :tile_rows, :] = jnp.where(col_ref[0] > 0, rows, jnp.zeros_like(rows))
    out_ref[:, tile_rows:, :] = (
        both_buf[:, tile_rows:, :].astype(jnp.float32) * col_ref[1]
    ).astype(out_ref.dtype)


def dispatch_rows(slot_token, rows, grads, valid, gate, block=128):
    slots = slot_token.shape[0]
    count, width = rows.shape
    tile_rows = width // 128
    cols = jnp.broadcast_to(jnp.stack([valid, gate])[:, :, None, None], (2, slots, 1, 128))
    both = jnp.concatenate([rows, grads], 1).reshape(count, 2 * tile_rows, 128)
    out = pl.pallas_call(
        dispatch_kernel,
        out_shape=jax.ShapeDtypeStruct((slots, 2 * tile_rows, 128), rows.dtype),
        grid_spec=pltpu.PrefetchScalarGridSpec(
            num_scalar_prefetch=1,
            grid=(slots // block,),
            in_specs=[
                pl.BlockSpec(memory_space=pl.ANY),
                pl.BlockSpec((2, block, 1, 128), lambda i, tok: (0, i, 0, 0)),
            ],
            out_specs=pl.BlockSpec((block, 2 * tile_rows, 128), lambda i, tok: (i, 0, 0)),
            scratch_shapes=[
                pltpu.VMEM((block, 2 * tile_rows, 128), rows.dtype),
                pltpu.SemaphoreType.DMA((block,)),
            ],
        ),
        cost_estimate=pl.CostEstimate(
            flops=slots * width, transcendentals=0, bytes_accessed=4 * slots * 2 * width
        ),
    )(slot_token, both, cols)
    return out


def combine_kernel(
    slot_ref, out_hbm, back_hbm, gate_ref, grad_ref, shared_out_ref, shared_back_ref,
    feed_ref, back_ref, part_ref, picked_out, picked_back, sems,
):
    top = picked_out.shape[0]
    block = picked_out.shape[1]
    last = out_hbm.shape[0] - 1
    base = pl.program_id(0) * block

    def start(r, carry):
        for k in range(top):
            slot = jnp.clip(slot_ref[(base + r) * top + k], 0, last)
            pltpu.make_async_copy(out_hbm.at[slot], picked_out.at[k, r], sems.at[0, k, r]).start()
            pltpu.make_async_copy(back_hbm.at[slot], picked_back.at[k, r], sems.at[1, k, r]).start()
        return carry

    lax.fori_loop(0, block, start, 0, unroll=2)

    def finish(r, carry):
        for k in range(top):
            pltpu.make_async_copy(out_hbm.at[0], picked_out.at[k, r], sems.at[0, k, r]).wait()
            pltpu.make_async_copy(back_hbm.at[0], picked_back.at[k, r], sems.at[1, k, r]).wait()
        return carry

    lax.fori_loop(0, block, finish, 0, unroll=2)
    grad = grad_ref[...].astype(jnp.float32)
    weighted = None
    backs = None
    lanes = lax.broadcasted_iota(jnp.int32, part_ref.shape, 2)
    parts = jnp.zeros(part_ref.shape, jnp.float32)
    for k in range(top):
        out_k = picked_out[k].astype(jnp.float32)
        term = gate_ref[k] * out_k
        weighted = term if weighted is None else weighted + term
        back_k = picked_back[k].astype(jnp.float32)
        backs = back_k if backs is None else backs + back_k
        dot_k = jnp.sum(jnp.sum(grad * out_k, 2, keepdims=True), 1, keepdims=True)
        parts = jnp.where(lanes == k, dot_k, parts)
    feed_ref[...] = (shared_out_ref[...] + weighted).astype(feed_ref.dtype)
    back_ref[...] = (backs + shared_back_ref[...]).astype(back_ref.dtype)
    part_ref[...] = parts


def combine_rows(slot_index, out_table, back_table, gate_values, grad, shared_out, shared_back, block=128):
    tokens, top = gate_values.shape
    width = grad.shape[1]
    tile_rows = width // 128
    gates = jnp.broadcast_to(gate_values.T[:, :, None, None], (top, tokens, 1, 128))
    row_spec = pl.BlockSpec((block, tile_rows, 128), lambda i, s: (i, 0, 0))
    feed, back, parts = pl.pallas_call(
        combine_kernel,
        out_shape=(
            jax.ShapeDtypeStruct((tokens, tile_rows, 128), jnp.bfloat16),
            jax.ShapeDtypeStruct((tokens, tile_rows, 128), jnp.bfloat16),
            jax.ShapeDtypeStruct((tokens, 1, 128), jnp.float32),
        ),
        grid_spec=pltpu.PrefetchScalarGridSpec(
            num_scalar_prefetch=1,
            grid=(tokens // block,),
            in_specs=[
                pl.BlockSpec(memory_space=pl.ANY),
                pl.BlockSpec(memory_space=pl.ANY),
                pl.BlockSpec((top, block, 1, 128), lambda i, s: (0, i, 0, 0)),
                row_spec,
                row_spec,
                row_spec,
            ],
            out_specs=[row_spec, row_spec, pl.BlockSpec((block, 1, 128), lambda i, s: (i, 0, 0))],
            scratch_shapes=[
                pltpu.VMEM((top, block, tile_rows, 128), out_table.dtype),
                pltpu.VMEM((top, block, tile_rows, 128), back_table.dtype),
                pltpu.SemaphoreType.DMA((2, top, block)),
            ],
        ),
        cost_estimate=pl.CostEstimate(
            flops=8 * tokens * top * width,
            transcendentals=0,
            bytes_accessed=tokens * (top * 4 * width + 2 * width + 8 * width + 4 * width),
        ),
    )(
        slot_index.reshape(-1),
        out_table,
        back_table,
        gates,
        grad.reshape(tokens, tile_rows, 128),
        shared_out.reshape(tokens, tile_rows, 128),
        shared_back.reshape(tokens, tile_rows, 128),
    )
    return feed.reshape(tokens, width), back.reshape(tokens, width), parts[:, 0, :top]


def shards(
    hidden,
    routes,
    prefix,
    attn_gain,
    query_proj,
    latent_proj,
    latent_gain,
    expand_proj,
    output_proj,
    second_gain,
    router_proj,
    expert_gate,
    expert_up,
    expert_down,
    shared_gate,
    shared_up,
    shared_down,
    out_grad,
):
    tok_dev = hidden.shape[0]
    tensor_size = lax.axis_size("tensor")
    tensor_rank = lax.axis_index("tensor")
    dp_size = lax.axis_size("dp")
    seq_len = tok_dev * tensor_size
    start_row = tensor_rank * tok_dev
    rows_dp = attn_gain.shape[0]
    kv_rows = latent_gain.shape[0]
    head_cols = query_proj.shape[1]
    latent_cols = latent_proj.shape[1]
    expand_cols = expand_proj.shape[1]
    expand_flat_cols = kv_rows * expand_cols // rows_dp
    first_pack = jnp.concatenate(
        [
            query_proj,
            latent_proj,
            expand_proj.reshape(rows_dp, expand_flat_cols),
            attn_gain[:, None],
            jnp.pad(latent_gain, (0, rows_dp - kv_rows))[:, None],
        ],
        1,
    )
    first_all = lax.all_gather(first_pack, "dp", axis=0, tiled=True)
    cut = [0]
    for width in (head_cols, latent_cols, expand_flat_cols, 1, 1):
        cut.append(cut[-1] + width)
    query_weights = first_all[:, cut[0] : cut[1]]
    latent_weights = first_all[:, cut[1] : cut[2]]
    expand_weights = first_all[:, cut[2] : cut[3]].reshape(dp_size * kv_rows, expand_cols)
    attn_gains = first_all[:, cut[3]]
    kv_gains = first_all[:, cut[4]].reshape(dp_size, rows_dp)[:, :kv_rows].reshape(-1)
    out_cols = output_proj.shape[0]
    experts = router_proj.shape[1]
    shared_cols = shared_gate.shape[1]
    second_pack = jnp.concatenate([output_proj.T, second_gain[:, None], router_proj], 1)
    second_all = lax.all_gather(second_pack, "dp", axis=0, tiled=True)
    output_weights_t = second_all[:, :out_cols]
    second_gains = second_all[:, out_cols]
    router_weights = second_all[:, out_cols + 1 :]
    shared_local = jnp.concatenate([shared_gate, shared_up, shared_down.T], 1)

    hidden_all = lax.all_gather(hidden, "tensor", axis=0, tiled=True)
    grad_blocks = jnp.broadcast_to(out_grad[None], (tensor_size,) + out_grad.shape)
    grad_blocks, hidden_all = lax.optimization_barrier((grad_blocks, hidden_all))
    grad_seq = lax.all_to_all(
        grad_blocks, "tensor", split_axis=0, concat_axis=0, tiled=True
    ).reshape(tensor_size * tok_dev, D)
    hidden_all_f = hidden_all.astype(jnp.float32)
    scale_one_all = norm_scale(hidden_all_f)
    gain_one = attn_gains.astype(jnp.float32)
    normed_all = (hidden_all_f * scale_one_all * gain_one).astype(jnp.bfloat16)
    hidden_f = lax.dynamic_slice_in_dim(hidden_all_f, start_row, tok_dev, 0)
    scale_one = lax.dynamic_slice_in_dim(scale_one_all, start_row, tok_dev, 0)
    normed_own = lax.dynamic_slice_in_dim(normed_all, start_row, tok_dev, 0)
    latent_raw_all = jnp.dot(normed_all, latent_weights, preferred_element_type=jnp.float32)
    compressed_all = latent_raw_all[:, :KVR]
    scale_kv_all = norm_scale(compressed_all)
    gain_kv = kv_gains.astype(jnp.float32)
    all_cosines, all_sines = rope_tables(jnp.arange(seq_len), DR)
    latent_seq = jnp.concatenate(
        [
            compressed_all * scale_kv_all * gain_kv,
            rotate(latent_raw_all[:, KVR:], all_cosines, all_sines),
        ],
        -1,
    ).astype(jnp.bfloat16)
    compressed = lax.dynamic_slice_in_dim(compressed_all, start_row, tok_dev, 0)
    scale_kv = lax.dynamic_slice_in_dim(scale_kv_all, start_row, tok_dev, 0)
    own_cosines = lax.dynamic_slice_in_dim(all_cosines, start_row, tok_dev, 0)
    own_sines = lax.dynamic_slice_in_dim(all_sines, start_row, tok_dev, 0)
    head_count = query_weights.shape[1] // (DN + DR)
    query_raw = jnp.dot(normed_all, query_weights, preferred_element_type=jnp.float32).reshape(
        seq_len, head_count, DN + DR
    )
    query_low = jnp.concatenate(
        [
            query_raw[..., :DN],
            rotate(query_raw[..., DN:], all_cosines[:, None, :], all_sines[:, None, :]),
        ],
        -1,
    ).astype(jnp.bfloat16)
    compressed_seq = latent_seq[:, :KVR]
    key_rope = latent_seq[:, KVR:]
    expanded = jnp.dot(compressed_seq, expand_weights, preferred_element_type=jnp.float32).reshape(
        seq_len, head_count, DN + DV
    )
    keys_nope = expanded[..., :DN].astype(jnp.bfloat16)
    values_low = expanded[..., DN:].astype(jnp.bfloat16)
    score_scale = 1.0 / math.sqrt(DN + DR)
    block_rows = min(512, seq_len)
    prefix_len = prefix[0]
    lse_list = []
    mixed_list = []
    for rows_start in range(0, seq_len, block_rows):
        query_block = query_low[rows_start : rows_start + block_rows]
        masked = block_scores(query_block, keys_nope, key_rope, rows_start, prefix_len, score_scale)
        top_score = jnp.max(masked, -1, keepdims=True)
        exp_scores = jnp.exp(masked - top_score)
        totals = jnp.sum(exp_scores, -1, keepdims=True)
        prob_low = (exp_scores / totals).astype(jnp.bfloat16)
        lse_list.append(top_score + jnp.log(totals))
        mixed_list.append(
            jnp.einsum(
                "hqk,khv->qhv", prob_low, values_low, preferred_element_type=jnp.float32
            ).astype(jnp.bfloat16)
        )
    mixed_all = jnp.concatenate(mixed_list, 0).reshape(seq_len, head_count * DV)
    attn_part = jnp.einsum(
        "tk,dk->td", mixed_all, output_weights_t, preferred_element_type=jnp.float32
    )
    branch_all = lax.psum(attn_part.astype(jnp.bfloat16), "tensor").astype(jnp.float32)
    shared_local, branch_all = lax.optimization_barrier((shared_local, branch_all))
    residual_all = hidden_all_f + branch_all
    residual_own = lax.dynamic_slice_in_dim(residual_all, start_row, tok_dev, 0)
    scale_two = norm_scale(residual_all)
    gain_two = second_gains.astype(jnp.float32)
    normed_two = (residual_all * scale_two * gain_two).astype(jnp.bfloat16)
    logits = jnp.dot(normed_two, router_weights, preferred_element_type=jnp.float32)
    top_count = routes.shape[1]
    chosen_hot = routes[:, :, None] == jnp.arange(experts)[None, None, :]
    chosen_logits = jnp.sum(jnp.where(chosen_hot, logits[:, None, :], 0.0), -1)
    gate_values = jax.nn.softmax(chosen_logits, axis=-1)
    assignments = seq_len * top_count
    flat_hot = chosen_hot.reshape(assignments, experts).astype(jnp.bfloat16)
    lower = (jnp.arange(assignments)[:, None] > jnp.arange(assignments)[None, :]).astype(jnp.bfloat16)
    earlier = jnp.dot(lower, flat_hot, preferred_element_type=jnp.float32)
    slot_pos = jnp.sum(earlier * flat_hot.astype(jnp.float32), -1).astype(jnp.int32)
    expert_ids = routes.reshape(-1)
    exp_dev = expert_gate.shape[0]
    capacity = tensor_size * (5 * seq_len * top_count // (4 * experts * tensor_size))
    slot_index = expert_ids * capacity + slot_pos
    token_ids = jnp.arange(seq_len * top_count) // top_count
    slot_token = jnp.full((experts * capacity,), seq_len, jnp.int32).at[slot_index].set(token_ids)
    slot_gate = (
        jnp.zeros((experts * capacity,), jnp.float32).at[slot_index].set(gate_values.reshape(-1))
    )
    slot_valid = (slot_token < seq_len).astype(jnp.float32)
    tile_rows = D // 128
    send_both = dispatch_rows(slot_token, normed_two, grad_seq, slot_valid, slot_gate).reshape(
        dp_size, exp_dev, capacity, 2 * tile_rows, 128
    )
    shared_all = lax.all_gather(shared_local, "dp", axis=0, tiled=True)
    shared_all, send_both = lax.optimization_barrier((shared_all, send_both))
    gate_shared = shared_all[:, :shared_cols]
    up_shared = shared_all[:, shared_cols : 2 * shared_cols]
    down_shared_t = shared_all[:, 2 * shared_cols :]
    recv_both = lax.all_to_all(send_both, "dp", split_axis=0, concat_axis=0, tiled=True)
    recv_both = recv_both.reshape(dp_size, exp_dev, capacity, 2 * D)
    recv_rows = recv_both[..., :D]
    recv_grads = recv_both[..., D:]
    gate_pre = jnp.einsum(
        "sjcd,jfd->sjcf", recv_rows, expert_gate, preferred_element_type=jnp.float32
    )
    up_pre = jnp.einsum("sjcd,jfd->sjcf", recv_rows, expert_up, preferred_element_type=jnp.float32)
    sigmoid_gate = jax.nn.sigmoid(gate_pre)
    expert_act = (gate_pre * sigmoid_gate * up_pre).astype(jnp.bfloat16)
    expert_out = jnp.einsum(
        "sjcf,jfd->sjcd", expert_act, expert_down, preferred_element_type=jnp.float32
    )
    back_out = lax.all_to_all(
        expert_out.astype(jnp.bfloat16).reshape(dp_size, exp_dev, capacity, tile_rows, 128),
        "dp",
        split_axis=0,
        concat_axis=0,
        tiled=True,
    )
    act_grad = jnp.einsum(
        "sjcd,jfd->sjcf", recv_grads, expert_down, preferred_element_type=jnp.float32
    )
    gate_low_grad, up_low_grad = silu_back(act_grad, gate_pre, up_pre, sigmoid_gate)
    expert_down_grad = jnp.einsum(
        "sjcf,sjcd->jfd", expert_act, recv_grads, preferred_element_type=jnp.float32
    )
    expert_gate_grad = jnp.einsum(
        "sjcf,sjcd->jfd", gate_low_grad, recv_rows, preferred_element_type=jnp.float32
    )
    expert_up_grad = jnp.einsum(
        "sjcf,sjcd->jfd", up_low_grad, recv_rows, preferred_element_type=jnp.float32
    )
    row_grads = jnp.einsum(
        "sjcf,jfd->sjcd", gate_low_grad, expert_gate, preferred_element_type=jnp.float32
    )
    row_grads = row_grads + jnp.einsum(
        "sjcf,jfd->sjcd", up_low_grad, expert_up, preferred_element_type=jnp.float32
    )
    grads_low = row_grads.astype(jnp.bfloat16).reshape(dp_size, exp_dev, capacity, tile_rows, 128)
    back_out, grads_low = lax.optimization_barrier((back_out, grads_low))
    back_grads = lax.all_to_all(
        grads_low,
        "dp",
        split_axis=0,
        concat_axis=0,
        tiled=True,
    )
    shared_pre_gate = jnp.dot(normed_two, gate_shared, preferred_element_type=jnp.float32)
    shared_pre_up = jnp.dot(normed_two, up_shared, preferred_element_type=jnp.float32)
    shared_sigmoid = jax.nn.sigmoid(shared_pre_gate)
    shared_act = (shared_pre_gate * shared_sigmoid * shared_pre_up).astype(jnp.bfloat16)
    shared_out = jnp.einsum(
        "tf,df->td", shared_act, down_shared_t, preferred_element_type=jnp.float32
    )
    shared_act_grad = jnp.dot(grad_seq, down_shared_t, preferred_element_type=jnp.float32)
    shared_gate_low, shared_up_low = silu_back(
        shared_act_grad, shared_pre_gate, shared_pre_up, shared_sigmoid
    )
    shared_down_grad_t = jnp.dot(grad_seq.T, shared_act, preferred_element_type=jnp.float32)
    shared_gate_grad = jnp.dot(normed_two.T, shared_gate_low, preferred_element_type=jnp.float32)
    shared_up_grad = jnp.dot(normed_two.T, shared_up_low, preferred_element_type=jnp.float32)
    shared_back = jnp.einsum(
        "tf,df->td", shared_gate_low, gate_shared, preferred_element_type=jnp.float32
    )
    shared_back = shared_back + jnp.einsum(
        "tf,df->td", shared_up_low, up_shared, preferred_element_type=jnp.float32
    )
    shared_grads_in = jnp.concatenate(
        [shared_gate_grad, shared_up_grad, shared_down_grad_t], 1
    ).astype(jnp.bfloat16)
    grad_seq_f = grad_seq.astype(jnp.float32)
    table_rows = experts * capacity
    feed_part, back_part, gate_cols = combine_rows(
        slot_index.reshape(seq_len, top_count),
        back_out.reshape(table_rows, tile_rows, 128),
        back_grads.reshape(table_rows, tile_rows, 128),
        gate_values,
        grad_seq,
        shared_out,
        shared_back,
    )
    gate_part = gate_cols[:, :top_count]
    feed_own = jnp.sum(
        lax.all_to_all(
            feed_part.reshape(tensor_size, tok_dev, D), "tensor", split_axis=0, concat_axis=0, tiled=True
        ).astype(jnp.float32),
        0,
    )
    reduced_back = lax.psum(
        jnp.concatenate([back_part, gate_cols.astype(jnp.bfloat16)], 1), "tensor"
    ).astype(jnp.float32)
    normed_two_grad = reduced_back[:, :D]
    gate_grads = reduced_back[:, D : D + top_count]
    weighted_total = jnp.sum(gate_values * gate_grads, -1, keepdims=True)
    chosen_grads = gate_values * (gate_grads - weighted_total)
    logit_grads = jnp.sum(jnp.where(chosen_hot, chosen_grads[:, :, None], 0.0), 1)
    normed_two_grad = normed_two_grad + jnp.dot(
        logit_grads, router_weights.astype(jnp.float32).T, precision=HIGH
    )
    residual_grad = grad_seq_f + norm_back(residual_all, scale_two, gain_two, normed_two_grad)
    branch_grad = residual_grad.astype(jnp.bfloat16)
    shared_grads_in, branch_grad = lax.optimization_barrier((shared_grads_in, branch_grad))
    shared_pack = jnp.sum(
        lax.all_to_all(
            shared_grads_in.reshape(dp_size, rows_dp, shared_grads_in.shape[1]),
            "dp",
            split_axis=0,
            concat_axis=0,
            tiled=True,
        ).astype(jnp.float32),
        0,
    )
    output_grad_w_t = jnp.dot(branch_grad.T, mixed_all, preferred_element_type=jnp.float32)
    mixed_grad = (
        jnp.dot(branch_grad, output_weights_t, preferred_element_type=jnp.float32)
        .astype(jnp.bfloat16)
        .reshape(seq_len, head_count, DV)
    )
    keys_nope_grad = jnp.zeros((seq_len, head_count, DN), jnp.float32)
    key_rope_grad = jnp.zeros((seq_len, DR), jnp.float32)
    values_grad = jnp.zeros((seq_len, head_count, DV), jnp.float32)
    query_grad_list = []
    for block_index, rows_start in enumerate(range(0, seq_len, block_rows)):
        query_block = query_low[rows_start : rows_start + block_rows]
        masked = block_scores(query_block, keys_nope, key_rope, rows_start, prefix_len, score_scale)
        prob_full = jnp.exp(masked - lse_list[block_index])
        prob_low = prob_full.astype(jnp.bfloat16)
        mixed_block = mixed_grad[rows_start : rows_start + block_rows]
        prob_grads = jnp.einsum(
            "qhv,khv->hqk", mixed_block, values_low, preferred_element_type=jnp.float32
        )
        row_delta = jnp.sum(prob_full * prob_grads, -1, keepdims=True)
        score_grads = (prob_full * (prob_grads - row_delta)).astype(jnp.bfloat16)
        query_nope_grad = (
            jnp.einsum("hqk,khd->qhd", score_grads, keys_nope, preferred_element_type=jnp.float32)
            * score_scale
        )
        query_rope_grad = (
            jnp.einsum("hqk,kr->qhr", score_grads, key_rope, preferred_element_type=jnp.float32)
            * score_scale
        )
        keys_nope_grad = (
            keys_nope_grad
            + jnp.einsum(
                "hqk,qhd->khd",
                score_grads,
                query_block[..., :DN],
                preferred_element_type=jnp.float32,
            )
            * score_scale
        )
        key_rope_grad = (
            key_rope_grad
            + jnp.einsum(
                "hqk,qhr->kr",
                score_grads,
                query_block[..., DN:],
                preferred_element_type=jnp.float32,
            )
            * score_scale
        )
        values_grad = values_grad + jnp.einsum(
            "hqk,qhv->khv", prob_low, mixed_block, preferred_element_type=jnp.float32
        )
        block_cosines = all_cosines[rows_start : rows_start + block_rows, None, :]
        block_sines = all_sines[rows_start : rows_start + block_rows, None, :]
        query_grad_list.append(
            jnp.concatenate(
                [
                    query_nope_grad,
                    rotate_back(round_trip(query_rope_grad), block_cosines, block_sines),
                ],
                -1,
            ).astype(jnp.bfloat16)
        )
    query_grads = jnp.concatenate(query_grad_list, 0).reshape(seq_len, head_count * (DN + DR))
    feed_own, shared_pack, query_grads = lax.optimization_barrier((feed_own, shared_pack, query_grads))
    output = (residual_own + feed_own).astype(jnp.bfloat16)
    query_grad_w = jnp.dot(normed_all.T, query_grads, preferred_element_type=jnp.float32)
    normed_grad_part = jnp.dot(query_grads, query_weights.T, preferred_element_type=jnp.float32)
    expand_grads = jnp.concatenate(
        [keys_nope_grad.astype(jnp.bfloat16), values_grad.astype(jnp.bfloat16)], -1
    ).reshape(seq_len, head_count * (DN + DV))
    expand_grad_w = jnp.dot(compressed_seq.T, expand_grads, preferred_element_type=jnp.float32)
    compressed_grad_part = jnp.dot(
        expand_grads, expand_weights.T, preferred_element_type=jnp.float32
    )
    latent_grad_part = jnp.concatenate([compressed_grad_part, key_rope_grad], -1)
    attn_grads_in = jnp.concatenate(
        [
            query_grad_w,
            output_grad_w_t,
            expand_grad_w.reshape(dp_size * rows_dp, expand_flat_cols),
        ],
        1,
    )
    token_all = lax.psum(
        jnp.concatenate([normed_grad_part, latent_grad_part], 1).astype(jnp.bfloat16), "tensor"
    ).astype(jnp.float32)
    compressed_grad_all = token_all[:, D : D + KVR]
    kv_gain_full = jnp.sum(compressed_grad_all * compressed_all * scale_kv_all, 0)
    raw_grad_all = jnp.concatenate(
        [
            norm_back(compressed_all, scale_kv_all, gain_kv, compressed_grad_all),
            rotate_back(token_all[:, D + KVR :], all_cosines, all_sines),
        ],
        -1,
    ).astype(jnp.bfloat16)
    normed_grad_all = token_all[:, :D] + jnp.dot(
        raw_grad_all, latent_weights.T, preferred_element_type=jnp.float32
    )
    normed_grad = lax.dynamic_slice_in_dim(normed_grad_all, start_row, tok_dev, 0)
    hidden_grad = lax.dynamic_slice_in_dim(residual_grad, start_row, tok_dev, 0) + norm_back(
        hidden_f, scale_one, gain_one, normed_grad
    )
    row_per = D // (dp_size * tensor_size)

    def own_rows(values):
        split = values.reshape(values.shape[0], dp_size, tensor_size, row_per)
        return lax.dynamic_slice_in_dim(split, tensor_rank, 1, 2).reshape(values.shape[0], -1)

    latent_rows = jnp.dot(own_rows(normed_all).T, raw_grad_all, preferred_element_type=jnp.float32)
    attn_gain_rows = jnp.sum(
        own_rows(normed_grad_all) * own_rows(hidden_all_f) * scale_one_all, 0
    )
    second_gain_rows = jnp.sum(
        own_rows(normed_two_grad) * own_rows(residual_all) * scale_two, 0
    )
    router_rows = jnp.dot(
        own_rows(normed_two).astype(jnp.float32).T, logit_grads, precision=HIGH
    )
    kv_per = kv_gain_full.shape[0] // (dp_size * tensor_size)
    kv_rows_own = lax.dynamic_slice_in_dim(
        kv_gain_full.reshape(dp_size, tensor_size, kv_per), tensor_rank, 1, 1
    ).reshape(dp_size, kv_per)
    kv_column = jnp.pad(kv_rows_own, ((0, 0), (0, row_per - kv_per))).reshape(-1)
    small_pack = jnp.concatenate(
        [
            latent_rows,
            router_rows,
            attn_gain_rows[:, None],
            second_gain_rows[:, None],
            kv_column[:, None],
        ],
        1,
    )
    attn_width = attn_grads_in.shape[1]
    small_width = small_pack.shape[1]
    small_count = row_per * small_width
    small_cols = -(-small_count // rows_dp)
    small_flat = jnp.pad(
        small_pack.reshape(dp_size, small_count), ((0, 0), (0, small_cols * rows_dp - small_count))
    ).reshape(dp_size * rows_dp, small_cols)
    merged_own = lax.psum_scatter(
        jnp.concatenate([attn_grads_in, small_flat], 1), "dp", scatter_dimension=0, tiled=True
    )
    attn_pack = merged_own[:, :attn_width]
    small_own = merged_own[:, attn_width:].reshape(-1)[:small_count].reshape(row_per, small_width)
    cut = [0]
    for width in (latent_cols, experts, 1, 1, 1):
        cut.append(cut[-1] + width)
    latent_proj_grad = small_own[:, cut[0] : cut[1]]
    router_out = small_own[:, cut[1] : cut[2]]
    attn_gain_out = small_own[:, cut[2]]
    second_gain_out = small_own[:, cut[3]]
    latent_gain_out = small_own[:kv_per, cut[4]]
    cut = [0]
    for width in (head_cols, out_cols, expand_flat_cols):
        cut.append(cut[-1] + width)
    query_proj_grad = attn_pack[:, cut[0] : cut[1]]
    output_proj_grad = attn_pack[:, cut[1] : cut[2]].T
    expand_proj_grad = attn_pack[:, cut[2] : cut[3]].reshape(kv_rows, expand_cols)
    shared_gate_out = shared_pack[:, :shared_cols]
    shared_up_out = shared_pack[:, shared_cols : 2 * shared_cols]
    shared_down_out = shared_pack[:, 2 * shared_cols :].T
    return (
        output,
        hidden_grad,
        attn_gain_out,
        query_proj_grad,
        latent_proj_grad,
        latent_gain_out,
        expand_proj_grad,
        output_proj_grad,
        second_gain_out,
        router_out,
        expert_gate_grad,
        expert_up_grad,
        expert_down_grad,
        shared_gate_out,
        shared_up_out,
        shared_down_out,
    )


def solution(mesh):
    return jax.shard_map(
        shards,
        mesh=mesh,
        in_specs=(
            P(("dp", "tensor"), None),
            P("dp", None),
            P("dp"),
            P("dp"),
            P("dp", "tensor"),
            P("dp", None),
            P("dp"),
            P("dp", "tensor"),
            P("tensor", "dp"),
            P("dp"),
            P("dp", None),
            P("dp", "tensor", None),
            P("dp", "tensor", None),
            P("dp", "tensor", None),
            P("dp", "tensor"),
            P("dp", "tensor"),
            P("tensor", "dp"),
            P(("dp", "tensor"), None),
        ),
        out_specs=(
            P(("dp", "tensor"), None),
            P(("dp", "tensor"), None),
            P(("dp", "tensor")),
            P("dp", "tensor"),
            P(("dp", "tensor"), None),
            P(("dp", "tensor")),
            P("dp", "tensor"),
            P("tensor", "dp"),
            P(("dp", "tensor")),
            P(("dp", "tensor"), None),
            P("dp", "tensor", None),
            P("dp", "tensor", None),
            P("dp", "tensor", None),
            P("dp", "tensor"),
            P("dp", "tensor"),
            P("tensor", "dp"),
        ),
        check_vma=False,
    )
```

```python
import math

import jax
import jax.numpy as jnp
from jax import lax
from jax.experimental import pallas as pl
from jax.experimental.pallas import tpu as pltpu
from jax.sharding import PartitionSpec as P

D = 2048
DN = 128
DR = 64
DV = 128
KVR = 512


EPS = 1e-06
HIGH = lax.Precision.HIGHEST
MASKED = -1e30


def norm_scale(values):
    return lax.rsqrt(jnp.mean(values * values, -1, keepdims=True) + EPS)


def norm_back(values, scales, gains, upstream):
    weighted = gains * upstream
    return scales * weighted - values * scales**3 * jnp.mean(values * weighted, -1, keepdims=True)


def rope_tables(positions, rope_width):
    half_width = rope_width // 2
    frequency = 10000.0 ** (-2.0 * jnp.arange(half_width).astype(jnp.float32) / rope_width)
    angles = positions.astype(jnp.float32)[:, None] * frequency[None, :]
    return (jnp.cos(angles), jnp.sin(angles))


def rotate(vectors, cosines, sine_values):
    half_width = vectors.shape[-1] // 2
    front_half = vectors[..., :half_width]
    back_half = vectors[..., half_width:]
    return jnp.concatenate(
        [
            front_half * cosines - back_half * sine_values,
            back_half * cosines + front_half * sine_values,
        ],
        -1,
    )


def rotate_back(gradients, cosines, sine_values):
    half_width = gradients.shape[-1] // 2
    front_half = gradients[..., :half_width]
    back_half = gradients[..., half_width:]
    return jnp.concatenate(
        [
            front_half * cosines + back_half * sine_values,
            back_half * cosines - front_half * sine_values,
        ],
        -1,
    )


def round_trip(values):
    return lax.optimization_barrier(values.astype(jnp.bfloat16)).astype(jnp.float32)


def block_scores(query_block, keys_nope, key_rope, rows_start, prefix_len, score_scale):
    raw_scores = jnp.einsum(
        "qhd,khd->hqk", query_block[..., :DN], keys_nope, preferred_element_type=jnp.float32
    )
    raw_scores = raw_scores + jnp.einsum(
        "qhr,kr->hqk", query_block[..., DN:], key_rope, preferred_element_type=jnp.float32
    )
    query_places = rows_start + jnp.arange(query_block.shape[0])
    key_places = jnp.arange(keys_nope.shape[0])
    visible = (key_places[None, :] <= query_places[:, None]) | (key_places[None, :] < prefix_len)
    return jnp.where(visible[None], raw_scores * score_scale, MASKED)


def silu_back(act_grad, gate_pre, up_pre, sigmoid_gate):
    up_grad = (act_grad * gate_pre * sigmoid_gate).astype(jnp.bfloat16)
    gate_grad = (act_grad * up_pre * sigmoid_gate * (1.0 + gate_pre * (1.0 - sigmoid_gate))).astype(
        jnp.bfloat16
    )
    return (gate_grad, up_grad)


def dispatch_kernel(tok_ref, both_hbm, col_ref, out_ref, both_buf, sems):
    block = both_buf.shape[0]
    tile_rows = both_buf.shape[1] // 2
    last = both_hbm.shape[0] - 1
    base = pl.program_id(0) * block

    def start(r, carry):
        tok = jnp.minimum(tok_ref[base + r], last)
        pltpu.make_async_copy(both_hbm.at[tok], both_buf.at[r], sems.at[r]).start()
        return carry

    lax.fori_loop(0, block, start, 0, unroll=4)

    def finish(r, carry):
        pltpu.make_async_copy(both_hbm.at[0], both_buf.at[r], sems.at[r]).wait()
        return carry

    lax.fori_loop(0, block, finish, 0, unroll=4)
    rows = both_buf[:, :tile_rows, :]
    out_ref[:, :tile_rows, :] = jnp.where(col_ref[0] > 0, rows, jnp.zeros_like(rows))
    out_ref[:, tile_rows:, :] = (
        both_buf[:, tile_rows:, :].astype(jnp.float32) * col_ref[1]
    ).astype(out_ref.dtype)


def dispatch_rows(slot_token, rows, grads, valid, gate, block=128):
    slots = slot_token.shape[0]
    count, width = rows.shape
    tile_rows = width // 128
    cols = jnp.broadcast_to(jnp.stack([valid, gate])[:, :, None, None], (2, slots, 1, 128))
    both = jnp.concatenate([rows, grads], 1).reshape(count, 2 * tile_rows, 128)
    out = pl.pallas_call(
        dispatch_kernel,
        out_shape=jax.ShapeDtypeStruct((slots, 2 * tile_rows, 128), rows.dtype),
        grid_spec=pltpu.PrefetchScalarGridSpec(
            num_scalar_prefetch=1,
            grid=(slots // block,),
            in_specs=[
                pl.BlockSpec(memory_space=pl.ANY),
                pl.BlockSpec((2, block, 1, 128), lambda i, tok: (0, i, 0, 0)),
            ],
            out_specs=pl.BlockSpec((block, 2 * tile_rows, 128), lambda i, tok: (i, 0, 0)),
            scratch_shapes=[
                pltpu.VMEM((block, 2 * tile_rows, 128), rows.dtype),
                pltpu.SemaphoreType.DMA((block,)),
            ],
        ),
        cost_estimate=pl.CostEstimate(
            flops=slots * width, transcendentals=0, bytes_accessed=4 * slots * 2 * width
        ),
    )(slot_token, both, cols)
    return out


def combine_kernel(
    slot_ref, out_hbm, back_hbm, gate_ref, grad_ref, shared_out_ref, shared_back_ref,
    feed_ref, back_ref, part_ref, picked_out, picked_back, sems,
):
    top = picked_out.shape[0]
    block = picked_out.shape[1]
    last = out_hbm.shape[0] - 1
    base = pl.program_id(0) * block

    def start(r, carry):
        for k in range(top):
            slot = jnp.clip(slot_ref[(base + r) * top + k], 0, last)
            pltpu.make_async_copy(out_hbm.at[slot], picked_out.at[k, r], sems.at[0, k, r]).start()
            pltpu.make_async_copy(back_hbm.at[slot], picked_back.at[k, r], sems.at[1, k, r]).start()
        return carry

    lax.fori_loop(0, block, start, 0, unroll=2)

    def finish(r, carry):
        for k in range(top):
            pltpu.make_async_copy(out_hbm.at[0], picked_out.at[k, r], sems.at[0, k, r]).wait()
            pltpu.make_async_copy(back_hbm.at[0], picked_back.at[k, r], sems.at[1, k, r]).wait()
        return carry

    lax.fori_loop(0, block, finish, 0, unroll=2)
    grad = grad_ref[...].astype(jnp.float32)
    weighted = None
    backs = None
    lanes = lax.broadcasted_iota(jnp.int32, part_ref.shape, 2)
    parts = jnp.zeros(part_ref.shape, jnp.float32)
    for k in range(top):
        out_k = picked_out[k].astype(jnp.float32)
        term = gate_ref[k] * out_k
        weighted = term if weighted is None else weighted + term
        back_k = picked_back[k].astype(jnp.float32)
        backs = back_k if backs is None else backs + back_k
        dot_k = jnp.sum(jnp.sum(grad * out_k, 2, keepdims=True), 1, keepdims=True)
        parts = jnp.where(lanes == k, dot_k, parts)
    feed_ref[...] = (shared_out_ref[...] + weighted).astype(feed_ref.dtype)
    back_ref[...] = (backs + shared_back_ref[...]).astype(back_ref.dtype)
    part_ref[...] = parts


def combine_rows(slot_index, out_table, back_table, gate_values, grad, shared_out, shared_back, block=128):
    tokens, top = gate_values.shape
    width = grad.shape[1]
    tile_rows = width // 128
    gates = jnp.broadcast_to(gate_values.T[:, :, None, None], (top, tokens, 1, 128))
    row_spec = pl.BlockSpec((block, tile_rows, 128), lambda i, s: (i, 0, 0))
    feed, back, parts = pl.pallas_call(
        combine_kernel,
        out_shape=(
            jax.ShapeDtypeStruct((tokens, tile_rows, 128), jnp.bfloat16),
            jax.ShapeDtypeStruct((tokens, tile_rows, 128), jnp.bfloat16),
            jax.ShapeDtypeStruct((tokens, 1, 128), jnp.float32),
        ),
        grid_spec=pltpu.PrefetchScalarGridSpec(
            num_scalar_prefetch=1,
            grid=(tokens // block,),
            in_specs=[
                pl.BlockSpec(memory_space=pl.ANY),
                pl.BlockSpec(memory_space=pl.ANY),
                pl.BlockSpec((top, block, 1, 128), lambda i, s: (0, i, 0, 0)),
                row_spec,
                row_spec,
                row_spec,
            ],
            out_specs=[row_spec, row_spec, pl.BlockSpec((block, 1, 128), lambda i, s: (i, 0, 0))],
            scratch_shapes=[
                pltpu.VMEM((top, block, tile_rows, 128), out_table.dtype),
                pltpu.VMEM((top, block, tile_rows, 128), back_table.dtype),
                pltpu.SemaphoreType.DMA((2, top, block)),
            ],
        ),
        cost_estimate=pl.CostEstimate(
            flops=8 * tokens * top * width,
            transcendentals=0,
            bytes_accessed=tokens * (top * 4 * width + 2 * width + 8 * width + 4 * width),
        ),
    )(
        slot_index.reshape(-1),
        out_table,
        back_table,
        gates,
        grad.reshape(tokens, tile_rows, 128),
        shared_out.reshape(tokens, tile_rows, 128),
        shared_back.reshape(tokens, tile_rows, 128),
    )
    return feed.reshape(tokens, width), back.reshape(tokens, width), parts[:, 0, :top]


def shards(
    hidden,
    routes,
    prefix,
    attn_gain,
    query_proj,
    latent_proj,
    latent_gain,
    expand_proj,
    output_proj,
    second_gain,
    router_proj,
    expert_gate,
    expert_up,
    expert_down,
    shared_gate,
    shared_up,
    shared_down,
    out_grad,
):
    tok_dev = hidden.shape[0]
    tensor_size = lax.axis_size("tensor")
    tensor_rank = lax.axis_index("tensor")
    dp_size = lax.axis_size("dp")
    seq_len = tok_dev * tensor_size
    start_row = tensor_rank * tok_dev
    rows_dp = attn_gain.shape[0]
    kv_rows = latent_gain.shape[0]
    head_cols = query_proj.shape[1]
    latent_cols = latent_proj.shape[1]
    expand_cols = expand_proj.shape[1]
    expand_flat_cols = kv_rows * expand_cols // rows_dp
    first_pack = jnp.concatenate(
        [
            query_proj,
            latent_proj,
            expand_proj.reshape(rows_dp, expand_flat_cols),
            attn_gain[:, None],
            jnp.pad(latent_gain, (0, rows_dp - kv_rows))[:, None],
        ],
        1,
    )
    first_all = lax.all_gather(first_pack, "dp", axis=0, tiled=True)
    cut = [0]
    for width in (head_cols, latent_cols, expand_flat_cols, 1, 1):
        cut.append(cut[-1] + width)
    query_weights = first_all[:, cut[0] : cut[1]]
    latent_weights = first_all[:, cut[1] : cut[2]]
    expand_weights = first_all[:, cut[2] : cut[3]].reshape(dp_size * kv_rows, expand_cols)
    attn_gains = first_all[:, cut[3]]
    kv_gains = first_all[:, cut[4]].reshape(dp_size, rows_dp)[:, :kv_rows].reshape(-1)
    out_cols = output_proj.shape[0]
    experts = router_proj.shape[1]
    shared_cols = shared_gate.shape[1]
    second_pack = jnp.concatenate([output_proj.T, second_gain[:, None], router_proj], 1)
    second_all = lax.all_gather(second_pack, "dp", axis=0, tiled=True)
    output_weights_t = second_all[:, :out_cols]
    second_gains = second_all[:, out_cols]
    router_weights = second_all[:, out_cols + 1 :]
    shared_local = jnp.concatenate([shared_gate, shared_up, shared_down.T], 1)

    hidden_all = lax.all_gather(hidden, "tensor", axis=0, tiled=True)
    grad_blocks = jnp.broadcast_to(out_grad[None], (tensor_size,) + out_grad.shape)
    grad_blocks, hidden_all = lax.optimization_barrier((grad_blocks, hidden_all))
    grad_seq = lax.all_to_all(
        grad_blocks, "tensor", split_axis=0, concat_axis=0, tiled=True
    ).reshape(tensor_size * tok_dev, D)
    grad_seq, query_weights, latent_weights = lax.optimization_barrier(
        (grad_seq, query_weights, latent_weights)
    )
    hidden_all_f = hidden_all.astype(jnp.float32)
    scale_one_all = norm_scale(hidden_all_f)
    gain_one = attn_gains.astype(jnp.float32)
    normed_all = (hidden_all_f * scale_one_all * gain_one).astype(jnp.bfloat16)
    hidden_f = lax.dynamic_slice_in_dim(hidden_all_f, start_row, tok_dev, 0)
    scale_one = lax.dynamic_slice_in_dim(scale_one_all, start_row, tok_dev, 0)
    normed_own = lax.dynamic_slice_in_dim(normed_all, start_row, tok_dev, 0)
    latent_raw_all = jnp.dot(normed_all, latent_weights, preferred_element_type=jnp.float32)
    compressed_all = latent_raw_all[:, :KVR]
    scale_kv_all = norm_scale(compressed_all)
    gain_kv = kv_gains.astype(jnp.float32)
    all_cosines, all_sines = rope_tables(jnp.arange(seq_len), DR)
    latent_seq = jnp.concatenate(
        [
            compressed_all * scale_kv_all * gain_kv,
            rotate(latent_raw_all[:, KVR:], all_cosines, all_sines),
        ],
        -1,
    ).astype(jnp.bfloat16)
    compressed = lax.dynamic_slice_in_dim(compressed_all, start_row, tok_dev, 0)
    scale_kv = lax.dynamic_slice_in_dim(scale_kv_all, start_row, tok_dev, 0)
    own_cosines = lax.dynamic_slice_in_dim(all_cosines, start_row, tok_dev, 0)
    own_sines = lax.dynamic_slice_in_dim(all_sines, start_row, tok_dev, 0)
    head_count = query_weights.shape[1] // (DN + DR)
    query_raw = jnp.dot(normed_all, query_weights, preferred_element_type=jnp.float32).reshape(
        seq_len, head_count, DN + DR
    )
    query_low = jnp.concatenate(
        [
            query_raw[..., :DN],
            rotate(query_raw[..., DN:], all_cosines[:, None, :], all_sines[:, None, :]),
        ],
        -1,
    ).astype(jnp.bfloat16)
    compressed_seq = latent_seq[:, :KVR]
    key_rope = latent_seq[:, KVR:]
    expanded = jnp.dot(compressed_seq, expand_weights, preferred_element_type=jnp.float32).reshape(
        seq_len, head_count, DN + DV
    )
    keys_nope = expanded[..., :DN].astype(jnp.bfloat16)
    values_low = expanded[..., DN:].astype(jnp.bfloat16)
    score_scale = 1.0 / math.sqrt(DN + DR)
    block_rows = min(512, seq_len)
    prefix_len = prefix[0]
    lse_list = []
    mixed_list = []
    for rows_start in range(0, seq_len, block_rows):
        query_block = query_low[rows_start : rows_start + block_rows]
        masked = block_scores(query_block, keys_nope, key_rope, rows_start, prefix_len, score_scale)
        top_score = jnp.max(masked, -1, keepdims=True)
        exp_scores = jnp.exp(masked - top_score)
        totals = jnp.sum(exp_scores, -1, keepdims=True)
        prob_low = (exp_scores / totals).astype(jnp.bfloat16)
        lse_list.append(top_score + jnp.log(totals))
        mixed_list.append(
            jnp.einsum(
                "hqk,khv->qhv", prob_low, values_low, preferred_element_type=jnp.float32
            ).astype(jnp.bfloat16)
        )
    mixed_all = jnp.concatenate(mixed_list, 0).reshape(seq_len, head_count * DV)
    attn_part = jnp.einsum(
        "tk,dk->td", mixed_all, output_weights_t, preferred_element_type=jnp.float32
    )
    branch_all = lax.psum(attn_part.astype(jnp.bfloat16), "tensor").astype(jnp.float32)
    shared_local, branch_all = lax.optimization_barrier((shared_local, branch_all))
    residual_all = hidden_all_f + branch_all
    residual_own = lax.dynamic_slice_in_dim(residual_all, start_row, tok_dev, 0)
    scale_two = norm_scale(residual_all)
    gain_two = second_gains.astype(jnp.float32)
    normed_two = (residual_all * scale_two * gain_two).astype(jnp.bfloat16)
    logits = jnp.dot(normed_two, router_weights, preferred_element_type=jnp.float32)
    top_count = routes.shape[1]
    chosen_hot = routes[:, :, None] == jnp.arange(experts)[None, None, :]
    chosen_logits = jnp.sum(jnp.where(chosen_hot, logits[:, None, :], 0.0), -1)
    gate_values = jax.nn.softmax(chosen_logits, axis=-1)
    assignments = seq_len * top_count
    flat_hot = chosen_hot.reshape(assignments, experts).astype(jnp.bfloat16)
    lower = (jnp.arange(assignments)[:, None] > jnp.arange(assignments)[None, :]).astype(jnp.bfloat16)
    earlier = jnp.dot(lower, flat_hot, preferred_element_type=jnp.float32)
    slot_pos = jnp.sum(earlier * flat_hot.astype(jnp.float32), -1).astype(jnp.int32)
    expert_ids = routes.reshape(-1)
    exp_dev = expert_gate.shape[0]
    capacity = tensor_size * (5 * seq_len * top_count // (4 * experts * tensor_size))
    slot_index = expert_ids * capacity + slot_pos
    token_ids = jnp.arange(seq_len * top_count) // top_count
    slot_token = jnp.full((experts * capacity,), seq_len, jnp.int32).at[slot_index].set(token_ids)
    slot_gate = (
        jnp.zeros((experts * capacity,), jnp.float32).at[slot_index].set(gate_values.reshape(-1))
    )
    slot_valid = (slot_token < seq_len).astype(jnp.float32)
    tile_rows = D // 128
    send_both = dispatch_rows(slot_token, normed_two, grad_seq, slot_valid, slot_gate).reshape(
        dp_size, exp_dev, capacity, 2 * tile_rows, 128
    )
    shared_all = lax.all_gather(shared_local, "dp", axis=0, tiled=True)
    shared_all, send_both = lax.optimization_barrier((shared_all, send_both))
    gate_shared = shared_all[:, :shared_cols]
    up_shared = shared_all[:, shared_cols : 2 * shared_cols]
    down_shared_t = shared_all[:, 2 * shared_cols :]
    recv_both = lax.all_to_all(send_both, "dp", split_axis=0, concat_axis=0, tiled=True)
    recv_both = recv_both.reshape(dp_size, exp_dev, capacity, 2 * D)
    recv_rows = recv_both[..., :D]
    recv_grads = recv_both[..., D:]
    gate_pre = jnp.einsum(
        "sjcd,jfd->sjcf", recv_rows, expert_gate, preferred_element_type=jnp.float32
    )
    up_pre = jnp.einsum("sjcd,jfd->sjcf", recv_rows, expert_up, preferred_element_type=jnp.float32)
    sigmoid_gate = jax.nn.sigmoid(gate_pre)
    expert_act = (gate_pre * sigmoid_gate * up_pre).astype(jnp.bfloat16)
    expert_out = jnp.einsum(
        "sjcf,jfd->sjcd", expert_act, expert_down, preferred_element_type=jnp.float32
    )
    back_out = lax.all_to_all(
        expert_out.astype(jnp.bfloat16).reshape(dp_size, exp_dev, capacity, tile_rows, 128),
        "dp",
        split_axis=0,
        concat_axis=0,
        tiled=True,
    )
    act_grad = jnp.einsum(
        "sjcd,jfd->sjcf", recv_grads, expert_down, preferred_element_type=jnp.float32
    )
    gate_low_grad, up_low_grad = silu_back(act_grad, gate_pre, up_pre, sigmoid_gate)
    expert_down_grad = jnp.einsum(
        "sjcf,sjcd->jfd", expert_act, recv_grads, preferred_element_type=jnp.float32
    )
    expert_gate_grad = jnp.einsum(
        "sjcf,sjcd->jfd", gate_low_grad, recv_rows, preferred_element_type=jnp.float32
    )
    expert_up_grad = jnp.einsum(
        "sjcf,sjcd->jfd", up_low_grad, recv_rows, preferred_element_type=jnp.float32
    )
    row_grads = jnp.einsum(
        "sjcf,jfd->sjcd", gate_low_grad, expert_gate, preferred_element_type=jnp.float32
    )
    row_grads = row_grads + jnp.einsum(
        "sjcf,jfd->sjcd", up_low_grad, expert_up, preferred_element_type=jnp.float32
    )
    grads_low = row_grads.astype(jnp.bfloat16).reshape(dp_size, exp_dev, capacity, tile_rows, 128)
    back_out, grads_low = lax.optimization_barrier((back_out, grads_low))
    back_grads = lax.all_to_all(
        grads_low,
        "dp",
        split_axis=0,
        concat_axis=0,
        tiled=True,
    )
    shared_pre_gate = jnp.dot(normed_two, gate_shared, preferred_element_type=jnp.float32)
    shared_pre_up = jnp.dot(normed_two, up_shared, preferred_element_type=jnp.float32)
    shared_sigmoid = jax.nn.sigmoid(shared_pre_gate)
    shared_act = (shared_pre_gate * shared_sigmoid * shared_pre_up).astype(jnp.bfloat16)
    shared_out = jnp.einsum(
        "tf,df->td", shared_act, down_shared_t, preferred_element_type=jnp.float32
    )
    shared_act_grad = jnp.dot(grad_seq, down_shared_t, preferred_element_type=jnp.float32)
    shared_gate_low, shared_up_low = silu_back(
        shared_act_grad, shared_pre_gate, shared_pre_up, shared_sigmoid
    )
    shared_down_grad_t = jnp.dot(grad_seq.T, shared_act, preferred_element_type=jnp.float32)
    shared_gate_grad = jnp.dot(normed_two.T, shared_gate_low, preferred_element_type=jnp.float32)
    shared_up_grad = jnp.dot(normed_two.T, shared_up_low, preferred_element_type=jnp.float32)
    shared_back = jnp.einsum(
        "tf,df->td", shared_gate_low, gate_shared, preferred_element_type=jnp.float32
    )
    shared_back = shared_back + jnp.einsum(
        "tf,df->td", shared_up_low, up_shared, preferred_element_type=jnp.float32
    )
    shared_grads_in = jnp.concatenate(
        [shared_gate_grad, shared_up_grad, shared_down_grad_t], 1
    ).astype(jnp.bfloat16)
    grad_seq_f = grad_seq.astype(jnp.float32)
    table_rows = experts * capacity
    feed_part, back_part, gate_cols = combine_rows(
        slot_index.reshape(seq_len, top_count),
        back_out.reshape(table_rows, tile_rows, 128),
        back_grads.reshape(table_rows, tile_rows, 128),
        gate_values,
        grad_seq,
        shared_out,
        shared_back,
    )
    gate_part = gate_cols[:, :top_count]
    feed_own = jnp.sum(
        lax.all_to_all(
            feed_part.reshape(tensor_size, tok_dev, D), "tensor", split_axis=0, concat_axis=0, tiled=True
        ).astype(jnp.float32),
        0,
    )
    reduced_back = lax.psum(
        jnp.concatenate([back_part, gate_cols.astype(jnp.bfloat16)], 1), "tensor"
    ).astype(jnp.float32)
    normed_two_grad = reduced_back[:, :D]
    gate_grads = reduced_back[:, D : D + top_count]
    weighted_total = jnp.sum(gate_values * gate_grads, -1, keepdims=True)
    chosen_grads = gate_values * (gate_grads - weighted_total)
    logit_grads = jnp.sum(jnp.where(chosen_hot, chosen_grads[:, :, None], 0.0), 1)
    normed_two_grad = normed_two_grad + jnp.dot(
        logit_grads, router_weights.astype(jnp.float32).T, precision=HIGH
    )
    residual_grad = grad_seq_f + norm_back(residual_all, scale_two, gain_two, normed_two_grad)
    branch_grad = residual_grad.astype(jnp.bfloat16)
    shared_grads_in, branch_grad = lax.optimization_barrier((shared_grads_in, branch_grad))
    shared_pack = jnp.sum(
        lax.all_to_all(
            shared_grads_in.reshape(dp_size, rows_dp, shared_grads_in.shape[1]),
            "dp",
            split_axis=0,
            concat_axis=0,
            tiled=True,
        ).astype(jnp.float32),
        0,
    )
    output_grad_w_t = jnp.dot(branch_grad.T, mixed_all, preferred_element_type=jnp.float32)
    mixed_grad = (
        jnp.dot(branch_grad, output_weights_t, preferred_element_type=jnp.float32)
        .astype(jnp.bfloat16)
        .reshape(seq_len, head_count, DV)
    )
    keys_nope_grad = jnp.zeros((seq_len, head_count, DN), jnp.float32)
    key_rope_grad = jnp.zeros((seq_len, DR), jnp.float32)
    values_grad = jnp.zeros((seq_len, head_count, DV), jnp.float32)
    query_grad_list = []
    for block_index, rows_start in enumerate(range(0, seq_len, block_rows)):
        query_block = query_low[rows_start : rows_start + block_rows]
        masked = block_scores(query_block, keys_nope, key_rope, rows_start, prefix_len, score_scale)
        prob_full = jnp.exp(masked - lse_list[block_index])
        prob_low = prob_full.astype(jnp.bfloat16)
        mixed_block = mixed_grad[rows_start : rows_start + block_rows]
        prob_grads = jnp.einsum(
            "qhv,khv->hqk", mixed_block, values_low, preferred_element_type=jnp.float32
        )
        row_delta = jnp.sum(prob_full * prob_grads, -1, keepdims=True)
        score_grads = (prob_full * (prob_grads - row_delta)).astype(jnp.bfloat16)
        query_nope_grad = (
            jnp.einsum("hqk,khd->qhd", score_grads, keys_nope, preferred_element_type=jnp.float32)
            * score_scale
        )
        query_rope_grad = (
            jnp.einsum("hqk,kr->qhr", score_grads, key_rope, preferred_element_type=jnp.float32)
            * score_scale
        )
        keys_nope_grad = (
            keys_nope_grad
            + jnp.einsum(
                "hqk,qhd->khd",
                score_grads,
                query_block[..., :DN],
                preferred_element_type=jnp.float32,
            )
            * score_scale
        )
        key_rope_grad = (
            key_rope_grad
            + jnp.einsum(
                "hqk,qhr->kr",
                score_grads,
                query_block[..., DN:],
                preferred_element_type=jnp.float32,
            )
            * score_scale
        )
        values_grad = values_grad + jnp.einsum(
            "hqk,qhv->khv", prob_low, mixed_block, preferred_element_type=jnp.float32
        )
        block_cosines = all_cosines[rows_start : rows_start + block_rows, None, :]
        block_sines = all_sines[rows_start : rows_start + block_rows, None, :]
        query_grad_list.append(
            jnp.concatenate(
                [
                    query_nope_grad,
                    rotate_back(round_trip(query_rope_grad), block_cosines, block_sines),
                ],
                -1,
            ).astype(jnp.bfloat16)
        )
    query_grads = jnp.concatenate(query_grad_list, 0).reshape(seq_len, head_count * (DN + DR))
    feed_own, shared_pack, query_grads = lax.optimization_barrier((feed_own, shared_pack, query_grads))
    output = (residual_own + feed_own).astype(jnp.bfloat16)
    query_grad_w = jnp.dot(normed_all.T, query_grads, preferred_element_type=jnp.float32)
    normed_grad_part = jnp.dot(query_grads, query_weights.T, preferred_element_type=jnp.float32)
    expand_grads = jnp.concatenate(
        [keys_nope_grad.astype(jnp.bfloat16), values_grad.astype(jnp.bfloat16)], -1
    ).reshape(seq_len, head_count * (DN + DV))
    expand_grad_w = jnp.dot(compressed_seq.T, expand_grads, preferred_element_type=jnp.float32)
    compressed_grad_part = jnp.dot(
        expand_grads, expand_weights.T, preferred_element_type=jnp.float32
    )
    latent_grad_part = jnp.concatenate([compressed_grad_part, key_rope_grad], -1)
    attn_grads_in = jnp.concatenate(
        [
            query_grad_w,
            output_grad_w_t,
            expand_grad_w.reshape(dp_size * rows_dp, expand_flat_cols),
        ],
        1,
    )
    token_all = lax.psum(
        jnp.concatenate([normed_grad_part, latent_grad_part], 1).astype(jnp.bfloat16), "tensor"
    ).astype(jnp.float32)
    compressed_grad_all = token_all[:, D : D + KVR]
    kv_gain_full = jnp.sum(compressed_grad_all * compressed_all * scale_kv_all, 0)
    raw_grad_all = jnp.concatenate(
        [
            norm_back(compressed_all, scale_kv_all, gain_kv, compressed_grad_all),
            rotate_back(token_all[:, D + KVR :], all_cosines, all_sines),
        ],
        -1,
    ).astype(jnp.bfloat16)
    normed_grad_all = token_all[:, :D] + jnp.dot(
        raw_grad_all, latent_weights.T, preferred_element_type=jnp.float32
    )
    normed_grad = lax.dynamic_slice_in_dim(normed_grad_all, start_row, tok_dev, 0)
    hidden_grad = lax.dynamic_slice_in_dim(residual_grad, start_row, tok_dev, 0) + norm_back(
        hidden_f, scale_one, gain_one, normed_grad
    )
    row_per = D // (dp_size * tensor_size)

    def own_rows(values):
        split = values.reshape(values.shape[0], dp_size, tensor_size, row_per)
        return lax.dynamic_slice_in_dim(split, tensor_rank, 1, 2).reshape(values.shape[0], -1)

    latent_rows = jnp.dot(own_rows(normed_all).T, raw_grad_all, preferred_element_type=jnp.float32)
    attn_gain_rows = jnp.sum(
        own_rows(normed_grad_all) * own_rows(hidden_all_f) * scale_one_all, 0
    )
    second_gain_rows = jnp.sum(
        own_rows(normed_two_grad) * own_rows(residual_all) * scale_two, 0
    )
    router_rows = jnp.dot(
        own_rows(normed_two).astype(jnp.float32).T, logit_grads, precision=HIGH
    )
    kv_per = kv_gain_full.shape[0] // (dp_size * tensor_size)
    kv_rows_own = lax.dynamic_slice_in_dim(
        kv_gain_full.reshape(dp_size, tensor_size, kv_per), tensor_rank, 1, 1
    ).reshape(dp_size, kv_per)
    kv_column = jnp.pad(kv_rows_own, ((0, 0), (0, row_per - kv_per))).reshape(-1)
    small_pack = jnp.concatenate(
        [
            latent_rows,
            router_rows,
            attn_gain_rows[:, None],
            second_gain_rows[:, None],
            kv_column[:, None],
        ],
        1,
    )
    attn_width = attn_grads_in.shape[1]
    small_width = small_pack.shape[1]
    small_count = row_per * small_width
    small_cols = -(-small_count // rows_dp)
    small_flat = jnp.pad(
        small_pack.reshape(dp_size, small_count), ((0, 0), (0, small_cols * rows_dp - small_count))
    ).reshape(dp_size * rows_dp, small_cols)
    merged_own = lax.psum_scatter(
        jnp.concatenate([attn_grads_in, small_flat], 1), "dp", scatter_dimension=0, tiled=True
    )
    attn_pack = merged_own[:, :attn_width]
    small_own = merged_own[:, attn_width:].reshape(-1)[:small_count].reshape(row_per, small_width)
    cut = [0]
    for width in (latent_cols, experts, 1, 1, 1):
        cut.append(cut[-1] + width)
    latent_proj_grad = small_own[:, cut[0] : cut[1]]
    router_out = small_own[:, cut[1] : cut[2]]
    attn_gain_out = small_own[:, cut[2]]
    second_gain_out = small_own[:, cut[3]]
    latent_gain_out = small_own[:kv_per, cut[4]]
    cut = [0]
    for width in (head_cols, out_cols, expand_flat_cols):
        cut.append(cut[-1] + width)
    query_proj_grad = attn_pack[:, cut[0] : cut[1]]
    output_proj_grad = attn_pack[:, cut[1] : cut[2]].T
    expand_proj_grad = attn_pack[:, cut[2] : cut[3]].reshape(kv_rows, expand_cols)
    shared_gate_out = shared_pack[:, :shared_cols]
    shared_up_out = shared_pack[:, shared_cols : 2 * shared_cols]
    shared_down_out = shared_pack[:, 2 * shared_cols :].T
    return (
        output,
        hidden_grad,
        attn_gain_out,
        query_proj_grad,
        latent_proj_grad,
        latent_gain_out,
        expand_proj_grad,
        output_proj_grad,
        second_gain_out,
        router_out,
        expert_gate_grad,
        expert_up_grad,
        expert_down_grad,
        shared_gate_out,
        shared_up_out,
        shared_down_out,
    )


def solution(mesh):
    return jax.shard_map(
        shards,
        mesh=mesh,
        in_specs=(
            P(("dp", "tensor"), None),
            P("dp", None),
            P("dp"),
            P("dp"),
            P("dp", "tensor"),
            P("dp", None),
            P("dp"),
            P("dp", "tensor"),
            P("tensor", "dp"),
            P("dp"),
            P("dp", None),
            P("dp", "tensor", None),
            P("dp", "tensor", None),
            P("dp", "tensor", None),
            P("dp", "tensor"),
            P("dp", "tensor"),
            P("tensor", "dp"),
            P(("dp", "tensor"), None),
        ),
        out_specs=(
            P(("dp", "tensor"), None),
            P(("dp", "tensor"), None),
            P(("dp", "tensor")),
            P("dp", "tensor"),
            P(("dp", "tensor"), None),
            P(("dp", "tensor")),
            P("dp", "tensor"),
            P("tensor", "dp"),
            P(("dp", "tensor")),
            P(("dp", "tensor"), None),
            P("dp", "tensor", None),
            P("dp", "tensor", None),
            P("dp", "tensor", None),
            P("dp", "tensor"),
            P("dp", "tensor"),
            P("tensor", "dp"),
        ),
        check_vma=False,
    )
```

```python
import math

import jax
import jax.numpy as jnp
from jax import lax
from jax.experimental import pallas as pl
from jax.experimental.pallas import tpu as pltpu
from jax.sharding import PartitionSpec as P

D = 2048
DN = 128
DR = 64
DV = 128
KVR = 512


EPS = 1e-06
HIGH = lax.Precision.HIGHEST
MASKED = -1e30


def norm_scale(values):
    return lax.rsqrt(jnp.mean(values * values, -1, keepdims=True) + EPS)


def norm_back(values, scales, gains, upstream):
    weighted = gains * upstream
    return scales * weighted - values * scales**3 * jnp.mean(values * weighted, -1, keepdims=True)


def rope_tables(positions, rope_width):
    half_width = rope_width // 2
    frequency = 10000.0 ** (-2.0 * jnp.arange(half_width).astype(jnp.float32) / rope_width)
    angles = positions.astype(jnp.float32)[:, None] * frequency[None, :]
    return (jnp.cos(angles), jnp.sin(angles))


def rotate(vectors, cosines, sine_values):
    half_width = vectors.shape[-1] // 2
    front_half = vectors[..., :half_width]
    back_half = vectors[..., half_width:]
    return jnp.concatenate(
        [
            front_half * cosines - back_half * sine_values,
            back_half * cosines + front_half * sine_values,
        ],
        -1,
    )


def rotate_back(gradients, cosines, sine_values):
    half_width = gradients.shape[-1] // 2
    front_half = gradients[..., :half_width]
    back_half = gradients[..., half_width:]
    return jnp.concatenate(
        [
            front_half * cosines + back_half * sine_values,
            back_half * cosines - front_half * sine_values,
        ],
        -1,
    )


def round_trip(values):
    return lax.optimization_barrier(values.astype(jnp.bfloat16)).astype(jnp.float32)


def block_scores(query_block, keys_nope, key_rope, rows_start, prefix_len, score_scale):
    raw_scores = jnp.einsum(
        "qhd,khd->hqk", query_block[..., :DN], keys_nope, preferred_element_type=jnp.float32
    )
    raw_scores = raw_scores + jnp.einsum(
        "qhr,kr->hqk", query_block[..., DN:], key_rope, preferred_element_type=jnp.float32
    )
    query_places = rows_start + jnp.arange(query_block.shape[0])
    key_places = jnp.arange(keys_nope.shape[0])
    visible = (key_places[None, :] <= query_places[:, None]) | (key_places[None, :] < prefix_len)
    return jnp.where(visible[None], raw_scores * score_scale, MASKED)


def silu_back(act_grad, gate_pre, up_pre, sigmoid_gate):
    up_grad = (act_grad * gate_pre * sigmoid_gate).astype(jnp.bfloat16)
    gate_grad = (act_grad * up_pre * sigmoid_gate * (1.0 + gate_pre * (1.0 - sigmoid_gate))).astype(
        jnp.bfloat16
    )
    return (gate_grad, up_grad)


def dispatch_kernel(tok_ref, both_hbm, col_ref, out_ref, both_buf, sems):
    block = both_buf.shape[0]
    tile_rows = both_buf.shape[1] // 2
    last = both_hbm.shape[0] - 1
    base = pl.program_id(0) * block

    def start(r, carry):
        tok = jnp.minimum(tok_ref[base + r], last)
        pltpu.make_async_copy(both_hbm.at[tok], both_buf.at[r], sems.at[r]).start()
        return carry

    lax.fori_loop(0, block, start, 0, unroll=4)

    def finish(r, carry):
        pltpu.make_async_copy(both_hbm.at[0], both_buf.at[r], sems.at[r]).wait()
        return carry

    lax.fori_loop(0, block, finish, 0, unroll=4)
    rows = both_buf[:, :tile_rows, :]
    out_ref[:, :tile_rows, :] = jnp.where(col_ref[0] > 0, rows, jnp.zeros_like(rows))
    out_ref[:, tile_rows:, :] = (
        both_buf[:, tile_rows:, :].astype(jnp.float32) * col_ref[1]
    ).astype(out_ref.dtype)


def dispatch_rows(slot_token, rows, grads, valid, gate, block=128):
    slots = slot_token.shape[0]
    count, width = rows.shape
    tile_rows = width // 128
    cols = jnp.broadcast_to(jnp.stack([valid, gate])[:, :, None, None], (2, slots, 1, 128))
    both = jnp.concatenate([rows, grads], 1).reshape(count, 2 * tile_rows, 128)
    out = pl.pallas_call(
        dispatch_kernel,
        out_shape=jax.ShapeDtypeStruct((slots, 2 * tile_rows, 128), rows.dtype),
        grid_spec=pltpu.PrefetchScalarGridSpec(
            num_scalar_prefetch=1,
            grid=(slots // block,),
            in_specs=[
                pl.BlockSpec(memory_space=pl.ANY),
                pl.BlockSpec((2, block, 1, 128), lambda i, tok: (0, i, 0, 0)),
            ],
            out_specs=pl.BlockSpec((block, 2 * tile_rows, 128), lambda i, tok: (i, 0, 0)),
            scratch_shapes=[
                pltpu.VMEM((block, 2 * tile_rows, 128), rows.dtype),
                pltpu.SemaphoreType.DMA((block,)),
            ],
        ),
        cost_estimate=pl.CostEstimate(
            flops=slots * width, transcendentals=0, bytes_accessed=4 * slots * 2 * width
        ),
    )(slot_token, both, cols)
    return out


def combine_kernel(
    slot_ref, out_hbm, back_hbm, gate_ref, grad_ref, shared_out_ref, shared_back_ref,
    feed_ref, back_ref, part_ref, picked_out, picked_back, sems,
):
    top = picked_out.shape[0]
    block = picked_out.shape[1]
    last = out_hbm.shape[0] - 1
    base = pl.program_id(0) * block

    def start(r, carry):
        for k in range(top):
            slot = jnp.clip(slot_ref[(base + r) * top + k], 0, last)
            pltpu.make_async_copy(out_hbm.at[slot], picked_out.at[k, r], sems.at[0, k, r]).start()
            pltpu.make_async_copy(back_hbm.at[slot], picked_back.at[k, r], sems.at[1, k, r]).start()
        return carry

    lax.fori_loop(0, block, start, 0, unroll=2)

    def finish(r, carry):
        for k in range(top):
            pltpu.make_async_copy(out_hbm.at[0], picked_out.at[k, r], sems.at[0, k, r]).wait()
            pltpu.make_async_copy(back_hbm.at[0], picked_back.at[k, r], sems.at[1, k, r]).wait()
        return carry

    lax.fori_loop(0, block, finish, 0, unroll=2)
    grad = grad_ref[...].astype(jnp.float32)
    weighted = None
    backs = None
    lanes = lax.broadcasted_iota(jnp.int32, part_ref.shape, 2)
    parts = jnp.zeros(part_ref.shape, jnp.float32)
    for k in range(top):
        out_k = picked_out[k].astype(jnp.float32)
        term = gate_ref[k] * out_k
        weighted = term if weighted is None else weighted + term
        back_k = picked_back[k].astype(jnp.float32)
        backs = back_k if backs is None else backs + back_k
        dot_k = jnp.sum(jnp.sum(grad * out_k, 2, keepdims=True), 1, keepdims=True)
        parts = jnp.where(lanes == k, dot_k, parts)
    feed_ref[...] = (shared_out_ref[...] + weighted).astype(feed_ref.dtype)
    back_ref[...] = (backs + shared_back_ref[...]).astype(back_ref.dtype)
    part_ref[...] = parts


def combine_rows(slot_index, out_table, back_table, gate_values, grad, shared_out, shared_back, block=128):
    tokens, top = gate_values.shape
    width = grad.shape[1]
    tile_rows = width // 128
    gates = jnp.broadcast_to(gate_values.T[:, :, None, None], (top, tokens, 1, 128))
    row_spec = pl.BlockSpec((block, tile_rows, 128), lambda i, s: (i, 0, 0))
    feed, back, parts = pl.pallas_call(
        combine_kernel,
        out_shape=(
            jax.ShapeDtypeStruct((tokens, tile_rows, 128), jnp.bfloat16),
            jax.ShapeDtypeStruct((tokens, tile_rows, 128), jnp.bfloat16),
            jax.ShapeDtypeStruct((tokens, 1, 128), jnp.float32),
        ),
        grid_spec=pltpu.PrefetchScalarGridSpec(
            num_scalar_prefetch=1,
            grid=(tokens // block,),
            in_specs=[
                pl.BlockSpec(memory_space=pl.ANY),
                pl.BlockSpec(memory_space=pl.ANY),
                pl.BlockSpec((top, block, 1, 128), lambda i, s: (0, i, 0, 0)),
                row_spec,
                row_spec,
                row_spec,
            ],
            out_specs=[row_spec, row_spec, pl.BlockSpec((block, 1, 128), lambda i, s: (i, 0, 0))],
            scratch_shapes=[
                pltpu.VMEM((top, block, tile_rows, 128), out_table.dtype),
                pltpu.VMEM((top, block, tile_rows, 128), back_table.dtype),
                pltpu.SemaphoreType.DMA((2, top, block)),
            ],
        ),
        cost_estimate=pl.CostEstimate(
            flops=8 * tokens * top * width,
            transcendentals=0,
            bytes_accessed=tokens * (top * 4 * width + 2 * width + 8 * width + 4 * width),
        ),
    )(
        slot_index.reshape(-1),
        out_table,
        back_table,
        gates,
        grad.reshape(tokens, tile_rows, 128),
        shared_out.reshape(tokens, tile_rows, 128),
        shared_back.reshape(tokens, tile_rows, 128),
    )
    return feed.reshape(tokens, width), back.reshape(tokens, width), parts[:, 0, :top]


def shards(
    hidden,
    routes,
    prefix,
    attn_gain,
    query_proj,
    latent_proj,
    latent_gain,
    expand_proj,
    output_proj,
    second_gain,
    router_proj,
    expert_gate,
    expert_up,
    expert_down,
    shared_gate,
    shared_up,
    shared_down,
    out_grad,
):
    tok_dev = hidden.shape[0]
    tensor_size = lax.axis_size("tensor")
    tensor_rank = lax.axis_index("tensor")
    dp_size = lax.axis_size("dp")
    seq_len = tok_dev * tensor_size
    start_row = tensor_rank * tok_dev
    rows_dp = attn_gain.shape[0]
    kv_rows = latent_gain.shape[0]
    head_cols = query_proj.shape[1]
    latent_cols = latent_proj.shape[1]
    expand_cols = expand_proj.shape[1]
    expand_flat_cols = kv_rows * expand_cols // rows_dp
    first_pack = jnp.concatenate(
        [
            query_proj,
            latent_proj,
            expand_proj.reshape(rows_dp, expand_flat_cols),
            attn_gain[:, None],
            jnp.pad(latent_gain, (0, rows_dp - kv_rows))[:, None],
        ],
        1,
    )
    first_all = lax.all_gather(first_pack, "dp", axis=0, tiled=True)
    cut = [0]
    for width in (head_cols, latent_cols, expand_flat_cols, 1, 1):
        cut.append(cut[-1] + width)
    query_weights = first_all[:, cut[0] : cut[1]]
    latent_weights = first_all[:, cut[1] : cut[2]]
    expand_weights = first_all[:, cut[2] : cut[3]].reshape(dp_size * kv_rows, expand_cols)
    attn_gains = first_all[:, cut[3]]
    kv_gains = first_all[:, cut[4]].reshape(dp_size, rows_dp)[:, :kv_rows].reshape(-1)
    out_cols = output_proj.shape[0]
    experts = router_proj.shape[1]
    shared_cols = shared_gate.shape[1]
    second_pack = jnp.concatenate([output_proj.T, second_gain[:, None], router_proj], 1)
    second_all = lax.all_gather(second_pack, "dp", axis=0, tiled=True)
    output_weights_t = second_all[:, :out_cols]
    second_gains = second_all[:, out_cols]
    router_weights = second_all[:, out_cols + 1 :]
    shared_local = jnp.concatenate([shared_gate, shared_up, shared_down.T], 1)

    hidden_all = lax.all_gather(hidden, "tensor", axis=0, tiled=True)
    grad_blocks = jnp.broadcast_to(out_grad[None], (tensor_size,) + out_grad.shape)
    grad_blocks, hidden_all = lax.optimization_barrier((grad_blocks, hidden_all))
    grad_seq = lax.all_to_all(
        grad_blocks, "tensor", split_axis=0, concat_axis=0, tiled=True
    ).reshape(tensor_size * tok_dev, D)
    grad_seq, query_weights, latent_weights = lax.optimization_barrier(
        (grad_seq, query_weights, latent_weights)
    )
    hidden_all_f = hidden_all.astype(jnp.float32)
    scale_one_all = norm_scale(hidden_all_f)
    gain_one = attn_gains.astype(jnp.float32)
    normed_all = (hidden_all_f * scale_one_all * gain_one).astype(jnp.bfloat16)
    hidden_f = lax.dynamic_slice_in_dim(hidden_all_f, start_row, tok_dev, 0)
    scale_one = lax.dynamic_slice_in_dim(scale_one_all, start_row, tok_dev, 0)
    normed_own = lax.dynamic_slice_in_dim(normed_all, start_row, tok_dev, 0)
    latent_raw_all = jnp.dot(normed_all, latent_weights, preferred_element_type=jnp.float32)
    compressed_all = latent_raw_all[:, :KVR]
    scale_kv_all = norm_scale(compressed_all)
    gain_kv = kv_gains.astype(jnp.float32)
    all_cosines, all_sines = rope_tables(jnp.arange(seq_len), DR)
    latent_seq = jnp.concatenate(
        [
            compressed_all * scale_kv_all * gain_kv,
            rotate(latent_raw_all[:, KVR:], all_cosines, all_sines),
        ],
        -1,
    ).astype(jnp.bfloat16)
    compressed = lax.dynamic_slice_in_dim(compressed_all, start_row, tok_dev, 0)
    scale_kv = lax.dynamic_slice_in_dim(scale_kv_all, start_row, tok_dev, 0)
    own_cosines = lax.dynamic_slice_in_dim(all_cosines, start_row, tok_dev, 0)
    own_sines = lax.dynamic_slice_in_dim(all_sines, start_row, tok_dev, 0)
    head_count = query_weights.shape[1] // (DN + DR)
    query_raw = jnp.dot(normed_all, query_weights, preferred_element_type=jnp.float32).reshape(
        seq_len, head_count, DN + DR
    )
    query_low = jnp.concatenate(
        [
            query_raw[..., :DN],
            rotate(query_raw[..., DN:], all_cosines[:, None, :], all_sines[:, None, :]),
        ],
        -1,
    ).astype(jnp.bfloat16)
    compressed_seq = latent_seq[:, :KVR]
    key_rope = latent_seq[:, KVR:]
    expanded = jnp.dot(compressed_seq, expand_weights, preferred_element_type=jnp.float32).reshape(
        seq_len, head_count, DN + DV
    )
    keys_nope = expanded[..., :DN].astype(jnp.bfloat16)
    values_low = expanded[..., DN:].astype(jnp.bfloat16)
    score_scale = 1.0 / math.sqrt(DN + DR)
    block_rows = min(512, seq_len)
    prefix_len = prefix[0]
    lse_list = []
    mixed_list = []
    for rows_start in range(0, seq_len, block_rows):
        query_block = query_low[rows_start : rows_start + block_rows]
        masked = block_scores(query_block, keys_nope, key_rope, rows_start, prefix_len, score_scale)
        top_score = jnp.max(masked, -1, keepdims=True)
        exp_scores = jnp.exp(masked - top_score)
        totals = jnp.sum(exp_scores, -1, keepdims=True)
        prob_low = (exp_scores / totals).astype(jnp.bfloat16)
        lse_list.append(top_score + jnp.log(totals))
        mixed_list.append(
            jnp.einsum(
                "hqk,khv->qhv", prob_low, values_low, preferred_element_type=jnp.float32
            ).astype(jnp.bfloat16)
        )
    mixed_all = jnp.concatenate(mixed_list, 0).reshape(seq_len, head_count * DV)
    attn_part = jnp.einsum(
        "tk,dk->td", mixed_all, output_weights_t, preferred_element_type=jnp.float32
    )
    top_count = routes.shape[1]
    chosen_hot = routes[:, :, None] == jnp.arange(experts)[None, None, :]
    assignments = seq_len * top_count
    flat_hot = chosen_hot.reshape(assignments, experts).astype(jnp.bfloat16)
    lower = (jnp.arange(assignments)[:, None] > jnp.arange(assignments)[None, :]).astype(jnp.bfloat16)
    earlier = jnp.dot(lower, flat_hot, preferred_element_type=jnp.float32)
    slot_pos = jnp.sum(earlier * flat_hot.astype(jnp.float32), -1).astype(jnp.int32)
    expert_ids = routes.reshape(-1)
    exp_dev = expert_gate.shape[0]
    capacity = tensor_size * (5 * seq_len * top_count // (4 * experts * tensor_size))
    slot_index = expert_ids * capacity + slot_pos
    token_ids = jnp.arange(seq_len * top_count) // top_count
    slot_token = jnp.full((experts * capacity,), seq_len, jnp.int32).at[slot_index].set(token_ids)
    slot_valid = (slot_token < seq_len).astype(jnp.float32)
    slot_index, slot_token, slot_valid, attn_part = lax.optimization_barrier(
        (slot_index, slot_token, slot_valid, attn_part)
    )
    branch_all = lax.psum(attn_part.astype(jnp.bfloat16), "tensor").astype(jnp.float32)
    shared_local, branch_all = lax.optimization_barrier((shared_local, branch_all))
    residual_all = hidden_all_f + branch_all
    residual_own = lax.dynamic_slice_in_dim(residual_all, start_row, tok_dev, 0)
    scale_two = norm_scale(residual_all)
    gain_two = second_gains.astype(jnp.float32)
    normed_two = (residual_all * scale_two * gain_two).astype(jnp.bfloat16)
    logits = jnp.dot(normed_two, router_weights, preferred_element_type=jnp.float32)
    chosen_logits = jnp.sum(jnp.where(chosen_hot, logits[:, None, :], 0.0), -1)
    gate_values = jax.nn.softmax(chosen_logits, axis=-1)
    slot_gate = (
        jnp.zeros((experts * capacity,), jnp.float32).at[slot_index].set(gate_values.reshape(-1))
    )
    tile_rows = D // 128
    send_both = dispatch_rows(slot_token, normed_two, grad_seq, slot_valid, slot_gate).reshape(
        dp_size, exp_dev, capacity, 2 * tile_rows, 128
    )
    shared_all = lax.all_gather(shared_local, "dp", axis=0, tiled=True)
    shared_all, send_both = lax.optimization_barrier((shared_all, send_both))
    gate_shared = shared_all[:, :shared_cols]
    up_shared = shared_all[:, shared_cols : 2 * shared_cols]
    down_shared_t = shared_all[:, 2 * shared_cols :]
    recv_both = lax.all_to_all(send_both, "dp", split_axis=0, concat_axis=0, tiled=True)
    recv_both = recv_both.reshape(dp_size, exp_dev, capacity, 2 * D)
    recv_rows = recv_both[..., :D]
    recv_grads = recv_both[..., D:]
    gate_pre = jnp.einsum(
        "sjcd,jfd->sjcf", recv_rows, expert_gate, preferred_element_type=jnp.float32
    )
    up_pre = jnp.einsum("sjcd,jfd->sjcf", recv_rows, expert_up, preferred_element_type=jnp.float32)
    sigmoid_gate = jax.nn.sigmoid(gate_pre)
    expert_act = (gate_pre * sigmoid_gate * up_pre).astype(jnp.bfloat16)
    expert_out = jnp.einsum(
        "sjcf,jfd->sjcd", expert_act, expert_down, preferred_element_type=jnp.float32
    )
    back_out = lax.all_to_all(
        expert_out.astype(jnp.bfloat16).reshape(dp_size, exp_dev, capacity, tile_rows, 128),
        "dp",
        split_axis=0,
        concat_axis=0,
        tiled=True,
    )
    act_grad = jnp.einsum(
        "sjcd,jfd->sjcf", recv_grads, expert_down, preferred_element_type=jnp.float32
    )
    gate_low_grad, up_low_grad = silu_back(act_grad, gate_pre, up_pre, sigmoid_gate)
    expert_down_grad = jnp.einsum(
        "sjcf,sjcd->jfd", expert_act, recv_grads, preferred_element_type=jnp.float32
    )
    expert_gate_grad = jnp.einsum(
        "sjcf,sjcd->jfd", gate_low_grad, recv_rows, preferred_element_type=jnp.float32
    )
    expert_up_grad = jnp.einsum(
        "sjcf,sjcd->jfd", up_low_grad, recv_rows, preferred_element_type=jnp.float32
    )
    row_grads = jnp.einsum(
        "sjcf,jfd->sjcd", gate_low_grad, expert_gate, preferred_element_type=jnp.float32
    )
    row_grads = row_grads + jnp.einsum(
        "sjcf,jfd->sjcd", up_low_grad, expert_up, preferred_element_type=jnp.float32
    )
    grads_low = row_grads.astype(jnp.bfloat16).reshape(dp_size, exp_dev, capacity, tile_rows, 128)
    back_out, grads_low = lax.optimization_barrier((back_out, grads_low))
    back_grads = lax.all_to_all(
        grads_low,
        "dp",
        split_axis=0,
        concat_axis=0,
        tiled=True,
    )
    shared_pre_gate = jnp.dot(normed_two, gate_shared, preferred_element_type=jnp.float32)
    shared_pre_up = jnp.dot(normed_two, up_shared, preferred_element_type=jnp.float32)
    shared_sigmoid = jax.nn.sigmoid(shared_pre_gate)
    shared_act = (shared_pre_gate * shared_sigmoid * shared_pre_up).astype(jnp.bfloat16)
    shared_out = jnp.einsum(
        "tf,df->td", shared_act, down_shared_t, preferred_element_type=jnp.float32
    )
    shared_act_grad = jnp.dot(grad_seq, down_shared_t, preferred_element_type=jnp.float32)
    shared_gate_low, shared_up_low = silu_back(
        shared_act_grad, shared_pre_gate, shared_pre_up, shared_sigmoid
    )
    shared_down_grad_t = jnp.dot(grad_seq.T, shared_act, preferred_element_type=jnp.float32)
    shared_gate_grad = jnp.dot(normed_two.T, shared_gate_low, preferred_element_type=jnp.float32)
    shared_up_grad = jnp.dot(normed_two.T, shared_up_low, preferred_element_type=jnp.float32)
    shared_back = jnp.einsum(
        "tf,df->td", shared_gate_low, gate_shared, preferred_element_type=jnp.float32
    )
    shared_back = shared_back + jnp.einsum(
        "tf,df->td", shared_up_low, up_shared, preferred_element_type=jnp.float32
    )
    shared_grads_in = jnp.concatenate(
        [shared_gate_grad, shared_up_grad, shared_down_grad_t], 1
    ).astype(jnp.bfloat16)
    grad_seq_f = grad_seq.astype(jnp.float32)
    table_rows = experts * capacity
    feed_part, back_part, gate_cols = combine_rows(
        slot_index.reshape(seq_len, top_count),
        back_out.reshape(table_rows, tile_rows, 128),
        back_grads.reshape(table_rows, tile_rows, 128),
        gate_values,
        grad_seq,
        shared_out,
        shared_back,
    )
    gate_part = gate_cols[:, :top_count]
    feed_own = jnp.sum(
        lax.all_to_all(
            feed_part.reshape(tensor_size, tok_dev, D), "tensor", split_axis=0, concat_axis=0, tiled=True
        ).astype(jnp.float32),
        0,
    )
    reduced_back = lax.psum(
        jnp.concatenate([back_part, gate_cols.astype(jnp.bfloat16)], 1), "tensor"
    ).astype(jnp.float32)
    normed_two_grad = reduced_back[:, :D]
    gate_grads = reduced_back[:, D : D + top_count]
    weighted_total = jnp.sum(gate_values * gate_grads, -1, keepdims=True)
    chosen_grads = gate_values * (gate_grads - weighted_total)
    logit_grads = jnp.sum(jnp.where(chosen_hot, chosen_grads[:, :, None], 0.0), 1)
    normed_two_grad = normed_two_grad + jnp.dot(
        logit_grads, router_weights.astype(jnp.float32).T, precision=HIGH
    )
    residual_grad = grad_seq_f + norm_back(residual_all, scale_two, gain_two, normed_two_grad)
    branch_grad = residual_grad.astype(jnp.bfloat16)
    shared_grads_in, branch_grad = lax.optimization_barrier((shared_grads_in, branch_grad))
    shared_pack = jnp.sum(
        lax.all_to_all(
            shared_grads_in.reshape(dp_size, rows_dp, shared_grads_in.shape[1]),
            "dp",
            split_axis=0,
            concat_axis=0,
            tiled=True,
        ).astype(jnp.float32),
        0,
    )
    output_grad_w_t = jnp.dot(branch_grad.T, mixed_all, preferred_element_type=jnp.float32)
    mixed_grad = (
        jnp.dot(branch_grad, output_weights_t, preferred_element_type=jnp.float32)
        .astype(jnp.bfloat16)
        .reshape(seq_len, head_count, DV)
    )
    keys_nope_grad = jnp.zeros((seq_len, head_count, DN), jnp.float32)
    key_rope_grad = jnp.zeros((seq_len, DR), jnp.float32)
    values_grad = jnp.zeros((seq_len, head_count, DV), jnp.float32)
    query_grad_list = []
    for block_index, rows_start in enumerate(range(0, seq_len, block_rows)):
        query_block = query_low[rows_start : rows_start + block_rows]
        masked = block_scores(query_block, keys_nope, key_rope, rows_start, prefix_len, score_scale)
        prob_full = jnp.exp(masked - lse_list[block_index])
        prob_low = prob_full.astype(jnp.bfloat16)
        mixed_block = mixed_grad[rows_start : rows_start + block_rows]
        prob_grads = jnp.einsum(
            "qhv,khv->hqk", mixed_block, values_low, preferred_element_type=jnp.float32
        )
        row_delta = jnp.sum(prob_full * prob_grads, -1, keepdims=True)
        score_grads = (prob_full * (prob_grads - row_delta)).astype(jnp.bfloat16)
        query_nope_grad = (
            jnp.einsum("hqk,khd->qhd", score_grads, keys_nope, preferred_element_type=jnp.float32)
            * score_scale
        )
        query_rope_grad = (
            jnp.einsum("hqk,kr->qhr", score_grads, key_rope, preferred_element_type=jnp.float32)
            * score_scale
        )
        keys_nope_grad = (
            keys_nope_grad
            + jnp.einsum(
                "hqk,qhd->khd",
                score_grads,
                query_block[..., :DN],
                preferred_element_type=jnp.float32,
            )
            * score_scale
        )
        key_rope_grad = (
            key_rope_grad
            + jnp.einsum(
                "hqk,qhr->kr",
                score_grads,
                query_block[..., DN:],
                preferred_element_type=jnp.float32,
            )
            * score_scale
        )
        values_grad = values_grad + jnp.einsum(
            "hqk,qhv->khv", prob_low, mixed_block, preferred_element_type=jnp.float32
        )
        block_cosines = all_cosines[rows_start : rows_start + block_rows, None, :]
        block_sines = all_sines[rows_start : rows_start + block_rows, None, :]
        query_grad_list.append(
            jnp.concatenate(
                [
                    query_nope_grad,
                    rotate_back(round_trip(query_rope_grad), block_cosines, block_sines),
                ],
                -1,
            ).astype(jnp.bfloat16)
        )
    query_grads = jnp.concatenate(query_grad_list, 0).reshape(seq_len, head_count * (DN + DR))
    feed_own, shared_pack, query_grads = lax.optimization_barrier((feed_own, shared_pack, query_grads))
    output = (residual_own + feed_own).astype(jnp.bfloat16)
    query_grad_w = jnp.dot(normed_all.T, query_grads, preferred_element_type=jnp.float32)
    normed_grad_part = jnp.dot(query_grads, query_weights.T, preferred_element_type=jnp.float32)
    expand_grads = jnp.concatenate(
        [keys_nope_grad.astype(jnp.bfloat16), values_grad.astype(jnp.bfloat16)], -1
    ).reshape(seq_len, head_count * (DN + DV))
    expand_grad_w = jnp.dot(compressed_seq.T, expand_grads, preferred_element_type=jnp.float32)
    compressed_grad_part = jnp.dot(
        expand_grads, expand_weights.T, preferred_element_type=jnp.float32
    )
    latent_grad_part = jnp.concatenate([compressed_grad_part, key_rope_grad], -1)
    attn_grads_in = jnp.concatenate(
        [
            query_grad_w,
            output_grad_w_t,
            expand_grad_w.reshape(dp_size * rows_dp, expand_flat_cols),
        ],
        1,
    )
    token_all = lax.psum(
        jnp.concatenate([normed_grad_part, latent_grad_part], 1).astype(jnp.bfloat16), "tensor"
    ).astype(jnp.float32)
    compressed_grad_all = token_all[:, D : D + KVR]
    kv_gain_full = jnp.sum(compressed_grad_all * compressed_all * scale_kv_all, 0)
    raw_grad_all = jnp.concatenate(
        [
            norm_back(compressed_all, scale_kv_all, gain_kv, compressed_grad_all),
            rotate_back(token_all[:, D + KVR :], all_cosines, all_sines),
        ],
        -1,
    ).astype(jnp.bfloat16)
    normed_grad_all = token_all[:, :D] + jnp.dot(
        raw_grad_all, latent_weights.T, preferred_element_type=jnp.float32
    )
    normed_grad = lax.dynamic_slice_in_dim(normed_grad_all, start_row, tok_dev, 0)
    hidden_grad = lax.dynamic_slice_in_dim(residual_grad, start_row, tok_dev, 0) + norm_back(
        hidden_f, scale_one, gain_one, normed_grad
    )
    row_per = D // (dp_size * tensor_size)

    def own_rows(values):
        split = values.reshape(values.shape[0], dp_size, tensor_size, row_per)
        return lax.dynamic_slice_in_dim(split, tensor_rank, 1, 2).reshape(values.shape[0], -1)

    latent_rows = jnp.dot(own_rows(normed_all).T, raw_grad_all, preferred_element_type=jnp.float32)
    attn_gain_rows = jnp.sum(
        own_rows(normed_grad_all) * own_rows(hidden_all_f) * scale_one_all, 0
    )
    second_gain_rows = jnp.sum(
        own_rows(normed_two_grad) * own_rows(residual_all) * scale_two, 0
    )
    router_rows = jnp.dot(
        own_rows(normed_two).astype(jnp.float32).T, logit_grads, precision=HIGH
    )
    kv_per = kv_gain_full.shape[0] // (dp_size * tensor_size)
    kv_rows_own = lax.dynamic_slice_in_dim(
        kv_gain_full.reshape(dp_size, tensor_size, kv_per), tensor_rank, 1, 1
    ).reshape(dp_size, kv_per)
    kv_column = jnp.pad(kv_rows_own, ((0, 0), (0, row_per - kv_per))).reshape(-1)
    small_pack = jnp.concatenate(
        [
            latent_rows,
            router_rows,
            attn_gain_rows[:, None],
            second_gain_rows[:, None],
            kv_column[:, None],
        ],
        1,
    )
    attn_width = attn_grads_in.shape[1]
    small_width = small_pack.shape[1]
    small_count = row_per * small_width
    small_cols = -(-small_count // rows_dp)
    small_flat = jnp.pad(
        small_pack.reshape(dp_size, small_count), ((0, 0), (0, small_cols * rows_dp - small_count))
    ).reshape(dp_size * rows_dp, small_cols)
    merged_own = lax.psum_scatter(
        jnp.concatenate([attn_grads_in, small_flat], 1), "dp", scatter_dimension=0, tiled=True
    )
    attn_pack = merged_own[:, :attn_width]
    small_own = merged_own[:, attn_width:].reshape(-1)[:small_count].reshape(row_per, small_width)
    cut = [0]
    for width in (latent_cols, experts, 1, 1, 1):
        cut.append(cut[-1] + width)
    latent_proj_grad = small_own[:, cut[0] : cut[1]]
    router_out = small_own[:, cut[1] : cut[2]]
    attn_gain_out = small_own[:, cut[2]]
    second_gain_out = small_own[:, cut[3]]
    latent_gain_out = small_own[:kv_per, cut[4]]
    cut = [0]
    for width in (head_cols, out_cols, expand_flat_cols):
        cut.append(cut[-1] + width)
    query_proj_grad = attn_pack[:, cut[0] : cut[1]]
    output_proj_grad = attn_pack[:, cut[1] : cut[2]].T
    expand_proj_grad = attn_pack[:, cut[2] : cut[3]].reshape(kv_rows, expand_cols)
    shared_gate_out = shared_pack[:, :shared_cols]
    shared_up_out = shared_pack[:, shared_cols : 2 * shared_cols]
    shared_down_out = shared_pack[:, 2 * shared_cols :].T
    return (
        output,
        hidden_grad,
        attn_gain_out,
        query_proj_grad,
        latent_proj_grad,
        latent_gain_out,
        expand_proj_grad,
        output_proj_grad,
        second_gain_out,
        router_out,
        expert_gate_grad,
        expert_up_grad,
        expert_down_grad,
        shared_gate_out,
        shared_up_out,
        shared_down_out,
    )


def solution(mesh):
    return jax.shard_map(
        shards,
        mesh=mesh,
        in_specs=(
            P(("dp", "tensor"), None),
            P("dp", None),
            P("dp"),
            P("dp"),
            P("dp", "tensor"),
            P("dp", None),
            P("dp"),
            P("dp", "tensor"),
            P("tensor", "dp"),
            P("dp"),
            P("dp", None),
            P("dp", "tensor", None),
            P("dp", "tensor", None),
            P("dp", "tensor", None),
            P("dp", "tensor"),
            P("dp", "tensor"),
            P("tensor", "dp"),
            P(("dp", "tensor"), None),
        ),
        out_specs=(
            P(("dp", "tensor"), None),
            P(("dp", "tensor"), None),
            P(("dp", "tensor")),
            P("dp", "tensor"),
            P(("dp", "tensor"), None),
            P(("dp", "tensor")),
            P("dp", "tensor"),
            P("tensor", "dp"),
            P(("dp", "tensor")),
            P(("dp", "tensor"), None),
            P("dp", "tensor", None),
            P("dp", "tensor", None),
            P("dp", "tensor", None),
            P("dp", "tensor"),
            P("dp", "tensor"),
            P("tensor", "dp"),
        ),
        check_vma=False,
    )
```

```python
import math

import jax
import jax.numpy as jnp
from jax import lax
from jax.experimental import pallas as pl
from jax.experimental.pallas import tpu as pltpu
from jax.sharding import PartitionSpec as P

D = 2048
DN = 128
DR = 64
DV = 128
KVR = 512


EPS = 1e-06
HIGH = lax.Precision.HIGHEST
MASKED = -1e30


def norm_scale(values):
    return lax.rsqrt(jnp.mean(values * values, -1, keepdims=True) + EPS)


def norm_back(values, scales, gains, upstream):
    weighted = gains * upstream
    return scales * weighted - values * scales**3 * jnp.mean(values * weighted, -1, keepdims=True)


def rope_tables(positions, rope_width):
    half_width = rope_width // 2
    frequency = 10000.0 ** (-2.0 * jnp.arange(half_width).astype(jnp.float32) / rope_width)
    angles = positions.astype(jnp.float32)[:, None] * frequency[None, :]
    return (jnp.cos(angles), jnp.sin(angles))


def rotate(vectors, cosines, sine_values):
    half_width = vectors.shape[-1] // 2
    front_half = vectors[..., :half_width]
    back_half = vectors[..., half_width:]
    return jnp.concatenate(
        [
            front_half * cosines - back_half * sine_values,
            back_half * cosines + front_half * sine_values,
        ],
        -1,
    )


def rotate_back(gradients, cosines, sine_values):
    half_width = gradients.shape[-1] // 2
    front_half = gradients[..., :half_width]
    back_half = gradients[..., half_width:]
    return jnp.concatenate(
        [
            front_half * cosines + back_half * sine_values,
            back_half * cosines - front_half * sine_values,
        ],
        -1,
    )


def round_trip(values):
    return lax.optimization_barrier(values.astype(jnp.bfloat16)).astype(jnp.float32)


def block_scores(query_block, keys_nope, key_rope, rows_start, prefix_len, score_scale):
    raw_scores = jnp.einsum(
        "qhd,khd->hqk", query_block[..., :DN], keys_nope, preferred_element_type=jnp.float32
    )
    raw_scores = raw_scores + jnp.einsum(
        "qhr,kr->hqk", query_block[..., DN:], key_rope, preferred_element_type=jnp.float32
    )
    query_places = rows_start + jnp.arange(query_block.shape[0])
    key_places = jnp.arange(keys_nope.shape[0])
    visible = (key_places[None, :] <= query_places[:, None]) | (key_places[None, :] < prefix_len)
    return jnp.where(visible[None], raw_scores * score_scale, MASKED)


def silu_back(act_grad, gate_pre, up_pre, sigmoid_gate):
    up_grad = (act_grad * gate_pre * sigmoid_gate).astype(jnp.bfloat16)
    gate_grad = (act_grad * up_pre * sigmoid_gate * (1.0 + gate_pre * (1.0 - sigmoid_gate))).astype(
        jnp.bfloat16
    )
    return (gate_grad, up_grad)


def dispatch_kernel(tok_ref, both_hbm, col_ref, out_ref, both_buf, sems):
    block = both_buf.shape[1]
    tile_rows = both_buf.shape[2] // 2
    last = both_hbm.shape[0] - 1
    step = pl.program_id(0)
    steps = pl.num_programs(0)

    def fetch(index, slot):
        def start(r, carry):
            tok = jnp.minimum(tok_ref[index * block + r], last)
            pltpu.make_async_copy(both_hbm.at[tok], both_buf.at[slot, r], sems.at[slot, r]).start()
            return carry

        lax.fori_loop(0, block, start, 0, unroll=4)

    @pl.when(step == 0)
    def _():
        fetch(0, 0)

    @pl.when(step + 1 < steps)
    def _():
        fetch(step + 1, (step + 1) % 2)

    slot = step % 2

    def finish(r, carry):
        pltpu.make_async_copy(both_hbm.at[0], both_buf.at[slot, r], sems.at[slot, r]).wait()
        return carry

    lax.fori_loop(0, block, finish, 0, unroll=4)
    rows = both_buf[slot, :, :tile_rows, :]
    out_ref[:, :tile_rows, :] = jnp.where(col_ref[0] > 0, rows, jnp.zeros_like(rows))
    out_ref[:, tile_rows:, :] = (
        both_buf[slot, :, tile_rows:, :].astype(jnp.float32) * col_ref[1]
    ).astype(out_ref.dtype)


def dispatch_rows(slot_token, rows, grads, valid, gate, block=128):
    slots = slot_token.shape[0]
    count, width = rows.shape
    tile_rows = width // 128
    cols = jnp.broadcast_to(jnp.stack([valid, gate])[:, :, None, None], (2, slots, 1, 128))
    both = jnp.concatenate([rows, grads], 1).reshape(count, 2 * tile_rows, 128)
    out = pl.pallas_call(
        dispatch_kernel,
        out_shape=jax.ShapeDtypeStruct((slots, 2 * tile_rows, 128), rows.dtype),
        grid_spec=pltpu.PrefetchScalarGridSpec(
            num_scalar_prefetch=1,
            grid=(slots // block,),
            in_specs=[
                pl.BlockSpec(memory_space=pl.ANY),
                pl.BlockSpec((2, block, 1, 128), lambda i, tok: (0, i, 0, 0)),
            ],
            out_specs=pl.BlockSpec((block, 2 * tile_rows, 128), lambda i, tok: (i, 0, 0)),
            scratch_shapes=[
                pltpu.VMEM((2, block, 2 * tile_rows, 128), rows.dtype),
                pltpu.SemaphoreType.DMA((2, block)),
            ],
        ),
        compiler_params=pltpu.CompilerParams(dimension_semantics=("arbitrary",)),
        cost_estimate=pl.CostEstimate(
            flops=slots * width, transcendentals=0, bytes_accessed=4 * slots * 2 * width
        ),
    )(slot_token, both, cols)
    return out


def combine_kernel(
    slot_ref, out_hbm, back_hbm, gate_ref, grad_ref, shared_out_ref, shared_back_ref,
    feed_ref, back_ref, part_ref, picked_out, picked_back, sems,
):
    top = picked_out.shape[0]
    block = picked_out.shape[1]
    last = out_hbm.shape[0] - 1
    base = pl.program_id(0) * block

    def start(r, carry):
        for k in range(top):
            slot = jnp.clip(slot_ref[(base + r) * top + k], 0, last)
            pltpu.make_async_copy(out_hbm.at[slot], picked_out.at[k, r], sems.at[0, k, r]).start()
            pltpu.make_async_copy(back_hbm.at[slot], picked_back.at[k, r], sems.at[1, k, r]).start()
        return carry

    lax.fori_loop(0, block, start, 0, unroll=2)

    def finish(r, carry):
        for k in range(top):
            pltpu.make_async_copy(out_hbm.at[0], picked_out.at[k, r], sems.at[0, k, r]).wait()
            pltpu.make_async_copy(back_hbm.at[0], picked_back.at[k, r], sems.at[1, k, r]).wait()
        return carry

    lax.fori_loop(0, block, finish, 0, unroll=2)
    grad = grad_ref[...].astype(jnp.float32)
    weighted = None
    backs = None
    lanes = lax.broadcasted_iota(jnp.int32, part_ref.shape, 2)
    parts = jnp.zeros(part_ref.shape, jnp.float32)
    for k in range(top):
        out_k = picked_out[k].astype(jnp.float32)
        term = gate_ref[k] * out_k
        weighted = term if weighted is None else weighted + term
        back_k = picked_back[k].astype(jnp.float32)
        backs = back_k if backs is None else backs + back_k
        dot_k = jnp.sum(jnp.sum(grad * out_k, 2, keepdims=True), 1, keepdims=True)
        parts = jnp.where(lanes == k, dot_k, parts)
    feed_ref[...] = (shared_out_ref[...] + weighted).astype(feed_ref.dtype)
    back_ref[...] = (backs + shared_back_ref[...]).astype(back_ref.dtype)
    part_ref[...] = parts


def combine_rows(slot_index, out_table, back_table, gate_values, grad, shared_out, shared_back, block=128):
    tokens, top = gate_values.shape
    width = grad.shape[1]
    tile_rows = width // 128
    gates = jnp.broadcast_to(gate_values.T[:, :, None, None], (top, tokens, 1, 128))
    row_spec = pl.BlockSpec((block, tile_rows, 128), lambda i, s: (i, 0, 0))
    feed, back, parts = pl.pallas_call(
        combine_kernel,
        out_shape=(
            jax.ShapeDtypeStruct((tokens, tile_rows, 128), jnp.bfloat16),
            jax.ShapeDtypeStruct((tokens, tile_rows, 128), jnp.bfloat16),
            jax.ShapeDtypeStruct((tokens, 1, 128), jnp.float32),
        ),
        grid_spec=pltpu.PrefetchScalarGridSpec(
            num_scalar_prefetch=1,
            grid=(tokens // block,),
            in_specs=[
                pl.BlockSpec(memory_space=pl.ANY),
                pl.BlockSpec(memory_space=pl.ANY),
                pl.BlockSpec((top, block, 1, 128), lambda i, s: (0, i, 0, 0)),
                row_spec,
                row_spec,
                row_spec,
            ],
            out_specs=[row_spec, row_spec, pl.BlockSpec((block, 1, 128), lambda i, s: (i, 0, 0))],
            scratch_shapes=[
                pltpu.VMEM((top, block, tile_rows, 128), out_table.dtype),
                pltpu.VMEM((top, block, tile_rows, 128), back_table.dtype),
                pltpu.SemaphoreType.DMA((2, top, block)),
            ],
        ),
        cost_estimate=pl.CostEstimate(
            flops=8 * tokens * top * width,
            transcendentals=0,
            bytes_accessed=tokens * (top * 4 * width + 2 * width + 8 * width + 4 * width),
        ),
    )(
        slot_index.reshape(-1),
        out_table,
        back_table,
        gates,
        grad.reshape(tokens, tile_rows, 128),
        shared_out.reshape(tokens, tile_rows, 128),
        shared_back.reshape(tokens, tile_rows, 128),
    )
    return feed.reshape(tokens, width), back.reshape(tokens, width), parts[:, 0, :top]


def shards(
    hidden,
    routes,
    prefix,
    attn_gain,
    query_proj,
    latent_proj,
    latent_gain,
    expand_proj,
    output_proj,
    second_gain,
    router_proj,
    expert_gate,
    expert_up,
    expert_down,
    shared_gate,
    shared_up,
    shared_down,
    out_grad,
):
    tok_dev = hidden.shape[0]
    tensor_size = lax.axis_size("tensor")
    tensor_rank = lax.axis_index("tensor")
    dp_size = lax.axis_size("dp")
    seq_len = tok_dev * tensor_size
    start_row = tensor_rank * tok_dev
    rows_dp = attn_gain.shape[0]
    kv_rows = latent_gain.shape[0]
    head_cols = query_proj.shape[1]
    latent_cols = latent_proj.shape[1]
    expand_cols = expand_proj.shape[1]
    expand_flat_cols = kv_rows * expand_cols // rows_dp
    first_pack = jnp.concatenate(
        [
            query_proj,
            latent_proj,
            expand_proj.reshape(rows_dp, expand_flat_cols),
            attn_gain[:, None],
            jnp.pad(latent_gain, (0, rows_dp - kv_rows))[:, None],
        ],
        1,
    )
    first_all = lax.all_gather(first_pack, "dp", axis=0, tiled=True)
    cut = [0]
    for width in (head_cols, latent_cols, expand_flat_cols, 1, 1):
        cut.append(cut[-1] + width)
    query_weights = first_all[:, cut[0] : cut[1]]
    latent_weights = first_all[:, cut[1] : cut[2]]
    expand_weights = first_all[:, cut[2] : cut[3]].reshape(dp_size * kv_rows, expand_cols)
    attn_gains = first_all[:, cut[3]]
    kv_gains = first_all[:, cut[4]].reshape(dp_size, rows_dp)[:, :kv_rows].reshape(-1)
    out_cols = output_proj.shape[0]
    experts = router_proj.shape[1]
    shared_cols = shared_gate.shape[1]
    second_pack = jnp.concatenate([output_proj.T, second_gain[:, None], router_proj], 1)
    second_all = lax.all_gather(second_pack, "dp", axis=0, tiled=True)
    output_weights_t = second_all[:, :out_cols]
    second_gains = second_all[:, out_cols]
    router_weights = second_all[:, out_cols + 1 :]
    shared_local = jnp.concatenate([shared_gate, shared_up, shared_down.T], 1)

    hidden_all = lax.all_gather(hidden, "tensor", axis=0, tiled=True)
    grad_blocks = jnp.broadcast_to(out_grad[None], (tensor_size,) + out_grad.shape)
    grad_blocks, hidden_all = lax.optimization_barrier((grad_blocks, hidden_all))
    grad_seq = lax.all_to_all(
        grad_blocks, "tensor", split_axis=0, concat_axis=0, tiled=True
    ).reshape(tensor_size * tok_dev, D)
    grad_seq, query_weights, latent_weights = lax.optimization_barrier(
        (grad_seq, query_weights, latent_weights)
    )
    hidden_all_f = hidden_all.astype(jnp.float32)
    scale_one_all = norm_scale(hidden_all_f)
    gain_one = attn_gains.astype(jnp.float32)
    normed_all = (hidden_all_f * scale_one_all * gain_one).astype(jnp.bfloat16)
    hidden_f = lax.dynamic_slice_in_dim(hidden_all_f, start_row, tok_dev, 0)
    scale_one = lax.dynamic_slice_in_dim(scale_one_all, start_row, tok_dev, 0)
    normed_own = lax.dynamic_slice_in_dim(normed_all, start_row, tok_dev, 0)
    latent_raw_all = jnp.dot(normed_all, latent_weights, preferred_element_type=jnp.float32)
    compressed_all = latent_raw_all[:, :KVR]
    scale_kv_all = norm_scale(compressed_all)
    gain_kv = kv_gains.astype(jnp.float32)
    all_cosines, all_sines = rope_tables(jnp.arange(seq_len), DR)
    latent_seq = jnp.concatenate(
        [
            compressed_all * scale_kv_all * gain_kv,
            rotate(latent_raw_all[:, KVR:], all_cosines, all_sines),
        ],
        -1,
    ).astype(jnp.bfloat16)
    compressed = lax.dynamic_slice_in_dim(compressed_all, start_row, tok_dev, 0)
    scale_kv = lax.dynamic_slice_in_dim(scale_kv_all, start_row, tok_dev, 0)
    own_cosines = lax.dynamic_slice_in_dim(all_cosines, start_row, tok_dev, 0)
    own_sines = lax.dynamic_slice_in_dim(all_sines, start_row, tok_dev, 0)
    head_count = query_weights.shape[1] // (DN + DR)
    query_raw = jnp.dot(normed_all, query_weights, preferred_element_type=jnp.float32).reshape(
        seq_len, head_count, DN + DR
    )
    query_low = jnp.concatenate(
        [
            query_raw[..., :DN],
            rotate(query_raw[..., DN:], all_cosines[:, None, :], all_sines[:, None, :]),
        ],
        -1,
    ).astype(jnp.bfloat16)
    compressed_seq = latent_seq[:, :KVR]
    key_rope = latent_seq[:, KVR:]
    expanded = jnp.dot(compressed_seq, expand_weights, preferred_element_type=jnp.float32).reshape(
        seq_len, head_count, DN + DV
    )
    keys_nope = expanded[..., :DN].astype(jnp.bfloat16)
    values_low = expanded[..., DN:].astype(jnp.bfloat16)
    score_scale = 1.0 / math.sqrt(DN + DR)
    block_rows = min(512, seq_len)
    prefix_len = prefix[0]
    lse_list = []
    mixed_list = []
    for rows_start in range(0, seq_len, block_rows):
        query_block = query_low[rows_start : rows_start + block_rows]
        masked = block_scores(query_block, keys_nope, key_rope, rows_start, prefix_len, score_scale)
        top_score = jnp.max(masked, -1, keepdims=True)
        exp_scores = jnp.exp(masked - top_score)
        totals = jnp.sum(exp_scores, -1, keepdims=True)
        prob_low = (exp_scores / totals).astype(jnp.bfloat16)
        lse_list.append(top_score + jnp.log(totals))
        mixed_list.append(
            jnp.einsum(
                "hqk,khv->qhv", prob_low, values_low, preferred_element_type=jnp.float32
            ).astype(jnp.bfloat16)
        )
    mixed_all = jnp.concatenate(mixed_list, 0).reshape(seq_len, head_count * DV)
    attn_part = jnp.einsum(
        "tk,dk->td", mixed_all, output_weights_t, preferred_element_type=jnp.float32
    )
    top_count = routes.shape[1]
    chosen_hot = routes[:, :, None] == jnp.arange(experts)[None, None, :]
    assignments = seq_len * top_count
    flat_hot = chosen_hot.reshape(assignments, experts).astype(jnp.bfloat16)
    lower = (jnp.arange(assignments)[:, None] > jnp.arange(assignments)[None, :]).astype(jnp.bfloat16)
    earlier = jnp.dot(lower, flat_hot, preferred_element_type=jnp.float32)
    slot_pos = jnp.sum(earlier * flat_hot.astype(jnp.float32), -1).astype(jnp.int32)
    expert_ids = routes.reshape(-1)
    exp_dev = expert_gate.shape[0]
    capacity = tensor_size * (5 * seq_len * top_count // (4 * experts * tensor_size))
    slot_index = expert_ids * capacity + slot_pos
    token_ids = jnp.arange(seq_len * top_count) // top_count
    slot_token = jnp.full((experts * capacity,), seq_len, jnp.int32).at[slot_index].set(token_ids)
    slot_valid = (slot_token < seq_len).astype(jnp.float32)
    slot_index, slot_token, slot_valid, attn_part = lax.optimization_barrier(
        (slot_index, slot_token, slot_valid, attn_part)
    )
    branch_all = lax.psum(attn_part.astype(jnp.bfloat16), "tensor").astype(jnp.float32)
    shared_local, branch_all = lax.optimization_barrier((shared_local, branch_all))
    residual_all = hidden_all_f + branch_all
    residual_own = lax.dynamic_slice_in_dim(residual_all, start_row, tok_dev, 0)
    scale_two = norm_scale(residual_all)
    gain_two = second_gains.astype(jnp.float32)
    normed_two = (residual_all * scale_two * gain_two).astype(jnp.bfloat16)
    logits = jnp.dot(normed_two, router_weights, preferred_element_type=jnp.float32)
    chosen_logits = jnp.sum(jnp.where(chosen_hot, logits[:, None, :], 0.0), -1)
    gate_values = jax.nn.softmax(chosen_logits, axis=-1)
    slot_gate = (
        jnp.zeros((experts * capacity,), jnp.float32).at[slot_index].set(gate_values.reshape(-1))
    )
    tile_rows = D // 128
    send_both = dispatch_rows(slot_token, normed_two, grad_seq, slot_valid, slot_gate).reshape(
        dp_size, exp_dev, capacity, 2 * tile_rows, 128
    )
    shared_all = lax.all_gather(shared_local, "dp", axis=0, tiled=True)
    shared_all, send_both = lax.optimization_barrier((shared_all, send_both))
    gate_shared = shared_all[:, :shared_cols]
    up_shared = shared_all[:, shared_cols : 2 * shared_cols]
    down_shared_t = shared_all[:, 2 * shared_cols :]
    recv_both = lax.all_to_all(send_both, "dp", split_axis=0, concat_axis=0, tiled=True)
    recv_both = recv_both.reshape(dp_size, exp_dev, capacity, 2 * D)
    recv_rows = recv_both[..., :D]
    recv_grads = recv_both[..., D:]
    gate_pre = jnp.einsum(
        "sjcd,jfd->sjcf", recv_rows, expert_gate, preferred_element_type=jnp.float32
    )
    up_pre = jnp.einsum("sjcd,jfd->sjcf", recv_rows, expert_up, preferred_element_type=jnp.float32)
    sigmoid_gate = jax.nn.sigmoid(gate_pre)
    expert_act = (gate_pre * sigmoid_gate * up_pre).astype(jnp.bfloat16)
    expert_out = jnp.einsum(
        "sjcf,jfd->sjcd", expert_act, expert_down, preferred_element_type=jnp.float32
    )
    back_out = lax.all_to_all(
        expert_out.astype(jnp.bfloat16).reshape(dp_size, exp_dev, capacity, tile_rows, 128),
        "dp",
        split_axis=0,
        concat_axis=0,
        tiled=True,
    )
    act_grad = jnp.einsum(
        "sjcd,jfd->sjcf", recv_grads, expert_down, preferred_element_type=jnp.float32
    )
    gate_low_grad, up_low_grad = silu_back(act_grad, gate_pre, up_pre, sigmoid_gate)
    expert_down_grad = jnp.einsum(
        "sjcf,sjcd->jfd", expert_act, recv_grads, preferred_element_type=jnp.float32
    )
    expert_gate_grad = jnp.einsum(
        "sjcf,sjcd->jfd", gate_low_grad, recv_rows, preferred_element_type=jnp.float32
    )
    expert_up_grad = jnp.einsum(
        "sjcf,sjcd->jfd", up_low_grad, recv_rows, preferred_element_type=jnp.float32
    )
    row_grads = jnp.einsum(
        "sjcf,jfd->sjcd", gate_low_grad, expert_gate, preferred_element_type=jnp.float32
    )
    row_grads = row_grads + jnp.einsum(
        "sjcf,jfd->sjcd", up_low_grad, expert_up, preferred_element_type=jnp.float32
    )
    grads_low = row_grads.astype(jnp.bfloat16).reshape(dp_size, exp_dev, capacity, tile_rows, 128)
    back_out, grads_low = lax.optimization_barrier((back_out, grads_low))
    back_grads = lax.all_to_all(
        grads_low,
        "dp",
        split_axis=0,
        concat_axis=0,
        tiled=True,
    )
    shared_pre_gate = jnp.dot(normed_two, gate_shared, preferred_element_type=jnp.float32)
    shared_pre_up = jnp.dot(normed_two, up_shared, preferred_element_type=jnp.float32)
    shared_sigmoid = jax.nn.sigmoid(shared_pre_gate)
    shared_act = (shared_pre_gate * shared_sigmoid * shared_pre_up).astype(jnp.bfloat16)
    shared_out = jnp.einsum(
        "tf,df->td", shared_act, down_shared_t, preferred_element_type=jnp.float32
    )
    shared_act_grad = jnp.dot(grad_seq, down_shared_t, preferred_element_type=jnp.float32)
    shared_gate_low, shared_up_low = silu_back(
        shared_act_grad, shared_pre_gate, shared_pre_up, shared_sigmoid
    )
    shared_down_grad_t = jnp.dot(grad_seq.T, shared_act, preferred_element_type=jnp.float32)
    shared_gate_grad = jnp.dot(normed_two.T, shared_gate_low, preferred_element_type=jnp.float32)
    shared_up_grad = jnp.dot(normed_two.T, shared_up_low, preferred_element_type=jnp.float32)
    shared_back = jnp.einsum(
        "tf,df->td", shared_gate_low, gate_shared, preferred_element_type=jnp.float32
    )
    shared_back = shared_back + jnp.einsum(
        "tf,df->td", shared_up_low, up_shared, preferred_element_type=jnp.float32
    )
    shared_grads_in = jnp.concatenate(
        [shared_gate_grad, shared_up_grad, shared_down_grad_t], 1
    ).astype(jnp.bfloat16)
    grad_seq_f = grad_seq.astype(jnp.float32)
    table_rows = experts * capacity
    feed_part, back_part, gate_cols = combine_rows(
        slot_index.reshape(seq_len, top_count),
        back_out.reshape(table_rows, tile_rows, 128),
        back_grads.reshape(table_rows, tile_rows, 128),
        gate_values,
        grad_seq,
        shared_out,
        shared_back,
    )
    gate_part = gate_cols[:, :top_count]
    feed_own = jnp.sum(
        lax.all_to_all(
            feed_part.reshape(tensor_size, tok_dev, D), "tensor", split_axis=0, concat_axis=0, tiled=True
        ).astype(jnp.float32),
        0,
    )
    reduced_back = lax.psum(
        jnp.concatenate([back_part, gate_cols.astype(jnp.bfloat16)], 1), "tensor"
    ).astype(jnp.float32)
    normed_two_grad = reduced_back[:, :D]
    gate_grads = reduced_back[:, D : D + top_count]
    weighted_total = jnp.sum(gate_values * gate_grads, -1, keepdims=True)
    chosen_grads = gate_values * (gate_grads - weighted_total)
    logit_grads = jnp.sum(jnp.where(chosen_hot, chosen_grads[:, :, None], 0.0), 1)
    normed_two_grad = normed_two_grad + jnp.dot(
        logit_grads, router_weights.astype(jnp.float32).T, precision=HIGH
    )
    residual_grad = grad_seq_f + norm_back(residual_all, scale_two, gain_two, normed_two_grad)
    branch_grad = residual_grad.astype(jnp.bfloat16)
    shared_grads_in, branch_grad = lax.optimization_barrier((shared_grads_in, branch_grad))
    shared_pack = jnp.sum(
        lax.all_to_all(
            shared_grads_in.reshape(dp_size, rows_dp, shared_grads_in.shape[1]),
            "dp",
            split_axis=0,
            concat_axis=0,
            tiled=True,
        ).astype(jnp.float32),
        0,
    )
    output_grad_w_t = jnp.dot(branch_grad.T, mixed_all, preferred_element_type=jnp.float32)
    mixed_grad = (
        jnp.dot(branch_grad, output_weights_t, preferred_element_type=jnp.float32)
        .astype(jnp.bfloat16)
        .reshape(seq_len, head_count, DV)
    )
    keys_nope_grad = jnp.zeros((seq_len, head_count, DN), jnp.float32)
    key_rope_grad = jnp.zeros((seq_len, DR), jnp.float32)
    values_grad = jnp.zeros((seq_len, head_count, DV), jnp.float32)
    query_grad_list = []
    for block_index, rows_start in enumerate(range(0, seq_len, block_rows)):
        query_block = query_low[rows_start : rows_start + block_rows]
        masked = block_scores(query_block, keys_nope, key_rope, rows_start, prefix_len, score_scale)
        prob_full = jnp.exp(masked - lse_list[block_index])
        prob_low = prob_full.astype(jnp.bfloat16)
        mixed_block = mixed_grad[rows_start : rows_start + block_rows]
        prob_grads = jnp.einsum(
            "qhv,khv->hqk", mixed_block, values_low, preferred_element_type=jnp.float32
        )
        row_delta = jnp.sum(prob_full * prob_grads, -1, keepdims=True)
        score_grads = (prob_full * (prob_grads - row_delta)).astype(jnp.bfloat16)
        query_nope_grad = (
            jnp.einsum("hqk,khd->qhd", score_grads, keys_nope, preferred_element_type=jnp.float32)
            * score_scale
        )
        query_rope_grad = (
            jnp.einsum("hqk,kr->qhr", score_grads, key_rope, preferred_element_type=jnp.float32)
            * score_scale
        )
        keys_nope_grad = (
            keys_nope_grad
            + jnp.einsum(
                "hqk,qhd->khd",
                score_grads,
                query_block[..., :DN],
                preferred_element_type=jnp.float32,
            )
            * score_scale
        )
        key_rope_grad = (
            key_rope_grad
            + jnp.einsum(
                "hqk,qhr->kr",
                score_grads,
                query_block[..., DN:],
                preferred_element_type=jnp.float32,
            )
            * score_scale
        )
        values_grad = values_grad + jnp.einsum(
            "hqk,qhv->khv", prob_low, mixed_block, preferred_element_type=jnp.float32
        )
        block_cosines = all_cosines[rows_start : rows_start + block_rows, None, :]
        block_sines = all_sines[rows_start : rows_start + block_rows, None, :]
        query_grad_list.append(
            jnp.concatenate(
                [
                    query_nope_grad,
                    rotate_back(round_trip(query_rope_grad), block_cosines, block_sines),
                ],
                -1,
            ).astype(jnp.bfloat16)
        )
    query_grads = jnp.concatenate(query_grad_list, 0).reshape(seq_len, head_count * (DN + DR))
    feed_own, shared_pack, query_grads = lax.optimization_barrier((feed_own, shared_pack, query_grads))
    output = (residual_own + feed_own).astype(jnp.bfloat16)
    query_grad_w = jnp.dot(normed_all.T, query_grads, preferred_element_type=jnp.float32)
    normed_grad_part = jnp.dot(query_grads, query_weights.T, preferred_element_type=jnp.float32)
    expand_grads = jnp.concatenate(
        [keys_nope_grad.astype(jnp.bfloat16), values_grad.astype(jnp.bfloat16)], -1
    ).reshape(seq_len, head_count * (DN + DV))
    expand_grad_w = jnp.dot(compressed_seq.T, expand_grads, preferred_element_type=jnp.float32)
    compressed_grad_part = jnp.dot(
        expand_grads, expand_weights.T, preferred_element_type=jnp.float32
    )
    latent_grad_part = jnp.concatenate([compressed_grad_part, key_rope_grad], -1)
    attn_grads_in = jnp.concatenate(
        [
            query_grad_w,
            output_grad_w_t,
            expand_grad_w.reshape(dp_size * rows_dp, expand_flat_cols),
        ],
        1,
    )
    token_all = lax.psum(
        jnp.concatenate([normed_grad_part, latent_grad_part], 1).astype(jnp.bfloat16), "tensor"
    ).astype(jnp.float32)
    compressed_grad_all = token_all[:, D : D + KVR]
    kv_gain_full = jnp.sum(compressed_grad_all * compressed_all * scale_kv_all, 0)
    raw_grad_all = jnp.concatenate(
        [
            norm_back(compressed_all, scale_kv_all, gain_kv, compressed_grad_all),
            rotate_back(token_all[:, D + KVR :], all_cosines, all_sines),
        ],
        -1,
    ).astype(jnp.bfloat16)
    normed_grad_all = token_all[:, :D] + jnp.dot(
        raw_grad_all, latent_weights.T, preferred_element_type=jnp.float32
    )
    normed_grad = lax.dynamic_slice_in_dim(normed_grad_all, start_row, tok_dev, 0)
    hidden_grad = lax.dynamic_slice_in_dim(residual_grad, start_row, tok_dev, 0) + norm_back(
        hidden_f, scale_one, gain_one, normed_grad
    )
    row_per = D // (dp_size * tensor_size)

    def own_rows(values):
        split = values.reshape(values.shape[0], dp_size, tensor_size, row_per)
        return lax.dynamic_slice_in_dim(split, tensor_rank, 1, 2).reshape(values.shape[0], -1)

    latent_rows = jnp.dot(own_rows(normed_all).T, raw_grad_all, preferred_element_type=jnp.float32)
    attn_gain_rows = jnp.sum(
        own_rows(normed_grad_all) * own_rows(hidden_all_f) * scale_one_all, 0
    )
    second_gain_rows = jnp.sum(
        own_rows(normed_two_grad) * own_rows(residual_all) * scale_two, 0
    )
    router_rows = jnp.dot(
        own_rows(normed_two).astype(jnp.float32).T, logit_grads, precision=HIGH
    )
    kv_per = kv_gain_full.shape[0] // (dp_size * tensor_size)
    kv_rows_own = lax.dynamic_slice_in_dim(
        kv_gain_full.reshape(dp_size, tensor_size, kv_per), tensor_rank, 1, 1
    ).reshape(dp_size, kv_per)
    kv_column = jnp.pad(kv_rows_own, ((0, 0), (0, row_per - kv_per))).reshape(-1)
    small_pack = jnp.concatenate(
        [
            latent_rows,
            router_rows,
            attn_gain_rows[:, None],
            second_gain_rows[:, None],
            kv_column[:, None],
        ],
        1,
    )
    attn_width = attn_grads_in.shape[1]
    small_width = small_pack.shape[1]
    small_count = row_per * small_width
    small_cols = -(-small_count // rows_dp)
    small_flat = jnp.pad(
        small_pack.reshape(dp_size, small_count), ((0, 0), (0, small_cols * rows_dp - small_count))
    ).reshape(dp_size * rows_dp, small_cols)
    merged_own = lax.psum_scatter(
        jnp.concatenate([attn_grads_in, small_flat], 1), "dp", scatter_dimension=0, tiled=True
    )
    attn_pack = merged_own[:, :attn_width]
    small_own = merged_own[:, attn_width:].reshape(-1)[:small_count].reshape(row_per, small_width)
    cut = [0]
    for width in (latent_cols, experts, 1, 1, 1):
        cut.append(cut[-1] + width)
    latent_proj_grad = small_own[:, cut[0] : cut[1]]
    router_out = small_own[:, cut[1] : cut[2]]
    attn_gain_out = small_own[:, cut[2]]
    second_gain_out = small_own[:, cut[3]]
    latent_gain_out = small_own[:kv_per, cut[4]]
    cut = [0]
    for width in (head_cols, out_cols, expand_flat_cols):
        cut.append(cut[-1] + width)
    query_proj_grad = attn_pack[:, cut[0] : cut[1]]
    output_proj_grad = attn_pack[:, cut[1] : cut[2]].T
    expand_proj_grad = attn_pack[:, cut[2] : cut[3]].reshape(kv_rows, expand_cols)
    shared_gate_out = shared_pack[:, :shared_cols]
    shared_up_out = shared_pack[:, shared_cols : 2 * shared_cols]
    shared_down_out = shared_pack[:, 2 * shared_cols :].T
    return (
        output,
        hidden_grad,
        attn_gain_out,
        query_proj_grad,
        latent_proj_grad,
        latent_gain_out,
        expand_proj_grad,
        output_proj_grad,
        second_gain_out,
        router_out,
        expert_gate_grad,
        expert_up_grad,
        expert_down_grad,
        shared_gate_out,
        shared_up_out,
        shared_down_out,
    )


def solution(mesh):
    return jax.shard_map(
        shards,
        mesh=mesh,
        in_specs=(
            P(("dp", "tensor"), None),
            P("dp", None),
            P("dp"),
            P("dp"),
            P("dp", "tensor"),
            P("dp", None),
            P("dp"),
            P("dp", "tensor"),
            P("tensor", "dp"),
            P("dp"),
            P("dp", None),
            P("dp", "tensor", None),
            P("dp", "tensor", None),
            P("dp", "tensor", None),
            P("dp", "tensor"),
            P("dp", "tensor"),
            P("tensor", "dp"),
            P(("dp", "tensor"), None),
        ),
        out_specs=(
            P(("dp", "tensor"), None),
            P(("dp", "tensor"), None),
            P(("dp", "tensor")),
            P("dp", "tensor"),
            P(("dp", "tensor"), None),
            P(("dp", "tensor")),
            P("dp", "tensor"),
            P("tensor", "dp"),
            P(("dp", "tensor")),
            P(("dp", "tensor"), None),
            P("dp", "tensor", None),
            P("dp", "tensor", None),
            P("dp", "tensor", None),
            P("dp", "tensor"),
            P("dp", "tensor"),
            P("tensor", "dp"),
        ),
        check_vma=False,
    )
```

```python
import math

import jax
import jax.numpy as jnp
from jax import lax
from jax.experimental import pallas as pl
from jax.experimental.pallas import tpu as pltpu
from jax.sharding import PartitionSpec as P

D = 2048
DN = 128
DR = 64
DV = 128
KVR = 512


EPS = 1e-06
HIGH = lax.Precision.HIGHEST
MASKED = -1e30


def norm_scale(values):
    return lax.rsqrt(jnp.mean(values * values, -1, keepdims=True) + EPS)


def norm_back(values, scales, gains, upstream):
    weighted = gains * upstream
    return scales * weighted - values * scales**3 * jnp.mean(values * weighted, -1, keepdims=True)


def rope_tables(positions, rope_width):
    half_width = rope_width // 2
    frequency = 10000.0 ** (-2.0 * jnp.arange(half_width).astype(jnp.float32) / rope_width)
    angles = positions.astype(jnp.float32)[:, None] * frequency[None, :]
    return (jnp.cos(angles), jnp.sin(angles))


def rotate(vectors, cosines, sine_values):
    half_width = vectors.shape[-1] // 2
    front_half = vectors[..., :half_width]
    back_half = vectors[..., half_width:]
    return jnp.concatenate(
        [
            front_half * cosines - back_half * sine_values,
            back_half * cosines + front_half * sine_values,
        ],
        -1,
    )


def rotate_back(gradients, cosines, sine_values):
    half_width = gradients.shape[-1] // 2
    front_half = gradients[..., :half_width]
    back_half = gradients[..., half_width:]
    return jnp.concatenate(
        [
            front_half * cosines + back_half * sine_values,
            back_half * cosines - front_half * sine_values,
        ],
        -1,
    )


def round_trip(values):
    return lax.optimization_barrier(values.astype(jnp.bfloat16)).astype(jnp.float32)


def block_scores(query_block, keys_nope, key_rope, rows_start, prefix_len, score_scale):
    raw_scores = jnp.einsum(
        "qhd,khd->hqk", query_block[..., :DN], keys_nope, preferred_element_type=jnp.float32
    )
    raw_scores = raw_scores + jnp.einsum(
        "qhr,kr->hqk", query_block[..., DN:], key_rope, preferred_element_type=jnp.float32
    )
    query_places = rows_start + jnp.arange(query_block.shape[0])
    key_places = jnp.arange(keys_nope.shape[0])
    visible = (key_places[None, :] <= query_places[:, None]) | (key_places[None, :] < prefix_len)
    return jnp.where(visible[None], raw_scores * score_scale, MASKED)


def silu_back(act_grad, gate_pre, up_pre, sigmoid_gate):
    up_grad = (act_grad * gate_pre * sigmoid_gate).astype(jnp.bfloat16)
    gate_grad = (act_grad * up_pre * sigmoid_gate * (1.0 + gate_pre * (1.0 - sigmoid_gate))).astype(
        jnp.bfloat16
    )
    return (gate_grad, up_grad)


def dispatch_kernel(tok_ref, both_hbm, col_ref, out_ref, both_buf, sems):
    block = both_buf.shape[1]
    tile_rows = both_buf.shape[2] // 2
    last = both_hbm.shape[0] - 1
    step = pl.program_id(0)
    steps = pl.num_programs(0)

    def fetch(index, slot):
        def start(r, carry):
            tok = jnp.minimum(tok_ref[index * block + r], last)
            pltpu.make_async_copy(both_hbm.at[tok], both_buf.at[slot, r], sems.at[slot, r]).start()
            return carry

        lax.fori_loop(0, block, start, 0, unroll=4)

    @pl.when(step == 0)
    def _():
        fetch(0, 0)

    @pl.when(step + 1 < steps)
    def _():
        fetch(step + 1, (step + 1) % 2)

    slot = step % 2

    def finish(r, carry):
        pltpu.make_async_copy(both_hbm.at[0], both_buf.at[slot, r], sems.at[slot, r]).wait()
        return carry

    lax.fori_loop(0, block, finish, 0, unroll=4)
    rows = both_buf[slot, :, :tile_rows, :]
    out_ref[:, :tile_rows, :] = jnp.where(col_ref[0] > 0, rows, jnp.zeros_like(rows))
    out_ref[:, tile_rows:, :] = (
        both_buf[slot, :, tile_rows:, :].astype(jnp.float32) * col_ref[1]
    ).astype(out_ref.dtype)


def dispatch_rows(slot_token, rows, grads, valid, gate, block=128):
    slots = slot_token.shape[0]
    count, width = rows.shape
    tile_rows = width // 128
    cols = jnp.broadcast_to(jnp.stack([valid, gate])[:, :, None, None], (2, slots, 1, 128))
    both = jnp.concatenate([rows, grads], 1).reshape(count, 2 * tile_rows, 128)
    out = pl.pallas_call(
        dispatch_kernel,
        out_shape=jax.ShapeDtypeStruct((slots, 2 * tile_rows, 128), rows.dtype),
        grid_spec=pltpu.PrefetchScalarGridSpec(
            num_scalar_prefetch=1,
            grid=(slots // block,),
            in_specs=[
                pl.BlockSpec(memory_space=pl.ANY),
                pl.BlockSpec((2, block, 1, 128), lambda i, tok: (0, i, 0, 0)),
            ],
            out_specs=pl.BlockSpec((block, 2 * tile_rows, 128), lambda i, tok: (i, 0, 0)),
            scratch_shapes=[
                pltpu.VMEM((2, block, 2 * tile_rows, 128), rows.dtype),
                pltpu.SemaphoreType.DMA((2, block)),
            ],
        ),
        compiler_params=pltpu.CompilerParams(dimension_semantics=("arbitrary",)),
        cost_estimate=pl.CostEstimate(
            flops=slots * width, transcendentals=0, bytes_accessed=4 * slots * 2 * width
        ),
    )(slot_token, both, cols)
    return out


def combine_kernel(
    slot_ref, out_hbm, back_hbm, gate_ref, grad_ref, shared_out_ref, shared_back_ref,
    feed_ref, back_ref, part_ref, picked_out, picked_back, sems,
):
    top = picked_out.shape[1]
    block = picked_out.shape[2]
    last = out_hbm.shape[0] - 1
    step = pl.program_id(0)
    steps = pl.num_programs(0)

    def fetch(index, buf):
        def start(r, carry):
            for k in range(top):
                slot = jnp.clip(slot_ref[(index * block + r) * top + k], 0, last)
                pltpu.make_async_copy(
                    out_hbm.at[slot], picked_out.at[buf, k, r], sems.at[buf, 0, k, r]
                ).start()
                pltpu.make_async_copy(
                    back_hbm.at[slot], picked_back.at[buf, k, r], sems.at[buf, 1, k, r]
                ).start()
            return carry

        lax.fori_loop(0, block, start, 0, unroll=2)

    @pl.when(step == 0)
    def _():
        fetch(0, 0)

    @pl.when(step + 1 < steps)
    def _():
        fetch(step + 1, (step + 1) % 2)

    now = step % 2

    def finish(r, carry):
        for k in range(top):
            pltpu.make_async_copy(out_hbm.at[0], picked_out.at[now, k, r], sems.at[now, 0, k, r]).wait()
            pltpu.make_async_copy(back_hbm.at[0], picked_back.at[now, k, r], sems.at[now, 1, k, r]).wait()
        return carry

    lax.fori_loop(0, block, finish, 0, unroll=2)
    grad = grad_ref[...].astype(jnp.float32)
    weighted = None
    backs = None
    lanes = lax.broadcasted_iota(jnp.int32, part_ref.shape, 2)
    parts = jnp.zeros(part_ref.shape, jnp.float32)
    for k in range(top):
        out_k = picked_out[now, k].astype(jnp.float32)
        term = gate_ref[k] * out_k
        weighted = term if weighted is None else weighted + term
        back_k = picked_back[now, k].astype(jnp.float32)
        backs = back_k if backs is None else backs + back_k
        dot_k = jnp.sum(jnp.sum(grad * out_k, 2, keepdims=True), 1, keepdims=True)
        parts = jnp.where(lanes == k, dot_k, parts)
    feed_ref[...] = (shared_out_ref[...] + weighted).astype(feed_ref.dtype)
    back_ref[...] = (backs + shared_back_ref[...]).astype(back_ref.dtype)
    part_ref[...] = parts


def combine_rows(slot_index, out_table, back_table, gate_values, grad, shared_out, shared_back, block=128):
    tokens, top = gate_values.shape
    width = grad.shape[1]
    tile_rows = width // 128
    gates = jnp.broadcast_to(gate_values.T[:, :, None, None], (top, tokens, 1, 128))
    row_spec = pl.BlockSpec((block, tile_rows, 128), lambda i, s: (i, 0, 0))
    feed, back, parts = pl.pallas_call(
        combine_kernel,
        out_shape=(
            jax.ShapeDtypeStruct((tokens, tile_rows, 128), jnp.bfloat16),
            jax.ShapeDtypeStruct((tokens, tile_rows, 128), jnp.bfloat16),
            jax.ShapeDtypeStruct((tokens, 1, 128), jnp.float32),
        ),
        grid_spec=pltpu.PrefetchScalarGridSpec(
            num_scalar_prefetch=1,
            grid=(tokens // block,),
            in_specs=[
                pl.BlockSpec(memory_space=pl.ANY),
                pl.BlockSpec(memory_space=pl.ANY),
                pl.BlockSpec((top, block, 1, 128), lambda i, s: (0, i, 0, 0)),
                row_spec,
                row_spec,
                row_spec,
            ],
            out_specs=[row_spec, row_spec, pl.BlockSpec((block, 1, 128), lambda i, s: (i, 0, 0))],
            scratch_shapes=[
                pltpu.VMEM((2, top, block, tile_rows, 128), out_table.dtype),
                pltpu.VMEM((2, top, block, tile_rows, 128), back_table.dtype),
                pltpu.SemaphoreType.DMA((2, 2, top, block)),
            ],
        ),
        compiler_params=pltpu.CompilerParams(dimension_semantics=("arbitrary",)),
        cost_estimate=pl.CostEstimate(
            flops=8 * tokens * top * width,
            transcendentals=0,
            bytes_accessed=tokens * (top * 4 * width + 2 * width + 8 * width + 4 * width),
        ),
    )(
        slot_index.reshape(-1),
        out_table,
        back_table,
        gates,
        grad.reshape(tokens, tile_rows, 128),
        shared_out.reshape(tokens, tile_rows, 128),
        shared_back.reshape(tokens, tile_rows, 128),
    )
    return feed.reshape(tokens, width), back.reshape(tokens, width), parts[:, 0, :top]


def shards(
    hidden,
    routes,
    prefix,
    attn_gain,
    query_proj,
    latent_proj,
    latent_gain,
    expand_proj,
    output_proj,
    second_gain,
    router_proj,
    expert_gate,
    expert_up,
    expert_down,
    shared_gate,
    shared_up,
    shared_down,
    out_grad,
):
    tok_dev = hidden.shape[0]
    tensor_size = lax.axis_size("tensor")
    tensor_rank = lax.axis_index("tensor")
    dp_size = lax.axis_size("dp")
    seq_len = tok_dev * tensor_size
    start_row = tensor_rank * tok_dev
    rows_dp = attn_gain.shape[0]
    kv_rows = latent_gain.shape[0]
    head_cols = query_proj.shape[1]
    latent_cols = latent_proj.shape[1]
    expand_cols = expand_proj.shape[1]
    expand_flat_cols = kv_rows * expand_cols // rows_dp
    first_pack = jnp.concatenate(
        [
            query_proj,
            latent_proj,
            expand_proj.reshape(rows_dp, expand_flat_cols),
            attn_gain[:, None],
            jnp.pad(latent_gain, (0, rows_dp - kv_rows))[:, None],
        ],
        1,
    )
    first_all = lax.all_gather(first_pack, "dp", axis=0, tiled=True)
    cut = [0]
    for width in (head_cols, latent_cols, expand_flat_cols, 1, 1):
        cut.append(cut[-1] + width)
    query_weights = first_all[:, cut[0] : cut[1]]
    latent_weights = first_all[:, cut[1] : cut[2]]
    expand_weights = first_all[:, cut[2] : cut[3]].reshape(dp_size * kv_rows, expand_cols)
    attn_gains = first_all[:, cut[3]]
    kv_gains = first_all[:, cut[4]].reshape(dp_size, rows_dp)[:, :kv_rows].reshape(-1)
    out_cols = output_proj.shape[0]
    experts = router_proj.shape[1]
    shared_cols = shared_gate.shape[1]
    second_pack = jnp.concatenate([output_proj.T, second_gain[:, None], router_proj], 1)
    second_all = lax.all_gather(second_pack, "dp", axis=0, tiled=True)
    output_weights_t = second_all[:, :out_cols]
    second_gains = second_all[:, out_cols]
    router_weights = second_all[:, out_cols + 1 :]
    shared_local = jnp.concatenate([shared_gate, shared_up, shared_down.T], 1)

    hidden_all = lax.all_gather(hidden, "tensor", axis=0, tiled=True)
    grad_blocks = jnp.broadcast_to(out_grad[None], (tensor_size,) + out_grad.shape)
    grad_blocks, hidden_all = lax.optimization_barrier((grad_blocks, hidden_all))
    grad_seq = lax.all_to_all(
        grad_blocks, "tensor", split_axis=0, concat_axis=0, tiled=True
    ).reshape(tensor_size * tok_dev, D)
    grad_seq, query_weights, latent_weights = lax.optimization_barrier(
        (grad_seq, query_weights, latent_weights)
    )
    hidden_all_f = hidden_all.astype(jnp.float32)
    scale_one_all = norm_scale(hidden_all_f)
    gain_one = attn_gains.astype(jnp.float32)
    normed_all = (hidden_all_f * scale_one_all * gain_one).astype(jnp.bfloat16)
    hidden_f = lax.dynamic_slice_in_dim(hidden_all_f, start_row, tok_dev, 0)
    scale_one = lax.dynamic_slice_in_dim(scale_one_all, start_row, tok_dev, 0)
    normed_own = lax.dynamic_slice_in_dim(normed_all, start_row, tok_dev, 0)
    latent_raw_all = jnp.dot(normed_all, latent_weights, preferred_element_type=jnp.float32)
    compressed_all = latent_raw_all[:, :KVR]
    scale_kv_all = norm_scale(compressed_all)
    gain_kv = kv_gains.astype(jnp.float32)
    all_cosines, all_sines = rope_tables(jnp.arange(seq_len), DR)
    latent_seq = jnp.concatenate(
        [
            compressed_all * scale_kv_all * gain_kv,
            rotate(latent_raw_all[:, KVR:], all_cosines, all_sines),
        ],
        -1,
    ).astype(jnp.bfloat16)
    compressed = lax.dynamic_slice_in_dim(compressed_all, start_row, tok_dev, 0)
    scale_kv = lax.dynamic_slice_in_dim(scale_kv_all, start_row, tok_dev, 0)
    own_cosines = lax.dynamic_slice_in_dim(all_cosines, start_row, tok_dev, 0)
    own_sines = lax.dynamic_slice_in_dim(all_sines, start_row, tok_dev, 0)
    head_count = query_weights.shape[1] // (DN + DR)
    query_raw = jnp.dot(normed_all, query_weights, preferred_element_type=jnp.float32).reshape(
        seq_len, head_count, DN + DR
    )
    query_low = jnp.concatenate(
        [
            query_raw[..., :DN],
            rotate(query_raw[..., DN:], all_cosines[:, None, :], all_sines[:, None, :]),
        ],
        -1,
    ).astype(jnp.bfloat16)
    compressed_seq = latent_seq[:, :KVR]
    key_rope = latent_seq[:, KVR:]
    expanded = jnp.dot(compressed_seq, expand_weights, preferred_element_type=jnp.float32).reshape(
        seq_len, head_count, DN + DV
    )
    keys_nope = expanded[..., :DN].astype(jnp.bfloat16)
    values_low = expanded[..., DN:].astype(jnp.bfloat16)
    score_scale = 1.0 / math.sqrt(DN + DR)
    block_rows = min(512, seq_len)
    prefix_len = prefix[0]
    lse_list = []
    mixed_list = []
    for rows_start in range(0, seq_len, block_rows):
        query_block = query_low[rows_start : rows_start + block_rows]
        masked = block_scores(query_block, keys_nope, key_rope, rows_start, prefix_len, score_scale)
        top_score = jnp.max(masked, -1, keepdims=True)
        exp_scores = jnp.exp(masked - top_score)
        totals = jnp.sum(exp_scores, -1, keepdims=True)
        prob_low = (exp_scores / totals).astype(jnp.bfloat16)
        lse_list.append(top_score + jnp.log(totals))
        mixed_list.append(
            jnp.einsum(
                "hqk,khv->qhv", prob_low, values_low, preferred_element_type=jnp.float32
            ).astype(jnp.bfloat16)
        )
    mixed_all = jnp.concatenate(mixed_list, 0).reshape(seq_len, head_count * DV)
    attn_part = jnp.einsum(
        "tk,dk->td", mixed_all, output_weights_t, preferred_element_type=jnp.float32
    )
    top_count = routes.shape[1]
    chosen_hot = routes[:, :, None] == jnp.arange(experts)[None, None, :]
    assignments = seq_len * top_count
    flat_hot = chosen_hot.reshape(assignments, experts).astype(jnp.bfloat16)
    lower = (jnp.arange(assignments)[:, None] > jnp.arange(assignments)[None, :]).astype(jnp.bfloat16)
    earlier = jnp.dot(lower, flat_hot, preferred_element_type=jnp.float32)
    slot_pos = jnp.sum(earlier * flat_hot.astype(jnp.float32), -1).astype(jnp.int32)
    expert_ids = routes.reshape(-1)
    exp_dev = expert_gate.shape[0]
    capacity = tensor_size * (5 * seq_len * top_count // (4 * experts * tensor_size))
    slot_index = expert_ids * capacity + slot_pos
    token_ids = jnp.arange(seq_len * top_count) // top_count
    slot_token = jnp.full((experts * capacity,), seq_len, jnp.int32).at[slot_index].set(token_ids)
    slot_valid = (slot_token < seq_len).astype(jnp.float32)
    slot_index, slot_token, slot_valid, attn_part = lax.optimization_barrier(
        (slot_index, slot_token, slot_valid, attn_part)
    )
    branch_all = lax.psum(attn_part.astype(jnp.bfloat16), "tensor").astype(jnp.float32)
    shared_local, branch_all = lax.optimization_barrier((shared_local, branch_all))
    residual_all = hidden_all_f + branch_all
    residual_own = lax.dynamic_slice_in_dim(residual_all, start_row, tok_dev, 0)
    scale_two = norm_scale(residual_all)
    gain_two = second_gains.astype(jnp.float32)
    normed_two = (residual_all * scale_two * gain_two).astype(jnp.bfloat16)
    logits = jnp.dot(normed_two, router_weights, preferred_element_type=jnp.float32)
    chosen_logits = jnp.sum(jnp.where(chosen_hot, logits[:, None, :], 0.0), -1)
    gate_values = jax.nn.softmax(chosen_logits, axis=-1)
    slot_gate = (
        jnp.zeros((experts * capacity,), jnp.float32).at[slot_index].set(gate_values.reshape(-1))
    )
    tile_rows = D // 128
    send_both = dispatch_rows(slot_token, normed_two, grad_seq, slot_valid, slot_gate).reshape(
        dp_size, exp_dev, capacity, 2 * tile_rows, 128
    )
    shared_all = lax.all_gather(shared_local, "dp", axis=0, tiled=True)
    shared_all, send_both = lax.optimization_barrier((shared_all, send_both))
    gate_shared = shared_all[:, :shared_cols]
    up_shared = shared_all[:, shared_cols : 2 * shared_cols]
    down_shared_t = shared_all[:, 2 * shared_cols :]
    recv_both = lax.all_to_all(send_both, "dp", split_axis=0, concat_axis=0, tiled=True)
    recv_both = recv_both.reshape(dp_size, exp_dev, capacity, 2 * D)
    recv_rows = recv_both[..., :D]
    recv_grads = recv_both[..., D:]
    gate_pre = jnp.einsum(
        "sjcd,jfd->sjcf", recv_rows, expert_gate, preferred_element_type=jnp.float32
    )
    up_pre = jnp.einsum("sjcd,jfd->sjcf", recv_rows, expert_up, preferred_element_type=jnp.float32)
    sigmoid_gate = jax.nn.sigmoid(gate_pre)
    expert_act = (gate_pre * sigmoid_gate * up_pre).astype(jnp.bfloat16)
    expert_out = jnp.einsum(
        "sjcf,jfd->sjcd", expert_act, expert_down, preferred_element_type=jnp.float32
    )
    back_out = lax.all_to_all(
        expert_out.astype(jnp.bfloat16).reshape(dp_size, exp_dev, capacity, tile_rows, 128),
        "dp",
        split_axis=0,
        concat_axis=0,
        tiled=True,
    )
    act_grad = jnp.einsum(
        "sjcd,jfd->sjcf", recv_grads, expert_down, preferred_element_type=jnp.float32
    )
    gate_low_grad, up_low_grad = silu_back(act_grad, gate_pre, up_pre, sigmoid_gate)
    expert_down_grad = jnp.einsum(
        "sjcf,sjcd->jfd", expert_act, recv_grads, preferred_element_type=jnp.float32
    )
    expert_gate_grad = jnp.einsum(
        "sjcf,sjcd->jfd", gate_low_grad, recv_rows, preferred_element_type=jnp.float32
    )
    expert_up_grad = jnp.einsum(
        "sjcf,sjcd->jfd", up_low_grad, recv_rows, preferred_element_type=jnp.float32
    )
    row_grads = jnp.einsum(
        "sjcf,jfd->sjcd", gate_low_grad, expert_gate, preferred_element_type=jnp.float32
    )
    row_grads = row_grads + jnp.einsum(
        "sjcf,jfd->sjcd", up_low_grad, expert_up, preferred_element_type=jnp.float32
    )
    grads_low = row_grads.astype(jnp.bfloat16).reshape(dp_size, exp_dev, capacity, tile_rows, 128)
    back_out, grads_low = lax.optimization_barrier((back_out, grads_low))
    back_grads = lax.all_to_all(
        grads_low,
        "dp",
        split_axis=0,
        concat_axis=0,
        tiled=True,
    )
    shared_pre_gate = jnp.dot(normed_two, gate_shared, preferred_element_type=jnp.float32)
    shared_pre_up = jnp.dot(normed_two, up_shared, preferred_element_type=jnp.float32)
    shared_sigmoid = jax.nn.sigmoid(shared_pre_gate)
    shared_act = (shared_pre_gate * shared_sigmoid * shared_pre_up).astype(jnp.bfloat16)
    shared_out = jnp.einsum(
        "tf,df->td", shared_act, down_shared_t, preferred_element_type=jnp.float32
    )
    shared_act_grad = jnp.dot(grad_seq, down_shared_t, preferred_element_type=jnp.float32)
    shared_gate_low, shared_up_low = silu_back(
        shared_act_grad, shared_pre_gate, shared_pre_up, shared_sigmoid
    )
    shared_down_grad_t = jnp.dot(grad_seq.T, shared_act, preferred_element_type=jnp.float32)
    shared_gate_grad = jnp.dot(normed_two.T, shared_gate_low, preferred_element_type=jnp.float32)
    shared_up_grad = jnp.dot(normed_two.T, shared_up_low, preferred_element_type=jnp.float32)
    shared_back = jnp.einsum(
        "tf,df->td", shared_gate_low, gate_shared, preferred_element_type=jnp.float32
    )
    shared_back = shared_back + jnp.einsum(
        "tf,df->td", shared_up_low, up_shared, preferred_element_type=jnp.float32
    )
    shared_grads_in = jnp.concatenate(
        [shared_gate_grad, shared_up_grad, shared_down_grad_t], 1
    ).astype(jnp.bfloat16)
    grad_seq_f = grad_seq.astype(jnp.float32)
    table_rows = experts * capacity
    feed_part, back_part, gate_cols = combine_rows(
        slot_index.reshape(seq_len, top_count),
        back_out.reshape(table_rows, tile_rows, 128),
        back_grads.reshape(table_rows, tile_rows, 128),
        gate_values,
        grad_seq,
        shared_out,
        shared_back,
    )
    gate_part = gate_cols[:, :top_count]
    feed_own = jnp.sum(
        lax.all_to_all(
            feed_part.reshape(tensor_size, tok_dev, D), "tensor", split_axis=0, concat_axis=0, tiled=True
        ).astype(jnp.float32),
        0,
    )
    reduced_back = lax.psum(
        jnp.concatenate([back_part, gate_cols.astype(jnp.bfloat16)], 1), "tensor"
    ).astype(jnp.float32)
    normed_two_grad = reduced_back[:, :D]
    gate_grads = reduced_back[:, D : D + top_count]
    weighted_total = jnp.sum(gate_values * gate_grads, -1, keepdims=True)
    chosen_grads = gate_values * (gate_grads - weighted_total)
    logit_grads = jnp.sum(jnp.where(chosen_hot, chosen_grads[:, :, None], 0.0), 1)
    normed_two_grad = normed_two_grad + jnp.dot(
        logit_grads, router_weights.astype(jnp.float32).T, precision=HIGH
    )
    residual_grad = grad_seq_f + norm_back(residual_all, scale_two, gain_two, normed_two_grad)
    branch_grad = residual_grad.astype(jnp.bfloat16)
    shared_grads_in, branch_grad = lax.optimization_barrier((shared_grads_in, branch_grad))
    shared_pack = jnp.sum(
        lax.all_to_all(
            shared_grads_in.reshape(dp_size, rows_dp, shared_grads_in.shape[1]),
            "dp",
            split_axis=0,
            concat_axis=0,
            tiled=True,
        ).astype(jnp.float32),
        0,
    )
    output_grad_w_t = jnp.dot(branch_grad.T, mixed_all, preferred_element_type=jnp.float32)
    mixed_grad = (
        jnp.dot(branch_grad, output_weights_t, preferred_element_type=jnp.float32)
        .astype(jnp.bfloat16)
        .reshape(seq_len, head_count, DV)
    )
    keys_nope_grad = jnp.zeros((seq_len, head_count, DN), jnp.float32)
    key_rope_grad = jnp.zeros((seq_len, DR), jnp.float32)
    values_grad = jnp.zeros((seq_len, head_count, DV), jnp.float32)
    query_grad_list = []
    for block_index, rows_start in enumerate(range(0, seq_len, block_rows)):
        query_block = query_low[rows_start : rows_start + block_rows]
        masked = block_scores(query_block, keys_nope, key_rope, rows_start, prefix_len, score_scale)
        prob_full = jnp.exp(masked - lse_list[block_index])
        prob_low = prob_full.astype(jnp.bfloat16)
        mixed_block = mixed_grad[rows_start : rows_start + block_rows]
        prob_grads = jnp.einsum(
            "qhv,khv->hqk", mixed_block, values_low, preferred_element_type=jnp.float32
        )
        row_delta = jnp.sum(prob_full * prob_grads, -1, keepdims=True)
        score_grads = (prob_full * (prob_grads - row_delta)).astype(jnp.bfloat16)
        query_nope_grad = (
            jnp.einsum("hqk,khd->qhd", score_grads, keys_nope, preferred_element_type=jnp.float32)
            * score_scale
        )
        query_rope_grad = (
            jnp.einsum("hqk,kr->qhr", score_grads, key_rope, preferred_element_type=jnp.float32)
            * score_scale
        )
        keys_nope_grad = (
            keys_nope_grad
            + jnp.einsum(
                "hqk,qhd->khd",
                score_grads,
                query_block[..., :DN],
                preferred_element_type=jnp.float32,
            )
            * score_scale
        )
        key_rope_grad = (
            key_rope_grad
            + jnp.einsum(
                "hqk,qhr->kr",
                score_grads,
                query_block[..., DN:],
                preferred_element_type=jnp.float32,
            )
            * score_scale
        )
        values_grad = values_grad + jnp.einsum(
            "hqk,qhv->khv", prob_low, mixed_block, preferred_element_type=jnp.float32
        )
        block_cosines = all_cosines[rows_start : rows_start + block_rows, None, :]
        block_sines = all_sines[rows_start : rows_start + block_rows, None, :]
        query_grad_list.append(
            jnp.concatenate(
                [
                    query_nope_grad,
                    rotate_back(round_trip(query_rope_grad), block_cosines, block_sines),
                ],
                -1,
            ).astype(jnp.bfloat16)
        )
    query_grads = jnp.concatenate(query_grad_list, 0).reshape(seq_len, head_count * (DN + DR))
    feed_own, shared_pack, query_grads = lax.optimization_barrier((feed_own, shared_pack, query_grads))
    output = (residual_own + feed_own).astype(jnp.bfloat16)
    query_grad_w = jnp.dot(normed_all.T, query_grads, preferred_element_type=jnp.float32)
    normed_grad_part = jnp.dot(query_grads, query_weights.T, preferred_element_type=jnp.float32)
    expand_grads = jnp.concatenate(
        [keys_nope_grad.astype(jnp.bfloat16), values_grad.astype(jnp.bfloat16)], -1
    ).reshape(seq_len, head_count * (DN + DV))
    expand_grad_w = jnp.dot(compressed_seq.T, expand_grads, preferred_element_type=jnp.float32)
    compressed_grad_part = jnp.dot(
        expand_grads, expand_weights.T, preferred_element_type=jnp.float32
    )
    latent_grad_part = jnp.concatenate([compressed_grad_part, key_rope_grad], -1)
    attn_grads_in = jnp.concatenate(
        [
            query_grad_w,
            output_grad_w_t,
            expand_grad_w.reshape(dp_size * rows_dp, expand_flat_cols),
        ],
        1,
    )
    token_all = lax.psum(
        jnp.concatenate([normed_grad_part, latent_grad_part], 1).astype(jnp.bfloat16), "tensor"
    ).astype(jnp.float32)
    compressed_grad_all = token_all[:, D : D + KVR]
    kv_gain_full = jnp.sum(compressed_grad_all * compressed_all * scale_kv_all, 0)
    raw_grad_all = jnp.concatenate(
        [
            norm_back(compressed_all, scale_kv_all, gain_kv, compressed_grad_all),
            rotate_back(token_all[:, D + KVR :], all_cosines, all_sines),
        ],
        -1,
    ).astype(jnp.bfloat16)
    normed_grad_all = token_all[:, :D] + jnp.dot(
        raw_grad_all, latent_weights.T, preferred_element_type=jnp.float32
    )
    normed_grad = lax.dynamic_slice_in_dim(normed_grad_all, start_row, tok_dev, 0)
    hidden_grad = lax.dynamic_slice_in_dim(residual_grad, start_row, tok_dev, 0) + norm_back(
        hidden_f, scale_one, gain_one, normed_grad
    )
    row_per = D // (dp_size * tensor_size)

    def own_rows(values):
        split = values.reshape(values.shape[0], dp_size, tensor_size, row_per)
        return lax.dynamic_slice_in_dim(split, tensor_rank, 1, 2).reshape(values.shape[0], -1)

    latent_rows = jnp.dot(own_rows(normed_all).T, raw_grad_all, preferred_element_type=jnp.float32)
    attn_gain_rows = jnp.sum(
        own_rows(normed_grad_all) * own_rows(hidden_all_f) * scale_one_all, 0
    )
    second_gain_rows = jnp.sum(
        own_rows(normed_two_grad) * own_rows(residual_all) * scale_two, 0
    )
    router_rows = jnp.dot(
        own_rows(normed_two).astype(jnp.float32).T, logit_grads, precision=HIGH
    )
    kv_per = kv_gain_full.shape[0] // (dp_size * tensor_size)
    kv_rows_own = lax.dynamic_slice_in_dim(
        kv_gain_full.reshape(dp_size, tensor_size, kv_per), tensor_rank, 1, 1
    ).reshape(dp_size, kv_per)
    kv_column = jnp.pad(kv_rows_own, ((0, 0), (0, row_per - kv_per))).reshape(-1)
    small_pack = jnp.concatenate(
        [
            latent_rows,
            router_rows,
            attn_gain_rows[:, None],
            second_gain_rows[:, None],
            kv_column[:, None],
        ],
        1,
    )
    attn_width = attn_grads_in.shape[1]
    small_width = small_pack.shape[1]
    small_count = row_per * small_width
    small_cols = -(-small_count // rows_dp)
    small_flat = jnp.pad(
        small_pack.reshape(dp_size, small_count), ((0, 0), (0, small_cols * rows_dp - small_count))
    ).reshape(dp_size * rows_dp, small_cols)
    merged_own = lax.psum_scatter(
        jnp.concatenate([attn_grads_in, small_flat], 1), "dp", scatter_dimension=0, tiled=True
    )
    attn_pack = merged_own[:, :attn_width]
    small_own = merged_own[:, attn_width:].reshape(-1)[:small_count].reshape(row_per, small_width)
    cut = [0]
    for width in (latent_cols, experts, 1, 1, 1):
        cut.append(cut[-1] + width)
    latent_proj_grad = small_own[:, cut[0] : cut[1]]
    router_out = small_own[:, cut[1] : cut[2]]
    attn_gain_out = small_own[:, cut[2]]
    second_gain_out = small_own[:, cut[3]]
    latent_gain_out = small_own[:kv_per, cut[4]]
    cut = [0]
    for width in (head_cols, out_cols, expand_flat_cols):
        cut.append(cut[-1] + width)
    query_proj_grad = attn_pack[:, cut[0] : cut[1]]
    output_proj_grad = attn_pack[:, cut[1] : cut[2]].T
    expand_proj_grad = attn_pack[:, cut[2] : cut[3]].reshape(kv_rows, expand_cols)
    shared_gate_out = shared_pack[:, :shared_cols]
    shared_up_out = shared_pack[:, shared_cols : 2 * shared_cols]
    shared_down_out = shared_pack[:, 2 * shared_cols :].T
    return (
        output,
        hidden_grad,
        attn_gain_out,
        query_proj_grad,
        latent_proj_grad,
        latent_gain_out,
        expand_proj_grad,
        output_proj_grad,
        second_gain_out,
        router_out,
        expert_gate_grad,
        expert_up_grad,
        expert_down_grad,
        shared_gate_out,
        shared_up_out,
        shared_down_out,
    )


def solution(mesh):
    return jax.shard_map(
        shards,
        mesh=mesh,
        in_specs=(
            P(("dp", "tensor"), None),
            P("dp", None),
            P("dp"),
            P("dp"),
            P("dp", "tensor"),
            P("dp", None),
            P("dp"),
            P("dp", "tensor"),
            P("tensor", "dp"),
            P("dp"),
            P("dp", None),
            P("dp", "tensor", None),
            P("dp", "tensor", None),
            P("dp", "tensor", None),
            P("dp", "tensor"),
            P("dp", "tensor"),
            P("tensor", "dp"),
            P(("dp", "tensor"), None),
        ),
        out_specs=(
            P(("dp", "tensor"), None),
            P(("dp", "tensor"), None),
            P(("dp", "tensor")),
            P("dp", "tensor"),
            P(("dp", "tensor"), None),
            P(("dp", "tensor")),
            P("dp", "tensor"),
            P("tensor", "dp"),
            P(("dp", "tensor")),
            P(("dp", "tensor"), None),
            P("dp", "tensor", None),
            P("dp", "tensor", None),
            P("dp", "tensor", None),
            P("dp", "tensor"),
            P("dp", "tensor"),
            P("tensor", "dp"),
        ),
        check_vma=False,
    )
```

```python
import math

import jax
import jax.numpy as jnp
from jax import lax
from jax.experimental import pallas as pl
from jax.experimental.pallas import tpu as pltpu
from jax.sharding import PartitionSpec as P

D = 2048
DN = 128
DR = 64
DV = 128
KVR = 512


EPS = 1e-06
HIGH = lax.Precision.HIGHEST
MASKED = -1e30


def norm_scale(values):
    return lax.rsqrt(jnp.mean(values * values, -1, keepdims=True) + EPS)


def norm_back(values, scales, gains, upstream):
    weighted = gains * upstream
    return scales * weighted - values * scales**3 * jnp.mean(values * weighted, -1, keepdims=True)


def rope_tables(positions, rope_width):
    half_width = rope_width // 2
    frequency = 10000.0 ** (-2.0 * jnp.arange(half_width).astype(jnp.float32) / rope_width)
    angles = positions.astype(jnp.float32)[:, None] * frequency[None, :]
    return (jnp.cos(angles), jnp.sin(angles))


def rotate(vectors, cosines, sine_values):
    half_width = vectors.shape[-1] // 2
    front_half = vectors[..., :half_width]
    back_half = vectors[..., half_width:]
    return jnp.concatenate(
        [
            front_half * cosines - back_half * sine_values,
            back_half * cosines + front_half * sine_values,
        ],
        -1,
    )


def rotate_back(gradients, cosines, sine_values):
    half_width = gradients.shape[-1] // 2
    front_half = gradients[..., :half_width]
    back_half = gradients[..., half_width:]
    return jnp.concatenate(
        [
            front_half * cosines + back_half * sine_values,
            back_half * cosines - front_half * sine_values,
        ],
        -1,
    )


def round_trip(values):
    return lax.optimization_barrier(values.astype(jnp.bfloat16)).astype(jnp.float32)


def block_scores(query_block, keys_nope, key_rope, rows_start, prefix_len, score_scale):
    raw_scores = jnp.einsum(
        "qhd,khd->hqk", query_block[..., :DN], keys_nope, preferred_element_type=jnp.float32
    )
    raw_scores = raw_scores + jnp.einsum(
        "qhr,kr->hqk", query_block[..., DN:], key_rope, preferred_element_type=jnp.float32
    )
    query_places = rows_start + jnp.arange(query_block.shape[0])
    key_places = jnp.arange(keys_nope.shape[0])
    visible = (key_places[None, :] <= query_places[:, None]) | (key_places[None, :] < prefix_len)
    return jnp.where(visible[None], raw_scores * score_scale, MASKED)


def silu_back(act_grad, gate_pre, up_pre, sigmoid_gate):
    up_grad = (act_grad * gate_pre * sigmoid_gate).astype(jnp.bfloat16)
    gate_grad = (act_grad * up_pre * sigmoid_gate * (1.0 + gate_pre * (1.0 - sigmoid_gate))).astype(
        jnp.bfloat16
    )
    return (gate_grad, up_grad)


def dispatch_kernel(tok_ref, both_hbm, col_ref, out_ref, both_buf, sems):
    block = both_buf.shape[1]
    tile_rows = both_buf.shape[2] // 2
    last = both_hbm.shape[0] - 1
    step = pl.program_id(0)
    steps = pl.num_programs(0)

    def fetch(index, slot):
        def start(r, carry):
            tok = jnp.minimum(tok_ref[index * block + r], last)
            pltpu.make_async_copy(both_hbm.at[tok], both_buf.at[slot, r], sems.at[slot, r]).start()
            return carry

        lax.fori_loop(0, block, start, 0, unroll=4)

    @pl.when(step == 0)
    def _():
        fetch(0, 0)

    @pl.when(step + 1 < steps)
    def _():
        fetch(step + 1, (step + 1) % 2)

    slot = step % 2

    def finish(r, carry):
        pltpu.make_async_copy(both_hbm.at[0], both_buf.at[slot, r], sems.at[slot, r]).wait()
        return carry

    lax.fori_loop(0, block, finish, 0, unroll=4)
    rows = both_buf[slot, :, :tile_rows, :]
    out_ref[:, :tile_rows, :] = jnp.where(col_ref[0] > 0, rows, jnp.zeros_like(rows))
    out_ref[:, tile_rows:, :] = (
        both_buf[slot, :, tile_rows:, :].astype(jnp.float32) * col_ref[1]
    ).astype(out_ref.dtype)


def dispatch_rows(slot_token, rows, grads, valid, gate, block=128):
    slots = slot_token.shape[0]
    count, width = rows.shape
    tile_rows = width // 128
    cols = jnp.broadcast_to(jnp.stack([valid, gate])[:, :, None, None], (2, slots, 1, 128))
    both = jnp.concatenate([rows, grads], 1).reshape(count, 2 * tile_rows, 128)
    out = pl.pallas_call(
        dispatch_kernel,
        out_shape=jax.ShapeDtypeStruct((slots, 2 * tile_rows, 128), rows.dtype),
        grid_spec=pltpu.PrefetchScalarGridSpec(
            num_scalar_prefetch=1,
            grid=(slots // block,),
            in_specs=[
                pl.BlockSpec(memory_space=pl.ANY),
                pl.BlockSpec((2, block, 1, 128), lambda i, tok: (0, i, 0, 0)),
            ],
            out_specs=pl.BlockSpec((block, 2 * tile_rows, 128), lambda i, tok: (i, 0, 0)),
            scratch_shapes=[
                pltpu.VMEM((2, block, 2 * tile_rows, 128), rows.dtype),
                pltpu.SemaphoreType.DMA((2, block)),
            ],
        ),
        compiler_params=pltpu.CompilerParams(dimension_semantics=("arbitrary",)),
        cost_estimate=pl.CostEstimate(
            flops=slots * width, transcendentals=0, bytes_accessed=4 * slots * 2 * width
        ),
    )(slot_token, both, cols)
    return out


def combine_kernel(
    slot_ref, out_hbm, back_hbm, gate_ref, grad_ref, shared_out_ref, shared_back_ref,
    feed_ref, back_ref, part_ref, picked_out, picked_back, sems,
):
    top = picked_out.shape[1]
    block = picked_out.shape[2]
    last = out_hbm.shape[0] - 1
    step = pl.program_id(0)
    steps = pl.num_programs(0)

    def fetch(index, buf):
        def start(r, carry):
            for k in range(top):
                slot = jnp.clip(slot_ref[(index * block + r) * top + k], 0, last)
                pltpu.make_async_copy(
                    out_hbm.at[slot], picked_out.at[buf, k, r], sems.at[buf, 0, k, r]
                ).start()
                pltpu.make_async_copy(
                    back_hbm.at[slot], picked_back.at[buf, k, r], sems.at[buf, 1, k, r]
                ).start()
            return carry

        lax.fori_loop(0, block, start, 0, unroll=2)

    @pl.when(step == 0)
    def _():
        fetch(0, 0)

    @pl.when(step + 1 < steps)
    def _():
        fetch(step + 1, (step + 1) % 2)

    now = step % 2

    def finish(r, carry):
        for k in range(top):
            pltpu.make_async_copy(out_hbm.at[0], picked_out.at[now, k, r], sems.at[now, 0, k, r]).wait()
            pltpu.make_async_copy(back_hbm.at[0], picked_back.at[now, k, r], sems.at[now, 1, k, r]).wait()
        return carry

    lax.fori_loop(0, block, finish, 0, unroll=2)
    grad = grad_ref[...].astype(jnp.float32)
    weighted = None
    backs = None
    lanes = lax.broadcasted_iota(jnp.int32, part_ref.shape, 2)
    parts = jnp.zeros(part_ref.shape, jnp.float32)
    for k in range(top):
        out_k = picked_out[now, k].astype(jnp.float32)
        term = gate_ref[k] * out_k
        weighted = term if weighted is None else weighted + term
        back_k = picked_back[now, k].astype(jnp.float32)
        backs = back_k if backs is None else backs + back_k
        dot_k = jnp.sum(jnp.sum(grad * out_k, 2, keepdims=True), 1, keepdims=True)
        parts = jnp.where(lanes == k, dot_k, parts)
    feed_ref[...] = (shared_out_ref[...] + weighted).astype(feed_ref.dtype)
    back_ref[...] = (backs + shared_back_ref[...]).astype(back_ref.dtype)
    part_ref[...] = parts


def combine_rows(slot_index, out_table, back_table, gate_values, grad, shared_out, shared_back, block=128):
    tokens, top = gate_values.shape
    width = grad.shape[1]
    tile_rows = width // 128
    gates = jnp.broadcast_to(gate_values.T[:, :, None, None], (top, tokens, 1, 128))
    row_spec = pl.BlockSpec((block, tile_rows, 128), lambda i, s: (i, 0, 0))
    feed, back, parts = pl.pallas_call(
        combine_kernel,
        out_shape=(
            jax.ShapeDtypeStruct((tokens, tile_rows, 128), jnp.bfloat16),
            jax.ShapeDtypeStruct((tokens, tile_rows, 128), jnp.bfloat16),
            jax.ShapeDtypeStruct((tokens, 1, 128), jnp.float32),
        ),
        grid_spec=pltpu.PrefetchScalarGridSpec(
            num_scalar_prefetch=1,
            grid=(tokens // block,),
            in_specs=[
                pl.BlockSpec(memory_space=pl.ANY),
                pl.BlockSpec(memory_space=pl.ANY),
                pl.BlockSpec((top, block, 1, 128), lambda i, s: (0, i, 0, 0)),
                row_spec,
                row_spec,
                row_spec,
            ],
            out_specs=[row_spec, row_spec, pl.BlockSpec((block, 1, 128), lambda i, s: (i, 0, 0))],
            scratch_shapes=[
                pltpu.VMEM((2, top, block, tile_rows, 128), out_table.dtype),
                pltpu.VMEM((2, top, block, tile_rows, 128), back_table.dtype),
                pltpu.SemaphoreType.DMA((2, 2, top, block)),
            ],
        ),
        compiler_params=pltpu.CompilerParams(dimension_semantics=("arbitrary",)),
        cost_estimate=pl.CostEstimate(
            flops=8 * tokens * top * width,
            transcendentals=0,
            bytes_accessed=tokens * (top * 4 * width + 2 * width + 8 * width + 4 * width),
        ),
    )(
        slot_index.reshape(-1),
        out_table,
        back_table,
        gates,
        grad.reshape(tokens, tile_rows, 128),
        shared_out.reshape(tokens, tile_rows, 128),
        shared_back.reshape(tokens, tile_rows, 128),
    )
    return feed.reshape(tokens, width), back.reshape(tokens, width), parts[:, 0, :top]


def shards(
    hidden,
    routes,
    prefix,
    attn_gain,
    query_proj,
    latent_proj,
    latent_gain,
    expand_proj,
    output_proj,
    second_gain,
    router_proj,
    expert_gate,
    expert_up,
    expert_down,
    shared_gate,
    shared_up,
    shared_down,
    out_grad,
):
    tok_dev = hidden.shape[0]
    tensor_size = lax.axis_size("tensor")
    tensor_rank = lax.axis_index("tensor")
    dp_size = lax.axis_size("dp")
    seq_len = tok_dev * tensor_size
    start_row = tensor_rank * tok_dev
    rows_dp = attn_gain.shape[0]
    kv_rows = latent_gain.shape[0]
    head_cols = query_proj.shape[1]
    latent_cols = latent_proj.shape[1]
    expand_cols = expand_proj.shape[1]
    expand_flat_cols = kv_rows * expand_cols // rows_dp
    first_pack = jnp.concatenate(
        [
            query_proj,
            latent_proj,
            expand_proj.reshape(rows_dp, expand_flat_cols),
            attn_gain[:, None],
            jnp.pad(latent_gain, (0, rows_dp - kv_rows))[:, None],
        ],
        1,
    )
    first_all = lax.all_gather(first_pack, "dp", axis=0, tiled=True)
    cut = [0]
    for width in (head_cols, latent_cols, expand_flat_cols, 1, 1):
        cut.append(cut[-1] + width)
    query_weights = first_all[:, cut[0] : cut[1]]
    latent_weights = first_all[:, cut[1] : cut[2]]
    expand_weights = first_all[:, cut[2] : cut[3]].reshape(dp_size * kv_rows, expand_cols)
    attn_gains = first_all[:, cut[3]]
    kv_gains = first_all[:, cut[4]].reshape(dp_size, rows_dp)[:, :kv_rows].reshape(-1)
    out_cols = output_proj.shape[0]
    experts = router_proj.shape[1]
    shared_cols = shared_gate.shape[1]
    second_pack = jnp.concatenate([output_proj.T, second_gain[:, None], router_proj], 1)
    second_all = lax.all_gather(second_pack, "dp", axis=0, tiled=True)
    output_weights_t = second_all[:, :out_cols]
    second_gains = second_all[:, out_cols]
    router_weights = second_all[:, out_cols + 1 :]
    shared_local = jnp.concatenate([shared_gate, shared_up, shared_down.T], 1)

    hidden_all = lax.all_gather(hidden, "tensor", axis=0, tiled=True)
    grad_blocks = jnp.broadcast_to(out_grad[None], (tensor_size,) + out_grad.shape)
    grad_blocks, hidden_all = lax.optimization_barrier((grad_blocks, hidden_all))
    grad_seq = lax.all_to_all(
        grad_blocks, "tensor", split_axis=0, concat_axis=0, tiled=True
    ).reshape(tensor_size * tok_dev, D)
    grad_seq, query_weights, latent_weights = lax.optimization_barrier(
        (grad_seq, query_weights, latent_weights)
    )
    hidden_all_f = hidden_all.astype(jnp.float32)
    scale_one_all = norm_scale(hidden_all_f)
    gain_one = attn_gains.astype(jnp.float32)
    normed_all = (hidden_all_f * scale_one_all * gain_one).astype(jnp.bfloat16)
    hidden_f = lax.dynamic_slice_in_dim(hidden_all_f, start_row, tok_dev, 0)
    scale_one = lax.dynamic_slice_in_dim(scale_one_all, start_row, tok_dev, 0)
    normed_own = lax.dynamic_slice_in_dim(normed_all, start_row, tok_dev, 0)
    latent_raw_all = jnp.dot(normed_all, latent_weights, preferred_element_type=jnp.float32)
    compressed_all = latent_raw_all[:, :KVR]
    scale_kv_all = norm_scale(compressed_all)
    gain_kv = kv_gains.astype(jnp.float32)
    all_cosines, all_sines = rope_tables(jnp.arange(seq_len), DR)
    latent_seq = jnp.concatenate(
        [
            compressed_all * scale_kv_all * gain_kv,
            rotate(latent_raw_all[:, KVR:], all_cosines, all_sines),
        ],
        -1,
    ).astype(jnp.bfloat16)
    compressed = lax.dynamic_slice_in_dim(compressed_all, start_row, tok_dev, 0)
    scale_kv = lax.dynamic_slice_in_dim(scale_kv_all, start_row, tok_dev, 0)
    own_cosines = lax.dynamic_slice_in_dim(all_cosines, start_row, tok_dev, 0)
    own_sines = lax.dynamic_slice_in_dim(all_sines, start_row, tok_dev, 0)
    head_count = query_weights.shape[1] // (DN + DR)
    query_raw = jnp.dot(normed_all, query_weights, preferred_element_type=jnp.float32).reshape(
        seq_len, head_count, DN + DR
    )
    query_low = jnp.concatenate(
        [
            query_raw[..., :DN],
            rotate(query_raw[..., DN:], all_cosines[:, None, :], all_sines[:, None, :]),
        ],
        -1,
    ).astype(jnp.bfloat16)
    compressed_seq = latent_seq[:, :KVR]
    key_rope = latent_seq[:, KVR:]
    expanded = jnp.dot(compressed_seq, expand_weights, preferred_element_type=jnp.float32).reshape(
        seq_len, head_count, DN + DV
    )
    keys_nope = expanded[..., :DN].astype(jnp.bfloat16)
    values_low = expanded[..., DN:].astype(jnp.bfloat16)
    score_scale = 1.0 / math.sqrt(DN + DR)
    block_rows = min(512, seq_len)
    prefix_len = prefix[0]
    lse_list = []
    mixed_list = []
    for rows_start in range(0, seq_len, block_rows):
        query_block = query_low[rows_start : rows_start + block_rows]
        masked = block_scores(query_block, keys_nope, key_rope, rows_start, prefix_len, score_scale)
        top_score = jnp.max(masked, -1, keepdims=True)
        exp_scores = jnp.exp(masked - top_score)
        totals = jnp.sum(exp_scores, -1, keepdims=True)
        prob_low = (exp_scores / totals).astype(jnp.bfloat16)
        lse_list.append(top_score + jnp.log(totals))
        mixed_list.append(
            jnp.einsum(
                "hqk,khv->qhv", prob_low, values_low, preferred_element_type=jnp.float32
            ).astype(jnp.bfloat16)
        )
    mixed_all = jnp.concatenate(mixed_list, 0).reshape(seq_len, head_count * DV)
    attn_part = jnp.einsum(
        "tk,dk->td", mixed_all, output_weights_t, preferred_element_type=jnp.float32
    )
    top_count = routes.shape[1]
    chosen_hot = routes[:, :, None] == jnp.arange(experts)[None, None, :]
    assignments = seq_len * top_count
    flat_hot = chosen_hot.reshape(assignments, experts).astype(jnp.bfloat16)
    lower = (jnp.arange(assignments)[:, None] > jnp.arange(assignments)[None, :]).astype(jnp.bfloat16)
    earlier = jnp.dot(lower, flat_hot, preferred_element_type=jnp.float32)
    slot_pos = jnp.sum(earlier * flat_hot.astype(jnp.float32), -1).astype(jnp.int32)
    expert_ids = routes.reshape(-1)
    exp_dev = expert_gate.shape[0]
    capacity = tensor_size * (5 * seq_len * top_count // (4 * experts * tensor_size))
    slot_index = expert_ids * capacity + slot_pos
    token_ids = jnp.arange(seq_len * top_count) // top_count
    slot_token = jnp.full((experts * capacity,), seq_len, jnp.int32).at[slot_index].set(token_ids)
    slot_valid = (slot_token < seq_len).astype(jnp.float32)
    slot_assign = jnp.zeros((experts * capacity,), jnp.int32).at[slot_index].set(
        jnp.arange(assignments, dtype=jnp.int32)
    )
    slot_index, slot_token, slot_valid, slot_assign, attn_part = lax.optimization_barrier(
        (slot_index, slot_token, slot_valid, slot_assign, attn_part)
    )
    branch_all = lax.psum(attn_part.astype(jnp.bfloat16), "tensor").astype(jnp.float32)
    shared_local, branch_all = lax.optimization_barrier((shared_local, branch_all))
    residual_all = hidden_all_f + branch_all
    residual_own = lax.dynamic_slice_in_dim(residual_all, start_row, tok_dev, 0)
    scale_two = norm_scale(residual_all)
    gain_two = second_gains.astype(jnp.float32)
    normed_two = (residual_all * scale_two * gain_two).astype(jnp.bfloat16)
    logits = jnp.dot(normed_two, router_weights, preferred_element_type=jnp.float32)
    chosen_logits = jnp.sum(jnp.where(chosen_hot, logits[:, None, :], 0.0), -1)
    gate_values = jax.nn.softmax(chosen_logits, axis=-1)
    slot_gate = jnp.take(gate_values.reshape(-1), slot_assign) * slot_valid
    tile_rows = D // 128
    send_both = dispatch_rows(slot_token, normed_two, grad_seq, slot_valid, slot_gate).reshape(
        dp_size, exp_dev, capacity, 2 * tile_rows, 128
    )
    shared_all = lax.all_gather(shared_local, "dp", axis=0, tiled=True)
    shared_all, send_both = lax.optimization_barrier((shared_all, send_both))
    gate_shared = shared_all[:, :shared_cols]
    up_shared = shared_all[:, shared_cols : 2 * shared_cols]
    down_shared_t = shared_all[:, 2 * shared_cols :]
    recv_both = lax.all_to_all(send_both, "dp", split_axis=0, concat_axis=0, tiled=True)
    recv_both = recv_both.reshape(dp_size, exp_dev, capacity, 2 * D)
    recv_rows = recv_both[..., :D]
    recv_grads = recv_both[..., D:]
    gate_pre = jnp.einsum(
        "sjcd,jfd->sjcf", recv_rows, expert_gate, preferred_element_type=jnp.float32
    )
    up_pre = jnp.einsum("sjcd,jfd->sjcf", recv_rows, expert_up, preferred_element_type=jnp.float32)
    sigmoid_gate = jax.nn.sigmoid(gate_pre)
    expert_act = (gate_pre * sigmoid_gate * up_pre).astype(jnp.bfloat16)
    expert_out = jnp.einsum(
        "sjcf,jfd->sjcd", expert_act, expert_down, preferred_element_type=jnp.float32
    )
    back_out = lax.all_to_all(
        expert_out.astype(jnp.bfloat16).reshape(dp_size, exp_dev, capacity, tile_rows, 128),
        "dp",
        split_axis=0,
        concat_axis=0,
        tiled=True,
    )
    act_grad = jnp.einsum(
        "sjcd,jfd->sjcf", recv_grads, expert_down, preferred_element_type=jnp.float32
    )
    gate_low_grad, up_low_grad = silu_back(act_grad, gate_pre, up_pre, sigmoid_gate)
    expert_down_grad = jnp.einsum(
        "sjcf,sjcd->jfd", expert_act, recv_grads, preferred_element_type=jnp.float32
    )
    expert_gate_grad = jnp.einsum(
        "sjcf,sjcd->jfd", gate_low_grad, recv_rows, preferred_element_type=jnp.float32
    )
    expert_up_grad = jnp.einsum(
        "sjcf,sjcd->jfd", up_low_grad, recv_rows, preferred_element_type=jnp.float32
    )
    row_grads = jnp.einsum(
        "sjcf,jfd->sjcd", gate_low_grad, expert_gate, preferred_element_type=jnp.float32
    )
    row_grads = row_grads + jnp.einsum(
        "sjcf,jfd->sjcd", up_low_grad, expert_up, preferred_element_type=jnp.float32
    )
    grads_low = row_grads.astype(jnp.bfloat16).reshape(dp_size, exp_dev, capacity, tile_rows, 128)
    back_out, grads_low = lax.optimization_barrier((back_out, grads_low))
    back_grads = lax.all_to_all(
        grads_low,
        "dp",
        split_axis=0,
        concat_axis=0,
        tiled=True,
    )
    shared_pre_gate = jnp.dot(normed_two, gate_shared, preferred_element_type=jnp.float32)
    shared_pre_up = jnp.dot(normed_two, up_shared, preferred_element_type=jnp.float32)
    shared_sigmoid = jax.nn.sigmoid(shared_pre_gate)
    shared_act = (shared_pre_gate * shared_sigmoid * shared_pre_up).astype(jnp.bfloat16)
    shared_out = jnp.einsum(
        "tf,df->td", shared_act, down_shared_t, preferred_element_type=jnp.float32
    )
    shared_act_grad = jnp.dot(grad_seq, down_shared_t, preferred_element_type=jnp.float32)
    shared_gate_low, shared_up_low = silu_back(
        shared_act_grad, shared_pre_gate, shared_pre_up, shared_sigmoid
    )
    shared_down_grad_t = jnp.dot(grad_seq.T, shared_act, preferred_element_type=jnp.float32)
    shared_gate_grad = jnp.dot(normed_two.T, shared_gate_low, preferred_element_type=jnp.float32)
    shared_up_grad = jnp.dot(normed_two.T, shared_up_low, preferred_element_type=jnp.float32)
    shared_back = jnp.einsum(
        "tf,df->td", shared_gate_low, gate_shared, preferred_element_type=jnp.float32
    )
    shared_back = shared_back + jnp.einsum(
        "tf,df->td", shared_up_low, up_shared, preferred_element_type=jnp.float32
    )
    shared_grads_in = jnp.concatenate(
        [shared_gate_grad, shared_up_grad, shared_down_grad_t], 1
    ).astype(jnp.bfloat16)
    grad_seq_f = grad_seq.astype(jnp.float32)
    table_rows = experts * capacity
    feed_part, back_part, gate_cols = combine_rows(
        slot_index.reshape(seq_len, top_count),
        back_out.reshape(table_rows, tile_rows, 128),
        back_grads.reshape(table_rows, tile_rows, 128),
        gate_values,
        grad_seq,
        shared_out,
        shared_back,
    )
    gate_part = gate_cols[:, :top_count]
    feed_own = jnp.sum(
        lax.all_to_all(
            feed_part.reshape(tensor_size, tok_dev, D), "tensor", split_axis=0, concat_axis=0, tiled=True
        ).astype(jnp.float32),
        0,
    )
    reduced_back = lax.psum(
        jnp.concatenate([back_part, gate_cols.astype(jnp.bfloat16)], 1), "tensor"
    ).astype(jnp.float32)
    normed_two_grad = reduced_back[:, :D]
    gate_grads = reduced_back[:, D : D + top_count]
    weighted_total = jnp.sum(gate_values * gate_grads, -1, keepdims=True)
    chosen_grads = gate_values * (gate_grads - weighted_total)
    logit_grads = jnp.sum(jnp.where(chosen_hot, chosen_grads[:, :, None], 0.0), 1)
    normed_two_grad = normed_two_grad + jnp.dot(
        logit_grads, router_weights.astype(jnp.float32).T, precision=HIGH
    )
    residual_grad = grad_seq_f + norm_back(residual_all, scale_two, gain_two, normed_two_grad)
    branch_grad = residual_grad.astype(jnp.bfloat16)
    shared_grads_in, branch_grad = lax.optimization_barrier((shared_grads_in, branch_grad))
    shared_pack = jnp.sum(
        lax.all_to_all(
            shared_grads_in.reshape(dp_size, rows_dp, shared_grads_in.shape[1]),
            "dp",
            split_axis=0,
            concat_axis=0,
            tiled=True,
        ).astype(jnp.float32),
        0,
    )
    output_grad_w_t = jnp.dot(branch_grad.T, mixed_all, preferred_element_type=jnp.float32)
    mixed_grad = (
        jnp.dot(branch_grad, output_weights_t, preferred_element_type=jnp.float32)
        .astype(jnp.bfloat16)
        .reshape(seq_len, head_count, DV)
    )
    keys_nope_grad = jnp.zeros((seq_len, head_count, DN), jnp.float32)
    key_rope_grad = jnp.zeros((seq_len, DR), jnp.float32)
    values_grad = jnp.zeros((seq_len, head_count, DV), jnp.float32)
    query_grad_list = []
    for block_index, rows_start in enumerate(range(0, seq_len, block_rows)):
        query_block = query_low[rows_start : rows_start + block_rows]
        masked = block_scores(query_block, keys_nope, key_rope, rows_start, prefix_len, score_scale)
        prob_full = jnp.exp(masked - lse_list[block_index])
        prob_low = prob_full.astype(jnp.bfloat16)
        mixed_block = mixed_grad[rows_start : rows_start + block_rows]
        prob_grads = jnp.einsum(
            "qhv,khv->hqk", mixed_block, values_low, preferred_element_type=jnp.float32
        )
        row_delta = jnp.sum(prob_full * prob_grads, -1, keepdims=True)
        score_grads = (prob_full * (prob_grads - row_delta)).astype(jnp.bfloat16)
        query_nope_grad = (
            jnp.einsum("hqk,khd->qhd", score_grads, keys_nope, preferred_element_type=jnp.float32)
            * score_scale
        )
        query_rope_grad = (
            jnp.einsum("hqk,kr->qhr", score_grads, key_rope, preferred_element_type=jnp.float32)
            * score_scale
        )
        keys_nope_grad = (
            keys_nope_grad
            + jnp.einsum(
                "hqk,qhd->khd",
                score_grads,
                query_block[..., :DN],
                preferred_element_type=jnp.float32,
            )
            * score_scale
        )
        key_rope_grad = (
            key_rope_grad
            + jnp.einsum(
                "hqk,qhr->kr",
                score_grads,
                query_block[..., DN:],
                preferred_element_type=jnp.float32,
            )
            * score_scale
        )
        values_grad = values_grad + jnp.einsum(
            "hqk,qhv->khv", prob_low, mixed_block, preferred_element_type=jnp.float32
        )
        block_cosines = all_cosines[rows_start : rows_start + block_rows, None, :]
        block_sines = all_sines[rows_start : rows_start + block_rows, None, :]
        query_grad_list.append(
            jnp.concatenate(
                [
                    query_nope_grad,
                    rotate_back(round_trip(query_rope_grad), block_cosines, block_sines),
                ],
                -1,
            ).astype(jnp.bfloat16)
        )
    query_grads = jnp.concatenate(query_grad_list, 0).reshape(seq_len, head_count * (DN + DR))
    feed_own, shared_pack, query_grads = lax.optimization_barrier((feed_own, shared_pack, query_grads))
    output = (residual_own + feed_own).astype(jnp.bfloat16)
    query_grad_w = jnp.dot(normed_all.T, query_grads, preferred_element_type=jnp.float32)
    normed_grad_part = jnp.dot(query_grads, query_weights.T, preferred_element_type=jnp.float32)
    expand_grads = jnp.concatenate(
        [keys_nope_grad.astype(jnp.bfloat16), values_grad.astype(jnp.bfloat16)], -1
    ).reshape(seq_len, head_count * (DN + DV))
    expand_grad_w = jnp.dot(compressed_seq.T, expand_grads, preferred_element_type=jnp.float32)
    compressed_grad_part = jnp.dot(
        expand_grads, expand_weights.T, preferred_element_type=jnp.float32
    )
    latent_grad_part = jnp.concatenate([compressed_grad_part, key_rope_grad], -1)
    attn_grads_in = jnp.concatenate(
        [
            query_grad_w,
            output_grad_w_t,
            expand_grad_w.reshape(dp_size * rows_dp, expand_flat_cols),
        ],
        1,
    )
    token_all = lax.psum(
        jnp.concatenate([normed_grad_part, latent_grad_part], 1).astype(jnp.bfloat16), "tensor"
    ).astype(jnp.float32)
    compressed_grad_all = token_all[:, D : D + KVR]
    kv_gain_full = jnp.sum(compressed_grad_all * compressed_all * scale_kv_all, 0)
    raw_grad_all = jnp.concatenate(
        [
            norm_back(compressed_all, scale_kv_all, gain_kv, compressed_grad_all),
            rotate_back(token_all[:, D + KVR :], all_cosines, all_sines),
        ],
        -1,
    ).astype(jnp.bfloat16)
    normed_grad_all = token_all[:, :D] + jnp.dot(
        raw_grad_all, latent_weights.T, preferred_element_type=jnp.float32
    )
    normed_grad = lax.dynamic_slice_in_dim(normed_grad_all, start_row, tok_dev, 0)
    hidden_grad = lax.dynamic_slice_in_dim(residual_grad, start_row, tok_dev, 0) + norm_back(
        hidden_f, scale_one, gain_one, normed_grad
    )
    row_per = D // (dp_size * tensor_size)

    def own_rows(values):
        split = values.reshape(values.shape[0], dp_size, tensor_size, row_per)
        return lax.dynamic_slice_in_dim(split, tensor_rank, 1, 2).reshape(values.shape[0], -1)

    latent_rows = jnp.dot(own_rows(normed_all).T, raw_grad_all, preferred_element_type=jnp.float32)
    attn_gain_rows = jnp.sum(
        own_rows(normed_grad_all) * own_rows(hidden_all_f) * scale_one_all, 0
    )
    second_gain_rows = jnp.sum(
        own_rows(normed_two_grad) * own_rows(residual_all) * scale_two, 0
    )
    router_rows = jnp.dot(
        own_rows(normed_two).astype(jnp.float32).T, logit_grads, precision=HIGH
    )
    kv_per = kv_gain_full.shape[0] // (dp_size * tensor_size)
    kv_rows_own = lax.dynamic_slice_in_dim(
        kv_gain_full.reshape(dp_size, tensor_size, kv_per), tensor_rank, 1, 1
    ).reshape(dp_size, kv_per)
    kv_column = jnp.pad(kv_rows_own, ((0, 0), (0, row_per - kv_per))).reshape(-1)
    small_pack = jnp.concatenate(
        [
            latent_rows,
            router_rows,
            attn_gain_rows[:, None],
            second_gain_rows[:, None],
            kv_column[:, None],
        ],
        1,
    )
    attn_width = attn_grads_in.shape[1]
    small_width = small_pack.shape[1]
    small_count = row_per * small_width
    small_cols = -(-small_count // rows_dp)
    small_flat = jnp.pad(
        small_pack.reshape(dp_size, small_count), ((0, 0), (0, small_cols * rows_dp - small_count))
    ).reshape(dp_size * rows_dp, small_cols)
    merged_own = lax.psum_scatter(
        jnp.concatenate([attn_grads_in, small_flat], 1), "dp", scatter_dimension=0, tiled=True
    )
    attn_pack = merged_own[:, :attn_width]
    small_own = merged_own[:, attn_width:].reshape(-1)[:small_count].reshape(row_per, small_width)
    cut = [0]
    for width in (latent_cols, experts, 1, 1, 1):
        cut.append(cut[-1] + width)
    latent_proj_grad = small_own[:, cut[0] : cut[1]]
    router_out = small_own[:, cut[1] : cut[2]]
    attn_gain_out = small_own[:, cut[2]]
    second_gain_out = small_own[:, cut[3]]
    latent_gain_out = small_own[:kv_per, cut[4]]
    cut = [0]
    for width in (head_cols, out_cols, expand_flat_cols):
        cut.append(cut[-1] + width)
    query_proj_grad = attn_pack[:, cut[0] : cut[1]]
    output_proj_grad = attn_pack[:, cut[1] : cut[2]].T
    expand_proj_grad = attn_pack[:, cut[2] : cut[3]].reshape(kv_rows, expand_cols)
    shared_gate_out = shared_pack[:, :shared_cols]
    shared_up_out = shared_pack[:, shared_cols : 2 * shared_cols]
    shared_down_out = shared_pack[:, 2 * shared_cols :].T
    return (
        output,
        hidden_grad,
        attn_gain_out,
        query_proj_grad,
        latent_proj_grad,
        latent_gain_out,
        expand_proj_grad,
        output_proj_grad,
        second_gain_out,
        router_out,
        expert_gate_grad,
        expert_up_grad,
        expert_down_grad,
        shared_gate_out,
        shared_up_out,
        shared_down_out,
    )


def solution(mesh):
    return jax.shard_map(
        shards,
        mesh=mesh,
        in_specs=(
            P(("dp", "tensor"), None),
            P("dp", None),
            P("dp"),
            P("dp"),
            P("dp", "tensor"),
            P("dp", None),
            P("dp"),
            P("dp", "tensor"),
            P("tensor", "dp"),
            P("dp"),
            P("dp", None),
            P("dp", "tensor", None),
            P("dp", "tensor", None),
            P("dp", "tensor", None),
            P("dp", "tensor"),
            P("dp", "tensor"),
            P("tensor", "dp"),
            P(("dp", "tensor"), None),
        ),
        out_specs=(
            P(("dp", "tensor"), None),
            P(("dp", "tensor"), None),
            P(("dp", "tensor")),
            P("dp", "tensor"),
            P(("dp", "tensor"), None),
            P(("dp", "tensor")),
            P("dp", "tensor"),
            P("tensor", "dp"),
            P(("dp", "tensor")),
            P(("dp", "tensor"), None),
            P("dp", "tensor", None),
            P("dp", "tensor", None),
            P("dp", "tensor", None),
            P("dp", "tensor"),
            P("dp", "tensor"),
            P("tensor", "dp"),
        ),
        check_vma=False,
    )
```

```python
import math

import jax
import jax.numpy as jnp
from jax import lax
from jax.experimental import pallas as pl
from jax.experimental.pallas import tpu as pltpu
from jax.sharding import PartitionSpec as P

D = 2048
DN = 128
DR = 64
DV = 128
KVR = 512


EPS = 1e-06
HIGH = lax.Precision.HIGHEST
MASKED = -1e30


def norm_scale(values):
    return lax.rsqrt(jnp.mean(values * values, -1, keepdims=True) + EPS)


def norm_back(values, scales, gains, upstream):
    weighted = gains * upstream
    return scales * weighted - values * scales**3 * jnp.mean(values * weighted, -1, keepdims=True)


def rope_tables(positions, rope_width):
    half_width = rope_width // 2
    frequency = 10000.0 ** (-2.0 * jnp.arange(half_width).astype(jnp.float32) / rope_width)
    angles = positions.astype(jnp.float32)[:, None] * frequency[None, :]
    return (jnp.cos(angles), jnp.sin(angles))


def rotate(vectors, cosines, sine_values):
    half_width = vectors.shape[-1] // 2
    front_half = vectors[..., :half_width]
    back_half = vectors[..., half_width:]
    return jnp.concatenate(
        [
            front_half * cosines - back_half * sine_values,
            back_half * cosines + front_half * sine_values,
        ],
        -1,
    )


def rotate_back(gradients, cosines, sine_values):
    half_width = gradients.shape[-1] // 2
    front_half = gradients[..., :half_width]
    back_half = gradients[..., half_width:]
    return jnp.concatenate(
        [
            front_half * cosines + back_half * sine_values,
            back_half * cosines - front_half * sine_values,
        ],
        -1,
    )


def round_trip(values):
    return lax.optimization_barrier(values.astype(jnp.bfloat16)).astype(jnp.float32)


def block_scores(query_block, keys_nope, key_rope, rows_start, prefix_len, score_scale):
    raw_scores = jnp.einsum(
        "qhd,khd->hqk", query_block[..., :DN], keys_nope, preferred_element_type=jnp.float32
    )
    raw_scores = raw_scores + jnp.einsum(
        "qhr,kr->hqk", query_block[..., DN:], key_rope, preferred_element_type=jnp.float32
    )
    query_places = rows_start + jnp.arange(query_block.shape[0])
    key_places = jnp.arange(keys_nope.shape[0])
    visible = (key_places[None, :] <= query_places[:, None]) | (key_places[None, :] < prefix_len)
    return jnp.where(visible[None], raw_scores * score_scale, MASKED)


def silu_back(act_grad, gate_pre, up_pre, sigmoid_gate):
    up_grad = (act_grad * gate_pre * sigmoid_gate).astype(jnp.bfloat16)
    gate_grad = (act_grad * up_pre * sigmoid_gate * (1.0 + gate_pre * (1.0 - sigmoid_gate))).astype(
        jnp.bfloat16
    )
    return (gate_grad, up_grad)


def dispatch_kernel(tok_ref, both_hbm, col_ref, out_ref, both_buf, sems):
    block = both_buf.shape[1]
    tile_rows = both_buf.shape[2] // 2
    last = both_hbm.shape[0] - 1
    step = pl.program_id(0)
    steps = pl.num_programs(0)

    def fetch(index, slot):
        def start(r, carry):
            tok = jnp.minimum(tok_ref[index * block + r], last)
            pltpu.make_async_copy(both_hbm.at[tok], both_buf.at[slot, r], sems.at[slot, r]).start()
            return carry

        lax.fori_loop(0, block, start, 0, unroll=4)

    @pl.when(step == 0)
    def _():
        fetch(0, 0)

    @pl.when(step + 1 < steps)
    def _():
        fetch(step + 1, (step + 1) % 2)

    slot = step % 2

    def finish(r, carry):
        pltpu.make_async_copy(both_hbm.at[0], both_buf.at[slot, r], sems.at[slot, r]).wait()
        return carry

    lax.fori_loop(0, block, finish, 0, unroll=4)
    rows = both_buf[slot, :, :tile_rows, :]
    out_ref[:, :tile_rows, :] = jnp.where(col_ref[0] > 0, rows, jnp.zeros_like(rows))
    out_ref[:, tile_rows:, :] = (
        both_buf[slot, :, tile_rows:, :].astype(jnp.float32) * col_ref[1]
    ).astype(out_ref.dtype)


def dispatch_rows(slot_token, rows, grads, valid, gate, block=256):
    slots = slot_token.shape[0]
    count, width = rows.shape
    tile_rows = width // 128
    cols = jnp.broadcast_to(jnp.stack([valid, gate])[:, :, None, None], (2, slots, 1, 128))
    both = jnp.concatenate([rows, grads], 1).reshape(count, 2 * tile_rows, 128)
    out = pl.pallas_call(
        dispatch_kernel,
        out_shape=jax.ShapeDtypeStruct((slots, 2 * tile_rows, 128), rows.dtype),
        grid_spec=pltpu.PrefetchScalarGridSpec(
            num_scalar_prefetch=1,
            grid=(slots // block,),
            in_specs=[
                pl.BlockSpec(memory_space=pl.ANY),
                pl.BlockSpec((2, block, 1, 128), lambda i, tok: (0, i, 0, 0)),
            ],
            out_specs=pl.BlockSpec((block, 2 * tile_rows, 128), lambda i, tok: (i, 0, 0)),
            scratch_shapes=[
                pltpu.VMEM((2, block, 2 * tile_rows, 128), rows.dtype),
                pltpu.SemaphoreType.DMA((2, block)),
            ],
        ),
        compiler_params=pltpu.CompilerParams(dimension_semantics=("arbitrary",)),
        cost_estimate=pl.CostEstimate(
            flops=slots * width, transcendentals=0, bytes_accessed=4 * slots * 2 * width
        ),
    )(slot_token, both, cols)
    return out


def combine_kernel(
    slot_ref, out_hbm, back_hbm, gate_ref, grad_ref, shared_out_ref, shared_back_ref,
    feed_ref, back_ref, part_ref, picked_out, picked_back, sems,
):
    top = picked_out.shape[1]
    block = picked_out.shape[2]
    last = out_hbm.shape[0] - 1
    step = pl.program_id(0)
    steps = pl.num_programs(0)

    def fetch(index, buf):
        def start(r, carry):
            for k in range(top):
                slot = jnp.clip(slot_ref[(index * block + r) * top + k], 0, last)
                pltpu.make_async_copy(
                    out_hbm.at[slot], picked_out.at[buf, k, r], sems.at[buf, 0, k, r]
                ).start()
                pltpu.make_async_copy(
                    back_hbm.at[slot], picked_back.at[buf, k, r], sems.at[buf, 1, k, r]
                ).start()
            return carry

        lax.fori_loop(0, block, start, 0, unroll=2)

    @pl.when(step == 0)
    def _():
        fetch(0, 0)

    @pl.when(step + 1 < steps)
    def _():
        fetch(step + 1, (step + 1) % 2)

    now = step % 2

    def finish(r, carry):
        for k in range(top):
            pltpu.make_async_copy(out_hbm.at[0], picked_out.at[now, k, r], sems.at[now, 0, k, r]).wait()
            pltpu.make_async_copy(back_hbm.at[0], picked_back.at[now, k, r], sems.at[now, 1, k, r]).wait()
        return carry

    lax.fori_loop(0, block, finish, 0, unroll=2)
    grad = grad_ref[...].astype(jnp.float32)
    weighted = None
    backs = None
    lanes = lax.broadcasted_iota(jnp.int32, part_ref.shape, 2)
    parts = jnp.zeros(part_ref.shape, jnp.float32)
    for k in range(top):
        out_k = picked_out[now, k].astype(jnp.float32)
        term = gate_ref[k] * out_k
        weighted = term if weighted is None else weighted + term
        back_k = picked_back[now, k].astype(jnp.float32)
        backs = back_k if backs is None else backs + back_k
        dot_k = jnp.sum(jnp.sum(grad * out_k, 2, keepdims=True), 1, keepdims=True)
        parts = jnp.where(lanes == k, dot_k, parts)
    feed_ref[...] = (shared_out_ref[...] + weighted).astype(feed_ref.dtype)
    back_ref[...] = (backs + shared_back_ref[...]).astype(back_ref.dtype)
    part_ref[...] = parts


def combine_rows(slot_index, out_table, back_table, gate_values, grad, shared_out, shared_back, block=128):
    tokens, top = gate_values.shape
    width = grad.shape[1]
    tile_rows = width // 128
    gates = jnp.broadcast_to(gate_values.T[:, :, None, None], (top, tokens, 1, 128))
    row_spec = pl.BlockSpec((block, tile_rows, 128), lambda i, s: (i, 0, 0))
    feed, back, parts = pl.pallas_call(
        combine_kernel,
        out_shape=(
            jax.ShapeDtypeStruct((tokens, tile_rows, 128), jnp.bfloat16),
            jax.ShapeDtypeStruct((tokens, tile_rows, 128), jnp.bfloat16),
            jax.ShapeDtypeStruct((tokens, 1, 128), jnp.float32),
        ),
        grid_spec=pltpu.PrefetchScalarGridSpec(
            num_scalar_prefetch=1,
            grid=(tokens // block,),
            in_specs=[
                pl.BlockSpec(memory_space=pl.ANY),
                pl.BlockSpec(memory_space=pl.ANY),
                pl.BlockSpec((top, block, 1, 128), lambda i, s: (0, i, 0, 0)),
                row_spec,
                row_spec,
                row_spec,
            ],
            out_specs=[row_spec, row_spec, pl.BlockSpec((block, 1, 128), lambda i, s: (i, 0, 0))],
            scratch_shapes=[
                pltpu.VMEM((2, top, block, tile_rows, 128), out_table.dtype),
                pltpu.VMEM((2, top, block, tile_rows, 128), back_table.dtype),
                pltpu.SemaphoreType.DMA((2, 2, top, block)),
            ],
        ),
        compiler_params=pltpu.CompilerParams(dimension_semantics=("arbitrary",)),
        cost_estimate=pl.CostEstimate(
            flops=8 * tokens * top * width,
            transcendentals=0,
            bytes_accessed=tokens * (top * 4 * width + 2 * width + 8 * width + 4 * width),
        ),
    )(
        slot_index.reshape(-1),
        out_table,
        back_table,
        gates,
        grad.reshape(tokens, tile_rows, 128),
        shared_out.reshape(tokens, tile_rows, 128),
        shared_back.reshape(tokens, tile_rows, 128),
    )
    return feed.reshape(tokens, width), back.reshape(tokens, width), parts[:, 0, :top]


def shards(
    hidden,
    routes,
    prefix,
    attn_gain,
    query_proj,
    latent_proj,
    latent_gain,
    expand_proj,
    output_proj,
    second_gain,
    router_proj,
    expert_gate,
    expert_up,
    expert_down,
    shared_gate,
    shared_up,
    shared_down,
    out_grad,
):
    tok_dev = hidden.shape[0]
    tensor_size = lax.axis_size("tensor")
    tensor_rank = lax.axis_index("tensor")
    dp_size = lax.axis_size("dp")
    seq_len = tok_dev * tensor_size
    start_row = tensor_rank * tok_dev
    rows_dp = attn_gain.shape[0]
    kv_rows = latent_gain.shape[0]
    head_cols = query_proj.shape[1]
    latent_cols = latent_proj.shape[1]
    expand_cols = expand_proj.shape[1]
    expand_flat_cols = kv_rows * expand_cols // rows_dp
    first_pack = jnp.concatenate(
        [
            query_proj,
            latent_proj,
            expand_proj.reshape(rows_dp, expand_flat_cols),
            attn_gain[:, None],
            jnp.pad(latent_gain, (0, rows_dp - kv_rows))[:, None],
        ],
        1,
    )
    first_all = lax.all_gather(first_pack, "dp", axis=0, tiled=True)
    cut = [0]
    for width in (head_cols, latent_cols, expand_flat_cols, 1, 1):
        cut.append(cut[-1] + width)
    query_weights = first_all[:, cut[0] : cut[1]]
    latent_weights = first_all[:, cut[1] : cut[2]]
    expand_weights = first_all[:, cut[2] : cut[3]].reshape(dp_size * kv_rows, expand_cols)
    attn_gains = first_all[:, cut[3]]
    kv_gains = first_all[:, cut[4]].reshape(dp_size, rows_dp)[:, :kv_rows].reshape(-1)
    out_cols = output_proj.shape[0]
    experts = router_proj.shape[1]
    shared_cols = shared_gate.shape[1]
    second_pack = jnp.concatenate([output_proj.T, second_gain[:, None], router_proj], 1)
    second_all = lax.all_gather(second_pack, "dp", axis=0, tiled=True)
    output_weights_t = second_all[:, :out_cols]
    second_gains = second_all[:, out_cols]
    router_weights = second_all[:, out_cols + 1 :]
    shared_local = jnp.concatenate([shared_gate, shared_up, shared_down.T], 1)

    hidden_all = lax.all_gather(hidden, "tensor", axis=0, tiled=True)
    grad_blocks = jnp.broadcast_to(out_grad[None], (tensor_size,) + out_grad.shape)
    grad_blocks, hidden_all = lax.optimization_barrier((grad_blocks, hidden_all))
    grad_seq = lax.all_to_all(
        grad_blocks, "tensor", split_axis=0, concat_axis=0, tiled=True
    ).reshape(tensor_size * tok_dev, D)
    grad_seq, query_weights, latent_weights = lax.optimization_barrier(
        (grad_seq, query_weights, latent_weights)
    )
    hidden_all_f = hidden_all.astype(jnp.float32)
    scale_one_all = norm_scale(hidden_all_f)
    gain_one = attn_gains.astype(jnp.float32)
    normed_all = (hidden_all_f * scale_one_all * gain_one).astype(jnp.bfloat16)
    hidden_f = lax.dynamic_slice_in_dim(hidden_all_f, start_row, tok_dev, 0)
    scale_one = lax.dynamic_slice_in_dim(scale_one_all, start_row, tok_dev, 0)
    normed_own = lax.dynamic_slice_in_dim(normed_all, start_row, tok_dev, 0)
    latent_raw_all = jnp.dot(normed_all, latent_weights, preferred_element_type=jnp.float32)
    compressed_all = latent_raw_all[:, :KVR]
    scale_kv_all = norm_scale(compressed_all)
    gain_kv = kv_gains.astype(jnp.float32)
    all_cosines, all_sines = rope_tables(jnp.arange(seq_len), DR)
    latent_seq = jnp.concatenate(
        [
            compressed_all * scale_kv_all * gain_kv,
            rotate(latent_raw_all[:, KVR:], all_cosines, all_sines),
        ],
        -1,
    ).astype(jnp.bfloat16)
    compressed = lax.dynamic_slice_in_dim(compressed_all, start_row, tok_dev, 0)
    scale_kv = lax.dynamic_slice_in_dim(scale_kv_all, start_row, tok_dev, 0)
    own_cosines = lax.dynamic_slice_in_dim(all_cosines, start_row, tok_dev, 0)
    own_sines = lax.dynamic_slice_in_dim(all_sines, start_row, tok_dev, 0)
    head_count = query_weights.shape[1] // (DN + DR)
    query_raw = jnp.dot(normed_all, query_weights, preferred_element_type=jnp.float32).reshape(
        seq_len, head_count, DN + DR
    )
    query_low = jnp.concatenate(
        [
            query_raw[..., :DN],
            rotate(query_raw[..., DN:], all_cosines[:, None, :], all_sines[:, None, :]),
        ],
        -1,
    ).astype(jnp.bfloat16)
    compressed_seq = latent_seq[:, :KVR]
    key_rope = latent_seq[:, KVR:]
    expanded = jnp.dot(compressed_seq, expand_weights, preferred_element_type=jnp.float32).reshape(
        seq_len, head_count, DN + DV
    )
    keys_nope = expanded[..., :DN].astype(jnp.bfloat16)
    values_low = expanded[..., DN:].astype(jnp.bfloat16)
    score_scale = 1.0 / math.sqrt(DN + DR)
    block_rows = min(512, seq_len)
    prefix_len = prefix[0]
    lse_list = []
    mixed_list = []
    for rows_start in range(0, seq_len, block_rows):
        query_block = query_low[rows_start : rows_start + block_rows]
        masked = block_scores(query_block, keys_nope, key_rope, rows_start, prefix_len, score_scale)
        top_score = jnp.max(masked, -1, keepdims=True)
        exp_scores = jnp.exp(masked - top_score)
        totals = jnp.sum(exp_scores, -1, keepdims=True)
        prob_low = (exp_scores / totals).astype(jnp.bfloat16)
        lse_list.append(top_score + jnp.log(totals))
        mixed_list.append(
            jnp.einsum(
                "hqk,khv->qhv", prob_low, values_low, preferred_element_type=jnp.float32
            ).astype(jnp.bfloat16)
        )
    mixed_all = jnp.concatenate(mixed_list, 0).reshape(seq_len, head_count * DV)
    attn_part = jnp.einsum(
        "tk,dk->td", mixed_all, output_weights_t, preferred_element_type=jnp.float32
    )
    top_count = routes.shape[1]
    chosen_hot = routes[:, :, None] == jnp.arange(experts)[None, None, :]
    assignments = seq_len * top_count
    flat_hot = chosen_hot.reshape(assignments, experts).astype(jnp.bfloat16)
    lower = (jnp.arange(assignments)[:, None] > jnp.arange(assignments)[None, :]).astype(jnp.bfloat16)
    earlier = jnp.dot(lower, flat_hot, preferred_element_type=jnp.float32)
    slot_pos = jnp.sum(earlier * flat_hot.astype(jnp.float32), -1).astype(jnp.int32)
    expert_ids = routes.reshape(-1)
    exp_dev = expert_gate.shape[0]
    capacity = tensor_size * (5 * seq_len * top_count // (4 * experts * tensor_size))
    slot_index = expert_ids * capacity + slot_pos
    token_ids = jnp.arange(seq_len * top_count) // top_count
    slot_token = jnp.full((experts * capacity,), seq_len, jnp.int32).at[slot_index].set(token_ids)
    slot_valid = (slot_token < seq_len).astype(jnp.float32)
    slot_index, slot_token, slot_valid, attn_part = lax.optimization_barrier(
        (slot_index, slot_token, slot_valid, attn_part)
    )
    branch_all = lax.psum(attn_part.astype(jnp.bfloat16), "tensor").astype(jnp.float32)
    shared_local, branch_all = lax.optimization_barrier((shared_local, branch_all))
    residual_all = hidden_all_f + branch_all
    residual_own = lax.dynamic_slice_in_dim(residual_all, start_row, tok_dev, 0)
    scale_two = norm_scale(residual_all)
    gain_two = second_gains.astype(jnp.float32)
    normed_two = (residual_all * scale_two * gain_two).astype(jnp.bfloat16)
    logits = jnp.dot(normed_two, router_weights, preferred_element_type=jnp.float32)
    chosen_logits = jnp.sum(jnp.where(chosen_hot, logits[:, None, :], 0.0), -1)
    gate_values = jax.nn.softmax(chosen_logits, axis=-1)
    slot_gate = (
        jnp.zeros((experts * capacity,), jnp.float32).at[slot_index].set(gate_values.reshape(-1))
    )
    tile_rows = D // 128
    send_both = dispatch_rows(slot_token, normed_two, grad_seq, slot_valid, slot_gate).reshape(
        dp_size, exp_dev, capacity, 2 * tile_rows, 128
    )
    shared_all = lax.all_gather(shared_local, "dp", axis=0, tiled=True)
    shared_all, send_both = lax.optimization_barrier((shared_all, send_both))
    gate_shared = shared_all[:, :shared_cols]
    up_shared = shared_all[:, shared_cols : 2 * shared_cols]
    down_shared_t = shared_all[:, 2 * shared_cols :]
    recv_both = lax.all_to_all(send_both, "dp", split_axis=0, concat_axis=0, tiled=True)
    recv_both = recv_both.reshape(dp_size, exp_dev, capacity, 2 * D)
    recv_rows = recv_both[..., :D]
    recv_grads = recv_both[..., D:]
    gate_pre = jnp.einsum(
        "sjcd,jfd->sjcf", recv_rows, expert_gate, preferred_element_type=jnp.float32
    )
    up_pre = jnp.einsum("sjcd,jfd->sjcf", recv_rows, expert_up, preferred_element_type=jnp.float32)
    sigmoid_gate = jax.nn.sigmoid(gate_pre)
    expert_act = (gate_pre * sigmoid_gate * up_pre).astype(jnp.bfloat16)
    expert_out = jnp.einsum(
        "sjcf,jfd->sjcd", expert_act, expert_down, preferred_element_type=jnp.float32
    )
    back_out = lax.all_to_all(
        expert_out.astype(jnp.bfloat16).reshape(dp_size, exp_dev, capacity, tile_rows, 128),
        "dp",
        split_axis=0,
        concat_axis=0,
        tiled=True,
    )
    act_grad = jnp.einsum(
        "sjcd,jfd->sjcf", recv_grads, expert_down, preferred_element_type=jnp.float32
    )
    gate_low_grad, up_low_grad = silu_back(act_grad, gate_pre, up_pre, sigmoid_gate)
    expert_down_grad = jnp.einsum(
        "sjcf,sjcd->jfd", expert_act, recv_grads, preferred_element_type=jnp.float32
    )
    expert_gate_grad = jnp.einsum(
        "sjcf,sjcd->jfd", gate_low_grad, recv_rows, preferred_element_type=jnp.float32
    )
    expert_up_grad = jnp.einsum(
        "sjcf,sjcd->jfd", up_low_grad, recv_rows, preferred_element_type=jnp.float32
    )
    row_grads = jnp.einsum(
        "sjcf,jfd->sjcd", gate_low_grad, expert_gate, preferred_element_type=jnp.float32
    )
    row_grads = row_grads + jnp.einsum(
        "sjcf,jfd->sjcd", up_low_grad, expert_up, preferred_element_type=jnp.float32
    )
    grads_low = row_grads.astype(jnp.bfloat16).reshape(dp_size, exp_dev, capacity, tile_rows, 128)
    back_out, grads_low = lax.optimization_barrier((back_out, grads_low))
    back_grads = lax.all_to_all(
        grads_low,
        "dp",
        split_axis=0,
        concat_axis=0,
        tiled=True,
    )
    shared_pre_gate = jnp.dot(normed_two, gate_shared, preferred_element_type=jnp.float32)
    shared_pre_up = jnp.dot(normed_two, up_shared, preferred_element_type=jnp.float32)
    shared_sigmoid = jax.nn.sigmoid(shared_pre_gate)
    shared_act = (shared_pre_gate * shared_sigmoid * shared_pre_up).astype(jnp.bfloat16)
    shared_out = jnp.einsum(
        "tf,df->td", shared_act, down_shared_t, preferred_element_type=jnp.float32
    )
    shared_act_grad = jnp.dot(grad_seq, down_shared_t, preferred_element_type=jnp.float32)
    shared_gate_low, shared_up_low = silu_back(
        shared_act_grad, shared_pre_gate, shared_pre_up, shared_sigmoid
    )
    shared_down_grad_t = jnp.dot(grad_seq.T, shared_act, preferred_element_type=jnp.float32)
    shared_gate_grad = jnp.dot(normed_two.T, shared_gate_low, preferred_element_type=jnp.float32)
    shared_up_grad = jnp.dot(normed_two.T, shared_up_low, preferred_element_type=jnp.float32)
    shared_back = jnp.einsum(
        "tf,df->td", shared_gate_low, gate_shared, preferred_element_type=jnp.float32
    )
    shared_back = shared_back + jnp.einsum(
        "tf,df->td", shared_up_low, up_shared, preferred_element_type=jnp.float32
    )
    shared_grads_in = jnp.concatenate(
        [shared_gate_grad, shared_up_grad, shared_down_grad_t], 1
    ).astype(jnp.bfloat16)
    grad_seq_f = grad_seq.astype(jnp.float32)
    table_rows = experts * capacity
    feed_part, back_part, gate_cols = combine_rows(
        slot_index.reshape(seq_len, top_count),
        back_out.reshape(table_rows, tile_rows, 128),
        back_grads.reshape(table_rows, tile_rows, 128),
        gate_values,
        grad_seq,
        shared_out,
        shared_back,
    )
    gate_part = gate_cols[:, :top_count]
    feed_own = jnp.sum(
        lax.all_to_all(
            feed_part.reshape(tensor_size, tok_dev, D), "tensor", split_axis=0, concat_axis=0, tiled=True
        ).astype(jnp.float32),
        0,
    )
    reduced_back = lax.psum(
        jnp.concatenate([back_part, gate_cols.astype(jnp.bfloat16)], 1), "tensor"
    ).astype(jnp.float32)
    normed_two_grad = reduced_back[:, :D]
    gate_grads = reduced_back[:, D : D + top_count]
    weighted_total = jnp.sum(gate_values * gate_grads, -1, keepdims=True)
    chosen_grads = gate_values * (gate_grads - weighted_total)
    logit_grads = jnp.sum(jnp.where(chosen_hot, chosen_grads[:, :, None], 0.0), 1)
    normed_two_grad = normed_two_grad + jnp.dot(
        logit_grads, router_weights.astype(jnp.float32).T, precision=HIGH
    )
    residual_grad = grad_seq_f + norm_back(residual_all, scale_two, gain_two, normed_two_grad)
    branch_grad = residual_grad.astype(jnp.bfloat16)
    shared_grads_in, branch_grad = lax.optimization_barrier((shared_grads_in, branch_grad))
    shared_pack = jnp.sum(
        lax.all_to_all(
            shared_grads_in.reshape(dp_size, rows_dp, shared_grads_in.shape[1]),
            "dp",
            split_axis=0,
            concat_axis=0,
            tiled=True,
        ).astype(jnp.float32),
        0,
    )
    output_grad_w_t = jnp.dot(branch_grad.T, mixed_all, preferred_element_type=jnp.float32)
    mixed_grad = (
        jnp.dot(branch_grad, output_weights_t, preferred_element_type=jnp.float32)
        .astype(jnp.bfloat16)
        .reshape(seq_len, head_count, DV)
    )
    keys_nope_grad = jnp.zeros((seq_len, head_count, DN), jnp.float32)
    key_rope_grad = jnp.zeros((seq_len, DR), jnp.float32)
    values_grad = jnp.zeros((seq_len, head_count, DV), jnp.float32)
    query_grad_list = []
    for block_index, rows_start in enumerate(range(0, seq_len, block_rows)):
        query_block = query_low[rows_start : rows_start + block_rows]
        masked = block_scores(query_block, keys_nope, key_rope, rows_start, prefix_len, score_scale)
        prob_full = jnp.exp(masked - lse_list[block_index])
        prob_low = prob_full.astype(jnp.bfloat16)
        mixed_block = mixed_grad[rows_start : rows_start + block_rows]
        prob_grads = jnp.einsum(
            "qhv,khv->hqk", mixed_block, values_low, preferred_element_type=jnp.float32
        )
        row_delta = jnp.sum(prob_full * prob_grads, -1, keepdims=True)
        score_grads = (prob_full * (prob_grads - row_delta)).astype(jnp.bfloat16)
        query_nope_grad = (
            jnp.einsum("hqk,khd->qhd", score_grads, keys_nope, preferred_element_type=jnp.float32)
            * score_scale
        )
        query_rope_grad = (
            jnp.einsum("hqk,kr->qhr", score_grads, key_rope, preferred_element_type=jnp.float32)
            * score_scale
        )
        keys_nope_grad = (
            keys_nope_grad
            + jnp.einsum(
                "hqk,qhd->khd",
                score_grads,
                query_block[..., :DN],
                preferred_element_type=jnp.float32,
            )
            * score_scale
        )
        key_rope_grad = (
            key_rope_grad
            + jnp.einsum(
                "hqk,qhr->kr",
                score_grads,
                query_block[..., DN:],
                preferred_element_type=jnp.float32,
            )
            * score_scale
        )
        values_grad = values_grad + jnp.einsum(
            "hqk,qhv->khv", prob_low, mixed_block, preferred_element_type=jnp.float32
        )
        block_cosines = all_cosines[rows_start : rows_start + block_rows, None, :]
        block_sines = all_sines[rows_start : rows_start + block_rows, None, :]
        query_grad_list.append(
            jnp.concatenate(
                [
                    query_nope_grad,
                    rotate_back(round_trip(query_rope_grad), block_cosines, block_sines),
                ],
                -1,
            ).astype(jnp.bfloat16)
        )
    query_grads = jnp.concatenate(query_grad_list, 0).reshape(seq_len, head_count * (DN + DR))
    feed_own, shared_pack, query_grads = lax.optimization_barrier((feed_own, shared_pack, query_grads))
    output = (residual_own + feed_own).astype(jnp.bfloat16)
    query_grad_w = jnp.dot(normed_all.T, query_grads, preferred_element_type=jnp.float32)
    normed_grad_part = jnp.dot(query_grads, query_weights.T, preferred_element_type=jnp.float32)
    expand_grads = jnp.concatenate(
        [keys_nope_grad.astype(jnp.bfloat16), values_grad.astype(jnp.bfloat16)], -1
    ).reshape(seq_len, head_count * (DN + DV))
    expand_grad_w = jnp.dot(compressed_seq.T, expand_grads, preferred_element_type=jnp.float32)
    compressed_grad_part = jnp.dot(
        expand_grads, expand_weights.T, preferred_element_type=jnp.float32
    )
    latent_grad_part = jnp.concatenate([compressed_grad_part, key_rope_grad], -1)
    attn_grads_in = jnp.concatenate(
        [
            query_grad_w,
            output_grad_w_t,
            expand_grad_w.reshape(dp_size * rows_dp, expand_flat_cols),
        ],
        1,
    )
    token_all = lax.psum(
        jnp.concatenate([normed_grad_part, latent_grad_part], 1).astype(jnp.bfloat16), "tensor"
    ).astype(jnp.float32)
    compressed_grad_all = token_all[:, D : D + KVR]
    kv_gain_full = jnp.sum(compressed_grad_all * compressed_all * scale_kv_all, 0)
    raw_grad_all = jnp.concatenate(
        [
            norm_back(compressed_all, scale_kv_all, gain_kv, compressed_grad_all),
            rotate_back(token_all[:, D + KVR :], all_cosines, all_sines),
        ],
        -1,
    ).astype(jnp.bfloat16)
    normed_grad_all = token_all[:, :D] + jnp.dot(
        raw_grad_all, latent_weights.T, preferred_element_type=jnp.float32
    )
    normed_grad = lax.dynamic_slice_in_dim(normed_grad_all, start_row, tok_dev, 0)
    hidden_grad = lax.dynamic_slice_in_dim(residual_grad, start_row, tok_dev, 0) + norm_back(
        hidden_f, scale_one, gain_one, normed_grad
    )
    row_per = D // (dp_size * tensor_size)

    def own_rows(values):
        split = values.reshape(values.shape[0], dp_size, tensor_size, row_per)
        return lax.dynamic_slice_in_dim(split, tensor_rank, 1, 2).reshape(values.shape[0], -1)

    latent_rows = jnp.dot(own_rows(normed_all).T, raw_grad_all, preferred_element_type=jnp.float32)
    attn_gain_rows = jnp.sum(
        own_rows(normed_grad_all) * own_rows(hidden_all_f) * scale_one_all, 0
    )
    second_gain_rows = jnp.sum(
        own_rows(normed_two_grad) * own_rows(residual_all) * scale_two, 0
    )
    router_rows = jnp.dot(
        own_rows(normed_two).astype(jnp.float32).T, logit_grads, precision=HIGH
    )
    kv_per = kv_gain_full.shape[0] // (dp_size * tensor_size)
    kv_rows_own = lax.dynamic_slice_in_dim(
        kv_gain_full.reshape(dp_size, tensor_size, kv_per), tensor_rank, 1, 1
    ).reshape(dp_size, kv_per)
    kv_column = jnp.pad(kv_rows_own, ((0, 0), (0, row_per - kv_per))).reshape(-1)
    small_pack = jnp.concatenate(
        [
            latent_rows,
            router_rows,
            attn_gain_rows[:, None],
            second_gain_rows[:, None],
            kv_column[:, None],
        ],
        1,
    )
    attn_width = attn_grads_in.shape[1]
    small_width = small_pack.shape[1]
    small_count = row_per * small_width
    small_cols = -(-small_count // rows_dp)
    small_flat = jnp.pad(
        small_pack.reshape(dp_size, small_count), ((0, 0), (0, small_cols * rows_dp - small_count))
    ).reshape(dp_size * rows_dp, small_cols)
    merged_own = lax.psum_scatter(
        jnp.concatenate([attn_grads_in, small_flat], 1), "dp", scatter_dimension=0, tiled=True
    )
    attn_pack = merged_own[:, :attn_width]
    small_own = merged_own[:, attn_width:].reshape(-1)[:small_count].reshape(row_per, small_width)
    cut = [0]
    for width in (latent_cols, experts, 1, 1, 1):
        cut.append(cut[-1] + width)
    latent_proj_grad = small_own[:, cut[0] : cut[1]]
    router_out = small_own[:, cut[1] : cut[2]]
    attn_gain_out = small_own[:, cut[2]]
    second_gain_out = small_own[:, cut[3]]
    latent_gain_out = small_own[:kv_per, cut[4]]
    cut = [0]
    for width in (head_cols, out_cols, expand_flat_cols):
        cut.append(cut[-1] + width)
    query_proj_grad = attn_pack[:, cut[0] : cut[1]]
    output_proj_grad = attn_pack[:, cut[1] : cut[2]].T
    expand_proj_grad = attn_pack[:, cut[2] : cut[3]].reshape(kv_rows, expand_cols)
    shared_gate_out = shared_pack[:, :shared_cols]
    shared_up_out = shared_pack[:, shared_cols : 2 * shared_cols]
    shared_down_out = shared_pack[:, 2 * shared_cols :].T
    return (
        output,
        hidden_grad,
        attn_gain_out,
        query_proj_grad,
        latent_proj_grad,
        latent_gain_out,
        expand_proj_grad,
        output_proj_grad,
        second_gain_out,
        router_out,
        expert_gate_grad,
        expert_up_grad,
        expert_down_grad,
        shared_gate_out,
        shared_up_out,
        shared_down_out,
    )


def solution(mesh):
    return jax.shard_map(
        shards,
        mesh=mesh,
        in_specs=(
            P(("dp", "tensor"), None),
            P("dp", None),
            P("dp"),
            P("dp"),
            P("dp", "tensor"),
            P("dp", None),
            P("dp"),
            P("dp", "tensor"),
            P("tensor", "dp"),
            P("dp"),
            P("dp", None),
            P("dp", "tensor", None),
            P("dp", "tensor", None),
            P("dp", "tensor", None),
            P("dp", "tensor"),
            P("dp", "tensor"),
            P("tensor", "dp"),
            P(("dp", "tensor"), None),
        ),
        out_specs=(
            P(("dp", "tensor"), None),
            P(("dp", "tensor"), None),
            P(("dp", "tensor")),
            P("dp", "tensor"),
            P(("dp", "tensor"), None),
            P(("dp", "tensor")),
            P("dp", "tensor"),
            P("tensor", "dp"),
            P(("dp", "tensor")),
            P(("dp", "tensor"), None),
            P("dp", "tensor", None),
            P("dp", "tensor", None),
            P("dp", "tensor", None),
            P("dp", "tensor"),
            P("dp", "tensor"),
            P("tensor", "dp"),
        ),
        check_vma=False,
    )
```

```python
import math

import jax
import jax.numpy as jnp
from jax import lax
from jax.experimental import pallas as pl
from jax.experimental.pallas import tpu as pltpu
from jax.sharding import PartitionSpec as P

D = 2048
DN = 128
DR = 64
DV = 128
KVR = 512


EPS = 1e-06
HIGH = lax.Precision.HIGHEST
MASKED = -1e30


def norm_scale(values):
    return lax.rsqrt(jnp.mean(values * values, -1, keepdims=True) + EPS)


def norm_back(values, scales, gains, upstream):
    weighted = gains * upstream
    return scales * weighted - values * scales**3 * jnp.mean(values * weighted, -1, keepdims=True)


def rope_tables(positions, rope_width):
    half_width = rope_width // 2
    frequency = 10000.0 ** (-2.0 * jnp.arange(half_width).astype(jnp.float32) / rope_width)
    angles = positions.astype(jnp.float32)[:, None] * frequency[None, :]
    return (jnp.cos(angles), jnp.sin(angles))


def rotate(vectors, cosines, sine_values):
    half_width = vectors.shape[-1] // 2
    front_half = vectors[..., :half_width]
    back_half = vectors[..., half_width:]
    return jnp.concatenate(
        [
            front_half * cosines - back_half * sine_values,
            back_half * cosines + front_half * sine_values,
        ],
        -1,
    )


def rotate_back(gradients, cosines, sine_values):
    half_width = gradients.shape[-1] // 2
    front_half = gradients[..., :half_width]
    back_half = gradients[..., half_width:]
    return jnp.concatenate(
        [
            front_half * cosines + back_half * sine_values,
            back_half * cosines - front_half * sine_values,
        ],
        -1,
    )


def round_trip(values):
    return lax.optimization_barrier(values.astype(jnp.bfloat16)).astype(jnp.float32)


def block_scores(query_block, keys_nope, key_rope, rows_start, prefix_len, score_scale):
    raw_scores = jnp.einsum(
        "qhd,khd->hqk", query_block[..., :DN], keys_nope, preferred_element_type=jnp.float32
    )
    raw_scores = raw_scores + jnp.einsum(
        "qhr,kr->hqk", query_block[..., DN:], key_rope, preferred_element_type=jnp.float32
    )
    query_places = rows_start + jnp.arange(query_block.shape[0])
    key_places = jnp.arange(keys_nope.shape[0])
    visible = (key_places[None, :] <= query_places[:, None]) | (key_places[None, :] < prefix_len)
    return jnp.where(visible[None], raw_scores * score_scale, MASKED)


def silu_back(act_grad, gate_pre, up_pre, sigmoid_gate):
    up_grad = (act_grad * gate_pre * sigmoid_gate).astype(jnp.bfloat16)
    gate_grad = (act_grad * up_pre * sigmoid_gate * (1.0 + gate_pre * (1.0 - sigmoid_gate))).astype(
        jnp.bfloat16
    )
    return (gate_grad, up_grad)


def dispatch_kernel(tok_ref, both_hbm, col_ref, out_ref, both_buf, sems):
    block = both_buf.shape[1]
    tile_rows = both_buf.shape[2] // 2
    last = both_hbm.shape[0] - 1
    step = pl.program_id(0)
    steps = pl.num_programs(0)

    def fetch(index, slot):
        def start(r, carry):
            tok = jnp.minimum(tok_ref[index * block + r], last)
            pltpu.make_async_copy(both_hbm.at[tok], both_buf.at[slot, r], sems.at[slot, r]).start()
            return carry

        lax.fori_loop(0, block, start, 0, unroll=4)

    @pl.when(step == 0)
    def _():
        fetch(0, 0)

    @pl.when(step + 1 < steps)
    def _():
        fetch(step + 1, (step + 1) % 2)

    slot = step % 2

    def finish(r, carry):
        pltpu.make_async_copy(both_hbm.at[0], both_buf.at[slot, r], sems.at[slot, r]).wait()
        return carry

    lax.fori_loop(0, block, finish, 0, unroll=4)
    rows = both_buf[slot, :, :tile_rows, :]
    out_ref[:, :tile_rows, :] = jnp.where(col_ref[0] > 0, rows, jnp.zeros_like(rows))
    out_ref[:, tile_rows:, :] = (
        both_buf[slot, :, tile_rows:, :].astype(jnp.float32) * col_ref[1]
    ).astype(out_ref.dtype)


def dispatch_rows(slot_token, rows, grads, valid, gate, block=256):
    slots = slot_token.shape[0]
    count, width = rows.shape
    tile_rows = width // 128
    cols = jnp.broadcast_to(jnp.stack([valid, gate])[:, :, None, None], (2, slots, 1, 128))
    both = jnp.concatenate([rows, grads], 1).reshape(count, 2 * tile_rows, 128)
    out = pl.pallas_call(
        dispatch_kernel,
        out_shape=jax.ShapeDtypeStruct((slots, 2 * tile_rows, 128), rows.dtype),
        grid_spec=pltpu.PrefetchScalarGridSpec(
            num_scalar_prefetch=1,
            grid=(slots // block,),
            in_specs=[
                pl.BlockSpec(memory_space=pl.ANY),
                pl.BlockSpec((2, block, 1, 128), lambda i, tok: (0, i, 0, 0)),
            ],
            out_specs=pl.BlockSpec((block, 2 * tile_rows, 128), lambda i, tok: (i, 0, 0)),
            scratch_shapes=[
                pltpu.VMEM((2, block, 2 * tile_rows, 128), rows.dtype),
                pltpu.SemaphoreType.DMA((2, block)),
            ],
        ),
        compiler_params=pltpu.CompilerParams(dimension_semantics=("arbitrary",)),
        cost_estimate=pl.CostEstimate(
            flops=slots * width, transcendentals=0, bytes_accessed=4 * slots * 2 * width
        ),
    )(slot_token, both, cols)
    return out


def combine_kernel(
    slot_ref, out_hbm, back_hbm, gate_ref, grad_ref, shared_out_ref, shared_back_ref,
    feed_ref, back_ref, part_ref, picked_out, picked_back, sems,
):
    top = picked_out.shape[1]
    block = picked_out.shape[2]
    last = out_hbm.shape[0] - 1
    step = pl.program_id(0)
    steps = pl.num_programs(0)

    def fetch(index, buf):
        def start(r, carry):
            for k in range(top):
                slot = jnp.clip(slot_ref[(index * block + r) * top + k], 0, last)
                pltpu.make_async_copy(
                    out_hbm.at[slot], picked_out.at[buf, k, r], sems.at[buf, 0, k, r]
                ).start()
                pltpu.make_async_copy(
                    back_hbm.at[slot], picked_back.at[buf, k, r], sems.at[buf, 1, k, r]
                ).start()
            return carry

        lax.fori_loop(0, block, start, 0, unroll=4)

    @pl.when(step == 0)
    def _():
        fetch(0, 0)

    @pl.when(step + 1 < steps)
    def _():
        fetch(step + 1, (step + 1) % 2)

    now = step % 2

    def finish(r, carry):
        for k in range(top):
            pltpu.make_async_copy(out_hbm.at[0], picked_out.at[now, k, r], sems.at[now, 0, k, r]).wait()
            pltpu.make_async_copy(back_hbm.at[0], picked_back.at[now, k, r], sems.at[now, 1, k, r]).wait()
        return carry

    lax.fori_loop(0, block, finish, 0, unroll=4)
    grad = grad_ref[...].astype(jnp.float32)
    weighted = None
    backs = None
    lanes = lax.broadcasted_iota(jnp.int32, part_ref.shape, 2)
    parts = jnp.zeros(part_ref.shape, jnp.float32)
    for k in range(top):
        out_k = picked_out[now, k].astype(jnp.float32)
        term = gate_ref[k] * out_k
        weighted = term if weighted is None else weighted + term
        back_k = picked_back[now, k].astype(jnp.float32)
        backs = back_k if backs is None else backs + back_k
        dot_k = jnp.sum(jnp.sum(grad * out_k, 2, keepdims=True), 1, keepdims=True)
        parts = jnp.where(lanes == k, dot_k, parts)
    feed_ref[...] = (shared_out_ref[...] + weighted).astype(feed_ref.dtype)
    back_ref[...] = (backs + shared_back_ref[...]).astype(back_ref.dtype)
    part_ref[...] = parts


def combine_rows(slot_index, out_table, back_table, gate_values, grad, shared_out, shared_back, block=128):
    tokens, top = gate_values.shape
    width = grad.shape[1]
    tile_rows = width // 128
    gates = jnp.broadcast_to(gate_values.T[:, :, None, None], (top, tokens, 1, 128))
    row_spec = pl.BlockSpec((block, tile_rows, 128), lambda i, s: (i, 0, 0))
    feed, back, parts = pl.pallas_call(
        combine_kernel,
        out_shape=(
            jax.ShapeDtypeStruct((tokens, tile_rows, 128), jnp.bfloat16),
            jax.ShapeDtypeStruct((tokens, tile_rows, 128), jnp.bfloat16),
            jax.ShapeDtypeStruct((tokens, 1, 128), jnp.float32),
        ),
        grid_spec=pltpu.PrefetchScalarGridSpec(
            num_scalar_prefetch=1,
            grid=(tokens // block,),
            in_specs=[
                pl.BlockSpec(memory_space=pl.ANY),
                pl.BlockSpec(memory_space=pl.ANY),
                pl.BlockSpec((top, block, 1, 128), lambda i, s: (0, i, 0, 0)),
                row_spec,
                row_spec,
                row_spec,
            ],
            out_specs=[row_spec, row_spec, pl.BlockSpec((block, 1, 128), lambda i, s: (i, 0, 0))],
            scratch_shapes=[
                pltpu.VMEM((2, top, block, tile_rows, 128), out_table.dtype),
                pltpu.VMEM((2, top, block, tile_rows, 128), back_table.dtype),
                pltpu.SemaphoreType.DMA((2, 2, top, block)),
            ],
        ),
        compiler_params=pltpu.CompilerParams(dimension_semantics=("arbitrary",)),
        cost_estimate=pl.CostEstimate(
            flops=8 * tokens * top * width,
            transcendentals=0,
            bytes_accessed=tokens * (top * 4 * width + 2 * width + 8 * width + 4 * width),
        ),
    )(
        slot_index.reshape(-1),
        out_table,
        back_table,
        gates,
        grad.reshape(tokens, tile_rows, 128),
        shared_out.reshape(tokens, tile_rows, 128),
        shared_back.reshape(tokens, tile_rows, 128),
    )
    return feed.reshape(tokens, width), back.reshape(tokens, width), parts[:, 0, :top]


def shards(
    hidden,
    routes,
    prefix,
    attn_gain,
    query_proj,
    latent_proj,
    latent_gain,
    expand_proj,
    output_proj,
    second_gain,
    router_proj,
    expert_gate,
    expert_up,
    expert_down,
    shared_gate,
    shared_up,
    shared_down,
    out_grad,
):
    tok_dev = hidden.shape[0]
    tensor_size = lax.axis_size("tensor")
    tensor_rank = lax.axis_index("tensor")
    dp_size = lax.axis_size("dp")
    seq_len = tok_dev * tensor_size
    start_row = tensor_rank * tok_dev
    rows_dp = attn_gain.shape[0]
    kv_rows = latent_gain.shape[0]
    head_cols = query_proj.shape[1]
    latent_cols = latent_proj.shape[1]
    expand_cols = expand_proj.shape[1]
    expand_flat_cols = kv_rows * expand_cols // rows_dp
    first_pack = jnp.concatenate(
        [
            query_proj,
            latent_proj,
            expand_proj.reshape(rows_dp, expand_flat_cols),
            attn_gain[:, None],
            jnp.pad(latent_gain, (0, rows_dp - kv_rows))[:, None],
        ],
        1,
    )
    first_all = lax.all_gather(first_pack, "dp", axis=0, tiled=True)
    cut = [0]
    for width in (head_cols, latent_cols, expand_flat_cols, 1, 1):
        cut.append(cut[-1] + width)
    query_weights = first_all[:, cut[0] : cut[1]]
    latent_weights = first_all[:, cut[1] : cut[2]]
    expand_weights = first_all[:, cut[2] : cut[3]].reshape(dp_size * kv_rows, expand_cols)
    attn_gains = first_all[:, cut[3]]
    kv_gains = first_all[:, cut[4]].reshape(dp_size, rows_dp)[:, :kv_rows].reshape(-1)
    out_cols = output_proj.shape[0]
    experts = router_proj.shape[1]
    shared_cols = shared_gate.shape[1]
    second_pack = jnp.concatenate([output_proj.T, second_gain[:, None], router_proj], 1)
    second_all = lax.all_gather(second_pack, "dp", axis=0, tiled=True)
    output_weights_t = second_all[:, :out_cols]
    second_gains = second_all[:, out_cols]
    router_weights = second_all[:, out_cols + 1 :]
    shared_local = jnp.concatenate([shared_gate, shared_up, shared_down.T], 1)

    hidden_all = lax.all_gather(hidden, "tensor", axis=0, tiled=True)
    grad_blocks = jnp.broadcast_to(out_grad[None], (tensor_size,) + out_grad.shape)
    grad_blocks, hidden_all = lax.optimization_barrier((grad_blocks, hidden_all))
    grad_seq = lax.all_to_all(
        grad_blocks, "tensor", split_axis=0, concat_axis=0, tiled=True
    ).reshape(tensor_size * tok_dev, D)
    grad_seq, query_weights, latent_weights = lax.optimization_barrier(
        (grad_seq, query_weights, latent_weights)
    )
    hidden_all_f = hidden_all.astype(jnp.float32)
    scale_one_all = norm_scale(hidden_all_f)
    gain_one = attn_gains.astype(jnp.float32)
    normed_all = (hidden_all_f * scale_one_all * gain_one).astype(jnp.bfloat16)
    hidden_f = lax.dynamic_slice_in_dim(hidden_all_f, start_row, tok_dev, 0)
    scale_one = lax.dynamic_slice_in_dim(scale_one_all, start_row, tok_dev, 0)
    normed_own = lax.dynamic_slice_in_dim(normed_all, start_row, tok_dev, 0)
    latent_raw_all = jnp.dot(normed_all, latent_weights, preferred_element_type=jnp.float32)
    compressed_all = latent_raw_all[:, :KVR]
    scale_kv_all = norm_scale(compressed_all)
    gain_kv = kv_gains.astype(jnp.float32)
    all_cosines, all_sines = rope_tables(jnp.arange(seq_len), DR)
    latent_seq = jnp.concatenate(
        [
            compressed_all * scale_kv_all * gain_kv,
            rotate(latent_raw_all[:, KVR:], all_cosines, all_sines),
        ],
        -1,
    ).astype(jnp.bfloat16)
    compressed = lax.dynamic_slice_in_dim(compressed_all, start_row, tok_dev, 0)
    scale_kv = lax.dynamic_slice_in_dim(scale_kv_all, start_row, tok_dev, 0)
    own_cosines = lax.dynamic_slice_in_dim(all_cosines, start_row, tok_dev, 0)
    own_sines = lax.dynamic_slice_in_dim(all_sines, start_row, tok_dev, 0)
    head_count = query_weights.shape[1] // (DN + DR)
    query_raw = jnp.dot(normed_all, query_weights, preferred_element_type=jnp.float32).reshape(
        seq_len, head_count, DN + DR
    )
    query_low = jnp.concatenate(
        [
            query_raw[..., :DN],
            rotate(query_raw[..., DN:], all_cosines[:, None, :], all_sines[:, None, :]),
        ],
        -1,
    ).astype(jnp.bfloat16)
    compressed_seq = latent_seq[:, :KVR]
    key_rope = latent_seq[:, KVR:]
    expanded = jnp.dot(compressed_seq, expand_weights, preferred_element_type=jnp.float32).reshape(
        seq_len, head_count, DN + DV
    )
    keys_nope = expanded[..., :DN].astype(jnp.bfloat16)
    values_low = expanded[..., DN:].astype(jnp.bfloat16)
    score_scale = 1.0 / math.sqrt(DN + DR)
    block_rows = min(512, seq_len)
    prefix_len = prefix[0]
    lse_list = []
    mixed_list = []
    for rows_start in range(0, seq_len, block_rows):
        query_block = query_low[rows_start : rows_start + block_rows]
        masked = block_scores(query_block, keys_nope, key_rope, rows_start, prefix_len, score_scale)
        top_score = jnp.max(masked, -1, keepdims=True)
        exp_scores = jnp.exp(masked - top_score)
        totals = jnp.sum(exp_scores, -1, keepdims=True)
        prob_low = (exp_scores / totals).astype(jnp.bfloat16)
        lse_list.append(top_score + jnp.log(totals))
        mixed_list.append(
            jnp.einsum(
                "hqk,khv->qhv", prob_low, values_low, preferred_element_type=jnp.float32
            ).astype(jnp.bfloat16)
        )
    mixed_all = jnp.concatenate(mixed_list, 0).reshape(seq_len, head_count * DV)
    attn_part = jnp.einsum(
        "tk,dk->td", mixed_all, output_weights_t, preferred_element_type=jnp.float32
    )
    top_count = routes.shape[1]
    chosen_hot = routes[:, :, None] == jnp.arange(experts)[None, None, :]
    assignments = seq_len * top_count
    flat_hot = chosen_hot.reshape(assignments, experts).astype(jnp.bfloat16)
    lower = (jnp.arange(assignments)[:, None] > jnp.arange(assignments)[None, :]).astype(jnp.bfloat16)
    earlier = jnp.dot(lower, flat_hot, preferred_element_type=jnp.float32)
    slot_pos = jnp.sum(earlier * flat_hot.astype(jnp.float32), -1).astype(jnp.int32)
    expert_ids = routes.reshape(-1)
    exp_dev = expert_gate.shape[0]
    capacity = tensor_size * (5 * seq_len * top_count // (4 * experts * tensor_size))
    slot_index = expert_ids * capacity + slot_pos
    token_ids = jnp.arange(seq_len * top_count) // top_count
    slot_token = jnp.full((experts * capacity,), seq_len, jnp.int32).at[slot_index].set(token_ids)
    slot_valid = (slot_token < seq_len).astype(jnp.float32)
    slot_index, slot_token, slot_valid, attn_part = lax.optimization_barrier(
        (slot_index, slot_token, slot_valid, attn_part)
    )
    branch_all = lax.psum(attn_part.astype(jnp.bfloat16), "tensor").astype(jnp.float32)
    shared_local, branch_all = lax.optimization_barrier((shared_local, branch_all))
    residual_all = hidden_all_f + branch_all
    residual_own = lax.dynamic_slice_in_dim(residual_all, start_row, tok_dev, 0)
    scale_two = norm_scale(residual_all)
    gain_two = second_gains.astype(jnp.float32)
    normed_two = (residual_all * scale_two * gain_two).astype(jnp.bfloat16)
    logits = jnp.dot(normed_two, router_weights, preferred_element_type=jnp.float32)
    chosen_logits = jnp.sum(jnp.where(chosen_hot, logits[:, None, :], 0.0), -1)
    gate_values = jax.nn.softmax(chosen_logits, axis=-1)
    slot_gate = (
        jnp.zeros((experts * capacity,), jnp.float32).at[slot_index].set(gate_values.reshape(-1))
    )
    tile_rows = D // 128
    send_both = dispatch_rows(slot_token, normed_two, grad_seq, slot_valid, slot_gate).reshape(
        dp_size, exp_dev, capacity, 2 * tile_rows, 128
    )
    shared_all = lax.all_gather(shared_local, "dp", axis=0, tiled=True)
    shared_all, send_both = lax.optimization_barrier((shared_all, send_both))
    gate_shared = shared_all[:, :shared_cols]
    up_shared = shared_all[:, shared_cols : 2 * shared_cols]
    down_shared_t = shared_all[:, 2 * shared_cols :]
    recv_both = lax.all_to_all(send_both, "dp", split_axis=0, concat_axis=0, tiled=True)
    recv_both = recv_both.reshape(dp_size, exp_dev, capacity, 2 * D)
    recv_rows = recv_both[..., :D]
    recv_grads = recv_both[..., D:]
    gate_pre = jnp.einsum(
        "sjcd,jfd->sjcf", recv_rows, expert_gate, preferred_element_type=jnp.float32
    )
    up_pre = jnp.einsum("sjcd,jfd->sjcf", recv_rows, expert_up, preferred_element_type=jnp.float32)
    sigmoid_gate = jax.nn.sigmoid(gate_pre)
    expert_act = (gate_pre * sigmoid_gate * up_pre).astype(jnp.bfloat16)
    expert_out = jnp.einsum(
        "sjcf,jfd->sjcd", expert_act, expert_down, preferred_element_type=jnp.float32
    )
    back_out = lax.all_to_all(
        expert_out.astype(jnp.bfloat16).reshape(dp_size, exp_dev, capacity, tile_rows, 128),
        "dp",
        split_axis=0,
        concat_axis=0,
        tiled=True,
    )
    act_grad = jnp.einsum(
        "sjcd,jfd->sjcf", recv_grads, expert_down, preferred_element_type=jnp.float32
    )
    gate_low_grad, up_low_grad = silu_back(act_grad, gate_pre, up_pre, sigmoid_gate)
    expert_down_grad = jnp.einsum(
        "sjcf,sjcd->jfd", expert_act, recv_grads, preferred_element_type=jnp.float32
    )
    expert_gate_grad = jnp.einsum(
        "sjcf,sjcd->jfd", gate_low_grad, recv_rows, preferred_element_type=jnp.float32
    )
    expert_up_grad = jnp.einsum(
        "sjcf,sjcd->jfd", up_low_grad, recv_rows, preferred_element_type=jnp.float32
    )
    row_grads = jnp.einsum(
        "sjcf,jfd->sjcd", gate_low_grad, expert_gate, preferred_element_type=jnp.float32
    )
    row_grads = row_grads + jnp.einsum(
        "sjcf,jfd->sjcd", up_low_grad, expert_up, preferred_element_type=jnp.float32
    )
    grads_low = row_grads.astype(jnp.bfloat16).reshape(dp_size, exp_dev, capacity, tile_rows, 128)
    back_out, grads_low = lax.optimization_barrier((back_out, grads_low))
    back_grads = lax.all_to_all(
        grads_low,
        "dp",
        split_axis=0,
        concat_axis=0,
        tiled=True,
    )
    shared_pre_gate = jnp.dot(normed_two, gate_shared, preferred_element_type=jnp.float32)
    shared_pre_up = jnp.dot(normed_two, up_shared, preferred_element_type=jnp.float32)
    shared_sigmoid = jax.nn.sigmoid(shared_pre_gate)
    shared_act = (shared_pre_gate * shared_sigmoid * shared_pre_up).astype(jnp.bfloat16)
    shared_out = jnp.einsum(
        "tf,df->td", shared_act, down_shared_t, preferred_element_type=jnp.float32
    )
    shared_act_grad = jnp.dot(grad_seq, down_shared_t, preferred_element_type=jnp.float32)
    shared_gate_low, shared_up_low = silu_back(
        shared_act_grad, shared_pre_gate, shared_pre_up, shared_sigmoid
    )
    shared_down_grad_t = jnp.dot(grad_seq.T, shared_act, preferred_element_type=jnp.float32)
    shared_gate_grad = jnp.dot(normed_two.T, shared_gate_low, preferred_element_type=jnp.float32)
    shared_up_grad = jnp.dot(normed_two.T, shared_up_low, preferred_element_type=jnp.float32)
    shared_back = jnp.einsum(
        "tf,df->td", shared_gate_low, gate_shared, preferred_element_type=jnp.float32
    )
    shared_back = shared_back + jnp.einsum(
        "tf,df->td", shared_up_low, up_shared, preferred_element_type=jnp.float32
    )
    shared_grads_in = jnp.concatenate(
        [shared_gate_grad, shared_up_grad, shared_down_grad_t], 1
    ).astype(jnp.bfloat16)
    grad_seq_f = grad_seq.astype(jnp.float32)
    table_rows = experts * capacity
    feed_part, back_part, gate_cols = combine_rows(
        slot_index.reshape(seq_len, top_count),
        back_out.reshape(table_rows, tile_rows, 128),
        back_grads.reshape(table_rows, tile_rows, 128),
        gate_values,
        grad_seq,
        shared_out,
        shared_back,
    )
    gate_part = gate_cols[:, :top_count]
    feed_own = jnp.sum(
        lax.all_to_all(
            feed_part.reshape(tensor_size, tok_dev, D), "tensor", split_axis=0, concat_axis=0, tiled=True
        ).astype(jnp.float32),
        0,
    )
    reduced_back = lax.psum(
        jnp.concatenate([back_part, gate_cols.astype(jnp.bfloat16)], 1), "tensor"
    ).astype(jnp.float32)
    normed_two_grad = reduced_back[:, :D]
    gate_grads = reduced_back[:, D : D + top_count]
    weighted_total = jnp.sum(gate_values * gate_grads, -1, keepdims=True)
    chosen_grads = gate_values * (gate_grads - weighted_total)
    logit_grads = jnp.sum(jnp.where(chosen_hot, chosen_grads[:, :, None], 0.0), 1)
    normed_two_grad = normed_two_grad + jnp.dot(
        logit_grads, router_weights.astype(jnp.float32).T, precision=HIGH
    )
    residual_grad = grad_seq_f + norm_back(residual_all, scale_two, gain_two, normed_two_grad)
    branch_grad = residual_grad.astype(jnp.bfloat16)
    shared_grads_in, branch_grad = lax.optimization_barrier((shared_grads_in, branch_grad))
    shared_pack = jnp.sum(
        lax.all_to_all(
            shared_grads_in.reshape(dp_size, rows_dp, shared_grads_in.shape[1]),
            "dp",
            split_axis=0,
            concat_axis=0,
            tiled=True,
        ).astype(jnp.float32),
        0,
    )
    output_grad_w_t = jnp.dot(branch_grad.T, mixed_all, preferred_element_type=jnp.float32)
    mixed_grad = (
        jnp.dot(branch_grad, output_weights_t, preferred_element_type=jnp.float32)
        .astype(jnp.bfloat16)
        .reshape(seq_len, head_count, DV)
    )
    keys_nope_grad = jnp.zeros((seq_len, head_count, DN), jnp.float32)
    key_rope_grad = jnp.zeros((seq_len, DR), jnp.float32)
    values_grad = jnp.zeros((seq_len, head_count, DV), jnp.float32)
    query_grad_list = []
    for block_index, rows_start in enumerate(range(0, seq_len, block_rows)):
        query_block = query_low[rows_start : rows_start + block_rows]
        masked = block_scores(query_block, keys_nope, key_rope, rows_start, prefix_len, score_scale)
        prob_full = jnp.exp(masked - lse_list[block_index])
        prob_low = prob_full.astype(jnp.bfloat16)
        mixed_block = mixed_grad[rows_start : rows_start + block_rows]
        prob_grads = jnp.einsum(
            "qhv,khv->hqk", mixed_block, values_low, preferred_element_type=jnp.float32
        )
        row_delta = jnp.sum(prob_full * prob_grads, -1, keepdims=True)
        score_grads = (prob_full * (prob_grads - row_delta)).astype(jnp.bfloat16)
        query_nope_grad = (
            jnp.einsum("hqk,khd->qhd", score_grads, keys_nope, preferred_element_type=jnp.float32)
            * score_scale
        )
        query_rope_grad = (
            jnp.einsum("hqk,kr->qhr", score_grads, key_rope, preferred_element_type=jnp.float32)
            * score_scale
        )
        keys_nope_grad = (
            keys_nope_grad
            + jnp.einsum(
                "hqk,qhd->khd",
                score_grads,
                query_block[..., :DN],
                preferred_element_type=jnp.float32,
            )
            * score_scale
        )
        key_rope_grad = (
            key_rope_grad
            + jnp.einsum(
                "hqk,qhr->kr",
                score_grads,
                query_block[..., DN:],
                preferred_element_type=jnp.float32,
            )
            * score_scale
        )
        values_grad = values_grad + jnp.einsum(
            "hqk,qhv->khv", prob_low, mixed_block, preferred_element_type=jnp.float32
        )
        block_cosines = all_cosines[rows_start : rows_start + block_rows, None, :]
        block_sines = all_sines[rows_start : rows_start + block_rows, None, :]
        query_grad_list.append(
            jnp.concatenate(
                [
                    query_nope_grad,
                    rotate_back(round_trip(query_rope_grad), block_cosines, block_sines),
                ],
                -1,
            ).astype(jnp.bfloat16)
        )
    query_grads = jnp.concatenate(query_grad_list, 0).reshape(seq_len, head_count * (DN + DR))
    feed_own, shared_pack, query_grads = lax.optimization_barrier((feed_own, shared_pack, query_grads))
    output = (residual_own + feed_own).astype(jnp.bfloat16)
    query_grad_w = jnp.dot(normed_all.T, query_grads, preferred_element_type=jnp.float32)
    normed_grad_part = jnp.dot(query_grads, query_weights.T, preferred_element_type=jnp.float32)
    expand_grads = jnp.concatenate(
        [keys_nope_grad.astype(jnp.bfloat16), values_grad.astype(jnp.bfloat16)], -1
    ).reshape(seq_len, head_count * (DN + DV))
    expand_grad_w = jnp.dot(compressed_seq.T, expand_grads, preferred_element_type=jnp.float32)
    compressed_grad_part = jnp.dot(
        expand_grads, expand_weights.T, preferred_element_type=jnp.float32
    )
    latent_grad_part = jnp.concatenate([compressed_grad_part, key_rope_grad], -1)
    attn_grads_in = jnp.concatenate(
        [
            query_grad_w,
            output_grad_w_t,
            expand_grad_w.reshape(dp_size * rows_dp, expand_flat_cols),
        ],
        1,
    )
    token_all = lax.psum(
        jnp.concatenate([normed_grad_part, latent_grad_part], 1).astype(jnp.bfloat16), "tensor"
    ).astype(jnp.float32)
    compressed_grad_all = token_all[:, D : D + KVR]
    kv_gain_full = jnp.sum(compressed_grad_all * compressed_all * scale_kv_all, 0)
    raw_grad_all = jnp.concatenate(
        [
            norm_back(compressed_all, scale_kv_all, gain_kv, compressed_grad_all),
            rotate_back(token_all[:, D + KVR :], all_cosines, all_sines),
        ],
        -1,
    ).astype(jnp.bfloat16)
    normed_grad_all = token_all[:, :D] + jnp.dot(
        raw_grad_all, latent_weights.T, preferred_element_type=jnp.float32
    )
    normed_grad = lax.dynamic_slice_in_dim(normed_grad_all, start_row, tok_dev, 0)
    hidden_grad = lax.dynamic_slice_in_dim(residual_grad, start_row, tok_dev, 0) + norm_back(
        hidden_f, scale_one, gain_one, normed_grad
    )
    row_per = D // (dp_size * tensor_size)

    def own_rows(values):
        split = values.reshape(values.shape[0], dp_size, tensor_size, row_per)
        return lax.dynamic_slice_in_dim(split, tensor_rank, 1, 2).reshape(values.shape[0], -1)

    latent_rows = jnp.dot(own_rows(normed_all).T, raw_grad_all, preferred_element_type=jnp.float32)
    attn_gain_rows = jnp.sum(
        own_rows(normed_grad_all) * own_rows(hidden_all_f) * scale_one_all, 0
    )
    second_gain_rows = jnp.sum(
        own_rows(normed_two_grad) * own_rows(residual_all) * scale_two, 0
    )
    router_rows = jnp.dot(
        own_rows(normed_two).astype(jnp.float32).T, logit_grads, precision=HIGH
    )
    kv_per = kv_gain_full.shape[0] // (dp_size * tensor_size)
    kv_rows_own = lax.dynamic_slice_in_dim(
        kv_gain_full.reshape(dp_size, tensor_size, kv_per), tensor_rank, 1, 1
    ).reshape(dp_size, kv_per)
    kv_column = jnp.pad(kv_rows_own, ((0, 0), (0, row_per - kv_per))).reshape(-1)
    small_pack = jnp.concatenate(
        [
            latent_rows,
            router_rows,
            attn_gain_rows[:, None],
            second_gain_rows[:, None],
            kv_column[:, None],
        ],
        1,
    )
    attn_width = attn_grads_in.shape[1]
    small_width = small_pack.shape[1]
    small_count = row_per * small_width
    small_cols = -(-small_count // rows_dp)
    small_flat = jnp.pad(
        small_pack.reshape(dp_size, small_count), ((0, 0), (0, small_cols * rows_dp - small_count))
    ).reshape(dp_size * rows_dp, small_cols)
    merged_own = lax.psum_scatter(
        jnp.concatenate([attn_grads_in, small_flat], 1), "dp", scatter_dimension=0, tiled=True
    )
    attn_pack = merged_own[:, :attn_width]
    small_own = merged_own[:, attn_width:].reshape(-1)[:small_count].reshape(row_per, small_width)
    cut = [0]
    for width in (latent_cols, experts, 1, 1, 1):
        cut.append(cut[-1] + width)
    latent_proj_grad = small_own[:, cut[0] : cut[1]]
    router_out = small_own[:, cut[1] : cut[2]]
    attn_gain_out = small_own[:, cut[2]]
    second_gain_out = small_own[:, cut[3]]
    latent_gain_out = small_own[:kv_per, cut[4]]
    cut = [0]
    for width in (head_cols, out_cols, expand_flat_cols):
        cut.append(cut[-1] + width)
    query_proj_grad = attn_pack[:, cut[0] : cut[1]]
    output_proj_grad = attn_pack[:, cut[1] : cut[2]].T
    expand_proj_grad = attn_pack[:, cut[2] : cut[3]].reshape(kv_rows, expand_cols)
    shared_gate_out = shared_pack[:, :shared_cols]
    shared_up_out = shared_pack[:, shared_cols : 2 * shared_cols]
    shared_down_out = shared_pack[:, 2 * shared_cols :].T
    return (
        output,
        hidden_grad,
        attn_gain_out,
        query_proj_grad,
        latent_proj_grad,
        latent_gain_out,
        expand_proj_grad,
        output_proj_grad,
        second_gain_out,
        router_out,
        expert_gate_grad,
        expert_up_grad,
        expert_down_grad,
        shared_gate_out,
        shared_up_out,
        shared_down_out,
    )


def solution(mesh):
    return jax.shard_map(
        shards,
        mesh=mesh,
        in_specs=(
            P(("dp", "tensor"), None),
            P("dp", None),
            P("dp"),
            P("dp"),
            P("dp", "tensor"),
            P("dp", None),
            P("dp"),
            P("dp", "tensor"),
            P("tensor", "dp"),
            P("dp"),
            P("dp", None),
            P("dp", "tensor", None),
            P("dp", "tensor", None),
            P("dp", "tensor", None),
            P("dp", "tensor"),
            P("dp", "tensor"),
            P("tensor", "dp"),
            P(("dp", "tensor"), None),
        ),
        out_specs=(
            P(("dp", "tensor"), None),
            P(("dp", "tensor"), None),
            P(("dp", "tensor")),
            P("dp", "tensor"),
            P(("dp", "tensor"), None),
            P(("dp", "tensor")),
            P("dp", "tensor"),
            P("tensor", "dp"),
            P(("dp", "tensor")),
            P(("dp", "tensor"), None),
            P("dp", "tensor", None),
            P("dp", "tensor", None),
            P("dp", "tensor", None),
            P("dp", "tensor"),
            P("dp", "tensor"),
            P("tensor", "dp"),
        ),
        check_vma=False,
    )
```
